32 devices in a mesh: rep: 2 (over y), fsdp: 16 (over z, x, core).
Axes of the slice: x: 2, y: 2, z: 4, core: 2. Of those that a mesh axis runs over, the one named last changes fastest.
Arguments:
- block_input: bfloat16 [24576, 768], P(('rep', 'fsdp')), may hold values from -6 to 6
- cotangent: bfloat16 [24576, 768], P(('rep', 'fsdp')), may hold values from -6 to 6
- tie_index: int32 [1], replicated, may hold values from 0 to 11
- prefix_len: int32 [32, 1], P(('rep', 'fsdp')), may hold values from 1 to 2048, as said below
- pre_gain: bfloat16 [12, 768], P(None, 'fsdp'), may hold values from 0.5 to 1.5
- pre_shift: bfloat16 [12, 768], P(None, 'fsdp'), may hold values from -1.75 to 1.75
- w_qkv: bfloat16 [12, 768, 2304], P(None, 'fsdp'), may hold values from -0.3125 to 0.3125
- b_qv: bfloat16 [12, 1536], P(None, 'fsdp'), may hold values from -1.75 to 1.75
- w_out: bfloat16 [12, 768, 768], P(None, 'fsdp'), may hold values from -1.25 to 1.25
- b_out: bfloat16 [12, 768], P(None, 'fsdp'), may hold values from -1.75 to 1.75
- mid_gain: bfloat16 [12, 768], P(None, 'fsdp'), may hold values from 0.5 to 1.5
- mid_shift: bfloat16 [12, 768], P(None, 'fsdp'), may hold values from -1.75 to 1.75
- w_fc: bfloat16 [12, 768, 3072], P(None, 'fsdp'), may hold values from -0.21875 to 0.21875
- b_fc: bfloat16 [12, 3072], P(None, 'fsdp'), may hold values from -1.75 to 1.75
- w_proj: bfloat16 [12, 3072, 768], P(None, 'fsdp'), may hold values from -0.109375 to 0.109375
- b_proj: bfloat16 [12, 768], P(None, 'fsdp'), may hold values from -1.75 to 1.75
Outputs:
- block_output: bfloat16 [24576, 768], P(('rep', 'fsdp'))
- input_grad: float32 [24576, 768], P(('rep', 'fsdp'))
- dpre_gain: float32 [768], P('fsdp')
- dpre_shift: float32 [768], P('fsdp')
- dw_qkv: float32 [768, 2304], P('fsdp')
- db_qv: float32 [1536], P('fsdp')
- dw_out: float32 [768, 768], P('fsdp')
- db_out: float32 [768], P('fsdp')
- dmid_gain: float32 [768], P('fsdp')
- dmid_shift: float32 [768], P('fsdp')
- dw_fc: float32 [768, 3072], P('fsdp')
- db_fc: float32 [3072], P('fsdp')
- dw_proj: float32 [3072, 768], P('fsdp')
- db_proj: float32 [768], P('fsdp')
The draws below stay inside these ranges and needn't reach their ends.
Inputs may be any that keep to these rules, and one draw needn't show every extreme that they name: `tie_index`: the entry of every bank that the block uses. `prefix_len`: row d holds, for each continuation on device d of rep+fsdp in order, how many of its group's first prompt tokens it attends to; on the last device of every group the last continuation attends to all 2048.
All inputs are finite; a program needn't handle non-finite values.
Results may differ from the reference program's by a relative error of at most 0.014.
Values may be sent and summed in bfloat16 or wider, within the bound.
A program may use at most 256 MiB of HBM per device.

```python
import jax
import jax.numpy as jnp
from jax import lax

D = 768
HEADS = 12
HEAD = 64
FF = 3072
BANK = 12
GROUP_DEV = 4
CONT = 256
PROMPT_DEV = 512
CONT_DEV = 1
PROMPT = 2048
NCONT = 4
TOK_DEV = 768
GROUPS = 8
TOKENS = 24576


def draw_prefix_len(key, part):
    row_count = GROUPS * GROUP_DEV
    reaches = jax.random.randint(key, (row_count, CONT_DEV), 1, PROMPT + 1)
    last_row = jnp.arange(row_count)[:, None] % GROUP_DEV == GROUP_DEV - 1
    last_col = jnp.arange(CONT_DEV)[None, :] == CONT_DEV - 1
    return jnp.where(last_row & last_col, PROMPT, reaches).astype(jnp.int32)


def spiked(entries, key, source, target, shards_of, factor):
    def block_of(dim):
        return (jnp.arange(entries.shape[dim]) // (entries.shape[dim] // shards_of)).reshape((-1,) + (1,) * (entries.ndim - 1 - dim))

    first = jax.random.permutation(key, shards_of)[block_of(target)]
    far = (block_of(target) + shards_of // 2) % shards_of
    return jnp.where((block_of(source) == first) | (block_of(source) == far), factor * entries, entries)


def levels(stream_key, extent, split, least, largest):
    def one(position, shards_of):
        draws = jax.random.uniform(jax.random.fold_in(jax.random.fold_in(stream_key, 6), position), (shards_of,), jnp.float32, least / len(split), largest / len(split))
        return jnp.repeat(jnp.exp(draws), extent[position] // shards_of).reshape((-1,) + (1,) * (len(extent) - position - 1))

    level = one(*split[0])
    for cut in split[1:]:
        level = level * one(*cut)
    return level


def bell_draw(rng, dims, width, limit, cuts=(), kind=jnp.bfloat16):
    values = width * jax.random.normal(rng, dims, jnp.float32)
    if cuts:
        values = values * levels(rng, dims, cuts, -0.22, 0.18)
    return jnp.clip(values, -limit, limit).astype(kind)


def gaussian_with(rng, extent, scale, limit, shards, heavy, held_as=jnp.bfloat16):
    array = scale * jax.random.normal(rng, extent, jnp.float32)
    if shards:
        array = array * levels(rng, extent, shards, -0.22, 0.18)
    return jnp.clip(spiked(array, jax.random.fold_in(rng, 3), *heavy), -limit, limit).astype(held_as)


def setup_inputs(seed: int = 0) -> dict:
    seeds = jax.random.split(jax.random.key(seed), 17)
    block_input = gaussian_with(seeds[0], (TOKENS, D), 1.0, 6.0, ((0, 32),), (0, 1, 32, 2.75))
    cotangent = gaussian_with(seeds[1], (TOKENS, D), 1.0, 6.0, ((0, 32),), (0, 1, 32, 2.75))
    tie_index = jax.random.randint(seeds[2], (1,), 0, BANK).astype(jnp.int32)
    prefix_len = draw_prefix_len(jax.random.fold_in(seeds[16], 71), 0)
    pre_gain = jnp.clip(1.0 + 0.1 * jax.random.normal(seeds[4], (BANK, D), jnp.float32), 0.5, 1.5).astype(jnp.bfloat16)
    pre_shift = bell_draw(seeds[5], (BANK, D), 0.3, 1.75, ((1, 16),))
    w_qkv = bell_draw(seeds[6], (BANK, D, 3 * D), (D // 2) ** -0.5, 0.3125, ((1, 16),))
    b_qv = bell_draw(seeds[7], (BANK, 2 * D), 0.3, 1.75, ((1, 16),))
    w_out = bell_draw(seeds[8], (BANK, D, D), (D // 32) ** -0.5, 1.25, ((1, 16),))
    b_out = bell_draw(seeds[9], (BANK, D), 0.3, 1.75, ((1, 16),))
    mid_gain = jnp.clip(1.0 + 0.1 * jax.random.normal(seeds[10], (BANK, D), jnp.float32), 0.5, 1.5).astype(jnp.bfloat16)
    mid_shift = bell_draw(seeds[11], (BANK, D), 0.3, 1.75, ((1, 16),))
    w_fc = bell_draw(seeds[12], (BANK, D, FF), D ** -0.5, 0.21875, ((1, 16),))
    b_fc = bell_draw(seeds[13], (BANK, FF), 0.3, 1.75, ((1, 16),))
    w_proj = bell_draw(seeds[14], (BANK, FF, D), FF ** -0.5, 0.109375, ((1, 16),))
    b_proj = bell_draw(seeds[15], (BANK, D), 0.3, 1.75, ((1, 16),))
    return dict(block_input=block_input, cotangent=cotangent, tie_index=tie_index, prefix_len=prefix_len, pre_gain=pre_gain, pre_shift=pre_shift, w_qkv=w_qkv, b_qv=b_qv, w_out=w_out, b_out=b_out, mid_gain=mid_gain, mid_shift=mid_shift, w_fc=w_fc, b_fc=b_fc, w_proj=w_proj, b_proj=b_proj)


HIGH = lax.Precision.HIGHEST
MASKED = -1e+30

@jax.custom_vjp
def low(v):
    return lax.optimization_barrier(v.astype(jnp.bfloat16)).astype(jnp.float32)

@jax.custom_vjp
def low_back(v):
    return v

def low_keep(v):
    return (low(v), None)

def low_pass(kept, grad):
    return (grad,)

def back_keep(v):
    return (v, None)

def back_low(kept, grad):
    return (low(grad),)
low.defvjp(low_keep, low_pass)
low_back.defvjp(back_keep, back_low)

def layer_norm(values, gain, shift):
    center = values - lax.optimization_barrier(jnp.mean(values, axis=-1, keepdims=True))
    spread = lax.optimization_barrier(jnp.mean(center * center, axis=-1, keepdims=True))
    return center * lax.rsqrt(spread + 1e-05) * gain + shift

def split_heads(matrix):
    return matrix.reshape(matrix.shape[0], HEADS, HEAD).transpose(1, 0, 2)

def attend(queries, keys, values, key_mask):

    def one_head(members):
        head_q, head_k, head_v = members
        scores = low_back(jnp.dot(head_q, head_k.T, precision=HIGH) * 0.125)
        scores = jnp.where(key_mask, scores, MASKED)
        weights = low(jax.nn.softmax(scores, axis=-1))
        return jnp.dot(weights, head_v, precision=HIGH)
    stacked = lax.map(one_head, (split_heads(queries), split_heads(keys), split_heads(values)))
    return stacked.transpose(1, 0, 2).reshape(queries.shape[0], D)

def reference(block_input, cotangent, tie_index, prefix_len, pre_gain, pre_shift, w_qkv, b_qv, w_out, b_out, mid_gain, mid_shift, w_fc, b_fc, w_proj, b_proj):
    chosen_index = tie_index[0].astype(jnp.int32)

    def chosen(bank):
        return lax.dynamic_index_in_dim(bank, chosen_index, 0, keepdims=False).astype(jnp.float32)
    params = tuple((chosen(bank) for bank in (pre_gain, pre_shift, w_qkv, b_qv, w_out, b_out, mid_gain, mid_shift, w_fc, b_fc, w_proj, b_proj)))
    prompt_pos = jnp.arange(PROMPT, dtype=jnp.int32)
    causal_mask = prompt_pos[None, :] <= prompt_pos[:, None]
    cont_pos = jnp.arange(NCONT * CONT, dtype=jnp.int32)
    same_cont = cont_pos[:, None] // CONT == cont_pos[None, :] // CONT
    own_mask = same_cont & (cont_pos[None, :] <= cont_pos[:, None])
    reaches = jnp.repeat(prefix_len.reshape(GROUPS, NCONT), CONT, axis=1)

    def group_attend(members):
        prompt_q, prompt_k, prompt_v, cont_q, cont_k, cont_v, reach_row = members
        prompt_out = attend(prompt_q, prompt_k, prompt_v, causal_mask)
        cont_mask = jnp.concatenate([prompt_pos[None, :] < reach_row[:, None], own_mask], axis=1)
        cont_out = attend(cont_q, jnp.concatenate([prompt_k, cont_k], axis=0), jnp.concatenate([prompt_v, cont_v], axis=0), cont_mask)
        return (prompt_out, cont_out)

    def to_groups(matrix):
        blocked = matrix.reshape(GROUPS, GROUP_DEV, TOK_DEV, D)
        return (blocked[:, :, :PROMPT_DEV].reshape(GROUPS, PROMPT, D), blocked[:, :, PROMPT_DEV:].reshape(GROUPS, NCONT * CONT, D))

    def forward(inputs, gain_one, shift_one, weight_qkv, bias_qv, weight_out, bias_out, gain_two, shift_two, weight_fc, bias_fc, weight_proj, bias_proj):
        normed = low(layer_norm(inputs, gain_one, shift_one))
        mixed = jnp.dot(normed, weight_qkv, precision=HIGH)
        queries = low(low_back(mixed[:, :D] + bias_qv[:D]))
        keys = low(low_back(mixed[:, D:2 * D]))
        values = low(low_back(mixed[:, 2 * D:] + bias_qv[D:]))
        prompt_q, cont_q = to_groups(queries)
        prompt_k, cont_k = to_groups(keys)
        prompt_v, cont_v = to_groups(values)
        checked = jax.checkpoint(group_attend)
        _, outs_pair = lax.scan(lambda carry, members: (carry, checked(members)), None, (prompt_q, prompt_k, prompt_v, cont_q, cont_k, cont_v, reaches))
        prompt_out, cont_out = outs_pair
        joined = jnp.concatenate([prompt_out.reshape(GROUPS, GROUP_DEV, PROMPT_DEV, D), cont_out.reshape(GROUPS, GROUP_DEV, CONT_DEV * CONT, D)], axis=2).reshape(TOKENS, D)
        attended = low(low_back(joined))
        middle = inputs + low_back(jnp.dot(attended, weight_out, precision=HIGH) + bias_out)
        hidden_in = low(layer_norm(middle, gain_two, shift_two))
        gate = low_back(jnp.dot(hidden_in, weight_fc, precision=HIGH) + bias_fc)
        activ = low(jax.nn.gelu(gate, approximate=True))
        return middle + low_back(jnp.dot(activ, weight_proj, precision=HIGH) + bias_proj)
    result, pullback = jax.vjp(forward, block_input.astype(jnp.float32), *params)
    grads = pullback(cotangent.astype(jnp.float32))
    return (result.astype(jnp.bfloat16), grads[0], grads[1], grads[2], grads[3], grads[4], grads[5], grads[6], grads[7], grads[8], grads[9], grads[10], grads[11], grads[12])
```

```python
from functools import partial

import jax
import jax.numpy as jnp
from jax import lax
from jax.experimental import pallas as pl
from jax.experimental.pallas import tpu as pltpu
from jax.sharding import PartitionSpec as P

D = 768
HEADS = 12
HEAD = 64
FF = 3072
GROUP = 4
PROMPT = 512
CONT = 256
TOK = 768
ROWS = GROUP * TOK
OWN = HEADS // GROUP
SLICE = OWN * HEAD
WIDE = 3 * SLICE
PAIR = TOK // 2
CHUNK = 256
NEG = -1e30
EPS = 1e-5
GELU_A = 0.7978845608028654
GELU_B = 0.044715

f32 = jnp.float32
bf16 = jnp.bfloat16
MESH = pl.DeviceIdType.MESH
ANY = pl.BlockSpec(memory_space=pl.ANY)


def params(mib, **more):
    return pltpu.CompilerParams(vmem_limit_bytes=mib << 20, **more)


def dot(a, b):
    return jnp.dot(a, b, preferred_element_type=f32)


def dot_nt(a, b):
    return lax.dot_general(a, b, (((1,), (1,)), ((), ())), preferred_element_type=f32)


def dot_tn(a, b):
    return lax.dot_general(a, b, (((0,), (0,)), ((), ())), preferred_element_type=f32)


def moments(x):
    center = x - jnp.mean(x, axis=-1, keepdims=True)
    scale = lax.rsqrt(jnp.mean(center * center, axis=-1, keepdims=True) + EPS)
    return center * scale, scale


def greet(peers):
    sem = pltpu.get_barrier_semaphore()
    for peer in peers:
        pl.semaphore_signal(sem, inc=1, device_id={"fsdp": peer}, device_id_type=MESH)
    pl.semaphore_wait(sem, len(peers))


def gather_kernel(n, parts, x_ref, w_ref, xg_ref, wg_ref, xs, xr, ws, wr, local):
    me = lax.axis_index("fsdp")
    pos = lax.rem(me, GROUP)
    near, far = me ^ 1, me ^ 2
    greet([me ^ i for i in range(1, n)])
    own = pltpu.make_async_copy(x_ref, xg_ref.at[pos], local.at[0])
    own.start()
    own_w = pltpu.make_async_copy(w_ref.at[pos], wg_ref.at[me], local.at[1])
    own_w.start()
    rows = TOK // parts

    def piece(src, slot, part, i, peer):
        at = pl.ds(part * rows, rows)
        return pltpu.make_async_remote_copy(
            src_ref=src.at[at],
            dst_ref=xg_ref.at[slot, at],
            send_sem=xs.at[i],
            recv_sem=xr.at[i],
            device_id={"fsdp": peer},
            device_id_type=MESH,
        )

    across = [piece(x_ref, pos, part, part, far) for part in range(parts)]
    for copy in across:
        copy.start()
    beside = pltpu.make_async_remote_copy(
        src_ref=x_ref,
        dst_ref=xg_ref.at[pos],
        send_sem=xs.at[2 * parts],
        recv_sem=xr.at[2 * parts],
        device_id={"fsdp": near},
        device_id_type=MESH,
    )
    beside.start()
    slices = []
    for i in range(1, n):
        peer = me ^ i
        copy = pltpu.make_async_remote_copy(
            src_ref=w_ref.at[lax.rem(peer, GROUP)],
            dst_ref=wg_ref.at[me],
            send_sem=ws.at[i],
            recv_sem=wr.at[i],
            device_id={"fsdp": peer},
            device_id_type=MESH,
        )
        copy.start()
        slices.append(copy)
    passed = []
    for part in range(parts):
        across[part].wait_recv()
        copy = piece(xg_ref.at[pos ^ 2], pos ^ 2, part, parts + part, near)
        copy.start()
        passed.append(copy)
    for copy in across:
        copy.wait_send()
    beside.wait()
    own.wait()
    own_w.wait()
    for copy in passed + slices:
        copy.wait()


def gather_group(n, x, pieces):
    parts = 4
    dma = pltpu.SemaphoreType.DMA
    return pl.pallas_call(
        partial(gather_kernel, n, parts),
        name="gather_group",
        out_shape=(
            jax.ShapeDtypeStruct((GROUP,) + x.shape, x.dtype),
            jax.ShapeDtypeStruct((n,) + pieces.shape[1:], pieces.dtype),
        ),
        in_specs=[ANY, ANY],
        out_specs=(ANY, ANY),
        scratch_shapes=[
            dma((2 * parts + 1,)),
            dma((2 * parts + 1,)),
            dma((n,)),
            dma((n,)),
            dma((2,)),
        ],
        compiler_params=params(32, collective_id=0, has_side_effects=True),
    )(x, pieces)


def swap_kernel(count, x_ref, o_ref, send, recv, local):
    me = lax.axis_index("fsdp")
    greet([me ^ i for i in range(1, count)])
    slot = lax.rem(me, count)
    own = pltpu.make_async_copy(x_ref.at[slot], o_ref.at[slot], local)
    own.start()
    copies = []
    for i in range(1, count):
        copy = pltpu.make_async_remote_copy(
            src_ref=x_ref.at[slot ^ i],
            dst_ref=o_ref.at[slot],
            send_sem=send.at[i],
            recv_sem=recv.at[i],
            device_id={"fsdp": me ^ i},
            device_id_type=MESH,
        )
        copy.start()
        copies.append(copy)
    own.wait()
    for copy in copies:
        copy.wait()


def swap(x, collective_id, name):
    count = x.shape[0]
    dma = pltpu.SemaphoreType.DMA
    return pl.pallas_call(
        partial(swap_kernel, count),
        name=name,
        out_shape=jax.ShapeDtypeStruct(x.shape, x.dtype),
        in_specs=[ANY],
        out_specs=ANY,
        scratch_shapes=[dma((count,)), dma((count,)), dma],
        compiler_params=params(32, collective_id=collective_id, has_side_effects=True),
    )(x)


def project_kernel(x_ref, w_ref, g_ref, s_ref, b_ref, a_ref, q_ref, k_ref, v_ref):
    n, _ = moments(x_ref[...].astype(f32))
    a_low = (n * g_ref[...] + s_ref[...]).astype(bf16)
    a_ref[...] = a_low
    mixed = (dot(a_low, w_ref[...]) + b_ref[...]).astype(bf16)
    ones = jnp.ones((x_ref.shape[0], HEAD), bf16)
    for h in range(OWN):
        q = mixed[:, h * HEAD : (h + 1) * HEAD] * 0.125
        k = mixed[:, SLICE + h * HEAD : SLICE + (h + 1) * HEAD]
        v = mixed[:, 2 * SLICE + h * HEAD : 2 * SLICE + (h + 1) * HEAD]
        q_ref[h] = jnp.concatenate([q.astype(bf16), jnp.zeros_like(ones)], axis=1)
        k_ref[h] = jnp.concatenate([k, ones], axis=1)
        v_ref[h] = jnp.concatenate([v, ones], axis=1)


def project(x, w, gain, shift, bias):
    tile = 384
    heads = jax.ShapeDtypeStruct((OWN, ROWS, 2 * HEAD), bf16)
    head_spec = pl.BlockSpec((OWN, tile, 2 * HEAD), lambda i: (0, i, 0))
    whole = lambda i: (0, 0)
    return pl.pallas_call(
        project_kernel,
        name="project",
        grid=(ROWS // tile,),
        out_shape=(jax.ShapeDtypeStruct((ROWS, D), bf16), heads, heads, heads),
        in_specs=[
            pl.BlockSpec((tile, D), lambda i: (i, 0)),
            pl.BlockSpec((D, WIDE), whole),
            pl.BlockSpec((1, D), whole),
            pl.BlockSpec((1, D), whole),
            pl.BlockSpec((1, WIDE), whole),
        ],
        out_specs=(pl.BlockSpec((tile, D), lambda i: (i, 0)), head_spec, head_spec, head_spec),
        compiler_params=params(48),
    )(x, w, gain, shift, bias)


def lanes(rows):
    return lax.broadcasted_iota(jnp.int32, (rows, 2 * HEAD), 1)


def split_columns(base, lane, column):
    hi = column.astype(bf16).astype(f32)
    mid = (column - hi).astype(bf16).astype(f32)
    low = column - hi - mid
    tail = jnp.where(lane == HEAD, -hi, jnp.where(lane == HEAD + 1, -mid, -low))
    return jnp.where(lane < HEAD, base, jnp.where(lane < HEAD + 3, tail, 0.0)).astype(bf16)


def below(rows, cols, low_key):
    row = lax.broadcasted_iota(jnp.int32, (rows, cols), 0)
    col = lax.broadcasted_iota(jnp.int32, (rows, cols), 1)
    return row <= col if low_key else col <= row


def attend_kernel(reach_ref, q_ref, k_ref, v_ref, o_ref, f_ref, x_ref):
    T = CONT
    lane = lanes(T)
    causal = below(T, T, False)

    def tile(at, blocks):
        q = q_ref[0, pl.ds(at, T), :]
        scores = []
        for start, size, mask in blocks:
            s = dot_nt(q, k_ref[0, pl.ds(start, size), :])
            scores.append(s if mask is None else jnp.where(mask, s, NEG))
        peak = scores[0].max(axis=1, keepdims=True)
        for s in scores[1:]:
            peak = jnp.maximum(peak, s.max(axis=1, keepdims=True))
        total = jnp.zeros((T, 2 * HEAD), f32)
        for s, (start, size, _) in zip(scores, blocks):
            total += dot(jnp.exp(s - peak).astype(bf16), v_ref[0, pl.ds(start, size), :])
        mass = total[:, HEAD : HEAD + 1]
        f_ref[0, pl.ds(at, T), :] = total / mass
        lse = peak + jnp.log(mass)
        x_ref[0, pl.ds(at, T), :] = split_columns(q.astype(f32), lane, lse)

    for p in range(GROUP):
        past = [(i * TOK, PROMPT, None) for i in range(p)]
        base = p * TOK
        tile(base, past + [(base, T, causal)])
        tile(base + T, past + [(base, T, None), (base + T, T, causal)])

    def cont(c, carry):
        at = pl.multiple_of(c * TOK + PROMPT, CONT)
        reach = reach_ref[c]
        col = lax.broadcasted_iota(jnp.int32, (T, PROMPT), 1)
        blocks = [(i * TOK, PROMPT, col < reach - i * PROMPT) for i in range(GROUP)]
        tile(at, blocks + [(at, T, causal)])
        return carry

    lax.fori_loop(0, GROUP, cont, 0)

    half = lanes(PAIR) < HEAD
    for p in range(GROUP):
        top = f_ref[0, p * TOK : p * TOK + PAIR, :]
        low = f_ref[0, p * TOK + PAIR : (p + 1) * TOK, :]
        o_ref[p, 0] = jnp.where(half, top, pltpu.roll(low, HEAD, 1)).astype(bf16)


def attend(reach, q, k, v):
    head = lambda h: (h, 0, 0)
    spec = pl.BlockSpec((1, ROWS, 2 * HEAD), head)
    return pl.pallas_call(
        attend_kernel,
        name="attend",
        grid=(OWN,),
        out_shape=(
            jax.ShapeDtypeStruct((GROUP, OWN, PAIR, 2 * HEAD), bf16),
            jax.ShapeDtypeStruct((OWN, ROWS, 2 * HEAD), f32),
            jax.ShapeDtypeStruct((OWN, ROWS, 2 * HEAD), bf16),
        ),
        in_specs=[pl.BlockSpec(memory_space=pltpu.SMEM), spec, spec, spec],
        out_specs=(
            pl.BlockSpec((GROUP, 1, PAIR, 2 * HEAD), lambda h: (0, h, 0, 0)),
            spec,
            spec,
        ),
        compiler_params=params(56),
    )(reach, q, k, v)


def attend_back_kernel(
    reach_ref, q_ref, k_ref, v_ref, f_ref, g_ref, dq_ref, dk_ref, dv_ref, g_s, dq_s, kt_s, dk_s, dv_s
):
    T = CONT
    half = lanes(PAIR) < HEAD
    lane = lanes(PAIR)
    for p in range(GROUP):
        packed = g_ref[p, 0].astype(f32)
        for i, block in enumerate((packed, pltpu.roll(packed, HEAD, 1))):
            at = p * TOK + i * PAIR
            prod = jnp.where(half, block * f_ref[0, at : at + PAIR, :], 0.0)
            inner = jnp.sum(prod, axis=1, keepdims=True)
            g_s[at : at + PAIR, :] = split_columns(block, lane, inner)
        kt_s[:, p * TOK : (p + 1) * TOK] = k_ref[0, p * TOK : (p + 1) * TOK, :].T[:HEAD]
    dq_s[...] = jnp.zeros_like(dq_s)

    def block(keys, size, rows, count, mask, first, key_at):
        kb = k_ref[0, pl.ds(keys, size), :]
        vb = v_ref[0, pl.ds(keys, size), :]
        q = q_ref[0, pl.ds(rows, count), :]
        g = g_s[pl.ds(rows, count), :]
        probs = jnp.exp(dot_nt(kb, q))
        if mask is not None:
            probs = jnp.where(mask, probs, 0.0)
        ds = (probs * dot_nt(vb, g)).astype(bf16)
        dv = dot(probs.astype(bf16), g)
        dk = dot(ds, q)
        at = pl.ds(key_at, size)
        dv_s[at, :] = dv if first else dv_s[at, :] + dv
        dk_s[at, :] = dk if first else dk_s[at, :] + dk
        dq_s[:, pl.ds(rows, count)] += dot(kt_s[:, pl.ds(keys, size)], ds)

    causal = below(T, T, True)
    for p in range(GROUP):
        base = p * TOK
        block(base, T, base, T, causal, True, 0)
        block(base + T, T, base + T, T, causal, True, T)
        block(base, T, base + T, T, None, False, 0)

        def later(i, carry):
            rows = pl.multiple_of(i * TOK, CONT)
            block(base, PROMPT, rows, PROMPT, None, False, 0)
            return carry

        lax.fori_loop(p + 1, GROUP, later, 0)

        def cont(c, carry):
            rows = pl.multiple_of(c * TOK + PROMPT, CONT)
            key = lax.broadcasted_iota(jnp.int32, (PROMPT, T), 0)
            block(base, PROMPT, rows, T, key < reach_ref[c] - p * PROMPT, False, 0)
            return carry

        lax.fori_loop(0, GROUP, cont, 0)
        dk_ref[0, base : base + PROMPT, :] = dk_s[:, :HEAD].astype(bf16)
        dv_ref[0, base : base + PROMPT, :] = dv_s[:, :HEAD].astype(bf16)

    def own(c, carry):
        at = pl.multiple_of(c * TOK + PROMPT, CONT)
        block(at, T, at, T, causal, True, 0)
        dk_ref[0, pl.ds(at, T), :] = dk_s[:T, :HEAD].astype(bf16)
        dv_ref[0, pl.ds(at, T), :] = dv_s[:T, :HEAD].astype(bf16)
        return carry

    lax.fori_loop(0, GROUP, own, 0)
    for i in range(ROWS // PROMPT):
        at = i * PROMPT
        dq_ref[0, at : at + PROMPT, :] = (dq_s[:, at : at + PROMPT].T * 0.125).astype(bf16)


def attend_back(reach, q, k, v, f, g):
    head = lambda h: (h, 0, 0)
    spec = pl.BlockSpec((1, ROWS, 2 * HEAD), head)
    out = jax.ShapeDtypeStruct((OWN, ROWS, HEAD), bf16)
    out_spec = pl.BlockSpec((1, ROWS, HEAD), head)
    return pl.pallas_call(
        attend_back_kernel,
        name="attend_back",
        grid=(OWN,),
        out_shape=(out, out, out),
        in_specs=[pl.BlockSpec(memory_space=pltpu.SMEM), spec, spec, spec, spec]
        + [pl.BlockSpec((GROUP, 1, PAIR, 2 * HEAD), lambda h: (0, h, 0, 0))],
        out_specs=(out_spec, out_spec, out_spec),
        scratch_shapes=[
            pltpu.VMEM((ROWS, 2 * HEAD), bf16),
            pltpu.VMEM((HEAD, ROWS), f32),
            pltpu.VMEM((HEAD, ROWS), bf16),
            pltpu.VMEM((PROMPT, 2 * HEAD), f32),
            pltpu.VMEM((PROMPT, 2 * HEAD), f32),
        ],
        compiler_params=params(56),
    )(reach, q, k, v, f, g)


def middle_kernel(
    x_ref, o_ref, dy_ref, wo_ref, bo_ref, g_ref, s_ref, wf_ref, bf_ref, wp_ref, bp_ref,
    y_ref, dwf_ref, dwp_ref, dbf_ref, dwo_ref, dh_ref, do_ref, small_ref,
    o_s, h_s, b_s, bt_s, y_s, dn_s,
):
    step = pl.program_id(0)
    half = lanes(PAIR) < HEAD

    @pl.when(step == 0)
    def _():
        for t in range(HEADS // 2):
            one = o_ref[2 * t // OWN, 2 * t % OWN].astype(f32)
            two = o_ref[(2 * t + 1) // OWN, (2 * t + 1) % OWN].astype(f32)
            at = slice(2 * t * HEAD, (2 * t + 2) * HEAD)
            o_s[:PAIR, at] = jnp.where(half, one, pltpu.roll(two, HEAD, 1)).astype(bf16)
            o_s[PAIR:, at] = jnp.where(half, pltpu.roll(one, HEAD, 1), two).astype(bf16)
        h = x_ref[...].astype(f32) + dot(o_s[...], wo_ref[...]) + bo_ref[...]
        h_s[...] = h
        n, _ = moments(h)
        b_low = (n * g_ref[...] + s_ref[...]).astype(bf16)
        b_s[...] = b_low
        bt_s[...] = b_low.T
        y_s[...] = jnp.zeros_like(y_s)
        dn_s[...] = jnp.zeros_like(dn_s)

    dy = dy_ref[...]
    u = dot(b_s[...], wf_ref[...]) + bf_ref[...]
    square = u * u
    t = jnp.tanh(GELU_A * (u + GELU_B * (square * u)))
    m_low = (0.5 * u * (1.0 + t)).astype(bf16)
    slope = 0.5 * (1.0 + t) + 0.5 * u * (1.0 - t * t) * (GELU_A * (1.0 + 3.0 * GELU_B * square))
    y_s[...] += dot(m_low, wp_ref[...])
    du = (dot_nt(dy, wp_ref[...]) * slope).astype(bf16)
    dbf_ref[...] = jnp.sum(du.astype(f32), axis=0, keepdims=True)
    dn_s[...] += dot_nt(du, wf_ref[...])
    dwf_ref[...] = dot(bt_s[...], du).astype(bf16)
    dwp_ref[...] = dot_tn(m_low, dy).astype(bf16)

    @pl.when(step == pl.num_programs(0) - 1)
    def _():
        h = h_s[...]
        y_ref[...] = (h + y_s[...] + bp_ref[...]).astype(bf16)
        n, r = moments(h)
        dn = dn_s[...]
        grad = dy_ref[...].astype(f32)
        small_ref[...] = jnp.zeros_like(small_ref)
        small_ref[0:1, :] = jnp.sum(grad, axis=0, keepdims=True)
        small_ref[1:2, :] = jnp.sum(dn * n, axis=0, keepdims=True)
        small_ref[2:3, :] = jnp.sum(dn, axis=0, keepdims=True)
        e = dn * g_ref[...]
        lean = jnp.mean(e, axis=-1, keepdims=True) + n * jnp.mean(e * n, axis=-1, keepdims=True)
        dh = grad + r * (e - lean)
        dh_ref[...] = dh
        dh_low = dh.astype(bf16)
        small_ref[3:4, :] = jnp.sum(dh_low.astype(f32), axis=0, keepdims=True)
        dwo_ref[...] = dot_tn(o_s[...], dh_low).astype(bf16)
        h_s[...] = dot_nt(dh_low, wo_ref[...])
        for t in range(HEADS // 2):
            at = slice(2 * t * HEAD, (2 * t + 2) * HEAD)
            top, low = h_s[:PAIR, at], h_s[PAIR:, at]
            one = jnp.where(half, top, pltpu.roll(low, HEAD, 1))
            two = jnp.where(half, pltpu.roll(top, HEAD, 1), low)
            do_ref[2 * t // OWN, 2 * t % OWN] = one.astype(bf16)
            do_ref[(2 * t + 1) // OWN, (2 * t + 1) % OWN] = two.astype(bf16)


def middle(x, o, dy, wo, bo, gain, shift, wf, bf, wp, bp):
    fixed2 = lambda i: (0, 0)
    fixed4 = lambda i: (0, 0, 0, 0)
    square = pl.BlockSpec((TOK, D), fixed2)
    row = pl.BlockSpec((1, D), fixed2)
    heads = pl.BlockSpec((GROUP, OWN, PAIR, 2 * HEAD), fixed4)
    columns = pl.BlockSpec((D, CHUNK), lambda i: (0, i))
    down = pl.BlockSpec((CHUNK, D), lambda i: (i, 0))
    line = pl.BlockSpec((1, CHUNK), lambda i: (0, i))
    shape = jax.ShapeDtypeStruct
    return pl.pallas_call(
        middle_kernel,
        name="middle",
        grid=(FF // CHUNK,),
        out_shape=(
            shape((TOK, D), bf16),
            shape((D, FF), bf16),
            shape((FF, D), bf16),
            shape((1, FF), f32),
            shape((D, D), bf16),
            shape((TOK, D), f32),
            shape((GROUP, OWN, PAIR, 2 * HEAD), bf16),
            shape((8, D), f32),
        ),
        in_specs=[square, heads, square, square, row, row, row, columns, line, down, row],
        out_specs=(
            square, columns, down, line, square, square, heads, pl.BlockSpec((8, D), fixed2),
        ),
        scratch_shapes=[
            pltpu.VMEM((TOK, D), bf16),
            pltpu.VMEM((TOK, D), f32),
            pltpu.VMEM((TOK, D), bf16),
            pltpu.VMEM((D, TOK), bf16),
            pltpu.VMEM((TOK, D), f32),
            pltpu.VMEM((TOK, D), f32),
        ],
        compiler_params=params(60),
    )(x, o, dy, wo, bo, gain, shift, wf, bf, wp, bp)


def unproject_kernel(dq_ref, dk_ref, dv_ref, a_ref, w_ref, dn_ref, dw_ref, db_ref):
    step = pl.program_id(0)
    mixed = jnp.concatenate(
        [ref[h] for ref in (dq_ref, dk_ref, dv_ref) for h in range(OWN)], axis=1
    )
    dn_ref[...] = dot_nt(mixed, w_ref[...]).astype(bf16)
    dw = dot_tn(a_ref[...], mixed)
    db = jnp.sum(mixed.astype(f32), axis=0, keepdims=True)

    @pl.when(step == 0)
    def _():
        dw_ref[...] = dw
        db_ref[...] = db

    @pl.when(step > 0)
    def _():
        dw_ref[...] += dw
        db_ref[...] += db


def unproject(dq, dk, dv, a, w):
    tile = 768
    head = pl.BlockSpec((OWN, tile, HEAD), lambda i: (0, i, 0))
    whole = lambda i: (0, 0)
    shape = jax.ShapeDtypeStruct
    return pl.pallas_call(
        unproject_kernel,
        name="unproject",
        grid=(ROWS // tile,),
        out_shape=(shape((ROWS, D), bf16), shape((D, WIDE), f32), shape((1, WIDE), f32)),
        in_specs=[
            head, head, head,
            pl.BlockSpec((tile, D), lambda i: (i, 0)),
            pl.BlockSpec((D, WIDE), whole),
        ],
        out_specs=(
            pl.BlockSpec((tile, D), lambda i: (i, 0)),
            pl.BlockSpec((D, WIDE), whole),
            pl.BlockSpec((1, WIDE), whole),
        ),
        compiler_params=params(48),
    )(dq, dk, dv, a, w)


def finish_kernel(x_ref, dh_ref, g_ref, one_ref, two_ref, three_ref, out_ref):
    n, r = moments(x_ref[...].astype(f32))
    dn = one_ref[...].astype(f32) + two_ref[...].astype(f32) + three_ref[...].astype(f32)
    e = dn * g_ref[...]
    lean = jnp.mean(e, axis=-1, keepdims=True) + n * jnp.mean(e * n, axis=-1, keepdims=True)
    out_ref[...] = dh_ref[...] + r * (e - lean)


def finish(x, dh, gain, one, two, three):
    tile = 256
    rows = pl.BlockSpec((tile, D), lambda i: (i, 0))
    return pl.pallas_call(
        finish_kernel,
        name="finish",
        grid=(TOK // tile,),
        out_shape=jax.ShapeDtypeStruct((TOK, D), f32),
        in_specs=[rows, rows, pl.BlockSpec((1, D), lambda i: (0, 0)), rows, rows, rows],
        out_specs=rows,
        compiler_params=params(48),
    )(x, dh, gain, one, two, three)


def flip(block, bit):
    count = lax.axis_size("fsdp")
    return lax.ppermute(block, "fsdp", [(i, i ^ bit) for i in range(count)])


def over_replicas(block):
    count = lax.axis_size("rep")
    held = lax.optimization_barrier(block)
    if count == 2:
        other = lax.ppermute(held, "rep", [(0, 1), (1, 0)])
        return held.astype(f32) + other.astype(f32)
    return lax.psum(held.astype(f32), "rep")


def body(
    block_input, cotangent, tie_index, prefix_len, pre_gain, pre_shift, w_qkv, b_qv, w_out, b_out,
    mid_gain, mid_shift, w_fc, b_fc, w_proj, b_proj,
):
    n = lax.axis_size("fsdp")
    me = lax.axis_index("fsdp")
    pos = lax.rem(me, GROUP)
    rows = D // n
    index = tie_index[0]

    def chosen(bank):
        return lax.dynamic_index_in_dim(bank, index, 0, keepdims=False)

    vectors = (pre_gain, pre_shift, b_qv, b_out, mid_gain, mid_shift, b_fc, b_proj)
    sizes = [bank.shape[1] for bank in vectors]
    count = sum(sizes)
    small = jnp.concatenate([chosen(bank) for bank in vectors])
    high = -(-(rows + 2) // 16) * 16
    reach = prefix_len[0]
    reach_row = jnp.concatenate([reach // 16, reach % 16]).astype(bf16)
    wq = chosen(w_qkv).reshape(rows, 3, GROUP, SLICE).transpose(2, 0, 1, 3).reshape(GROUP, rows, WIDE)
    extra = jnp.stack(
        [jnp.pad(small, (0, WIDE - count)), jnp.pad(reach_row, (0, WIDE - reach_row.shape[0]))]
    )
    extra = jnp.pad(extra, ((0, high - rows - 2), (0, 0)))
    pieces = jnp.concatenate([wq, jnp.broadcast_to(extra, (GROUP,) + extra.shape)], axis=1)

    wo = lax.all_gather(chosen(w_out), "fsdp", axis=0, tiled=True)
    wf = lax.all_gather(chosen(w_fc), "fsdp", axis=0, tiled=True)
    wp = lax.all_gather(chosen(w_proj), "fsdp", axis=0, tiled=True)

    xg, wg = gather_group(n, block_input, pieces)
    wq = wg[:, :rows].reshape(D, WIDE)
    smalls = wg[:, rows, :count].astype(f32)
    group_rows = lax.dynamic_slice_in_dim(wg[:, rows + 1, :2], me - pos, GROUP, 0)
    reaches = (group_rows[:, 0].astype(f32) * 16 + group_rows[:, 1].astype(f32)).astype(jnp.int32)
    cuts = [sum(sizes[:i]) for i in range(len(sizes) + 1)]
    g1, s1, bqv, bo, g2, s2, bf, bp = (
        smalls[:, cuts[i] : cuts[i + 1]].reshape(1, -1) for i in range(len(sizes))
    )
    own_bias = lax.dynamic_index_in_dim(bqv.reshape(2, GROUP, SLICE), pos, 1, keepdims=False)
    bias = jnp.concatenate([own_bias[0], jnp.zeros((SLICE,), f32), own_bias[1]])[None]

    a_low, q, k, v = project(xg.reshape(ROWS, D), wq, g1, s1, bias)
    o_send, o_full, qx = attend(reaches, q, k, v)
    o_recv = swap(o_send, 1, "swap_o")
    y, dwf, dwp, dbf, dwo, dh, do_send, sums = middle(
        block_input, o_recv, cotangent, wo, bo, g2, s2, wf, bf, wp, bp
    )
    dwf = lax.psum_scatter(dwf, "fsdp", scatter_dimension=0, tiled=True)
    dwp = lax.psum_scatter(dwp, "fsdp", scatter_dimension=0, tiled=True)
    dwo = lax.psum_scatter(dwo, "fsdp", scatter_dimension=0, tiled=True)
    do_recv = swap(do_send, 2, "swap_do")
    dq, dk, dv = attend_back(reaches, qx, k, v, o_full, do_recv)
    dn, dwq, db = unproject(dq, dk, dv, a_low, wq)

    dn = dn.reshape(GROUP, TOK, D)
    block_of = lambda bit: lax.dynamic_index_in_dim(dn, pos ^ bit, 0, keepdims=False)
    beside = flip(block_of(1), 1)
    across = flip(block_of(3), 1)
    across = flip((across.astype(f32) + block_of(2).astype(f32)).astype(bf16), 2)

    wq_wide = wq.astype(f32)
    dshift = jnp.sum(wq_wide * db, axis=1)
    dgain = jnp.sum(wq_wide * (dwq - s1.reshape(D, 1) * db), axis=1) / g1.reshape(D)
    where = (jnp.arange(GROUP) == pos).astype(f32)[:, None]
    dbias = jnp.concatenate(
        [(where * db[:, :SLICE]).reshape(-1), (where * db[:, 2 * SLICE :]).reshape(-1)]
    )
    line = jnp.concatenate(
        [
            part.reshape(n, -1)
            for part in (dgain, dshift, dbias, sums[3], sums[1], sums[2], dbf, sums[0])
        ],
        axis=1,
    )
    line_hi = line.astype(bf16)
    line_low = (line - lax.reduce_precision(line, 8, 7)).astype(bf16)
    lines = jnp.pad(jnp.stack([line_hi, line_low], axis=1), ((0, 0), (0, 0), (0, WIDE - count)))
    lines = jnp.pad(lines, ((0, 0), (0, high - rows - 2), (0, 0)))
    back = jnp.concatenate([dwq.astype(bf16).reshape(n, rows, WIDE), lines], axis=1)
    back = swap(back, 3, "swap_grad")
    dwq = jnp.sum(back[:, :rows].astype(f32).reshape(n // GROUP, GROUP, rows, 3, SLICE), axis=0)
    dwq = dwq.transpose(1, 2, 0, 3).reshape(rows, 3 * D)
    line = jnp.sum(back[:, rows, :count].astype(f32) + back[:, rows + 1, :count].astype(f32), axis=0)

    grad = finish(block_input, dh, g1, block_of(0), beside, across)
    dwq = over_replicas(dwq.astype(bf16))
    dwo, dwf, dwp = over_replicas(dwo), over_replicas(dwf), over_replicas(dwp)
    line = over_replicas(line)
    dg1, ds1, dbqv, dbo, dg2, ds2, dbf, dbp = (
        line[cuts[i] : cuts[i + 1]] for i in range(len(sizes))
    )
    return (y, grad, dg1, ds1, dwq, dbqv, dwo, dbo, dg2, ds2, dwf, dbf, dwp, dbp)


def solution(mesh):
    tokens = P(("rep", "fsdp"), None)
    vector, matrix = P(None, "fsdp"), P(None, "fsdp", None)
    return jax.shard_map(
        body,
        mesh=mesh,
        in_specs=(
            tokens, tokens, P(), tokens, vector, vector, matrix, vector, matrix, vector,
            vector, vector, matrix, vector, matrix, vector,
        ),
        out_specs=(
            tokens, tokens, P("fsdp"), P("fsdp"), P("fsdp", None), P("fsdp"), P("fsdp", None),
            P("fsdp"), P("fsdp"), P("fsdp"), P("fsdp", None), P("fsdp"), P("fsdp", None), P("fsdp"),
        ),
        check_vma=False,
    )
```

```python
from functools import partial

import jax
import jax.numpy as jnp
from jax import lax
from jax.experimental import pallas as pl
from jax.experimental.pallas import tpu as pltpu
from jax.sharding import PartitionSpec as P

D = 768
HEADS = 12
HEAD = 64
FF = 3072
GROUP = 4
PROMPT = 512
CONT = 256
TOK = 768
ROWS = GROUP * TOK
OWN = HEADS // GROUP
SLICE = OWN * HEAD
WIDE = 3 * SLICE
PAIR = TOK // 2
CHUNK = 768
BLOCKS = 16
UNIT = 432
NEG = -1e30
EPS = 1e-5
GELU_A = 0.7978845608028654
GELU_B = 0.044715

f32 = jnp.float32
bf16 = jnp.bfloat16
MESH = pl.DeviceIdType.MESH
ANY = pl.BlockSpec(memory_space=pl.ANY)


def params(mib, **more):
    return pltpu.CompilerParams(vmem_limit_bytes=mib << 20, **more)


def dot(a, b):
    return jnp.dot(a, b, preferred_element_type=f32)


def dot_nt(a, b):
    return lax.dot_general(a, b, (((1,), (1,)), ((), ())), preferred_element_type=f32)


def dot_tn(a, b):
    return lax.dot_general(a, b, (((0,), (0,)), ((), ())), preferred_element_type=f32)


def moments(x):
    center = x - jnp.mean(x, axis=-1, keepdims=True)
    scale = lax.rsqrt(jnp.mean(center * center, axis=-1, keepdims=True) + EPS)
    return center * scale, scale


def greet(peers):
    sem = pltpu.get_barrier_semaphore()
    for peer in peers:
        pl.semaphore_signal(sem, inc=1, device_id={"fsdp": peer}, device_id_type=MESH)
    pl.semaphore_wait(sem, len(peers))


def gather_kernel(n, parts, x_ref, w_ref, xg_ref, wg_ref, xs, xr, ws, wr, local):
    me = lax.axis_index("fsdp")
    pos = lax.rem(me, GROUP)
    near, far = me ^ 1, me ^ 2
    greet([me ^ i for i in range(1, n)])
    own = pltpu.make_async_copy(x_ref, xg_ref.at[pos], local.at[0])
    own.start()
    own_w = pltpu.make_async_copy(w_ref.at[pos], wg_ref.at[me], local.at[1])
    own_w.start()
    rows = TOK // parts

    def piece(src, slot, part, i, peer):
        at = pl.ds(part * rows, rows)
        return pltpu.make_async_remote_copy(
            src_ref=src.at[at],
            dst_ref=xg_ref.at[slot, at],
            send_sem=xs.at[i],
            recv_sem=xr.at[i],
            device_id={"fsdp": peer},
            device_id_type=MESH,
        )

    across = [piece(x_ref, pos, part, part, far) for part in range(parts)]
    for copy in across:
        copy.start()
    beside = pltpu.make_async_remote_copy(
        src_ref=x_ref,
        dst_ref=xg_ref.at[pos],
        send_sem=xs.at[2 * parts],
        recv_sem=xr.at[2 * parts],
        device_id={"fsdp": near},
        device_id_type=MESH,
    )
    beside.start()
    slices = []
    for i in range(1, n):
        peer = me ^ i
        copy = pltpu.make_async_remote_copy(
            src_ref=w_ref.at[lax.rem(peer, GROUP)],
            dst_ref=wg_ref.at[me],
            send_sem=ws.at[i],
            recv_sem=wr.at[i],
            device_id={"fsdp": peer},
            device_id_type=MESH,
        )
        copy.start()
        slices.append(copy)
    passed = []
    for part in range(parts):
        across[part].wait_recv()
        copy = piece(xg_ref.at[pos ^ 2], pos ^ 2, part, parts + part, near)
        copy.start()
        passed.append(copy)
    for copy in across:
        copy.wait_send()
    beside.wait()
    own.wait()
    own_w.wait()
    for copy in passed + slices:
        copy.wait()


def gather_group(n, x, pieces):
    parts = 4
    dma = pltpu.SemaphoreType.DMA
    return pl.pallas_call(
        partial(gather_kernel, n, parts),
        name="gather_group",
        out_shape=(
            jax.ShapeDtypeStruct((GROUP,) + x.shape, x.dtype),
            jax.ShapeDtypeStruct((n,) + pieces.shape[1:], pieces.dtype),
        ),
        in_specs=[ANY, ANY],
        out_specs=(ANY, ANY),
        scratch_shapes=[
            dma((2 * parts + 1,)),
            dma((2 * parts + 1,)),
            dma((n,)),
            dma((n,)),
            dma((2,)),
        ],
        compiler_params=params(32, collective_id=0, has_side_effects=True),
    )(x, pieces)


def swap_kernel(count, x_ref, o_ref, send, recv, local):
    me = lax.axis_index("fsdp")
    greet([me ^ i for i in range(1, count)])
    slot = lax.rem(me, count)
    own = pltpu.make_async_copy(x_ref.at[slot], o_ref.at[slot], local)
    own.start()
    copies = []
    for i in range(1, count):
        copy = pltpu.make_async_remote_copy(
            src_ref=x_ref.at[slot ^ i],
            dst_ref=o_ref.at[slot],
            send_sem=send.at[i],
            recv_sem=recv.at[i],
            device_id={"fsdp": me ^ i},
            device_id_type=MESH,
        )
        copy.start()
        copies.append(copy)
    own.wait()
    for copy in copies:
        copy.wait()


def swap(x, collective_id, name):
    count = x.shape[0]
    dma = pltpu.SemaphoreType.DMA
    return pl.pallas_call(
        partial(swap_kernel, count),
        name=name,
        out_shape=jax.ShapeDtypeStruct(x.shape, x.dtype),
        in_specs=[ANY],
        out_specs=ANY,
        scratch_shapes=[dma((count,)), dma((count,)), dma],
        compiler_params=params(32, collective_id=collective_id, has_side_effects=True),
    )(x)


def project_kernel(x_ref, w_ref, g_ref, s_ref, b_ref, a_ref, q_ref, k_ref, v_ref):
    n, _ = moments(x_ref[...].astype(f32))
    a_low = (n * g_ref[...] + s_ref[...]).astype(bf16)
    a_ref[...] = a_low
    mixed = (dot(a_low, w_ref[...]) + b_ref[...]).astype(bf16)
    ones = jnp.ones((x_ref.shape[0], HEAD), bf16)
    for h in range(OWN):
        q = mixed[:, h * HEAD : (h + 1) * HEAD] * 0.125
        k = mixed[:, SLICE + h * HEAD : SLICE + (h + 1) * HEAD]
        v = mixed[:, 2 * SLICE + h * HEAD : 2 * SLICE + (h + 1) * HEAD]
        q_ref[h] = jnp.concatenate([q.astype(bf16), jnp.zeros_like(ones)], axis=1)
        k_ref[h] = jnp.concatenate([k, ones], axis=1)
        v_ref[h] = jnp.concatenate([v, ones], axis=1)


def project(x, w, gain, shift, bias):
    tile = 384
    heads = jax.ShapeDtypeStruct((OWN, ROWS, 2 * HEAD), bf16)
    head_spec = pl.BlockSpec((OWN, tile, 2 * HEAD), lambda i: (0, i, 0))
    whole = lambda i: (0, 0)
    return pl.pallas_call(
        project_kernel,
        name="project",
        grid=(ROWS // tile,),
        out_shape=(jax.ShapeDtypeStruct((ROWS, D), bf16), heads, heads, heads),
        in_specs=[
            pl.BlockSpec((tile, D), lambda i: (i, 0)),
            pl.BlockSpec((D, WIDE), whole),
            pl.BlockSpec((1, D), whole),
            pl.BlockSpec((1, D), whole),
            pl.BlockSpec((1, WIDE), whole),
        ],
        out_specs=(pl.BlockSpec((tile, D), lambda i: (i, 0)), head_spec, head_spec, head_spec),
        compiler_params=params(48),
    )(x, w, gain, shift, bias)


def lanes(rows):
    return lax.broadcasted_iota(jnp.int32, (rows, 2 * HEAD), 1)


def split_columns(base, lane, column):
    hi = column.astype(bf16).astype(f32)
    mid = (column - hi).astype(bf16).astype(f32)
    low = column - hi - mid
    tail = jnp.where(lane == HEAD, -hi, jnp.where(lane == HEAD + 1, -mid, -low))
    return jnp.where(lane < HEAD, base, jnp.where(lane < HEAD + 3, tail, 0.0)).astype(bf16)


def below(rows, cols, low_key):
    row = lax.broadcasted_iota(jnp.int32, (rows, cols), 0)
    col = lax.broadcasted_iota(jnp.int32, (rows, cols), 1)
    return row <= col if low_key else col <= row


def attend_kernel(reach_ref, q_ref, k_ref, v_ref, o_ref, f_ref, x_ref):
    T = CONT
    lane = lanes(T)
    causal = below(T, T, False)

    def tile(at, blocks):
        q = q_ref[0, pl.ds(at, T), :]
        scores = []
        for start, size, mask in blocks:
            s = dot_nt(q, k_ref[0, pl.ds(start, size), :])
            scores.append(s if mask is None else jnp.where(mask, s, NEG))
        peak = scores[0].max(axis=1, keepdims=True)
        for s in scores[1:]:
            peak = jnp.maximum(peak, s.max(axis=1, keepdims=True))
        total = jnp.zeros((T, 2 * HEAD), f32)
        for s, (start, size, _) in zip(scores, blocks):
            total += dot(jnp.exp(s - peak).astype(bf16), v_ref[0, pl.ds(start, size), :])
        mass = total[:, HEAD : HEAD + 1]
        f_ref[0, pl.ds(at, T), :] = total / mass
        lse = peak + jnp.log(mass)
        x_ref[0, pl.ds(at, T), :] = split_columns(q.astype(f32), lane, lse)

    for p in range(GROUP):
        past = [(i * TOK, PROMPT, None) for i in range(p)]
        base = p * TOK
        tile(base, past + [(base, T, causal)])
        tile(base + T, past + [(base, T, None), (base + T, T, causal)])

    def cont(c, carry):
        at = pl.multiple_of(c * TOK + PROMPT, CONT)
        reach = reach_ref[c]
        col = lax.broadcasted_iota(jnp.int32, (T, PROMPT), 1)
        blocks = [(i * TOK, PROMPT, col < reach - i * PROMPT) for i in range(GROUP)]
        tile(at, blocks + [(at, T, causal)])
        return carry

    lax.fori_loop(0, GROUP, cont, 0)

    half = lanes(PAIR) < HEAD
    for p in range(GROUP):
        top = f_ref[0, p * TOK : p * TOK + PAIR, :]
        low = f_ref[0, p * TOK + PAIR : (p + 1) * TOK, :]
        o_ref[p, 0] = jnp.where(half, top, pltpu.roll(low, HEAD, 1)).astype(bf16)


def attend(reach, q, k, v):
    head = lambda h: (h, 0, 0)
    spec = pl.BlockSpec((1, ROWS, 2 * HEAD), head)
    return pl.pallas_call(
        attend_kernel,
        name="attend",
        grid=(OWN,),
        out_shape=(
            jax.ShapeDtypeStruct((GROUP, OWN, PAIR, 2 * HEAD), bf16),
            jax.ShapeDtypeStruct((OWN, ROWS, 2 * HEAD), f32),
            jax.ShapeDtypeStruct((OWN, ROWS, 2 * HEAD), bf16),
        ),
        in_specs=[pl.BlockSpec(memory_space=pltpu.SMEM), spec, spec, spec],
        out_specs=(
            pl.BlockSpec((GROUP, 1, PAIR, 2 * HEAD), lambda h: (0, h, 0, 0)),
            spec,
            spec,
        ),
        compiler_params=params(56),
    )(reach, q, k, v)


def attend_back_kernel(
    reach_ref, q_ref, k_ref, v_ref, f_ref, g_ref, dq_ref, dk_ref, dv_ref, g_s, dq_s, kt_s, dk_s, dv_s
):
    T = CONT
    half = lanes(PAIR) < HEAD
    lane = lanes(PAIR)
    for p in range(GROUP):
        packed = g_ref[p, 0].astype(f32)
        for i, block in enumerate((packed, pltpu.roll(packed, HEAD, 1))):
            at = p * TOK + i * PAIR
            prod = jnp.where(half, block * f_ref[0, at : at + PAIR, :], 0.0)
            inner = jnp.sum(prod, axis=1, keepdims=True)
            g_s[at : at + PAIR, :] = split_columns(block, lane, inner)
        kt_s[:, p * TOK : (p + 1) * TOK] = k_ref[0, p * TOK : (p + 1) * TOK, :].T[:HEAD]
    dq_s[...] = jnp.zeros_like(dq_s)

    def block(keys, size, rows, count, mask, first, key_at):
        kb = k_ref[0, pl.ds(keys, size), :]
        vb = v_ref[0, pl.ds(keys, size), :]
        q = q_ref[0, pl.ds(rows, count), :]
        g = g_s[pl.ds(rows, count), :]
        probs = jnp.exp(dot_nt(kb, q))
        if mask is not None:
            probs = jnp.where(mask, probs, 0.0)
        ds = (probs * dot_nt(vb, g)).astype(bf16)
        dv = dot(probs.astype(bf16), g)
        dk = dot(ds, q)
        at = pl.ds(key_at, size)
        dv_s[at, :] = dv if first else dv_s[at, :] + dv
        dk_s[at, :] = dk if first else dk_s[at, :] + dk
        dq_s[:, pl.ds(rows, count)] += dot(kt_s[:, pl.ds(keys, size)], ds)

    causal = below(T, T, True)
    for p in range(GROUP):
        base = p * TOK
        block(base, T, base, T, causal, True, 0)
        block(base + T, T, base + T, T, causal, True, T)
        block(base, T, base + T, T, None, False, 0)

        def later(i, carry):
            rows = pl.multiple_of(i * TOK, CONT)
            block(base, PROMPT, rows, PROMPT, None, False, 0)
            return carry

        lax.fori_loop(p + 1, GROUP, later, 0)

        def cont(c, carry):
            rows = pl.multiple_of(c * TOK + PROMPT, CONT)
            key = lax.broadcasted_iota(jnp.int32, (PROMPT, T), 0)
            block(base, PROMPT, rows, T, key < reach_ref[c] - p * PROMPT, False, 0)
            return carry

        lax.fori_loop(0, GROUP, cont, 0)
        dk_ref[0, base : base + PROMPT, :] = dk_s[:, :HEAD].astype(bf16)
        dv_ref[0, base : base + PROMPT, :] = dv_s[:, :HEAD].astype(bf16)

    def own(c, carry):
        at = pl.multiple_of(c * TOK + PROMPT, CONT)
        block(at, T, at, T, causal, True, 0)
        dk_ref[0, pl.ds(at, T), :] = dk_s[:T, :HEAD].astype(bf16)
        dv_ref[0, pl.ds(at, T), :] = dv_s[:T, :HEAD].astype(bf16)
        return carry

    lax.fori_loop(0, GROUP, own, 0)
    for i in range(ROWS // PROMPT):
        at = i * PROMPT
        dq_ref[0, at : at + PROMPT, :] = (dq_s[:, at : at + PROMPT].T * 0.125).astype(bf16)


def attend_back(reach, q, k, v, f, g):
    head = lambda h: (h, 0, 0)
    spec = pl.BlockSpec((1, ROWS, 2 * HEAD), head)
    out = jax.ShapeDtypeStruct((OWN, ROWS, HEAD), bf16)
    out_spec = pl.BlockSpec((1, ROWS, HEAD), head)
    return pl.pallas_call(
        attend_back_kernel,
        name="attend_back",
        grid=(OWN,),
        out_shape=(out, out, out),
        in_specs=[pl.BlockSpec(memory_space=pltpu.SMEM), spec, spec, spec, spec]
        + [pl.BlockSpec((GROUP, 1, PAIR, 2 * HEAD), lambda h: (0, h, 0, 0))],
        out_specs=(out_spec, out_spec, out_spec),
        scratch_shapes=[
            pltpu.VMEM((ROWS, 2 * HEAD), bf16),
            pltpu.VMEM((HEAD, ROWS), f32),
            pltpu.VMEM((HEAD, ROWS), bf16),
            pltpu.VMEM((PROMPT, 2 * HEAD), f32),
            pltpu.VMEM((PROMPT, 2 * HEAD), f32),
        ],
        compiler_params=params(56),
    )(reach, q, k, v, f, g)


def ring_of(me):
    chip, core = me // 2, lax.rem(me, 2)
    z, x = chip // 2, lax.rem(chip, 2)
    chips = BLOCKS // 2
    half = chips // 2
    place = z * (1 - x) + (chips - 1 - z) * x

    def device(at):
        at = lax.rem(at + 2 * chips, chips)
        side = at // half
        z_at = at * (1 - side) + (chips - 1 - at) * side
        return (z_at * 2 + side) * 2 + core

    return place, device


def forward_kernel(
    x_ref, sm_ref, pc_ref, wp_ref, wo_ref, wf_ref,
    wall_ref, smo_ref, wq_ref, a_ref, q_ref, k_ref, v_ref, f_ref, o_ref,
    xg, smg, wg, w_s, q_s, k_s, v_s, f_s, o_s,
    local, sm_send, sm_recv, w_send, w_recv, x_send, x_recv, r_send, r_recv, n_send, n_recv,
    o_send, o_recv, out_sem,
):
    n = BLOCKS
    me = lax.axis_index("fsdp")
    pos = lax.rem(me, GROUP)
    base = me - pos
    near, far = me ^ 1, me ^ 2
    place, device = ring_of(me)
    parts = 4
    part_rows = TOK // parts
    T = CONT

    def remote(src, dst, send, recv, peer):
        return pltpu.make_async_remote_copy(
            src_ref=src,
            dst_ref=dst,
            send_sem=send,
            recv_sem=recv,
            device_id={"fsdp": peer},
            device_id_type=MESH,
        )

    greet([me ^ i for i in range(1, n)])

    shard = [
        pltpu.make_async_copy(wp_ref, wall_ref.at[me, pl.ds(0, 192)], local.at[0]),
        pltpu.make_async_copy(wo_ref, wall_ref.at[me, pl.ds(192, 48)], local.at[1]),
    ]
    for c in range(4):
        shard.append(
            pltpu.make_async_copy(
                wf_ref.at[:, pl.ds(c * D, D)], wall_ref.at[me, pl.ds(240 + 48 * c, 48)], local.at[2 + c]
            )
        )
    own_x = pltpu.make_async_copy(x_ref, xg.at[pos], local.at[6])
    own_w = pltpu.make_async_copy(pc_ref.at[pos], wg.at[me], local.at[7])
    own_s = pltpu.make_async_copy(sm_ref, smg.at[me], local.at[8])
    for copy in [own_s, own_x, own_w] + shard:
        copy.start()

    smalls, slices = [], []
    for i in range(1, n):
        copy = remote(sm_ref, smg.at[me], sm_send.at[i], sm_recv.at[i], me ^ i)
        copy.start()
        smalls.append(copy)
    beside = remote(x_ref, xg.at[pos], x_send.at[2 * parts], x_recv.at[2 * parts], near)
    beside.start()
    for i in range(1, n):
        peer = me ^ i
        copy = remote(pc_ref.at[lax.rem(peer, GROUP)], wg.at[me], w_send.at[i], w_recv.at[i], peer)
        copy.start()
        slices.append(copy)

    def x_part(src, slot, part, i, peer):
        at = pl.ds(part * part_rows, part_rows)
        return remote(src.at[at], xg.at[slot, at], x_send.at[i], x_recv.at[i], peer)

    across = [x_part(x_ref, pos, part, part, far) for part in range(parts)]
    for copy in across:
        copy.start()

    def hop(t, right):
        at = place - t if right else place + t
        block = wall_ref.at[device(at)]
        i = t if right else 4 + t
        return remote(block, block, r_send.at[i], r_recv.at[i], device(place + 1 if right else place - 1))

    def beside_hop(t, right):
        at = place - 1 - t if right else place + 1 + t
        block = wall_ref.at[device(at)]
        i = 1 + (t if right else 4 + t)
        return remote(block, block, n_send.at[i], n_recv.at[i], near)

    hops, shared = {}, []

    def launch(t):
        for right in (True, False):
            if t < (4 if right else 3):
                hops[t, right] = hop(t, right)
                hops[t, right].start()

    def arrive(t):
        for right in (True, False):
            if t < (4 if right else 3):
                hops[t, right].wait_recv()
        if t < 3:
            launch(t + 1)
        for right in (True, False):
            if t < (4 if right else 3):
                copy = beside_hop(t, right)
                copy.start()
                shared.append(copy)

    for copy in shard:
        copy.wait()
    launch(0)
    own_block = remote(wall_ref.at[me], wall_ref.at[me], n_send.at[0], n_recv.at[0], near)
    own_block.start()
    shared.append(own_block)

    own_s.wait()
    for copy in smalls:
        copy.wait_recv()
    rows48 = D // n
    gain = jnp.concatenate([smg[d, 0:1, 0:rows48] for d in range(n)], axis=1).astype(f32)
    shift = jnp.concatenate([smg[d, 0:1, rows48 : 2 * rows48] for d in range(n)], axis=1).astype(f32)
    at = 2 * rows48
    two = 2 * rows48
    zeros = jnp.zeros((1, SLICE), bf16)
    bias = jnp.concatenate(
        [smg[2 * pos + i, 0:1, at : at + two] for i in range(2)]
        + [zeros]
        + [smg[n // 2 + 2 * pos + i, 0:1, at : at + two] for i in range(2)],
        axis=1,
    ).astype(f32)

    def norm(slot):
        def some(i, carry):
            at = pl.ds(pl.multiple_of(i * PAIR, PAIR), PAIR)
            n_rows, _ = moments(xg[slot, at, :].astype(f32))
            xg[slot, at, :] = (n_rows * gain + shift).astype(bf16)
            return carry

        lax.fori_loop(0, 2, some, 0)

    def project_block(slot):
        def some(i, carry):
            at = pl.ds(pl.multiple_of(i * PAIR, PAIR), PAIR)
            out = pl.ds(pl.multiple_of(slot * TOK + i * PAIR, PAIR), PAIR)
            mixed = (dot(xg[slot, at, :], w_s[...]) + bias).astype(bf16)
            ones = jnp.ones((PAIR, HEAD), bf16)
            for h in range(OWN):
                q = mixed[:, h * HEAD : (h + 1) * HEAD] * 0.125
                k = mixed[:, SLICE + h * HEAD : SLICE + (h + 1) * HEAD]
                v = mixed[:, 2 * SLICE + h * HEAD : 2 * SLICE + (h + 1) * HEAD]
                q_s[h, out, :] = jnp.concatenate([q.astype(bf16), jnp.zeros_like(ones)], axis=1)
                k_s[h, out, :] = jnp.concatenate([k, ones], axis=1)
                v_s[h, out, :] = jnp.concatenate([v, ones], axis=1)
            return carry

        lax.fori_loop(0, 2, some, 0)

    own_x.wait()
    norm(pos)
    beside.wait()
    norm(pos ^ 1)
    own_w.wait()
    for copy in slices:
        copy.wait_recv()
    w_s[...] = wg[:, :rows48, :].reshape(D, WIDE)
    project_block(pos)
    project_block(pos ^ 1)
    passed = []
    for part in range(parts):
        across[part].wait_recv()
        copy = x_part(xg.at[pos ^ 2], pos ^ 2, part, parts + part, near)
        copy.start()
        passed.append(copy)
    for copy in passed:
        copy.wait()
    norm(pos ^ 2)
    project_block(pos ^ 2)
    norm(pos ^ 3)
    project_block(pos ^ 3)
    arrive(0)

    outs = [
        pltpu.make_async_copy(smg, smo_ref, out_sem.at[0]),
        pltpu.make_async_copy(w_s, wq_ref, out_sem.at[1]),
        pltpu.make_async_copy(xg, a_ref, out_sem.at[2]),
        pltpu.make_async_copy(k_s, k_ref, out_sem.at[3]),
        pltpu.make_async_copy(v_s, v_ref, out_sem.at[4]),
    ]
    for copy in outs:
        copy.start()

    lane = lanes(T)
    causal = below(T, T, False)
    half = lanes(PAIR) < HEAD
    code = [smg[base + c, 1:2, 0:2].astype(f32) for c in range(GROUP)]
    reaches = [c[:, 0:1] * 16.0 + c[:, 1:2] for c in code]
    column = lax.broadcasted_iota(jnp.int32, (T, PROMPT), 1).astype(f32)

    for h in range(OWN):

        def tile(at, blocks):
            q = q_s[h, pl.ds(at, T), :]
            scores = []
            for start, size, mask in blocks:
                s = dot_nt(q, k_s[h, pl.ds(start, size), :])
                scores.append(s if mask is None else jnp.where(mask, s, NEG))
            peak = scores[0].max(axis=1, keepdims=True)
            for s in scores[1:]:
                peak = jnp.maximum(peak, s.max(axis=1, keepdims=True))
            total = jnp.zeros((T, 2 * HEAD), f32)
            for s, (start, size, _) in zip(scores, blocks):
                total += dot(jnp.exp(s - peak).astype(bf16), v_s[h, pl.ds(start, size), :])
            mass = total[:, HEAD : HEAD + 1]
            f_s[h, pl.ds(at, T), :] = total / mass
            lse = peak + jnp.log(mass)
            q_s[h, pl.ds(at, T), :] = split_columns(q.astype(f32), lane, lse)

        for p in range(GROUP):
            past = [(i * TOK, PROMPT, None) for i in range(p)]
            at = p * TOK
            tile(at, past + [(at, T, causal)])
            tile(at + T, past + [(at, T, None), (at + T, T, causal)])
        if h < 2:
            arrive(1 + h)
        for c in range(GROUP):
            at = c * TOK + PROMPT
            blocks = [(i * TOK, PROMPT, column < reaches[c] - i * PROMPT) for i in range(GROUP)]
            tile(at, blocks + [(at, T, causal)])
        for p in range(GROUP):
            top = f_s[h, p * TOK : p * TOK + PAIR, :]
            low = f_s[h, p * TOK + PAIR : (p + 1) * TOK, :]
            o_s[h, p] = jnp.where(half, top, pltpu.roll(low, HEAD, 1)).astype(bf16)
        for i in range(1, GROUP):
            copy = remote(
                o_s.at[h, pos ^ i], o_ref.at[pos, h], o_send.at[h, i], o_recv.at[h, i], me ^ i
            )
            copy.start()
            shared.append(copy)
        for src, dst, i in (
            (o_s.at[h, pos], o_ref.at[pos, h], 5 + h),
            (f_s.at[h], f_ref.at[h], 8 + h),
            (q_s.at[h], q_ref.at[h], 11 + h),
        ):
            copy = pltpu.make_async_copy(src, dst, out_sem.at[i])
            copy.start()
            outs.append(copy)

    arrive(3)
    for copy in across + smalls + slices + list(hops.values()):
        copy.wait_send()
    for copy in shared + outs:
        copy.wait()


def forward(x, small, pieces, wp, wo, wf):
    dma = pltpu.SemaphoreType.DMA
    n = BLOCKS
    shape = jax.ShapeDtypeStruct
    head = (OWN, ROWS, 2 * HEAD)
    return pl.pallas_call(
        forward_kernel,
        name="forward",
        out_shape=(
            shape((n, UNIT, D), bf16),
            shape((n,) + small.shape, bf16),
            shape((D, WIDE), bf16),
            shape((GROUP, TOK, D), bf16),
            shape(head, bf16),
            shape(head, bf16),
            shape(head, bf16),
            shape(head, f32),
            shape((GROUP, OWN, PAIR, 2 * HEAD), bf16),
        ),
        in_specs=[ANY] * 6,
        out_specs=(ANY,) * 9,
        scratch_shapes=[
            pltpu.VMEM((GROUP, TOK, D), bf16),
            pltpu.VMEM((n,) + small.shape, bf16),
            pltpu.VMEM((n,) + pieces.shape[1:], bf16),
            pltpu.VMEM((D, WIDE), bf16),
            pltpu.VMEM(head, bf16),
            pltpu.VMEM(head, bf16),
            pltpu.VMEM(head, bf16),
            pltpu.VMEM(head, f32),
            pltpu.VMEM((OWN, GROUP, PAIR, 2 * HEAD), bf16),
            dma((9,)),
            dma((n,)),
            dma((n,)),
            dma((n,)),
            dma((n,)),
            dma((9,)),
            dma((9,)),
            dma((7,)),
            dma((7,)),
            dma((8,)),
            dma((8,)),
            dma((OWN, GROUP)),
            dma((OWN, GROUP)),
            dma((14,)),
        ],
        compiler_params=params(60, collective_id=0, has_side_effects=True),
    )(x, small, pieces, wp, wo, wf)


def middle_kernel(
    x_ref, o_ref, dy_ref, wo_ref, wf_ref, wp_ref, bo_ref, g_ref, s_ref, bf_ref, bp_ref,
    y_ref, dwf_ref, dwp_ref, dbf_ref, dwo_ref, dh_ref, do_ref, small_ref,
    o_s, h_s, b_s, bt_s, y_s, dn_s,
):
    step = pl.program_id(0)
    half = lanes(PAIR) < HEAD
    wf = wf_ref[...].reshape(D, CHUNK)
    wp = wp_ref[...].reshape(CHUNK, D)
    wo = wo_ref[...].reshape(D, D)

    @pl.when(step == 0)
    def _():
        for t in range(HEADS // 2):
            one = o_ref[2 * t // OWN, 2 * t % OWN].astype(f32)
            two = o_ref[(2 * t + 1) // OWN, (2 * t + 1) % OWN].astype(f32)
            at = slice(2 * t * HEAD, (2 * t + 2) * HEAD)
            o_s[:PAIR, at] = jnp.where(half, one, pltpu.roll(two, HEAD, 1)).astype(bf16)
            o_s[PAIR:, at] = jnp.where(half, pltpu.roll(one, HEAD, 1), two).astype(bf16)
        h = x_ref[...].astype(f32) + dot(o_s[...], wo) + bo_ref[...]
        h_s[...] = h
        n, _ = moments(h)
        b_low = (n * g_ref[...] + s_ref[...]).astype(bf16)
        b_s[...] = b_low
        bt_s[...] = b_low.T
        y_s[...] = jnp.zeros_like(y_s)
        dn_s[...] = jnp.zeros_like(dn_s)

    dy = dy_ref[...]
    u = dot(b_s[...], wf) + bf_ref[...]
    square = u * u
    t = jnp.tanh(GELU_A * (u + GELU_B * (square * u)))
    m_low = (0.5 * u * (1.0 + t)).astype(bf16)
    slope = 0.5 * (1.0 + t) + 0.5 * u * (1.0 - t * t) * (GELU_A * (1.0 + 3.0 * GELU_B * square))
    y_s[...] += dot(m_low, wp)
    du = (dot_nt(dy, wp) * slope).astype(bf16)
    dbf_ref[...] = jnp.sum(du.astype(f32), axis=0, keepdims=True)
    dn_s[...] += dot_nt(du, wf)
    dwf_ref[...] = dot(bt_s[...], du).astype(bf16)
    dwp_ref[...] = dot_tn(m_low, dy).astype(bf16)

    @pl.when(step == pl.num_programs(0) - 1)
    def _():
        h = h_s[...]
        y_ref[...] = (h + y_s[...] + bp_ref[...]).astype(bf16)
        n, r = moments(h)
        dn = dn_s[...]
        grad = dy_ref[...].astype(f32)
        small_ref[...] = jnp.zeros_like(small_ref)
        small_ref[0:1, :] = jnp.sum(grad, axis=0, keepdims=True)
        small_ref[1:2, :] = jnp.sum(dn * n, axis=0, keepdims=True)
        small_ref[2:3, :] = jnp.sum(dn, axis=0, keepdims=True)
        e = dn * g_ref[...]
        lean = jnp.mean(e, axis=-1, keepdims=True) + n * jnp.mean(e * n, axis=-1, keepdims=True)
        dh = grad + r * (e - lean)
        dh_ref[...] = dh
        dh_low = dh.astype(bf16)
        small_ref[3:4, :] = jnp.sum(dh_low.astype(f32), axis=0, keepdims=True)
        dwo_ref[...] = dot_tn(o_s[...], dh_low).astype(bf16)
        h_s[...] = dot_nt(dh_low, wo)
        for t in range(HEADS // 2):
            at = slice(2 * t * HEAD, (2 * t + 2) * HEAD)
            top, low = h_s[:PAIR, at], h_s[PAIR:, at]
            one = jnp.where(half, top, pltpu.roll(low, HEAD, 1))
            two = jnp.where(half, pltpu.roll(top, HEAD, 1), low)
            do_ref[2 * t // OWN, 2 * t % OWN] = one.astype(bf16)
            do_ref[(2 * t + 1) // OWN, (2 * t + 1) % OWN] = two.astype(bf16)


def middle(x, o, dy, wall, bo, gain, shift, bf, bp):
    fixed2 = lambda i: (0, 0)
    fixed4 = lambda i: (0, 0, 0, 0)
    square = pl.BlockSpec((TOK, D), fixed2)
    row = pl.BlockSpec((1, D), fixed2)
    heads = pl.BlockSpec((GROUP, OWN, PAIR, 2 * HEAD), fixed4)
    columns = pl.BlockSpec((D, CHUNK), lambda i: (0, i))
    down = pl.BlockSpec((CHUNK, D), lambda i: (i, 0))
    line = pl.BlockSpec((1, CHUNK), lambda i: (0, i))
    shape = jax.ShapeDtypeStruct
    return pl.pallas_call(
        middle_kernel,
        name="middle",
        grid=(FF // CHUNK,),
        out_shape=(
            shape((TOK, D), bf16),
            shape((D, FF), bf16),
            shape((FF, D), bf16),
            shape((1, FF), f32),
            shape((D, D), bf16),
            shape((TOK, D), f32),
            shape((GROUP, OWN, PAIR, 2 * HEAD), bf16),
            shape((8, D), f32),
        ),
        in_specs=[
            square, heads, square,
            pl.BlockSpec((BLOCKS, 48, D), lambda i: (0, 4, 0)),
            pl.BlockSpec((BLOCKS, 48, D), lambda i: (0, 5 + i, 0)),
            pl.BlockSpec((BLOCKS // 4, 192, D), lambda i: (i, 0, 0)),
            row, row, row, line, row,
        ],
        out_specs=(
            square, columns, down, line, square, square, heads, pl.BlockSpec((8, D), fixed2),
        ),
        scratch_shapes=[
            pltpu.VMEM((TOK, D), bf16),
            pltpu.VMEM((TOK, D), f32),
            pltpu.VMEM((TOK, D), bf16),
            pltpu.VMEM((D, TOK), bf16),
            pltpu.VMEM((TOK, D), f32),
            pltpu.VMEM((TOK, D), f32),
        ],
        compiler_params=params(60),
    )(x, o, dy, wall, wall, wall, bo, gain, shift, bf, bp)


def unproject_kernel(dq_ref, dk_ref, dv_ref, a_ref, w_ref, dn_ref, dw_ref, db_ref):
    step = pl.program_id(0)
    mixed = jnp.concatenate(
        [ref[h] for ref in (dq_ref, dk_ref, dv_ref) for h in range(OWN)], axis=1
    )
    dn_ref[...] = dot_nt(mixed, w_ref[...]).astype(bf16)
    dw = dot_tn(a_ref[...], mixed)
    db = jnp.sum(mixed.astype(f32), axis=0, keepdims=True)

    @pl.when(step == 0)
    def _():
        dw_ref[...] = dw
        db_ref[...] = db

    @pl.when(step > 0)
    def _():
        dw_ref[...] += dw
        db_ref[...] += db


def unproject(dq, dk, dv, a, w):
    tile = 768
    head = pl.BlockSpec((OWN, tile, HEAD), lambda i: (0, i, 0))
    whole = lambda i: (0, 0)
    shape = jax.ShapeDtypeStruct
    return pl.pallas_call(
        unproject_kernel,
        name="unproject",
        grid=(ROWS // tile,),
        out_shape=(shape((ROWS, D), bf16), shape((D, WIDE), f32), shape((1, WIDE), f32)),
        in_specs=[
            head, head, head,
            pl.BlockSpec((tile, D), lambda i: (i, 0)),
            pl.BlockSpec((D, WIDE), whole),
        ],
        out_specs=(
            pl.BlockSpec((tile, D), lambda i: (i, 0)),
            pl.BlockSpec((D, WIDE), whole),
            pl.BlockSpec((1, WIDE), whole),
        ),
        compiler_params=params(48),
    )(dq, dk, dv, a, w)


def finish_kernel(x_ref, dh_ref, g_ref, one_ref, two_ref, three_ref, out_ref):
    n, r = moments(x_ref[...].astype(f32))
    dn = one_ref[...].astype(f32) + two_ref[...].astype(f32) + three_ref[...].astype(f32)
    e = dn * g_ref[...]
    lean = jnp.mean(e, axis=-1, keepdims=True) + n * jnp.mean(e * n, axis=-1, keepdims=True)
    out_ref[...] = dh_ref[...] + r * (e - lean)


def finish(x, dh, gain, one, two, three):
    tile = 256
    rows = pl.BlockSpec((tile, D), lambda i: (i, 0))
    return pl.pallas_call(
        finish_kernel,
        name="finish",
        grid=(TOK // tile,),
        out_shape=jax.ShapeDtypeStruct((TOK, D), f32),
        in_specs=[rows, rows, pl.BlockSpec((1, D), lambda i: (0, 0)), rows, rows, rows],
        out_specs=rows,
        compiler_params=params(48),
    )(x, dh, gain, one, two, three)


def flip(block, bit):
    count = lax.axis_size("fsdp")
    return lax.ppermute(block, "fsdp", [(i, i ^ bit) for i in range(count)])


def over_replicas(block):
    count = lax.axis_size("rep")
    held = lax.optimization_barrier(block)
    if count == 2:
        other = lax.ppermute(held, "rep", [(0, 1), (1, 0)])
        return held.astype(f32) + other.astype(f32)
    return lax.psum(held.astype(f32), "rep")


def body(
    block_input, cotangent, tie_index, prefix_len, pre_gain, pre_shift, w_qkv, b_qv, w_out, b_out,
    mid_gain, mid_shift, w_fc, b_fc, w_proj, b_proj,
):
    n = lax.axis_size("fsdp")
    me = lax.axis_index("fsdp")
    pos = lax.rem(me, GROUP)
    rows = D // n
    index = tie_index[0]

    def chosen(bank):
        return lax.dynamic_index_in_dim(bank, index, 0, keepdims=False)

    vectors = (pre_gain, pre_shift, b_qv, b_out, mid_gain, mid_shift, b_fc, b_proj)
    sizes = [bank.shape[1] for bank in vectors]
    count = sum(sizes)
    small = jnp.concatenate([chosen(bank) for bank in vectors])
    high = -(-(rows + 2) // 16) * 16
    reach = prefix_len[0]
    reach_row = jnp.concatenate([reach // 16, reach % 16]).astype(bf16)
    wq = chosen(w_qkv).reshape(rows, 3, GROUP, SLICE).transpose(2, 0, 1, 3).reshape(GROUP, rows, WIDE)
    width = -(-WIDE // 128) * 128
    extra = jnp.stack(
        [jnp.pad(small, (0, width - count)), jnp.pad(reach_row, (0, width - reach_row.shape[0]))]
    )
    wo, wf, wp = chosen(w_out), chosen(w_fc), chosen(w_proj)
    cuts = [sum(sizes[:i]) for i in range(len(sizes) + 1)]

    def vectors_of(lines):
        smalls = lines[:, 0, :count].astype(f32)
        group_rows = lax.dynamic_slice_in_dim(lines[:, 1, :2], me - pos, GROUP, 0)
        reaches = group_rows[:, 0].astype(f32) * 16 + group_rows[:, 1].astype(f32)
        return [
            smalls[:, cuts[i] : cuts[i + 1]].reshape(1, -1) for i in range(len(sizes))
        ], reaches.astype(jnp.int32)

    if n == BLOCKS:
        wall, lines, wq, a_low, qx, k, v, o_full, o_recv = forward(block_input, extra, wq, wp, wo, wf)
        a_low = a_low.reshape(ROWS, D)
        (g1, s1, _, bo, g2, s2, bf, bp), reaches = vectors_of(lines)
    else:
        extra = jnp.pad(extra[:, :WIDE], ((0, high - rows - 2), (0, 0)))
        pieces = jnp.concatenate([wq, jnp.broadcast_to(extra, (GROUP,) + extra.shape)], axis=1)
        wo = lax.all_gather(wo, "fsdp", axis=0, tiled=True).reshape(BLOCKS, -1, D)
        wf = lax.all_gather(wf, "fsdp", axis=0, tiled=True)
        wf = wf.reshape(BLOCKS, D // BLOCKS, FF // D, D).transpose(0, 2, 1, 3)
        wp = lax.all_gather(wp, "fsdp", axis=0, tiled=True).reshape(BLOCKS, -1, D)
        wall = jnp.concatenate([wp, wo, wf.reshape(BLOCKS, -1, D)], axis=1)
        xg, wg = gather_group(n, block_input, pieces)
        wq = wg[:, :rows].reshape(D, WIDE)
        (g1, s1, bqv, bo, g2, s2, bf, bp), reaches = vectors_of(wg[:, rows : rows + 2])
        own_bias = lax.dynamic_index_in_dim(bqv.reshape(2, GROUP, SLICE), pos, 1, keepdims=False)
        bias = jnp.concatenate([own_bias[0], jnp.zeros((SLICE,), f32), own_bias[1]])[None]
        a_low, q, k, v = project(xg.reshape(ROWS, D), wq, g1, s1, bias)
        o_send, o_full, qx = attend(reaches, q, k, v)
        o_recv = swap(o_send, 1, "swap_o")

    y, dwf, dwp, dbf, dwo, dh, do_send, sums = middle(
        block_input, o_recv, cotangent, wall, bo, g2, s2, bf, bp
    )
    dwf = lax.psum_scatter(dwf, "fsdp", scatter_dimension=0, tiled=True)
    dwp = lax.psum_scatter(dwp, "fsdp", scatter_dimension=0, tiled=True)
    dwo = lax.psum_scatter(dwo, "fsdp", scatter_dimension=0, tiled=True)
    do_recv = swap(do_send, 2, "swap_do")
    dq, dk, dv = attend_back(reaches, qx, k, v, o_full, do_recv)
    dn, dwq, db = unproject(dq, dk, dv, a_low, wq)

    dn = dn.reshape(GROUP, TOK, D)
    block_of = lambda bit: lax.dynamic_index_in_dim(dn, pos ^ bit, 0, keepdims=False)
    beside = flip(block_of(1), 1)
    across = flip(block_of(3), 1)
    across = flip((across.astype(f32) + block_of(2).astype(f32)).astype(bf16), 2)

    wq_wide = wq.astype(f32)
    dshift = jnp.sum(wq_wide * db, axis=1)
    dgain = jnp.sum(wq_wide * (dwq - s1.reshape(D, 1) * db), axis=1) / g1.reshape(D)
    where = (jnp.arange(GROUP) == pos).astype(f32)[:, None]
    dbias = jnp.concatenate(
        [(where * db[:, :SLICE]).reshape(-1), (where * db[:, 2 * SLICE :]).reshape(-1)]
    )
    line = jnp.concatenate(
        [
            part.reshape(n, -1)
            for part in (dgain, dshift, dbias, sums[3], sums[1], sums[2], dbf, sums[0])
        ],
        axis=1,
    )
    line_hi = line.astype(bf16)
    line_low = (line - lax.reduce_precision(line, 8, 7)).astype(bf16)
    lines = jnp.pad(jnp.stack([line_hi, line_low], axis=1), ((0, 0), (0, 0), (0, WIDE - count)))
    lines = jnp.pad(lines, ((0, 0), (0, high - rows - 2), (0, 0)))
    back = jnp.concatenate([dwq.astype(bf16).reshape(n, rows, WIDE), lines], axis=1)
    back = swap(back, 3, "swap_grad")
    dwq = jnp.sum(back[:, :rows].astype(f32).reshape(n // GROUP, GROUP, rows, 3, SLICE), axis=0)
    dwq = dwq.transpose(1, 2, 0, 3).reshape(rows, 3 * D)
    line = jnp.sum(back[:, rows, :count].astype(f32) + back[:, rows + 1, :count].astype(f32), axis=0)

    grad = finish(block_input, dh, g1, block_of(0), beside, across)
    dwq = over_replicas(dwq.astype(bf16))
    dwo, dwf, dwp = over_replicas(dwo), over_replicas(dwf), over_replicas(dwp)
    line = over_replicas(line)
    dg1, ds1, dbqv, dbo, dg2, ds2, dbf, dbp = (
        line[cuts[i] : cuts[i + 1]] for i in range(len(sizes))
    )
    return (y, grad, dg1, ds1, dwq, dbqv, dwo, dbo, dg2, ds2, dwf, dbf, dwp, dbp)


def solution(mesh):
    tokens = P(("rep", "fsdp"), None)
    vector, matrix = P(None, "fsdp"), P(None, "fsdp", None)
    return jax.shard_map(
        body,
        mesh=mesh,
        in_specs=(
            tokens, tokens, P(), tokens, vector, vector, matrix, vector, matrix, vector,
            vector, vector, matrix, vector, matrix, vector,
        ),
        out_specs=(
            tokens, tokens, P("fsdp"), P("fsdp"), P("fsdp", None), P("fsdp"), P("fsdp", None),
            P("fsdp"), P("fsdp"), P("fsdp"), P("fsdp", None), P("fsdp"), P("fsdp", None), P("fsdp"),
        ),
        check_vma=False,
    )
```

```python
from functools import partial

import jax
import jax.numpy as jnp
from jax import lax
from jax.experimental import pallas as pl
from jax.experimental.pallas import tpu as pltpu
from jax.sharding import PartitionSpec as P

D = 768
HEADS = 12
HEAD = 64
FF = 3072
GROUP = 4
PROMPT = 512
CONT = 256
TOK = 768
ROWS = GROUP * TOK
OWN = HEADS // GROUP
SLICE = OWN * HEAD
WIDE = 3 * SLICE
PAIR = TOK // 2
CHUNK = 768
BLOCKS = 16
UNIT = 432
NEG = -1e30
EPS = 1e-5
GELU_A = 0.7978845608028654
GELU_B = 0.044715

f32 = jnp.float32
bf16 = jnp.bfloat16
MESH = pl.DeviceIdType.MESH
ANY = pl.BlockSpec(memory_space=pl.ANY)


def params(mib, **more):
    return pltpu.CompilerParams(vmem_limit_bytes=mib << 20, **more)


def dot(a, b):
    return jnp.dot(a, b, preferred_element_type=f32)


def dot_nt(a, b):
    return lax.dot_general(a, b, (((1,), (1,)), ((), ())), preferred_element_type=f32)


def dot_tn(a, b):
    return lax.dot_general(a, b, (((0,), (0,)), ((), ())), preferred_element_type=f32)


def moments(x):
    center = x - jnp.mean(x, axis=-1, keepdims=True)
    scale = lax.rsqrt(jnp.mean(center * center, axis=-1, keepdims=True) + EPS)
    return center * scale, scale


def greet(peers, replica=None):
    sem = pltpu.get_barrier_semaphore()
    for peer in peers:
        pl.semaphore_signal(sem, inc=1, device_id={"fsdp": peer}, device_id_type=MESH)
    if replica is not None:
        pl.semaphore_signal(sem, inc=1, device_id={"rep": replica}, device_id_type=MESH)
    pl.semaphore_wait(sem, len(peers) + (replica is not None))


def gather_kernel(n, parts, x_ref, w_ref, xg_ref, wg_ref, xs, xr, ws, wr, local):
    me = lax.axis_index("fsdp")
    pos = lax.rem(me, GROUP)
    near, far = me ^ 1, me ^ 2
    greet([me ^ i for i in range(1, n)])
    own = pltpu.make_async_copy(x_ref, xg_ref.at[pos], local.at[0])
    own.start()
    own_w = pltpu.make_async_copy(w_ref.at[pos], wg_ref.at[me], local.at[1])
    own_w.start()
    rows = TOK // parts

    def piece(src, slot, part, i, peer):
        at = pl.ds(part * rows, rows)
        return pltpu.make_async_remote_copy(
            src_ref=src.at[at],
            dst_ref=xg_ref.at[slot, at],
            send_sem=xs.at[i],
            recv_sem=xr.at[i],
            device_id={"fsdp": peer},
            device_id_type=MESH,
        )

    across = [piece(x_ref, pos, part, part, far) for part in range(parts)]
    for copy in across:
        copy.start()
    beside = pltpu.make_async_remote_copy(
        src_ref=x_ref,
        dst_ref=xg_ref.at[pos],
        send_sem=xs.at[2 * parts],
        recv_sem=xr.at[2 * parts],
        device_id={"fsdp": near},
        device_id_type=MESH,
    )
    beside.start()
    slices = []
    for i in range(1, n):
        peer = me ^ i
        copy = pltpu.make_async_remote_copy(
            src_ref=w_ref.at[lax.rem(peer, GROUP)],
            dst_ref=wg_ref.at[me],
            send_sem=ws.at[i],
            recv_sem=wr.at[i],
            device_id={"fsdp": peer},
            device_id_type=MESH,
        )
        copy.start()
        slices.append(copy)
    passed = []
    for part in range(parts):
        across[part].wait_recv()
        copy = piece(xg_ref.at[pos ^ 2], pos ^ 2, part, parts + part, near)
        copy.start()
        passed.append(copy)
    for copy in across:
        copy.wait_send()
    beside.wait()
    own.wait()
    own_w.wait()
    for copy in passed + slices:
        copy.wait()


def gather_group(n, x, pieces):
    parts = 4
    dma = pltpu.SemaphoreType.DMA
    return pl.pallas_call(
        partial(gather_kernel, n, parts),
        name="gather_group",
        out_shape=(
            jax.ShapeDtypeStruct((GROUP,) + x.shape, x.dtype),
            jax.ShapeDtypeStruct((n,) + pieces.shape[1:], pieces.dtype),
        ),
        in_specs=[ANY, ANY],
        out_specs=(ANY, ANY),
        scratch_shapes=[
            dma((2 * parts + 1,)),
            dma((2 * parts + 1,)),
            dma((n,)),
            dma((n,)),
            dma((2,)),
        ],
        compiler_params=params(32, collective_id=0, has_side_effects=True),
    )(x, pieces)


def swap_kernel(count, x_ref, o_ref, send, recv, local):
    me = lax.axis_index("fsdp")
    greet([me ^ i for i in range(1, count)])
    slot = lax.rem(me, count)
    own = pltpu.make_async_copy(x_ref.at[slot], o_ref.at[slot], local)
    own.start()
    copies = []
    for i in range(1, count):
        copy = pltpu.make_async_remote_copy(
            src_ref=x_ref.at[slot ^ i],
            dst_ref=o_ref.at[slot],
            send_sem=send.at[i],
            recv_sem=recv.at[i],
            device_id={"fsdp": me ^ i},
            device_id_type=MESH,
        )
        copy.start()
        copies.append(copy)
    own.wait()
    for copy in copies:
        copy.wait()


def swap(x, collective_id, name):
    count = x.shape[0]
    dma = pltpu.SemaphoreType.DMA
    return pl.pallas_call(
        partial(swap_kernel, count),
        name=name,
        out_shape=jax.ShapeDtypeStruct(x.shape, x.dtype),
        in_specs=[ANY],
        out_specs=ANY,
        scratch_shapes=[dma((count,)), dma((count,)), dma],
        compiler_params=params(32, collective_id=collective_id, has_side_effects=True),
    )(x)


def project_kernel(x_ref, w_ref, g_ref, s_ref, b_ref, a_ref, q_ref, k_ref, v_ref):
    n, _ = moments(x_ref[...].astype(f32))
    a_low = (n * g_ref[...] + s_ref[...]).astype(bf16)
    a_ref[...] = a_low
    mixed = (dot(a_low, w_ref[...]) + b_ref[...]).astype(bf16)
    ones = jnp.ones((x_ref.shape[0], HEAD), bf16)
    for h in range(OWN):
        q = mixed[:, h * HEAD : (h + 1) * HEAD] * 0.125
        k = mixed[:, SLICE + h * HEAD : SLICE + (h + 1) * HEAD]
        v = mixed[:, 2 * SLICE + h * HEAD : 2 * SLICE + (h + 1) * HEAD]
        q_ref[h] = jnp.concatenate([q.astype(bf16), jnp.zeros_like(ones)], axis=1)
        k_ref[h] = jnp.concatenate([k, ones], axis=1)
        v_ref[h] = jnp.concatenate([v, ones], axis=1)


def project(x, w, gain, shift, bias):
    tile = 384
    heads = jax.ShapeDtypeStruct((OWN, ROWS, 2 * HEAD), bf16)
    head_spec = pl.BlockSpec((OWN, tile, 2 * HEAD), lambda i: (0, i, 0))
    whole = lambda i: (0, 0)
    return pl.pallas_call(
        project_kernel,
        name="project",
        grid=(ROWS // tile,),
        out_shape=(jax.ShapeDtypeStruct((ROWS, D), bf16), heads, heads, heads),
        in_specs=[
            pl.BlockSpec((tile, D), lambda i: (i, 0)),
            pl.BlockSpec((D, WIDE), whole),
            pl.BlockSpec((1, D), whole),
            pl.BlockSpec((1, D), whole),
            pl.BlockSpec((1, WIDE), whole),
        ],
        out_specs=(pl.BlockSpec((tile, D), lambda i: (i, 0)), head_spec, head_spec, head_spec),
        compiler_params=params(48),
    )(x, w, gain, shift, bias)


def lanes(rows):
    return lax.broadcasted_iota(jnp.int32, (rows, 2 * HEAD), 1)


def split_columns(base, lane, column):
    hi = column.astype(bf16).astype(f32)
    mid = (column - hi).astype(bf16).astype(f32)
    low = column - hi - mid
    tail = jnp.where(lane == HEAD, -hi, jnp.where(lane == HEAD + 1, -mid, -low))
    return jnp.where(lane < HEAD, base, jnp.where(lane < HEAD + 3, tail, 0.0)).astype(bf16)


def below(rows, cols, low_key):
    row = lax.broadcasted_iota(jnp.int32, (rows, cols), 0)
    col = lax.broadcasted_iota(jnp.int32, (rows, cols), 1)
    return row <= col if low_key else col <= row


def attend_kernel(reach_ref, q_ref, k_ref, v_ref, o_ref, f_ref, x_ref):
    T = CONT
    lane = lanes(T)
    causal = below(T, T, False)

    def tile(at, blocks):
        q = q_ref[0, pl.ds(at, T), :]
        scores = []
        for start, size, mask in blocks:
            s = dot_nt(q, k_ref[0, pl.ds(start, size), :])
            scores.append(s if mask is None else jnp.where(mask, s, NEG))
        peak = scores[0].max(axis=1, keepdims=True)
        for s in scores[1:]:
            peak = jnp.maximum(peak, s.max(axis=1, keepdims=True))
        total = jnp.zeros((T, 2 * HEAD), f32)
        for s, (start, size, _) in zip(scores, blocks):
            total += dot(jnp.exp(s - peak).astype(bf16), v_ref[0, pl.ds(start, size), :])
        mass = total[:, HEAD : HEAD + 1]
        f_ref[0, pl.ds(at, T), :] = total / mass
        lse = peak + jnp.log(mass)
        x_ref[0, pl.ds(at, T), :] = split_columns(q.astype(f32), lane, lse)

    for p in range(GROUP):
        past = [(i * TOK, PROMPT, None) for i in range(p)]
        base = p * TOK
        tile(base, past + [(base, T, causal)])
        tile(base + T, past + [(base, T, None), (base + T, T, causal)])

    def cont(c, carry):
        at = pl.multiple_of(c * TOK + PROMPT, CONT)
        reach = reach_ref[c]
        col = lax.broadcasted_iota(jnp.int32, (T, PROMPT), 1)
        blocks = [(i * TOK, PROMPT, col < reach - i * PROMPT) for i in range(GROUP)]
        tile(at, blocks + [(at, T, causal)])
        return carry

    lax.fori_loop(0, GROUP, cont, 0)

    half = lanes(PAIR) < HEAD
    for p in range(GROUP):
        top = f_ref[0, p * TOK : p * TOK + PAIR, :]
        low = f_ref[0, p * TOK + PAIR : (p + 1) * TOK, :]
        o_ref[p, 0] = jnp.where(half, top, pltpu.roll(low, HEAD, 1)).astype(bf16)


def attend(reach, q, k, v):
    head = lambda h: (h, 0, 0)
    spec = pl.BlockSpec((1, ROWS, 2 * HEAD), head)
    return pl.pallas_call(
        attend_kernel,
        name="attend",
        grid=(OWN,),
        out_shape=(
            jax.ShapeDtypeStruct((GROUP, OWN, PAIR, 2 * HEAD), bf16),
            jax.ShapeDtypeStruct((OWN, ROWS, 2 * HEAD), f32),
            jax.ShapeDtypeStruct((OWN, ROWS, 2 * HEAD), bf16),
        ),
        in_specs=[pl.BlockSpec(memory_space=pltpu.SMEM), spec, spec, spec],
        out_specs=(
            pl.BlockSpec((GROUP, 1, PAIR, 2 * HEAD), lambda h: (0, h, 0, 0)),
            spec,
            spec,
        ),
        compiler_params=params(56),
    )(reach, q, k, v)


def attend_back_kernel(
    reach_ref, q_ref, k_ref, v_ref, f_ref, g_ref, dq_ref, dk_ref, dv_ref, g_s, dq_s, kt_s, dk_s, dv_s
):
    T = CONT
    half = lanes(PAIR) < HEAD
    lane = lanes(PAIR)
    for p in range(GROUP):
        packed = g_ref[p, 0].astype(f32)
        for i, block in enumerate((packed, pltpu.roll(packed, HEAD, 1))):
            at = p * TOK + i * PAIR
            prod = jnp.where(half, block * f_ref[0, at : at + PAIR, :], 0.0)
            inner = jnp.sum(prod, axis=1, keepdims=True)
            g_s[at : at + PAIR, :] = split_columns(block, lane, inner)
        kt_s[:, p * TOK : (p + 1) * TOK] = k_ref[0, p * TOK : (p + 1) * TOK, :].T[:HEAD]
    dq_s[...] = jnp.zeros_like(dq_s)

    def block(keys, size, rows, count, mask, first, key_at):
        kb = k_ref[0, pl.ds(keys, size), :]
        vb = v_ref[0, pl.ds(keys, size), :]
        q = q_ref[0, pl.ds(rows, count), :]
        g = g_s[pl.ds(rows, count), :]
        probs = jnp.exp(dot_nt(kb, q))
        if mask is not None:
            probs = jnp.where(mask, probs, 0.0)
        ds = (probs * dot_nt(vb, g)).astype(bf16)
        dv = dot(probs.astype(bf16), g)
        dk = dot(ds, q)
        at = pl.ds(key_at, size)
        dv_s[at, :] = dv if first else dv_s[at, :] + dv
        dk_s[at, :] = dk if first else dk_s[at, :] + dk
        dq_s[:, pl.ds(rows, count)] += dot(kt_s[:, pl.ds(keys, size)], ds)

    causal = below(T, T, True)
    for p in range(GROUP):
        base = p * TOK
        block(base, T, base, T, causal, True, 0)
        block(base + T, T, base + T, T, causal, True, T)
        block(base, T, base + T, T, None, False, 0)

        def later(i, carry):
            rows = pl.multiple_of(i * TOK, CONT)
            block(base, PROMPT, rows, PROMPT, None, False, 0)
            return carry

        lax.fori_loop(p + 1, GROUP, later, 0)

        def cont(c, carry):
            rows = pl.multiple_of(c * TOK + PROMPT, CONT)
            key = lax.broadcasted_iota(jnp.int32, (PROMPT, T), 0)
            block(base, PROMPT, rows, T, key < reach_ref[c] - p * PROMPT, False, 0)
            return carry

        lax.fori_loop(0, GROUP, cont, 0)
        dk_ref[0, base : base + PROMPT, :] = dk_s[:, :HEAD].astype(bf16)
        dv_ref[0, base : base + PROMPT, :] = dv_s[:, :HEAD].astype(bf16)

    def own(c, carry):
        at = pl.multiple_of(c * TOK + PROMPT, CONT)
        block(at, T, at, T, causal, True, 0)
        dk_ref[0, pl.ds(at, T), :] = dk_s[:T, :HEAD].astype(bf16)
        dv_ref[0, pl.ds(at, T), :] = dv_s[:T, :HEAD].astype(bf16)
        return carry

    lax.fori_loop(0, GROUP, own, 0)
    for i in range(ROWS // PROMPT):
        at = i * PROMPT
        dq_ref[0, at : at + PROMPT, :] = (dq_s[:, at : at + PROMPT].T * 0.125).astype(bf16)


def attend_back(reach, q, k, v, f, g):
    head = lambda h: (h, 0, 0)
    spec = pl.BlockSpec((1, ROWS, 2 * HEAD), head)
    out = jax.ShapeDtypeStruct((OWN, ROWS, HEAD), bf16)
    out_spec = pl.BlockSpec((1, ROWS, HEAD), head)
    return pl.pallas_call(
        attend_back_kernel,
        name="attend_back",
        grid=(OWN,),
        out_shape=(out, out, out),
        in_specs=[pl.BlockSpec(memory_space=pltpu.SMEM), spec, spec, spec, spec]
        + [pl.BlockSpec((GROUP, 1, PAIR, 2 * HEAD), lambda h: (0, h, 0, 0))],
        out_specs=(out_spec, out_spec, out_spec),
        scratch_shapes=[
            pltpu.VMEM((ROWS, 2 * HEAD), bf16),
            pltpu.VMEM((HEAD, ROWS), f32),
            pltpu.VMEM((HEAD, ROWS), bf16),
            pltpu.VMEM((PROMPT, 2 * HEAD), f32),
            pltpu.VMEM((PROMPT, 2 * HEAD), f32),
        ],
        compiler_params=params(56),
    )(reach, q, k, v, f, g)


def pick_kernel(index_ref, reach_ref, *refs):
    vectors, (wq_ref, wo_ref, wf_ref, wp_ref), (small_ref, piece_ref, shard_ref) = (
        refs[:8], refs[8:12], refs[12:],
    )
    index = index_ref[0]
    rows = []
    for ref in vectors:
        bank = ref[...].astype(f32)
        chosen = lax.broadcasted_iota(jnp.int32, bank.shape, 0) == index
        rows.append(jnp.sum(jnp.where(chosen, bank, 0.0), axis=0, keepdims=True))
    width = sum(row.shape[1] for row in rows)
    rest = small_ref.shape[1] - width
    small_ref[0:1, :] = jnp.concatenate(rows + [jnp.zeros((1, rest), f32)], axis=1).astype(bf16)
    reach = reach_ref[0, 0]
    lane = lax.broadcasted_iota(jnp.int32, (1, small_ref.shape[1]), 1)
    code = jnp.where(lane == 0, reach // 16, jnp.where(lane == 1, lax.rem(reach, 16), 0))
    small_ref[1:2, :] = code.astype(f32).astype(bf16)
    for j in range(GROUP):
        for part in range(3):
            at = part * D + j * SLICE
            piece_ref[j, :, part * SLICE : (part + 1) * SLICE] = wq_ref[0, :, at : at + SLICE]
    shard_ref[:192, :] = wp_ref[0]
    shard_ref[192:240, :] = wo_ref[0]
    for c in range(FF // D):
        shard_ref[240 + 48 * c : 288 + 48 * c, :] = wf_ref[0, :, c * D : (c + 1) * D]


def pick(index, reach, vectors, wq, wo, wf, wp):
    shape = jax.ShapeDtypeStruct
    chosen = lambda bank: pl.BlockSpec((1,) + bank.shape[1:], lambda i, at: (at[0], 0, 0))
    whole = lambda bank: pl.BlockSpec(bank.shape, lambda i, at: (0, 0))
    fixed3 = lambda i, at: (0, 0, 0)
    return pl.pallas_call(
        pick_kernel,
        name="pick",
        out_shape=(
            shape((2, 640), bf16), shape((GROUP, D // BLOCKS, WIDE), bf16), shape((UNIT, D), bf16),
        ),
        grid_spec=pltpu.PrefetchScalarGridSpec(
            num_scalar_prefetch=1,
            grid=(1,),
            in_specs=[pl.BlockSpec(memory_space=pltpu.SMEM)]
            + [whole(bank) for bank in vectors]
            + [chosen(bank) for bank in (wq, wo, wf, wp)],
            out_specs=(
                pl.BlockSpec((2, 640), lambda i, at: (0, 0)),
                pl.BlockSpec((GROUP, D // BLOCKS, WIDE), fixed3),
                pl.BlockSpec((UNIT, D), lambda i, at: (0, 0)),
            ),
        ),
        compiler_params=params(60),
    )(index, reach, *vectors, wq, wo, wf, wp)


def ring_of(me):
    chip, core = me // 2, lax.rem(me, 2)
    z, x = chip // 2, lax.rem(chip, 2)
    chips = BLOCKS // 2
    half = chips // 2
    place = z * (1 - x) + (chips - 1 - z) * x

    def device(at):
        at = lax.rem(at + 2 * chips, chips)
        side = at // half
        z_at = at * (1 - side) + (chips - 1 - at) * side
        return (z_at * 2 + side) * 2 + core

    return place, device


def forward_kernel(
    x_ref, sm_ref, pc_ref, sh_ref,
    wall_ref, smo_ref, wq_ref, a_ref, q_ref, k_ref, v_ref, f_ref, o_ref,
    xg, smg, wg, w_s, q_s, k_s, v_s, f_s, o_s,
    local, sm_send, sm_recv, w_send, w_recv, x_send, x_recv, r_send, r_recv, n_send, n_recv,
    y_send, y_recv, o_send, o_recv, out_sem,
):
    n = BLOCKS
    me = lax.axis_index("fsdp")
    rep = lax.axis_index("rep")
    pos = lax.rem(me, GROUP)
    base = me - pos
    near, far = me ^ 1, me ^ 2
    place, device = ring_of(me)
    parts = 4
    part_rows = TOK // parts
    T = CONT

    def remote(src, dst, send, recv, peer):
        return pltpu.make_async_remote_copy(
            src_ref=src,
            dst_ref=dst,
            send_sem=send,
            recv_sem=recv,
            device_id=peer if isinstance(peer, dict) else {"fsdp": peer},
            device_id_type=MESH,
        )

    greet([me ^ i for i in range(1, n)], 1 - rep)

    own_block = pltpu.make_async_copy(sh_ref, wall_ref.at[me], local.at[0])
    own_x = pltpu.make_async_copy(x_ref, xg.at[pos], local.at[1])
    own_w = pltpu.make_async_copy(pc_ref.at[pos], wg.at[me], local.at[2])
    own_s = pltpu.make_async_copy(sm_ref, smg.at[me], local.at[3])
    for copy in (own_s, own_w, own_x, own_block):
        copy.start()

    slices = []
    for i in range(1, GROUP):
        copy = remote(pc_ref.at[pos ^ i], wg.at[me], w_send.at[i], w_recv.at[i], me ^ i)
        copy.start()
        slices.append(copy)
    smalls = []
    for i in range(1, n):
        copy = remote(sm_ref, smg.at[me], sm_send.at[i], sm_recv.at[i], me ^ i)
        copy.start()
        smalls.append(copy)
    beside = remote(x_ref, xg.at[pos], x_send.at[2 * parts], x_recv.at[2 * parts], near)
    beside.start()

    def x_part(src, slot, part, i, peer):
        at = pl.ds(part * part_rows, part_rows)
        return remote(src.at[at], xg.at[slot, at], x_send.at[i], x_recv.at[i], peer)

    across = [x_part(x_ref, pos, part, part, far) for part in range(parts)]
    for copy in across:
        copy.start()

    mine = pl.ds(pl.multiple_of(rep * (D // 2), D // 2), D // 2)
    other = pl.ds(pl.multiple_of((1 - rep) * (D // 2), D // 2), D // 2)
    sides = lambda t: (True, False) if t < 3 else (True,)
    key = lambda t, right: t if right else 4 + t

    def came(t, right):
        return device(place - 1 - t if right else place + 1 + t)

    def hop(t, right):
        block = wall_ref.at[device(place - t if right else place + t), :, mine]
        src = sh_ref.at[:, mine] if t == 0 else block
        i = key(t, right)
        return remote(src, block, r_send.at[i], r_recv.at[i], device(place + 1 if right else place - 1))

    def to_near(t, right, columns, i):
        block = wall_ref.at[came(t, right), :, columns]
        return remote(block, block, n_send.at[i], n_recv.at[i], near)

    def to_replica(t, right):
        block = wall_ref.at[came(t, right), :, mine]
        i = key(t, right)
        return remote(block, block, y_send.at[i], y_recv.at[i], {"rep": 1 - rep})

    def from_replica(t, right):
        block = wall_ref.at[came(t, right), :, other]
        i = key(t, right)
        return remote(block, block, y_send.at[i], y_recv.at[i], {"rep": 1 - rep})

    hops, sent, shared = {}, [], []

    def begin(copy, keep):
        copy.start()
        keep.append(copy)

    def launch(t):
        for right in sides(t):
            hops[t, right] = hop(t, right)
            hops[t, right].start()

    def arrive(t):
        for right in sides(t):
            hops[t, right].wait_recv()
        if t < 3:
            launch(t + 1)
        for right in sides(t):
            begin(to_replica(t, right), sent)
            begin(to_near(t, right, mine, 1 + key(t, right)), shared)

    def settle(t):
        for right in sides(t):
            from_replica(t, right).wait_recv()
            begin(to_near(t, right, other, 8 + key(t, right)), shared)

    launch(0)
    begin(remote(sh_ref, wall_ref.at[me], n_send.at[0], n_recv.at[0], near), shared)

    own_s.wait()
    for copy in smalls:
        copy.wait_recv()
    rows48 = D // n
    gain = jnp.concatenate([smg[d, 0:1, 0:rows48] for d in range(n)], axis=1).astype(f32)
    shift = jnp.concatenate([smg[d, 0:1, rows48 : 2 * rows48] for d in range(n)], axis=1).astype(f32)
    at = 2 * rows48
    two = 2 * rows48
    zeros = jnp.zeros((1, SLICE), bf16)
    bias = jnp.concatenate(
        [smg[2 * pos + i, 0:1, at : at + two] for i in range(2)]
        + [zeros]
        + [smg[n // 2 + 2 * pos + i, 0:1, at : at + two] for i in range(2)],
        axis=1,
    ).astype(f32)

    def norm(slot):
        def some(i, carry):
            at = pl.ds(pl.multiple_of(i * PAIR, PAIR), PAIR)
            n_rows, _ = moments(xg[slot, at, :].astype(f32))
            xg[slot, at, :] = (n_rows * gain + shift).astype(bf16)
            return carry

        lax.fori_loop(0, 2, some, 0)

    def project_block(slot):
        def some(i, carry):
            at = pl.ds(pl.multiple_of(i * PAIR, PAIR), PAIR)
            out = pl.ds(pl.multiple_of(slot * TOK + i * PAIR, PAIR), PAIR)
            mixed = (dot(xg[slot, at, :], w_s[...]) + bias).astype(bf16)
            ones = jnp.ones((PAIR, HEAD), bf16)
            for h in range(OWN):
                q = mixed[:, h * HEAD : (h + 1) * HEAD] * 0.125
                k = mixed[:, SLICE + h * HEAD : SLICE + (h + 1) * HEAD]
                v = mixed[:, 2 * SLICE + h * HEAD : 2 * SLICE + (h + 1) * HEAD]
                q_s[h, out, :] = jnp.concatenate([q.astype(bf16), jnp.zeros_like(ones)], axis=1)
                k_s[h, out, :] = jnp.concatenate([k, ones], axis=1)
                v_s[h, out, :] = jnp.concatenate([v, ones], axis=1)
            return carry

        lax.fori_loop(0, 2, some, 0)

    own_w.wait()
    for copy in slices:
        copy.wait_recv()
    group = pl.ds(base, GROUP)
    wide = []
    for i in range(1, n // GROUP):
        begin(
            remote(wg.at[group], wg.at[group], w_send.at[GROUP + i], w_recv.at[GROUP + i], me ^ (GROUP * i)),
            wide,
        )
    own_x.wait()
    norm(pos)
    beside.wait()
    norm(pos ^ 1)
    for copy in wide:
        copy.wait_recv()
    arrive(0)
    w_s[...] = wg[:, :rows48, :].reshape(D, WIDE)
    project_block(pos)
    project_block(pos ^ 1)
    passed = []
    for part in range(parts):
        across[part].wait_recv()
        copy = x_part(xg.at[pos ^ 2], pos ^ 2, part, parts + part, near)
        copy.start()
        passed.append(copy)
    for copy in passed:
        copy.wait()
    norm(pos ^ 2)
    project_block(pos ^ 2)
    norm(pos ^ 3)
    project_block(pos ^ 3)
    arrive(1)

    outs = [
        pltpu.make_async_copy(smg, smo_ref, out_sem.at[0]),
        pltpu.make_async_copy(w_s, wq_ref, out_sem.at[1]),
        pltpu.make_async_copy(xg, a_ref, out_sem.at[2]),
        pltpu.make_async_copy(k_s, k_ref, out_sem.at[3]),
        pltpu.make_async_copy(v_s, v_ref, out_sem.at[4]),
    ]
    for copy in outs:
        copy.start()

    lane = lanes(T)
    causal = below(T, T, False)
    half = lanes(PAIR) < HEAD
    code = [smg[base + c, 1:2, 0:2].astype(f32) for c in range(GROUP)]
    reaches = [c[:, 0:1] * 16.0 + c[:, 1:2] for c in code]
    column = lax.broadcasted_iota(jnp.int32, (T, PROMPT), 1).astype(f32)

    for h in range(OWN):

        def tile(at, blocks):
            q = q_s[h, pl.ds(at, T), :]
            scores = []
            for start, size, mask in blocks:
                s = dot_nt(q, k_s[h, pl.ds(start, size), :])
                scores.append(s if mask is None else jnp.where(mask, s, NEG))
            peak = scores[0].max(axis=1, keepdims=True)
            for s in scores[1:]:
                peak = jnp.maximum(peak, s.max(axis=1, keepdims=True))
            total = jnp.zeros((T, 2 * HEAD), f32)
            for s, (start, size, _) in zip(scores, blocks):
                total += dot(jnp.exp(s - peak).astype(bf16), v_s[h, pl.ds(start, size), :])
            mass = total[:, HEAD : HEAD + 1]
            f_s[h, pl.ds(at, T), :] = total / mass
            lse = peak + jnp.log(mass)
            q_s[h, pl.ds(at, T), :] = split_columns(q.astype(f32), lane, lse)

        for p in range(GROUP):
            past = [(i * TOK, PROMPT, None) for i in range(p)]
            at = p * TOK
            tile(at, past + [(at, T, causal)])
            tile(at + T, past + [(at, T, None), (at + T, T, causal)])
        if h == 0:
            arrive(2)
        if h == 1:
            arrive(3)
            settle(0)
        if h == 2:
            settle(1)
        for c in range(GROUP):
            at = c * TOK + PROMPT
            blocks = [(i * TOK, PROMPT, column < reaches[c] - i * PROMPT) for i in range(GROUP)]
            tile(at, blocks + [(at, T, causal)])
        for p in range(GROUP):
            top = f_s[h, p * TOK : p * TOK + PAIR, :]
            low = f_s[h, p * TOK + PAIR : (p + 1) * TOK, :]
            o_s[h, p] = jnp.where(half, top, pltpu.roll(low, HEAD, 1)).astype(bf16)
        for i in range(1, GROUP):
            copy = remote(
                o_s.at[h, pos ^ i], o_ref.at[pos, h], o_send.at[h, i], o_recv.at[h, i], me ^ i
            )
            copy.start()
            shared.append(copy)
        for src, dst, i in (
            (o_s.at[h, pos], o_ref.at[pos, h], 5 + h),
            (f_s.at[h], f_ref.at[h], 8 + h),
            (q_s.at[h], q_ref.at[h], 11 + h),
        ):
            copy = pltpu.make_async_copy(src, dst, out_sem.at[i])
            copy.start()
            outs.append(copy)

    settle(2)
    settle(3)
    for copy in across + smalls + slices + wide + list(hops.values()) + sent:
        copy.wait_send()
    own_block.wait()
    for copy in shared + outs:
        copy.wait()


def forward(x, small, pieces, shard):
    dma = pltpu.SemaphoreType.DMA
    n = BLOCKS
    shape = jax.ShapeDtypeStruct
    head = (OWN, ROWS, 2 * HEAD)
    return pl.pallas_call(
        forward_kernel,
        name="forward",
        out_shape=(
            shape((n, UNIT, D), bf16),
            shape((n,) + small.shape, bf16),
            shape((D, WIDE), bf16),
            shape((GROUP, TOK, D), bf16),
            shape(head, bf16),
            shape(head, bf16),
            shape(head, bf16),
            shape(head, f32),
            shape((GROUP, OWN, PAIR, 2 * HEAD), bf16),
        ),
        in_specs=[ANY] * 4,
        out_specs=(ANY,) * 9,
        scratch_shapes=[
            pltpu.VMEM((GROUP, TOK, D), bf16),
            pltpu.VMEM((n,) + small.shape, bf16),
            pltpu.VMEM((n,) + pieces.shape[1:], bf16),
            pltpu.VMEM((D, WIDE), bf16),
            pltpu.VMEM(head, bf16),
            pltpu.VMEM(head, bf16),
            pltpu.VMEM(head, bf16),
            pltpu.VMEM(head, f32),
            pltpu.VMEM((OWN, GROUP, PAIR, 2 * HEAD), bf16),
            dma((4,)),
            dma((n,)),
            dma((n,)),
            dma((2 * GROUP,)),
            dma((2 * GROUP,)),
            dma((9,)),
            dma((9,)),
            dma((7,)),
            dma((7,)),
            dma((15,)),
            dma((15,)),
            dma((7,)),
            dma((7,)),
            dma((OWN, GROUP)),
            dma((OWN, GROUP)),
            dma((14,)),
        ],
        compiler_params=params(60, collective_id=0, has_side_effects=True),
    )(x, small, pieces, shard)


def middle_kernel(
    x_ref, o_ref, dy_ref, wo_ref, wf_ref, wp_ref, bo_ref, g_ref, s_ref, bf_ref, bp_ref,
    y_ref, dwf_ref, dwp_ref, dbf_ref, dwo_ref, dh_ref, do_ref, small_ref,
    o_s, h_s, b_s, bt_s, y_s, dn_s,
):
    step = pl.program_id(0)
    half = lanes(PAIR) < HEAD
    wf = wf_ref[...].reshape(D, CHUNK)
    wp = wp_ref[...].reshape(CHUNK, D)
    wo = wo_ref[...].reshape(D, D)

    @pl.when(step == 0)
    def _():
        for t in range(HEADS // 2):
            one = o_ref[2 * t // OWN, 2 * t % OWN].astype(f32)
            two = o_ref[(2 * t + 1) // OWN, (2 * t + 1) % OWN].astype(f32)
            at = slice(2 * t * HEAD, (2 * t + 2) * HEAD)
            o_s[:PAIR, at] = jnp.where(half, one, pltpu.roll(two, HEAD, 1)).astype(bf16)
            o_s[PAIR:, at] = jnp.where(half, pltpu.roll(one, HEAD, 1), two).astype(bf16)
        h = x_ref[...].astype(f32) + dot(o_s[...], wo) + bo_ref[...]
        h_s[...] = h
        n, _ = moments(h)
        b_low = (n * g_ref[...] + s_ref[...]).astype(bf16)
        b_s[...] = b_low
        bt_s[...] = b_low.T
        y_s[...] = jnp.zeros_like(y_s)
        dn_s[...] = jnp.zeros_like(dn_s)

    dy = dy_ref[...]
    u = dot(b_s[...], wf) + bf_ref[...]
    square = u * u
    t = jnp.tanh(GELU_A * (u + GELU_B * (square * u)))
    m_low = (0.5 * u * (1.0 + t)).astype(bf16)
    slope = 0.5 * (1.0 + t) + 0.5 * u * (1.0 - t * t) * (GELU_A * (1.0 + 3.0 * GELU_B * square))
    y_s[...] += dot(m_low, wp)
    du = (dot_nt(dy, wp) * slope).astype(bf16)
    dbf_ref[...] = jnp.sum(du.astype(f32), axis=0, keepdims=True)
    dn_s[...] += dot_nt(du, wf)
    dwf_ref[...] = dot(bt_s[...], du).astype(bf16).reshape(dwf_ref.shape)
    dwp_ref[...] = dot_tn(m_low, dy).astype(bf16)

    @pl.when(step == pl.num_programs(0) - 1)
    def _():
        h = h_s[...]
        y_ref[...] = (h + y_s[...] + bp_ref[...]).astype(bf16)
        n, r = moments(h)
        dn = dn_s[...]
        grad = dy_ref[...].astype(f32)
        small_ref[...] = jnp.zeros_like(small_ref)
        small_ref[0:1, :] = jnp.sum(grad, axis=0, keepdims=True)
        small_ref[1:2, :] = jnp.sum(dn * n, axis=0, keepdims=True)
        small_ref[2:3, :] = jnp.sum(dn, axis=0, keepdims=True)
        e = dn * g_ref[...]
        lean = jnp.mean(e, axis=-1, keepdims=True) + n * jnp.mean(e * n, axis=-1, keepdims=True)
        dh = grad + r * (e - lean)
        dh_ref[...] = dh
        dh_low = dh.astype(bf16)
        small_ref[3:4, :] = jnp.sum(dh_low.astype(f32), axis=0, keepdims=True)
        dwo_ref[...] = dot_tn(o_s[...], dh_low).astype(bf16)
        h_s[...] = dot_nt(dh_low, wo)
        for t in range(HEADS // 2):
            at = slice(2 * t * HEAD, (2 * t + 2) * HEAD)
            top, low = h_s[:PAIR, at], h_s[PAIR:, at]
            one = jnp.where(half, top, pltpu.roll(low, HEAD, 1))
            two = jnp.where(half, pltpu.roll(top, HEAD, 1), low)
            do_ref[2 * t // OWN, 2 * t % OWN] = one.astype(bf16)
            do_ref[(2 * t + 1) // OWN, (2 * t + 1) % OWN] = two.astype(bf16)


def middle(x, o, dy, wall, bo, gain, shift, bf, bp):
    fixed2 = lambda i: (0, 0)
    fixed4 = lambda i: (0, 0, 0, 0)
    square = pl.BlockSpec((TOK, D), fixed2)
    row = pl.BlockSpec((1, D), fixed2)
    heads = pl.BlockSpec((GROUP, OWN, PAIR, 2 * HEAD), fixed4)
    columns = pl.BlockSpec((BLOCKS, 1, D // BLOCKS, D), lambda i: (0, i, 0, 0))
    down = pl.BlockSpec((CHUNK, D), lambda i: (i, 0))
    line = pl.BlockSpec((1, CHUNK), lambda i: (0, i))
    shape = jax.ShapeDtypeStruct
    return pl.pallas_call(
        middle_kernel,
        name="middle",
        grid=(FF // CHUNK,),
        out_shape=(
            shape((TOK, D), bf16),
            shape((BLOCKS, FF // D, D // BLOCKS, D), bf16),
            shape((FF, D), bf16),
            shape((1, FF), f32),
            shape((D, D), bf16),
            shape((TOK, D), f32),
            shape((GROUP, OWN, PAIR, 2 * HEAD), bf16),
            shape((8, D), f32),
        ),
        in_specs=[
            square, heads, square,
            pl.BlockSpec((BLOCKS, 48, D), lambda i: (0, 4, 0)),
            pl.BlockSpec((BLOCKS, 48, D), lambda i: (0, 5 + i, 0)),
            pl.BlockSpec((BLOCKS // 4, 192, D), lambda i: (i, 0, 0)),
            row, row, row, line, row,
        ],
        out_specs=(
            square, columns, down, line, square, square, heads, pl.BlockSpec((8, D), fixed2),
        ),
        scratch_shapes=[
            pltpu.VMEM((TOK, D), bf16),
            pltpu.VMEM((TOK, D), f32),
            pltpu.VMEM((TOK, D), bf16),
            pltpu.VMEM((D, TOK), bf16),
            pltpu.VMEM((TOK, D), f32),
            pltpu.VMEM((TOK, D), f32),
        ],
        compiler_params=params(60),
    )(x, o, dy, wall, wall, wall, bo, gain, shift, bf, bp)


ORDER = (4, -3, 3, -2, 2, -1, 1, 0)
SMALL = 16


def backward_kernel(
    do_ref, q_ref, k_ref, v_ref, f_ref, a_ref, w_ref, x_ref, dh_ref, lines_ref, sums_ref, dbf_ref,
    dwp_ref, dwo_ref, dwf_ref,
    grad_ref, gq_ref, gp_ref, go_ref, gf_ref, small_ref,
    g_b, q_s, k_s, v_s, f_b, a_s, w_s, x_s, dh_s, lines_s, sums_s, dbf_s,
    near_b, mine_b, ring_b, fin_b, fin_r, fin_o,
    g_s, dq_s, kt_s, dk_s, dv_s, dm_s, w_h, acc_s, db_s,
    dw_b, z_b, j_b, j_r, rep_b, rep_r, gq_o,
    dn_a, dn_b, dn_c, dn_ra, dn_rb, dn_rc, dn_o, sm_b, sm_r,
    load, mine_sem, g_send, g_recv, n_send, n_recv, r_send, r_recv, fin_send, fin_recv,
    z_send, z_recv, j_send, j_recv, rep_send, rep_recv, d_send, d_recv, s_send, s_recv, out_sem,
):
    n = BLOCKS
    me = lax.axis_index("fsdp")
    rep = lax.axis_index("rep")
    pos = lax.rem(me, GROUP)
    base = me - pos
    level = me // GROUP
    near, far = me ^ 1, me ^ 2
    place, device = ring_of(me)
    T = CONT
    W3 = 3 * HEAD
    other = {"rep": 1 - rep}

    def remote(src, dst, send, recv, peer):
        return pltpu.make_async_remote_copy(
            src_ref=src,
            dst_ref=dst,
            send_sem=send,
            recv_sem=recv,
            device_id=peer if isinstance(peer, dict) else {"fsdp": peer},
            device_id_type=MESH,
        )

    greet([me ^ i for i in range(1, n)], 1 - rep)

    def do_copy(h, i):
        return remote(do_ref.at[pos ^ i, h], g_b.at[pos, h], g_send.at[h, i], g_recv.at[h, i], me ^ i)

    own_do = pltpu.make_async_copy(do_ref.at[pos], g_b.at[pos], load.at[0])
    own_do.start()
    for h in range(OWN):
        for i in range(1, GROUP):
            do_copy(h, i).start()

    def f_copy(h):
        return pltpu.make_async_copy(f_ref.at[h], f_b, load.at[1])

    first = [
        pltpu.make_async_copy(src, dst, load.at[2 + i])
        for i, (src, dst) in enumerate(
            ((q_ref, q_s), (k_ref, k_s), (v_ref, v_s), (lines_ref, lines_s), (w_ref, w_s))
        )
    ]
    later = [
        pltpu.make_async_copy(src, dst, load.at[7 + i])
        for i, (src, dst) in enumerate(
            ((a_ref, a_s), (x_ref, x_s), (dh_ref, dh_s), (sums_ref, sums_s), (dbf_ref, dbf_s))
        )
    ]
    f_copy(0).start()
    for copy in first:
        copy.start()

    cut = ((0, 192), (192, 48), (240, 192))

    def near_copies(i):
        d = device(place + ORDER[i]) ^ 1
        return [
            remote(ref.at[d], near_b.at[i, pl.ds(at, size)], n_send.at[i, k], n_recv.at[i, k], near)
            for k, (ref, (at, size)) in enumerate(zip((dwp_ref, dwo_ref, dwf_ref), cut))
        ]

    def mine_copies(i):
        d = device(place + ORDER[i])
        return [
            pltpu.make_async_copy(ref.at[d], mine_b.at[i % 4, pl.ds(at, size)], mine_sem.at[i, k])
            for k, (ref, (at, size)) in enumerate(zip((dwp_ref, dwo_ref, dwf_ref), cut))
        ]

    for i in range(8):
        for copy in near_copies(i):
            copy.start()
    for i in range(4):
        for copy in mine_copies(i):
            copy.start()
    for copy in later:
        copy.start()

    def ready(i):
        for copy in near_copies(i):
            copy.wait_recv()
        for copy in mine_copies(i):
            copy.wait()

    def ring_copy(t, right):
        i = 2 * t if right else 2 * t + 1
        slot = t if right else 4 + t
        peer = device(place + 1 if right else place - 1)
        return remote(near_b.at[i], ring_b.at[slot], r_send.at[slot], r_recv.at[slot], peer)

    def rounds(some):
        def chunk(c, carry):
            some(pl.ds(pl.multiple_of(c * 144, 144), 144))
            return carry

        lax.fori_loop(0, UNIT // 144, chunk, 0)

    def ring_step(t):
        for right in (True, False) if t < 3 else (True,):
            i = 2 * t if right else 2 * t + 1
            ready(i)
            if t > 0:
                ring_copy(t - 1, right).wait_recv()
            slot = (t if right else 4 + t) - 1

            def some(at):
                total = near_b[i, at, :].astype(f32) + mine_b[i % 4, at, :].astype(f32)
                if t > 0:
                    total = total + ring_b[slot, at, :].astype(f32)
                near_b[i, at, :] = total.astype(bf16)

            rounds(some)
            ring_copy(t, right).start()
            if i + 4 < 8:
                for copy in mine_copies(i + 4):
                    copy.start()

    fin_copy = remote(fin_b, fin_r, fin_send, fin_recv, other)

    def ring_end():
        ready(7)
        ring_copy(3, True).wait_recv()
        ring_copy(2, False).wait_recv()

        def some(at):
            total = near_b[7, at, :].astype(f32) + mine_b[3, at, :].astype(f32)
            fin_b[at, :] = (total + ring_b[3, at, :].astype(f32) + ring_b[6, at, :].astype(f32)).astype(bf16)

        rounds(some)
        fin_copy.start()

    def z_copy(h, i):
        return remote(
            dw_b.at[h, level ^ i], z_b.at[h, i], z_send.at[h, i], z_recv.at[h, i], me ^ (GROUP * i)
        )

    def j_copy(h, i):
        return remote(j_b.at[h, pos ^ i], j_r.at[pos, h], j_send.at[h, i], j_recv.at[h, i], me ^ i)

    def gather_rows(h):
        for i in range(1, GROUP):
            z_copy(h, i).wait_recv()
        total = dw_b[h, level].astype(f32)
        for i in range(1, GROUP):
            total = total + z_b[h, i].astype(f32)
        total = total.astype(bf16).reshape(GROUP, D // n, W3)
        j_b[h] = total
        j_r[pos, h] = j_b[h, pos]
        for i in range(1, GROUP):
            j_copy(h, i).start()

    half = lanes(PAIR) < HEAD
    lane = lanes(PAIR)
    causal = below(T, T, True)
    key_row = lax.broadcasted_iota(jnp.int32, (PROMPT, T), 0).astype(f32)
    narrow = lanes(T) < HEAD

    first[3].wait()
    first[4].wait()
    for h in range(OWN):
        w_h[h] = jnp.concatenate(
            [
                w_s[:, part * SLICE + h * HEAD : part * SLICE + (h + 1) * HEAD]
                for part in (1, 2, 0)
            ],
            axis=1,
        )
    for copy in first[:3]:
        copy.wait()
    own_do.wait()

    def one_head(h, carry):
        for i in range(1, GROUP):
            do_copy(h, i).wait_recv()
        f_copy(h).wait()
        for p in range(GROUP):
            packed = g_b[p, h].astype(f32)
            for i, block in enumerate((packed, pltpu.roll(packed, HEAD, 1))):
                at = p * TOK + i * PAIR
                prod = jnp.where(half, block * f_b[at : at + PAIR, :], 0.0)
                inner = jnp.sum(prod, axis=1, keepdims=True)
                g_s[at : at + PAIR, :] = split_columns(block, lane, inner)
            kt_s[:, p * TOK : (p + 1) * TOK] = k_s[h, p * TOK : (p + 1) * TOK, :].T[:HEAD]

        @pl.when(h + 1 < OWN)
        def _():
            f_copy(h + 1).start()

        @pl.when(h == 0)
        def _():
            ring_step(0)

        dq_s[...] = jnp.zeros_like(dq_s)

        def block(keys, size, rows, count, mask, first, key_at):
            kb = k_s[h, pl.ds(keys, size), :]
            vb = v_s[h, pl.ds(keys, size), :]
            q = q_s[h, pl.ds(rows, count), :]
            g = g_s[pl.ds(rows, count), :]
            probs = jnp.exp(dot_nt(kb, q))
            if mask is not None:
                probs = jnp.where(mask, probs, 0.0)
            ds = (probs * dot_nt(vb, g)).astype(bf16)
            dv = dot(probs.astype(bf16), g)
            dk = dot(ds, q)
            at = pl.ds(key_at, size)
            dv_s[at, :] = dv if first else dv_s[at, :] + dv
            dk_s[at, :] = dk if first else dk_s[at, :] + dk
            dq_s[:, pl.ds(rows, count)] += dot(kt_s[:, pl.ds(keys, size)], ds)

        def flush(at, size):
            for i in range(size // T):
                part = slice(i * T, (i + 1) * T)
                pair = jnp.where(narrow, dk_s[part, :], pltpu.roll(dv_s[part, :], HEAD, 1))
                dm_s[h, pl.ds(at + i * T, T), : 2 * HEAD] = pair.astype(bf16)

        for p in range(GROUP):
            base_row = p * TOK
            block(base_row, T, base_row, T, causal, True, 0)
            block(base_row + T, T, base_row + T, T, causal, True, T)
            block(base_row, T, base_row + T, T, None, False, 0)

            def past(i, carry):
                rows = pl.multiple_of(i * TOK, CONT)
                block(base_row, PROMPT, rows, PROMPT, None, False, 0)
                return carry

            lax.fori_loop(p + 1, GROUP, past, 0)

            def cont(c, carry):
                rows = pl.multiple_of(c * TOK + PROMPT, CONT)
                code = lines_s[base + c, 1:2, 0:128].astype(f32)
                reach = code[:, 0:1] * 16.0 + code[:, 1:2] - p * PROMPT
                block(base_row, PROMPT, rows, T, key_row < reach, False, 0)
                return carry

            lax.fori_loop(0, GROUP, cont, 0)
            flush(base_row, PROMPT)
            if p == 1:

                @pl.when(h > 0)
                def _():
                    gather_rows(h - 1)

        def own(c, carry):
            at = pl.multiple_of(c * TOK + PROMPT, CONT)
            block(at, T, at, T, causal, True, 0)
            flush(at, T)
            return carry

        lax.fori_loop(0, GROUP, own, 0)
        for i in range(ROWS // PROMPT):
            at = i * PROMPT
            dm_s[h, at : at + PROMPT, 2 * HEAD :] = (dq_s[:, at : at + PROMPT].T * 0.125).astype(bf16)

        @pl.when(h == 0)
        def _():
            later[0].wait()

        def weight():
            dw_t = jnp.zeros((W3, D), f32)
            for i in range(GROUP):
                rows = slice(i * TOK, (i + 1) * TOK)
                dw_t = dw_t + dot_tn(dm_s[h, rows, :], a_s[rows, :])
            acc_s[...] = dw_t
            dw = acc_s[...].T
            dw_b[h] = dw.astype(bf16).reshape(GROUP, D // GROUP, W3)
            for i in range(1, GROUP):
                z_copy(h, i).start()
            db = jnp.zeros((1, W3), f32)
            for i in range(GROUP):
                db = db + jnp.sum(dm_s[h, i * TOK : (i + 1) * TOK, :].astype(f32), axis=0, keepdims=True)
            hi = db.astype(bf16)
            mid = (db - hi.astype(f32)).astype(bf16)
            low = (db - hi.astype(f32) - mid.astype(f32)).astype(bf16)
            split = jnp.concatenate([hi, mid, low, jnp.zeros((13, W3), bf16)], axis=0)
            shift_rows = dot_nt(split, w_h[h])
            shift_part = jnp.sum(shift_rows, axis=0, keepdims=True)
            ones = jnp.ones((8, W3), f32)
            gain_rows = lax.dot_general(
                ones,
                w_h[h].astype(f32) * dw,
                (((1,), (1,)), ((), ())),
                precision=lax.Precision.HIGHEST,
                preferred_element_type=f32,
            )
            db_s[h, 0:1, :W3] = db
            db_s[h, 1:2, W3 : W3 + D] = shift_part
            db_s[h, 2:3, W3 : W3 + D] = gain_rows[0:1]

        @pl.when(h < OWN - 1)
        def _():
            weight()
            ring_step_at(h)

        @pl.when(h == OWN - 1)
        def _():
            ring_step(3)
            send_rows()
            weight()

        return carry

    def ring_step_at(h):
        @pl.when(h == 0)
        def _():
            ring_step(1)

        @pl.when(h == 1)
        def _():
            ring_step(2)

    def dn_rows(block, part):
        rows = pl.ds(pl.multiple_of((pos ^ block) * TOK + part * PAIR, PAIR), PAIR)
        total = dot_nt(dm_s[0, rows, :], w_h[0])
        for h in range(1, OWN):
            total = total + dot_nt(dm_s[h, rows, :], w_h[h])
        return total

    def dn_copy(kind, part):
        at = pl.ds(part * PAIR, PAIR)
        src, dst, peer = ((dn_a, dn_ra, near), (dn_b, dn_rb, far), (dn_c, dn_rc, near))[kind]
        i = 2 * kind + part
        return remote(src.at[at], dst.at[at], d_send.at[i], d_recv.at[i], peer)

    def send_rows():
        for part in range(2):
            dn_a[part * PAIR : (part + 1) * PAIR, :] = dn_rows(3, part).astype(bf16)
            dn_copy(0, part).start()
        for part in range(2):
            at = slice(part * PAIR, (part + 1) * PAIR)
            rows = dn_rows(2, part)
            dn_copy(0, part).wait_recv()
            dn_b[at, :] = (rows + dn_ra[at, :].astype(f32)).astype(bf16)
            dn_copy(1, part).start()
        for part in range(2):
            dn_c[part * PAIR : (part + 1) * PAIR, :] = dn_rows(1, part).astype(bf16)
            dn_copy(2, part).start()

    lax.fori_loop(0, OWN, one_head, 0)

    for copy in later[1:]:
        copy.wait()
    for part in range(2):
        dn_o[part * PAIR : (part + 1) * PAIR, :] = dn_rows(0, part)

    rows48 = D // n
    gain = jnp.concatenate([lines_s[d, 0:1, 0:rows48] for d in range(n)], axis=1).astype(f32)
    shift = jnp.concatenate([lines_s[d, 0:1, rows48 : 2 * rows48] for d in range(n)], axis=1).astype(f32)
    d_shift = db_s[0, 1:2, W3 : W3 + D] + db_s[1, 1:2, W3 : W3 + D] + db_s[2, 1:2, W3 : W3 + D]
    d_gain = db_s[0, 2:3, W3 : W3 + D] + db_s[1, 2:3, W3 : W3 + D] + db_s[2, 2:3, W3 : W3 + D]
    blank = jnp.zeros((1, D - SLICE), f32)

    def biases(lo):
        row = jnp.concatenate([db_s[h, 0:1, lo : lo + HEAD] for h in range(OWN)] + [blank], axis=1)
        return pltpu.roll(jnp.broadcast_to(row, (8, D)), pos * SLICE, 1)[0:1]

    sm_b[0] = jnp.concatenate(
        [
            (d_gain - shift * d_shift) / gain,
            d_shift,
            biases(2 * HEAD),
            biases(HEAD),
            sums_s[3:4, :],
            sums_s[1:2, :],
            sums_s[2:3, :],
            sums_s[0:1, :],
        ]
        + [dbf_s[0:1, c * D : (c + 1) * D] for c in range(FF // D)]
        + [jnp.zeros((SMALL - 12, D), f32)],
        axis=0,
    )
    peers = [me ^ 1, me ^ 2, me ^ 4, me ^ 8, other]

    def small_copy(i):
        return remote(sm_b.at[i], sm_r.at[i], s_send.at[i], s_recv.at[i], peers[i])

    def small_step(i):
        small_copy(i).wait_recv()
        sm_b[i + 1] = sm_b[i] + sm_r[i]
        if i < 4:
            small_copy(i + 1).start()

    small_copy(0).start()
    small_step(0)
    gather_rows(OWN - 1)
    small_step(1)
    small_step(2)
    for h in range(OWN):
        for i in range(1, GROUP):
            j_copy(h, i).wait_recv()
    rep_b[...] = j_r[...]
    rep_copy = remote(rep_b, rep_r, rep_send, rep_recv, other)
    rep_copy.start()
    ring_end()
    small_step(3)

    outs = []
    for part in range(2):
        at = slice(part * PAIR, (part + 1) * PAIR)
        dn_copy(2, part).wait_recv()
        dn_copy(1, part).wait_recv()
        n_rows, r = moments(x_s[at, :].astype(f32))
        e = (dn_o[at, :] + dn_rb[at, :].astype(f32) + dn_rc[at, :].astype(f32)) * gain
        lean = jnp.mean(e, axis=-1, keepdims=True) + n_rows * jnp.mean(e * n_rows, axis=-1, keepdims=True)
        dh_s[at, :] = dh_s[at, :] + r * (e - lean)
        copy = pltpu.make_async_copy(dh_s.at[at], grad_ref.at[at], out_sem.at[part])
        copy.start()
        outs.append(copy)

    small_step(4)
    total = sm_b[5]
    turned = pltpu.roll(total, lax.rem(n - me, n) * rows48, 1)
    eighth = lax.rem(me, 8)
    biased = pltpu.roll(total, lax.rem(8 - eighth, 8) * (2 * rows48), 1)
    quarter = lax.rem(me, 4)
    wide = pltpu.roll(total, lax.rem(4 - quarter, 4) * (4 * rows48), 1)
    row = lax.broadcasted_iota(jnp.int32, (SMALL, D), 0)
    bias_row = jnp.sum(jnp.where(row == 2 + me // 8, biased, 0.0), axis=0, keepdims=True)
    wide_row = jnp.sum(jnp.where(row == 8 + me // 4, wide, 0.0), axis=0, keepdims=True)
    small_copy(0).wait_send()
    sm_b[0] = jnp.where(row == 2, bias_row, jnp.where(row == 3, wide_row, turned))
    copy = pltpu.make_async_copy(sm_b.at[0], small_ref, out_sem.at[2])
    copy.start()
    outs.append(copy)

    rep_copy.wait_recv()
    for part, (at, piece) in enumerate(((2 * HEAD, 0), (0, 1), (HEAD, 2))):
        row = jnp.concatenate(
            [
                rep_b[j, h, :, at : at + HEAD].astype(f32) + rep_r[j, h, :, at : at + HEAD].astype(f32)
                for j in range(GROUP)
                for h in range(OWN)
            ],
            axis=1,
        )
        gq_o[:, piece * D : (piece + 1) * D] = row
    copy = pltpu.make_async_copy(gq_o, gq_ref, out_sem.at[3])
    copy.start()
    outs.append(copy)

    fin_copy.wait_recv()

    def some(at):
        fin_o[at, :] = fin_b[at, :].astype(f32) + fin_r[at, :].astype(f32)

    rounds(some)
    targets = [(gp_ref, 0, 192), (go_ref, 192, 48)]
    targets += [(gf_ref.at[:, pl.ds(c * D, D)], 240 + 48 * c, 48) for c in range(FF // D)]
    for i, (ref, at, size) in enumerate(targets):
        copy = pltpu.make_async_copy(fin_o.at[pl.ds(at, size)], ref, out_sem.at[4 + i])
        copy.start()
        outs.append(copy)

    for h in range(OWN):
        for i in range(1, GROUP):
            for copy in (do_copy(h, i), z_copy(h, i), j_copy(h, i)):
                copy.wait_send()
    for i in range(8):
        for copy in near_copies(i):
            copy.wait_send()
    for t in range(4):
        for right in (True, False) if t < 3 else (True,):
            ring_copy(t, right).wait_send()
    for kind in range(3):
        for part in range(2):
            dn_copy(kind, part).wait_send()
    for i in range(1, 5):
        small_copy(i).wait_send()
    rep_copy.wait_send()
    fin_copy.wait_send()
    for copy in outs:
        copy.wait()


def backward(do, q, k, v, f, a, w, x, dh, lines, sums, dbf, dwp, dwo, dwf):
    dma = pltpu.SemaphoreType.DMA
    n = BLOCKS
    shape = jax.ShapeDtypeStruct
    vmem = pltpu.VMEM
    rows = D // n
    head = (OWN, ROWS, 2 * HEAD)
    W3 = 3 * HEAD
    pairs = (OWN, GROUP)
    return pl.pallas_call(
        backward_kernel,
        name="backward",
        out_shape=(
            shape((TOK, D), f32),
            shape((rows, 3 * D), f32),
            shape((FF // n, D), f32),
            shape((rows, D), f32),
            shape((rows, FF), f32),
            shape((SMALL, D), f32),
        ),
        in_specs=[ANY] * 15,
        out_specs=(ANY,) * 6,
        scratch_shapes=[
            vmem((GROUP, OWN, PAIR, 2 * HEAD), bf16),
            vmem(head, bf16),
            vmem(head, bf16),
            vmem(head, bf16),
            vmem(head[1:], f32),
            vmem((ROWS, D), bf16),
            vmem((D, WIDE), bf16),
            vmem((TOK, D), bf16),
            vmem((TOK, D), f32),
            vmem(lines.shape, bf16),
            vmem(sums.shape, f32),
            vmem(dbf.shape, f32),
            vmem((8, UNIT, D), bf16),
            vmem((4, UNIT, D), bf16),
            vmem((7, UNIT, D), bf16),
            vmem((UNIT, D), bf16),
            vmem((UNIT, D), bf16),
            vmem((UNIT, D), f32),
            vmem((ROWS, 2 * HEAD), bf16),
            vmem((HEAD, ROWS), f32),
            vmem((HEAD, ROWS), bf16),
            vmem((PROMPT, 2 * HEAD), f32),
            vmem((PROMPT, 2 * HEAD), f32),
            vmem((OWN, ROWS, W3), bf16),
            vmem((OWN, D, W3), bf16),
            vmem((W3, D), f32),
            vmem((OWN, 8, W3 + D), f32),
            vmem((OWN, GROUP, D // GROUP, W3), bf16),
            vmem((OWN, GROUP, D // GROUP, W3), bf16),
            vmem((OWN, GROUP, rows, W3), bf16),
            vmem((GROUP, OWN, rows, W3), bf16),
            vmem((GROUP, OWN, rows, W3), bf16),
            vmem((GROUP, OWN, rows, W3), bf16),
            vmem((rows, 3 * D), f32),
            vmem((TOK, D), bf16),
            vmem((TOK, D), bf16),
            vmem((TOK, D), bf16),
            vmem((TOK, D), bf16),
            vmem((TOK, D), bf16),
            vmem((TOK, D), bf16),
            vmem((TOK, D), f32),
            vmem((6, SMALL, D), f32),
            vmem((5, SMALL, D), f32),
            dma((12,)),
            dma((8, 3)),
            dma(pairs),
            dma(pairs),
            dma((8, 3)),
            dma((8, 3)),
            dma((7,)),
            dma((7,)),
            dma,
            dma,
            dma(pairs),
            dma(pairs),
            dma(pairs),
            dma(pairs),
            dma,
            dma,
            dma((6,)),
            dma((6,)),
            dma((5,)),
            dma((5,)),
            dma((10,)),
        ],
        compiler_params=params(63, collective_id=4, has_side_effects=True),
    )(do, q, k, v, f, a, w, x, dh, lines, sums, dbf, dwp, dwo, dwf)


def unproject_kernel(dq_ref, dk_ref, dv_ref, a_ref, w_ref, dn_ref, dw_ref, db_ref):
    step = pl.program_id(0)
    mixed = jnp.concatenate(
        [ref[h] for ref in (dq_ref, dk_ref, dv_ref) for h in range(OWN)], axis=1
    )
    dn_ref[...] = dot_nt(mixed, w_ref[...]).astype(bf16)
    dw = dot_tn(a_ref[...], mixed)
    db = jnp.sum(mixed.astype(f32), axis=0, keepdims=True)

    @pl.when(step == 0)
    def _():
        dw_ref[...] = dw
        db_ref[...] = db

    @pl.when(step > 0)
    def _():
        dw_ref[...] += dw
        db_ref[...] += db


def unproject(dq, dk, dv, a, w):
    tile = 768
    head = pl.BlockSpec((OWN, tile, HEAD), lambda i: (0, i, 0))
    whole = lambda i: (0, 0)
    shape = jax.ShapeDtypeStruct
    return pl.pallas_call(
        unproject_kernel,
        name="unproject",
        grid=(ROWS // tile,),
        out_shape=(shape((ROWS, D), bf16), shape((D, WIDE), f32), shape((1, WIDE), f32)),
        in_specs=[
            head, head, head,
            pl.BlockSpec((tile, D), lambda i: (i, 0)),
            pl.BlockSpec((D, WIDE), whole),
        ],
        out_specs=(
            pl.BlockSpec((tile, D), lambda i: (i, 0)),
            pl.BlockSpec((D, WIDE), whole),
            pl.BlockSpec((1, WIDE), whole),
        ),
        compiler_params=params(48),
    )(dq, dk, dv, a, w)


def finish_kernel(x_ref, dh_ref, g_ref, one_ref, two_ref, three_ref, out_ref):
    n, r = moments(x_ref[...].astype(f32))
    dn = one_ref[...].astype(f32) + two_ref[...].astype(f32) + three_ref[...].astype(f32)
    e = dn * g_ref[...]
    lean = jnp.mean(e, axis=-1, keepdims=True) + n * jnp.mean(e * n, axis=-1, keepdims=True)
    out_ref[...] = dh_ref[...] + r * (e - lean)


def finish(x, dh, gain, one, two, three):
    tile = 256
    rows = pl.BlockSpec((tile, D), lambda i: (i, 0))
    return pl.pallas_call(
        finish_kernel,
        name="finish",
        grid=(TOK // tile,),
        out_shape=jax.ShapeDtypeStruct((TOK, D), f32),
        in_specs=[rows, rows, pl.BlockSpec((1, D), lambda i: (0, 0)), rows, rows, rows],
        out_specs=rows,
        compiler_params=params(48),
    )(x, dh, gain, one, two, three)


def flip(block, bit):
    count = lax.axis_size("fsdp")
    return lax.ppermute(block, "fsdp", [(i, i ^ bit) for i in range(count)])


def over_replicas(block):
    count = lax.axis_size("rep")
    held = lax.optimization_barrier(block)
    if count == 2:
        other = lax.ppermute(held, "rep", [(0, 1), (1, 0)])
        return held.astype(f32) + other.astype(f32)
    return lax.psum(held.astype(f32), "rep")


def body(
    block_input, cotangent, tie_index, prefix_len, pre_gain, pre_shift, w_qkv, b_qv, w_out, b_out,
    mid_gain, mid_shift, w_fc, b_fc, w_proj, b_proj,
):
    n = lax.axis_size("fsdp")
    me = lax.axis_index("fsdp")
    pos = lax.rem(me, GROUP)
    rows = D // n
    index = tie_index[0]

    def chosen(bank):
        return lax.dynamic_index_in_dim(bank, index, 0, keepdims=False)

    vectors = (pre_gain, pre_shift, b_qv, b_out, mid_gain, mid_shift, b_fc, b_proj)
    sizes = [bank.shape[1] for bank in vectors]
    count = sum(sizes)
    high = -(-(rows + 2) // 16) * 16
    cuts = [sum(sizes[:i]) for i in range(len(sizes) + 1)]

    def vectors_of(lines):
        smalls = lines[:, 0, :count].astype(f32)
        group_rows = lax.dynamic_slice_in_dim(lines[:, 1, :2], me - pos, GROUP, 0)
        reaches = group_rows[:, 0].astype(f32) * 16 + group_rows[:, 1].astype(f32)
        return [
            smalls[:, cuts[i] : cuts[i + 1]].reshape(1, -1) for i in range(len(sizes))
        ], reaches.astype(jnp.int32)

    fused = n == BLOCKS and lax.axis_size("rep") == 2
    if fused:
        small, pieces, shard = pick(tie_index, prefix_len, vectors, w_qkv, w_out, w_fc, w_proj)
        wall, lines, wq, a_low, qx, k, v, o_full, o_recv = forward(block_input, small, pieces, shard)
        a_low = a_low.reshape(ROWS, D)
        (g1, s1, _, bo, g2, s2, bf, bp), reaches = vectors_of(lines)
    else:
        small = jnp.concatenate([chosen(bank) for bank in vectors])
        reach = prefix_len[0]
        reach_row = jnp.concatenate([reach // 16, reach % 16]).astype(bf16)
        wq = chosen(w_qkv).reshape(rows, 3, GROUP, SLICE).transpose(2, 0, 1, 3)
        wq = wq.reshape(GROUP, rows, WIDE)
        extra = jnp.stack([jnp.pad(line, (0, WIDE - line.shape[0])) for line in (small, reach_row)])
        wo, wf, wp = chosen(w_out), chosen(w_fc), chosen(w_proj)
        extra = jnp.pad(extra, ((0, high - rows - 2), (0, 0)))
        pieces = jnp.concatenate([wq, jnp.broadcast_to(extra, (GROUP,) + extra.shape)], axis=1)
        wo = lax.all_gather(wo, "fsdp", axis=0, tiled=True).reshape(BLOCKS, -1, D)
        wf = lax.all_gather(wf, "fsdp", axis=0, tiled=True)
        wf = wf.reshape(BLOCKS, D // BLOCKS, FF // D, D).transpose(0, 2, 1, 3)
        wp = lax.all_gather(wp, "fsdp", axis=0, tiled=True).reshape(BLOCKS, -1, D)
        wall = jnp.concatenate([wp, wo, wf.reshape(BLOCKS, -1, D)], axis=1)
        xg, wg = gather_group(n, block_input, pieces)
        wq = wg[:, :rows].reshape(D, WIDE)
        (g1, s1, bqv, bo, g2, s2, bf, bp), reaches = vectors_of(wg[:, rows : rows + 2])
        own_bias = lax.dynamic_index_in_dim(bqv.reshape(2, GROUP, SLICE), pos, 1, keepdims=False)
        bias = jnp.concatenate([own_bias[0], jnp.zeros((SLICE,), f32), own_bias[1]])[None]
        a_low, q, k, v = project(xg.reshape(ROWS, D), wq, g1, s1, bias)
        o_send, o_full, qx = attend(reaches, q, k, v)
        o_recv = swap(o_send, 1, "swap_o")

    y, dwf, dwp, dbf, dwo, dh, do_send, sums = middle(
        block_input, o_recv, cotangent, wall, bo, g2, s2, bf, bp
    )
    if fused:
        grad, dwq, dwp, dwo, dwf, sums = backward(
            do_send, qx, k, v, o_full, a_low, wq, block_input, dh, lines, sums, dbf,
            dwp.reshape(BLOCKS, -1, D), dwo.reshape(BLOCKS, -1, D), dwf.reshape(BLOCKS, -1, D),
        )
        rows48 = D // n
        dg1, ds1, dbo, dg2, ds2, dbp = (sums[i, :rows48] for i in (0, 1, 4, 5, 6, 7))
        dbqv, dbf = sums[2, : 2 * rows48], sums[3, : 4 * rows48]
        return (y, grad, dg1, ds1, dwq, dbqv, dwo, dbo, dg2, ds2, dwf, dbf, dwp, dbp)
    dwf = dwf.transpose(0, 2, 1, 3).reshape(D, FF)
    dwf = lax.psum_scatter(dwf, "fsdp", scatter_dimension=0, tiled=True)
    dwp = lax.psum_scatter(dwp, "fsdp", scatter_dimension=0, tiled=True)
    dwo = lax.psum_scatter(dwo, "fsdp", scatter_dimension=0, tiled=True)
    do_recv = swap(do_send, 2, "swap_do")
    dq, dk, dv = attend_back(reaches, qx, k, v, o_full, do_recv)
    dn, dwq, db = unproject(dq, dk, dv, a_low, wq)

    dn = dn.reshape(GROUP, TOK, D)
    block_of = lambda bit: lax.dynamic_index_in_dim(dn, pos ^ bit, 0, keepdims=False)
    beside = flip(block_of(1), 1)
    across = flip(block_of(3), 1)
    across = flip((across.astype(f32) + block_of(2).astype(f32)).astype(bf16), 2)

    wq_wide = wq.astype(f32)
    dshift = jnp.sum(wq_wide * db, axis=1)
    dgain = jnp.sum(wq_wide * (dwq - s1.reshape(D, 1) * db), axis=1) / g1.reshape(D)
    where = (jnp.arange(GROUP) == pos).astype(f32)[:, None]
    dbias = jnp.concatenate(
        [(where * db[:, :SLICE]).reshape(-1), (where * db[:, 2 * SLICE :]).reshape(-1)]
    )
    line = jnp.concatenate(
        [
            part.reshape(n, -1)
            for part in (dgain, dshift, dbias, sums[3], sums[1], sums[2], dbf, sums[0])
        ],
        axis=1,
    )
    line_hi = line.astype(bf16)
    line_low = (line - lax.reduce_precision(line, 8, 7)).astype(bf16)
    lines = jnp.pad(jnp.stack([line_hi, line_low], axis=1), ((0, 0), (0, 0), (0, WIDE - count)))
    lines = jnp.pad(lines, ((0, 0), (0, high - rows - 2), (0, 0)))
    back = jnp.concatenate([dwq.astype(bf16).reshape(n, rows, WIDE), lines], axis=1)
    back = swap(back, 3, "swap_grad")
    dwq = jnp.sum(back[:, :rows].astype(f32).reshape(n // GROUP, GROUP, rows, 3, SLICE), axis=0)
    dwq = dwq.transpose(1, 2, 0, 3).reshape(rows, 3 * D)
    line = jnp.sum(back[:, rows, :count].astype(f32) + back[:, rows + 1, :count].astype(f32), axis=0)

    grad = finish(block_input, dh, g1, block_of(0), beside, across)
    dwq = over_replicas(dwq.astype(bf16))
    dwo, dwf, dwp = over_replicas(dwo), over_replicas(dwf), over_replicas(dwp)
    line = over_replicas(line)
    dg1, ds1, dbqv, dbo, dg2, ds2, dbf, dbp = (
        line[cuts[i] : cuts[i + 1]] for i in range(len(sizes))
    )
    return (y, grad, dg1, ds1, dwq, dbqv, dwo, dbo, dg2, ds2, dwf, dbf, dwp, dbp)


def solution(mesh):
    tokens = P(("rep", "fsdp"), None)
    vector, matrix = P(None, "fsdp"), P(None, "fsdp", None)
    return jax.shard_map(
        body,
        mesh=mesh,
        in_specs=(
            tokens, tokens, P(), tokens, vector, vector, matrix, vector, matrix, vector,
            vector, vector, matrix, vector, matrix, vector,
        ),
        out_specs=(
            tokens, tokens, P("fsdp"), P("fsdp"), P("fsdp", None), P("fsdp"), P("fsdp", None),
            P("fsdp"), P("fsdp"), P("fsdp"), P("fsdp", None), P("fsdp"), P("fsdp", None), P("fsdp"),
        ),
        check_vma=False,
    )
```

```python
from functools import partial

import jax
import jax.numpy as jnp
from jax import lax
from jax.experimental import pallas as pl
from jax.experimental.pallas import tpu as pltpu
from jax.sharding import PartitionSpec as P

D = 768
HEADS = 12
HEAD = 64
FF = 3072
GROUP = 4
PROMPT = 512
CONT = 256
TOK = 768
ROWS = GROUP * TOK
OWN = HEADS // GROUP
SLICE = OWN * HEAD
WIDE = 3 * SLICE
PAIR = TOK // 2
CHUNK = 768
BLOCKS = 16
UNIT = 432
NEG = -1e30
EPS = 1e-5
PACK = ((512, 640, 128, 0), (0, 256, 256, 128))
GELU_A = 0.7978845608028654
GELU_B = 0.044715

f32 = jnp.float32
bf16 = jnp.bfloat16
MESH = pl.DeviceIdType.MESH
ANY = pl.BlockSpec(memory_space=pl.ANY)


def params(mib, **more):
    return pltpu.CompilerParams(vmem_limit_bytes=mib << 20, **more)


def dot(a, b):
    return jnp.dot(a, b, preferred_element_type=f32)


def dot_nt(a, b):
    return lax.dot_general(a, b, (((1,), (1,)), ((), ())), preferred_element_type=f32)


def dot_tn(a, b):
    return lax.dot_general(a, b, (((0,), (0,)), ((), ())), preferred_element_type=f32)


def moments(x):
    center = x - jnp.mean(x, axis=-1, keepdims=True)
    scale = lax.rsqrt(jnp.mean(center * center, axis=-1, keepdims=True) + EPS)
    return center * scale, scale


def greet(peers, replica=None):
    sem = pltpu.get_barrier_semaphore()
    for peer in peers:
        pl.semaphore_signal(sem, inc=1, device_id={"fsdp": peer}, device_id_type=MESH)
    if replica is not None:
        pl.semaphore_signal(sem, inc=1, device_id={"rep": replica}, device_id_type=MESH)
    pl.semaphore_wait(sem, len(peers) + (replica is not None))


def gather_kernel(n, parts, x_ref, w_ref, xg_ref, wg_ref, xs, xr, ws, wr, local):
    me = lax.axis_index("fsdp")
    pos = lax.rem(me, GROUP)
    near, far = me ^ 1, me ^ 2
    greet([me ^ i for i in range(1, n)])
    own = pltpu.make_async_copy(x_ref, xg_ref.at[pos], local.at[0])
    own.start()
    own_w = pltpu.make_async_copy(w_ref.at[pos], wg_ref.at[me], local.at[1])
    own_w.start()
    rows = TOK // parts

    def piece(src, slot, part, i, peer):
        at = pl.ds(part * rows, rows)
        return pltpu.make_async_remote_copy(
            src_ref=src.at[at],
            dst_ref=xg_ref.at[slot, at],
            send_sem=xs.at[i],
            recv_sem=xr.at[i],
            device_id={"fsdp": peer},
            device_id_type=MESH,
        )

    across = [piece(x_ref, pos, part, part, far) for part in range(parts)]
    for copy in across:
        copy.start()
    beside = pltpu.make_async_remote_copy(
        src_ref=x_ref,
        dst_ref=xg_ref.at[pos],
        send_sem=xs.at[2 * parts],
        recv_sem=xr.at[2 * parts],
        device_id={"fsdp": near},
        device_id_type=MESH,
    )
    beside.start()
    slices = []
    for i in range(1, n):
        peer = me ^ i
        copy = pltpu.make_async_remote_copy(
            src_ref=w_ref.at[lax.rem(peer, GROUP)],
            dst_ref=wg_ref.at[me],
            send_sem=ws.at[i],
            recv_sem=wr.at[i],
            device_id={"fsdp": peer},
            device_id_type=MESH,
        )
        copy.start()
        slices.append(copy)
    passed = []
    for part in range(parts):
        across[part].wait_recv()
        copy = piece(xg_ref.at[pos ^ 2], pos ^ 2, part, parts + part, near)
        copy.start()
        passed.append(copy)
    for copy in across:
        copy.wait_send()
    beside.wait()
    own.wait()
    own_w.wait()
    for copy in passed + slices:
        copy.wait()


def gather_group(n, x, pieces):
    parts = 4
    dma = pltpu.SemaphoreType.DMA
    return pl.pallas_call(
        partial(gather_kernel, n, parts),
        name="gather_group",
        out_shape=(
            jax.ShapeDtypeStruct((GROUP,) + x.shape, x.dtype),
            jax.ShapeDtypeStruct((n,) + pieces.shape[1:], pieces.dtype),
        ),
        in_specs=[ANY, ANY],
        out_specs=(ANY, ANY),
        scratch_shapes=[
            dma((2 * parts + 1,)),
            dma((2 * parts + 1,)),
            dma((n,)),
            dma((n,)),
            dma((2,)),
        ],
        compiler_params=params(32, collective_id=0, has_side_effects=True),
    )(x, pieces)


def swap_kernel(count, x_ref, o_ref, send, recv, local):
    me = lax.axis_index("fsdp")
    greet([me ^ i for i in range(1, count)])
    slot = lax.rem(me, count)
    own = pltpu.make_async_copy(x_ref.at[slot], o_ref.at[slot], local)
    own.start()
    copies = []
    for i in range(1, count):
        copy = pltpu.make_async_remote_copy(
            src_ref=x_ref.at[slot ^ i],
            dst_ref=o_ref.at[slot],
            send_sem=send.at[i],
            recv_sem=recv.at[i],
            device_id={"fsdp": me ^ i},
            device_id_type=MESH,
        )
        copy.start()
        copies.append(copy)
    own.wait()
    for copy in copies:
        copy.wait()


def swap(x, collective_id, name):
    count = x.shape[0]
    dma = pltpu.SemaphoreType.DMA
    return pl.pallas_call(
        partial(swap_kernel, count),
        name=name,
        out_shape=jax.ShapeDtypeStruct(x.shape, x.dtype),
        in_specs=[ANY],
        out_specs=ANY,
        scratch_shapes=[dma((count,)), dma((count,)), dma],
        compiler_params=params(32, collective_id=collective_id, has_side_effects=True),
    )(x)


def project_kernel(x_ref, w_ref, g_ref, s_ref, b_ref, a_ref, q_ref, k_ref, v_ref):
    n, _ = moments(x_ref[...].astype(f32))
    a_low = (n * g_ref[...] + s_ref[...]).astype(bf16)
    a_ref[...] = a_low
    mixed = (dot(a_low, w_ref[...]) + b_ref[...]).astype(bf16)
    ones = jnp.ones((x_ref.shape[0], HEAD), bf16)
    for h in range(OWN):
        q = mixed[:, h * HEAD : (h + 1) * HEAD] * 0.125
        k = mixed[:, SLICE + h * HEAD : SLICE + (h + 1) * HEAD]
        v = mixed[:, 2 * SLICE + h * HEAD : 2 * SLICE + (h + 1) * HEAD]
        q_ref[h] = jnp.concatenate([q.astype(bf16), jnp.zeros_like(ones)], axis=1)
        k_ref[h] = jnp.concatenate([k, ones], axis=1)
        v_ref[h] = jnp.concatenate([v, ones], axis=1)


def project(x, w, gain, shift, bias):
    tile = 384
    heads = jax.ShapeDtypeStruct((OWN, ROWS, 2 * HEAD), bf16)
    head_spec = pl.BlockSpec((OWN, tile, 2 * HEAD), lambda i: (0, i, 0))
    whole = lambda i: (0, 0)
    return pl.pallas_call(
        project_kernel,
        name="project",
        grid=(ROWS // tile,),
        out_shape=(jax.ShapeDtypeStruct((ROWS, D), bf16), heads, heads, heads),
        in_specs=[
            pl.BlockSpec((tile, D), lambda i: (i, 0)),
            pl.BlockSpec((D, WIDE), whole),
            pl.BlockSpec((1, D), whole),
            pl.BlockSpec((1, D), whole),
            pl.BlockSpec((1, WIDE), whole),
        ],
        out_specs=(pl.BlockSpec((tile, D), lambda i: (i, 0)), head_spec, head_spec, head_spec),
        compiler_params=params(48),
    )(x, w, gain, shift, bias)


def lanes(rows):
    return lax.broadcasted_iota(jnp.int32, (rows, 2 * HEAD), 1)


def split_columns(base, lane, column):
    hi = column.astype(bf16).astype(f32)
    mid = (column - hi).astype(bf16).astype(f32)
    low = column - hi - mid
    tail = jnp.where(lane == HEAD, -hi, jnp.where(lane == HEAD + 1, -mid, -low))
    return jnp.where(lane < HEAD, base, jnp.where(lane < HEAD + 3, tail, 0.0)).astype(bf16)


def below(rows, cols, low_key):
    row = lax.broadcasted_iota(jnp.int32, (rows, cols), 0)
    col = lax.broadcasted_iota(jnp.int32, (rows, cols), 1)
    return row <= col if low_key else col <= row


def attend_kernel(reach_ref, q_ref, k_ref, v_ref, o_ref, f_ref, x_ref):
    T = CONT
    lane = lanes(T)
    causal = below(T, T, False)

    def tile(at, blocks):
        q = q_ref[0, pl.ds(at, T), :]
        scores = []
        for start, size, mask in blocks:
            s = dot_nt(q, k_ref[0, pl.ds(start, size), :])
            scores.append(s if mask is None else jnp.where(mask, s, NEG))
        peak = scores[0].max(axis=1, keepdims=True)
        for s in scores[1:]:
            peak = jnp.maximum(peak, s.max(axis=1, keepdims=True))
        total = jnp.zeros((T, 2 * HEAD), f32)
        for s, (start, size, _) in zip(scores, blocks):
            total += dot(jnp.exp(s - peak).astype(bf16), v_ref[0, pl.ds(start, size), :])
        mass = total[:, HEAD : HEAD + 1]
        f_ref[0, pl.ds(at, T), :] = total / mass
        lse = peak + jnp.log(mass)
        x_ref[0, pl.ds(at, T), :] = split_columns(q.astype(f32), lane, lse)

    for p in range(GROUP):
        past = [(i * TOK, PROMPT, None) for i in range(p)]
        base = p * TOK
        tile(base, past + [(base, T, causal)])
        tile(base + T, past + [(base, T, None), (base + T, T, causal)])

    def cont(c, carry):
        at = pl.multiple_of(c * TOK + PROMPT, CONT)
        reach = reach_ref[c]
        col = lax.broadcasted_iota(jnp.int32, (T, PROMPT), 1)
        blocks = [(i * TOK, PROMPT, col < reach - i * PROMPT) for i in range(GROUP)]
        tile(at, blocks + [(at, T, causal)])
        return carry

    lax.fori_loop(0, GROUP, cont, 0)

    half = lanes(PAIR) < HEAD
    for p in range(GROUP):
        top = f_ref[0, p * TOK : p * TOK + PAIR, :]
        low = f_ref[0, p * TOK + PAIR : (p + 1) * TOK, :]
        o_ref[p, 0] = jnp.where(half, top, pltpu.roll(low, HEAD, 1)).astype(bf16)


def attend(reach, q, k, v):
    head = lambda h: (h, 0, 0)
    spec = pl.BlockSpec((1, ROWS, 2 * HEAD), head)
    return pl.pallas_call(
        attend_kernel,
        name="attend",
        grid=(OWN,),
        out_shape=(
            jax.ShapeDtypeStruct((GROUP, OWN, PAIR, 2 * HEAD), bf16),
            jax.ShapeDtypeStruct((OWN, ROWS, 2 * HEAD), f32),
            jax.ShapeDtypeStruct((OWN, ROWS, 2 * HEAD), bf16),
        ),
        in_specs=[pl.BlockSpec(memory_space=pltpu.SMEM), spec, spec, spec],
        out_specs=(
            pl.BlockSpec((GROUP, 1, PAIR, 2 * HEAD), lambda h: (0, h, 0, 0)),
            spec,
            spec,
        ),
        compiler_params=params(56),
    )(reach, q, k, v)


def attend_back_kernel(
    reach_ref, q_ref, k_ref, v_ref, f_ref, g_ref, dq_ref, dk_ref, dv_ref, g_s, dq_s, kt_s, dk_s, dv_s
):
    T = CONT
    half = lanes(PAIR) < HEAD
    lane = lanes(PAIR)
    for p in range(GROUP):
        packed = g_ref[p, 0].astype(f32)
        for i, block in enumerate((packed, pltpu.roll(packed, HEAD, 1))):
            at = p * TOK + i * PAIR
            prod = jnp.where(half, block * f_ref[0, at : at + PAIR, :], 0.0)
            inner = jnp.sum(prod, axis=1, keepdims=True)
            g_s[at : at + PAIR, :] = split_columns(block, lane, inner)
        kt_s[:, p * TOK : (p + 1) * TOK] = k_ref[0, p * TOK : (p + 1) * TOK, :].T[:HEAD]
    dq_s[...] = jnp.zeros_like(dq_s)

    def block(keys, size, rows, count, mask, first, key_at):
        kb = k_ref[0, pl.ds(keys, size), :]
        vb = v_ref[0, pl.ds(keys, size), :]
        q = q_ref[0, pl.ds(rows, count), :]
        g = g_s[pl.ds(rows, count), :]
        probs = jnp.exp(dot_nt(kb, q))
        if mask is not None:
            probs = jnp.where(mask, probs, 0.0)
        ds = (probs * dot_nt(vb, g)).astype(bf16)
        dv = dot(probs.astype(bf16), g)
        dk = dot(ds, q)
        at = pl.ds(key_at, size)
        dv_s[at, :] = dv if first else dv_s[at, :] + dv
        dk_s[at, :] = dk if first else dk_s[at, :] + dk
        dq_s[:, pl.ds(rows, count)] += dot(kt_s[:, pl.ds(keys, size)], ds)

    causal = below(T, T, True)
    for p in range(GROUP):
        base = p * TOK
        block(base, T, base, T, causal, True, 0)
        block(base + T, T, base + T, T, causal, True, T)
        block(base, T, base + T, T, None, False, 0)

        def later(i, carry):
            rows = pl.multiple_of(i * TOK, CONT)
            block(base, PROMPT, rows, PROMPT, None, False, 0)
            return carry

        lax.fori_loop(p + 1, GROUP, later, 0)

        def cont(c, carry):
            rows = pl.multiple_of(c * TOK + PROMPT, CONT)
            key = lax.broadcasted_iota(jnp.int32, (PROMPT, T), 0)
            block(base, PROMPT, rows, T, key < reach_ref[c] - p * PROMPT, False, 0)
            return carry

        lax.fori_loop(0, GROUP, cont, 0)
        dk_ref[0, base : base + PROMPT, :] = dk_s[:, :HEAD].astype(bf16)
        dv_ref[0, base : base + PROMPT, :] = dv_s[:, :HEAD].astype(bf16)

    def own(c, carry):
        at = pl.multiple_of(c * TOK + PROMPT, CONT)
        block(at, T, at, T, causal, True, 0)
        dk_ref[0, pl.ds(at, T), :] = dk_s[:T, :HEAD].astype(bf16)
        dv_ref[0, pl.ds(at, T), :] = dv_s[:T, :HEAD].astype(bf16)
        return carry

    lax.fori_loop(0, GROUP, own, 0)
    for i in range(ROWS // PROMPT):
        at = i * PROMPT
        dq_ref[0, at : at + PROMPT, :] = (dq_s[:, at : at + PROMPT].T * 0.125).astype(bf16)


def attend_back(reach, q, k, v, f, g):
    head = lambda h: (h, 0, 0)
    spec = pl.BlockSpec((1, ROWS, 2 * HEAD), head)
    out = jax.ShapeDtypeStruct((OWN, ROWS, HEAD), bf16)
    out_spec = pl.BlockSpec((1, ROWS, HEAD), head)
    return pl.pallas_call(
        attend_back_kernel,
        name="attend_back",
        grid=(OWN,),
        out_shape=(out, out, out),
        in_specs=[pl.BlockSpec(memory_space=pltpu.SMEM), spec, spec, spec, spec]
        + [pl.BlockSpec((GROUP, 1, PAIR, 2 * HEAD), lambda h: (0, h, 0, 0))],
        out_specs=(out_spec, out_spec, out_spec),
        scratch_shapes=[
            pltpu.VMEM((ROWS, 2 * HEAD), bf16),
            pltpu.VMEM((HEAD, ROWS), f32),
            pltpu.VMEM((HEAD, ROWS), bf16),
            pltpu.VMEM((PROMPT, 2 * HEAD), f32),
            pltpu.VMEM((PROMPT, 2 * HEAD), f32),
        ],
        compiler_params=params(56),
    )(reach, q, k, v, f, g)


def pick_kernel(index_ref, reach_ref, *refs):
    vectors, (wq_ref, wo_ref, wf_ref, wp_ref), (small_ref, piece_ref, shard_ref) = (
        refs[:8], refs[8:12], refs[12:],
    )
    index = index_ref[0]
    rows = []
    for ref in vectors:
        bank = ref[...].astype(f32)
        chosen = lax.broadcasted_iota(jnp.int32, bank.shape, 0) == index
        rows.append(jnp.sum(jnp.where(chosen, bank, 0.0), axis=0, keepdims=True))
    width = sum(row.shape[1] for row in rows)
    rest = small_ref.shape[1] - width
    small_ref[0:1, :] = jnp.concatenate(rows + [jnp.zeros((1, rest), f32)], axis=1).astype(bf16)
    reach = reach_ref[0, 0]
    lane = lax.broadcasted_iota(jnp.int32, (1, small_ref.shape[1]), 1)
    code = jnp.where(lane == 0, reach // 16, jnp.where(lane == 1, lax.rem(reach, 16), 0))
    small_ref[1:2, :] = code.astype(f32).astype(bf16)
    for j in range(GROUP):
        for part in range(3):
            at = part * D + j * SLICE
            piece_ref[j, :, part * SLICE : (part + 1) * SLICE] = wq_ref[0, :, at : at + SLICE]
    shard_ref[:192, :] = wp_ref[0]
    shard_ref[192:240, :] = wo_ref[0]
    for c in range(FF // D):
        shard_ref[240 + 48 * c : 288 + 48 * c, :] = wf_ref[0, :, c * D : (c + 1) * D]


def pick(index, reach, vectors, wq, wo, wf, wp):
    shape = jax.ShapeDtypeStruct
    chosen = lambda bank: pl.BlockSpec((1,) + bank.shape[1:], lambda i, at: (at[0], 0, 0))
    whole = lambda bank: pl.BlockSpec(bank.shape, lambda i, at: (0, 0))
    fixed3 = lambda i, at: (0, 0, 0)
    return pl.pallas_call(
        pick_kernel,
        name="pick",
        out_shape=(
            shape((2, 640), bf16), shape((GROUP, D // BLOCKS, WIDE), bf16), shape((UNIT, D), bf16),
        ),
        grid_spec=pltpu.PrefetchScalarGridSpec(
            num_scalar_prefetch=1,
            grid=(1,),
            in_specs=[pl.BlockSpec(memory_space=pltpu.SMEM)]
            + [whole(bank) for bank in vectors]
            + [chosen(bank) for bank in (wq, wo, wf, wp)],
            out_specs=(
                pl.BlockSpec((2, 640), lambda i, at: (0, 0)),
                pl.BlockSpec((GROUP, D // BLOCKS, WIDE), fixed3),
                pl.BlockSpec((UNIT, D), lambda i, at: (0, 0)),
            ),
        ),
        compiler_params=params(60),
    )(index, reach, *vectors, wq, wo, wf, wp)


def ring_of(me):
    chip, core = me // 2, lax.rem(me, 2)
    z, x = chip // 2, lax.rem(chip, 2)
    chips = BLOCKS // 2
    half = chips // 2
    place = z * (1 - x) + (chips - 1 - z) * x

    def device(at):
        at = lax.rem(at + 2 * chips, chips)
        side = at // half
        z_at = at * (1 - side) + (chips - 1 - at) * side
        return (z_at * 2 + side) * 2 + core

    return place, device


def forward_kernel(
    x_ref, sm_ref, pc_ref, sh_ref,
    wall_ref, smo_ref, wq_ref, a_ref, q_ref, k_ref, v_ref, f_ref, o_ref,
    xg, smg, wg, w_s, q_s, k_s, v_s, f_s, o_s,
    local, sm_send, sm_recv, w_send, w_recv, x_send, x_recv, r_send, r_recv, n_send, n_recv,
    y_send, y_recv, o_send, o_recv, out_sem,
):
    n = BLOCKS
    me = lax.axis_index("fsdp")
    rep = lax.axis_index("rep")
    pos = lax.rem(me, GROUP)
    base = me - pos
    near, far = me ^ 1, me ^ 2
    place, device = ring_of(me)
    parts = 4
    part_rows = TOK // parts
    T = CONT

    def remote(src, dst, send, recv, peer):
        return pltpu.make_async_remote_copy(
            src_ref=src,
            dst_ref=dst,
            send_sem=send,
            recv_sem=recv,
            device_id=peer if isinstance(peer, dict) else {"fsdp": peer},
            device_id_type=MESH,
        )

    greet([me ^ i for i in range(1, n)], 1 - rep)

    own_block = pltpu.make_async_copy(sh_ref, wall_ref.at[me], local.at[0])
    own_x = pltpu.make_async_copy(x_ref, xg.at[pos], local.at[1])
    own_w = pltpu.make_async_copy(pc_ref.at[pos], wg.at[me], local.at[2])
    own_s = pltpu.make_async_copy(sm_ref, smg.at[me], local.at[3])
    for copy in (own_s, own_w, own_x, own_block):
        copy.start()

    slices = []
    for i in range(1, GROUP):
        copy = remote(pc_ref.at[pos ^ i], wg.at[me], w_send.at[i], w_recv.at[i], me ^ i)
        copy.start()
        slices.append(copy)
    smalls = []
    for i in range(1, n):
        copy = remote(sm_ref, smg.at[me], sm_send.at[i], sm_recv.at[i], me ^ i)
        copy.start()
        smalls.append(copy)
    beside = remote(x_ref, xg.at[pos], x_send.at[2 * parts], x_recv.at[2 * parts], near)
    beside.start()

    def x_part(src, slot, part, i, peer):
        at = pl.ds(part * part_rows, part_rows)
        return remote(src.at[at], xg.at[slot, at], x_send.at[i], x_recv.at[i], peer)

    across = [x_part(x_ref, pos, part, part, far) for part in range(parts)]
    for copy in across:
        copy.start()

    mine = pl.ds(pl.multiple_of(rep * (D // 2), D // 2), D // 2)
    other = pl.ds(pl.multiple_of((1 - rep) * (D // 2), D // 2), D // 2)
    sides = lambda t: (True, False) if t < 3 else (True,)
    key = lambda t, right: t if right else 4 + t

    def came(t, right):
        return device(place - 1 - t if right else place + 1 + t)

    def hop(t, right):
        block = wall_ref.at[device(place - t if right else place + t), :, mine]
        src = sh_ref.at[:, mine] if t == 0 else block
        i = key(t, right)
        return remote(src, block, r_send.at[i], r_recv.at[i], device(place + 1 if right else place - 1))

    def to_near(t, right, columns, i):
        block = wall_ref.at[came(t, right), :, columns]
        return remote(block, block, n_send.at[i], n_recv.at[i], near)

    def to_replica(t, right):
        block = wall_ref.at[came(t, right), :, mine]
        i = key(t, right)
        return remote(block, block, y_send.at[i], y_recv.at[i], {"rep": 1 - rep})

    def from_replica(t, right):
        block = wall_ref.at[came(t, right), :, other]
        i = key(t, right)
        return remote(block, block, y_send.at[i], y_recv.at[i], {"rep": 1 - rep})

    hops, sent, shared = {}, [], []

    def begin(copy, keep):
        copy.start()
        keep.append(copy)

    def launch(t):
        for right in sides(t):
            hops[t, right] = hop(t, right)
            hops[t, right].start()

    def arrive(t):
        for right in sides(t):
            hops[t, right].wait_recv()
        if t < 3:
            launch(t + 1)
        for right in sides(t):
            begin(to_replica(t, right), sent)
            begin(to_near(t, right, mine, 1 + key(t, right)), shared)

    def settle(t):
        for right in sides(t):
            from_replica(t, right).wait_recv()
            begin(to_near(t, right, other, 8 + key(t, right)), shared)

    launch(0)
    begin(remote(sh_ref, wall_ref.at[me], n_send.at[0], n_recv.at[0], near), shared)

    own_s.wait()
    for copy in smalls:
        copy.wait_recv()
    rows48 = D // n
    gain = jnp.concatenate([smg[d, 0:1, 0:rows48] for d in range(n)], axis=1).astype(f32)
    shift = jnp.concatenate([smg[d, 0:1, rows48 : 2 * rows48] for d in range(n)], axis=1).astype(f32)
    at = 2 * rows48
    two = 2 * rows48
    zeros = jnp.zeros((1, SLICE), bf16)
    bias = jnp.concatenate(
        [smg[2 * pos + i, 0:1, at : at + two] for i in range(2)]
        + [zeros]
        + [smg[n // 2 + 2 * pos + i, 0:1, at : at + two] for i in range(2)],
        axis=1,
    ).astype(f32)

    def norm(slot):
        def some(i, carry):
            at = pl.ds(pl.multiple_of(i * PAIR, PAIR), PAIR)
            n_rows, _ = moments(xg[slot, at, :].astype(f32))
            xg[slot, at, :] = (n_rows * gain + shift).astype(bf16)
            return carry

        lax.fori_loop(0, 2, some, 0)

    def project_block(slot):
        def some(i, carry):
            at = pl.ds(pl.multiple_of(i * PAIR, PAIR), PAIR)
            out = pl.ds(pl.multiple_of(slot * TOK + i * PAIR, PAIR), PAIR)
            mixed = (dot(xg[slot, at, :], w_s[...]) + bias).astype(bf16)
            ones = jnp.ones((PAIR, HEAD), bf16)
            for h in range(OWN):
                q = mixed[:, h * HEAD : (h + 1) * HEAD] * 0.125
                k = mixed[:, SLICE + h * HEAD : SLICE + (h + 1) * HEAD]
                v = mixed[:, 2 * SLICE + h * HEAD : 2 * SLICE + (h + 1) * HEAD]
                q_s[h, out, :] = jnp.concatenate([q.astype(bf16), jnp.zeros_like(ones)], axis=1)
                k_s[h, out, :] = jnp.concatenate([k, ones], axis=1)
                v_s[h, out, :] = jnp.concatenate([ones, v], axis=1)
            return carry

        lax.fori_loop(0, 2, some, 0)

    own_w.wait()
    for copy in slices:
        copy.wait_recv()
    group = pl.ds(base, GROUP)
    wide = []
    for i in range(1, n // GROUP):
        begin(
            remote(wg.at[group], wg.at[group], w_send.at[GROUP + i], w_recv.at[GROUP + i], me ^ (GROUP * i)),
            wide,
        )
    own_x.wait()
    norm(pos)
    beside.wait()
    norm(pos ^ 1)
    for copy in wide:
        copy.wait_recv()
    arrive(0)
    w_s[...] = wg[:, :rows48, :].reshape(D, WIDE)
    project_block(pos)
    project_block(pos ^ 1)
    passed = []
    for part in range(parts):
        across[part].wait_recv()
        copy = x_part(xg.at[pos ^ 2], pos ^ 2, part, parts + part, near)
        copy.start()
        passed.append(copy)
    for copy in passed:
        copy.wait()
    norm(pos ^ 2)
    project_block(pos ^ 2)
    norm(pos ^ 3)
    project_block(pos ^ 3)
    arrive(1)

    outs = [
        pltpu.make_async_copy(smg, smo_ref, out_sem.at[0]),
        pltpu.make_async_copy(w_s, wq_ref, out_sem.at[1]),
        pltpu.make_async_copy(xg, a_ref, out_sem.at[2]),
        pltpu.make_async_copy(k_s, k_ref, out_sem.at[3]),
        pltpu.make_async_copy(v_s, v_ref, out_sem.at[4]),
    ]
    for copy in outs:
        copy.start()

    lane = lanes(T)
    causal = below(T, T, False)
    code = [smg[base + c, 1:2, 0:2].astype(f32) for c in range(GROUP)]
    reaches = [c[:, 0:1] * 16.0 + c[:, 1:2] for c in code]
    column = lax.broadcasted_iota(jnp.int32, (T, PROMPT), 1).astype(f32)

    for h in range(OWN):

        def tile(at, blocks):
            q = q_s[h, pl.ds(at, T), :]
            scores = []
            for start, size, mask in blocks:
                s = dot_nt(q, k_s[h, pl.ds(start, size), :])
                scores.append(s if mask is None else jnp.where(mask, s, NEG))
            peak = scores[0].max(axis=1, keepdims=True)
            for s in scores[1:]:
                peak = jnp.maximum(peak, s.max(axis=1, keepdims=True))
            total = jnp.zeros((T, 2 * HEAD), f32)
            for s, (start, size, _) in zip(scores, blocks):
                total += dot(jnp.exp(s - peak).astype(bf16), v_s[h, pl.ds(start, size), :])
            mass = total[:, 0:1]
            f_s[h, pl.ds(at, T), :] = total / mass
            lse = peak + jnp.log(mass)
            q_s[h, pl.ds(at, T), :] = split_columns(q.astype(f32), lane, lse)

        for p in range(GROUP):
            past = [(i * TOK, PROMPT, None) for i in range(p)]
            at = p * TOK
            tile(at, past + [(at, T, causal)])
            tile(at + T, past + [(at, T, None), (at + T, T, causal)])
        if h == 0:
            arrive(2)
        if h == 1:
            arrive(3)
            settle(0)
        if h == 2:
            settle(1)
        for c in range(GROUP):
            at = c * TOK + PROMPT
            blocks = [(i * TOK, PROMPT, column < reaches[c] - i * PROMPT) for i in range(GROUP)]
            tile(at, blocks + [(at, T, causal)])
        for p in range(GROUP):
            for left, right, size, to in PACK:
                top = f_s[h, p * TOK + left : p * TOK + left + size, :]
                low = f_s[h, p * TOK + right : p * TOK + right + size, :]
                pair = jnp.where(lanes(size) < HEAD, pltpu.roll(top, HEAD, 1), low)
                o_s[h, p, to : to + size, :] = pair.astype(bf16)
        for i in range(1, GROUP):
            copy = remote(
                o_s.at[h, pos ^ i], o_ref.at[pos, h], o_send.at[h, i], o_recv.at[h, i], me ^ i
            )
            copy.start()
            shared.append(copy)
        for src, dst, i in (
            (o_s.at[h, pos], o_ref.at[pos, h], 5 + h),
            (f_s.at[h], f_ref.at[h], 8 + h),
            (q_s.at[h], q_ref.at[h], 11 + h),
        ):
            copy = pltpu.make_async_copy(src, dst, out_sem.at[i])
            copy.start()
            outs.append(copy)

    settle(2)
    settle(3)
    for copy in across + smalls + slices + wide + list(hops.values()) + sent:
        copy.wait_send()
    own_block.wait()
    for copy in shared + outs:
        copy.wait()


def forward(x, small, pieces, shard):
    dma = pltpu.SemaphoreType.DMA
    n = BLOCKS
    shape = jax.ShapeDtypeStruct
    head = (OWN, ROWS, 2 * HEAD)
    return pl.pallas_call(
        forward_kernel,
        name="forward",
        out_shape=(
            shape((n, UNIT, D), bf16),
            shape((n,) + small.shape, bf16),
            shape((D, WIDE), bf16),
            shape((GROUP, TOK, D), bf16),
            shape(head, bf16),
            shape(head, bf16),
            shape(head, bf16),
            shape(head, f32),
            shape((GROUP, OWN, PAIR, 2 * HEAD), bf16),
        ),
        in_specs=[ANY] * 4,
        out_specs=(ANY,) * 9,
        scratch_shapes=[
            pltpu.VMEM((GROUP, TOK, D), bf16),
            pltpu.VMEM((n,) + small.shape, bf16),
            pltpu.VMEM((n,) + pieces.shape[1:], bf16),
            pltpu.VMEM((D, WIDE), bf16),
            pltpu.VMEM(head, bf16),
            pltpu.VMEM(head, bf16),
            pltpu.VMEM(head, bf16),
            pltpu.VMEM(head, f32),
            pltpu.VMEM((OWN, GROUP, PAIR, 2 * HEAD), bf16),
            dma((4,)),
            dma((n,)),
            dma((n,)),
            dma((2 * GROUP,)),
            dma((2 * GROUP,)),
            dma((9,)),
            dma((9,)),
            dma((7,)),
            dma((7,)),
            dma((15,)),
            dma((15,)),
            dma((7,)),
            dma((7,)),
            dma((OWN, GROUP)),
            dma((OWN, GROUP)),
            dma((14,)),
        ],
        compiler_params=params(60, collective_id=0, has_side_effects=True),
    )(x, small, pieces, shard)


def middle_kernel(
    x_ref, o_ref, dy_ref, wo_ref, wf_ref, wp_ref, bo_ref, g_ref, s_ref, bf_ref, bp_ref,
    y_ref, dwf_ref, dwp_ref, dbf_ref, dwo_ref, dh_ref, do_ref, small_ref,
    o_s, h_s, b_s, bt_s, y_s, dn_s,
):
    step = pl.program_id(0)
    half = lanes(PAIR) < HEAD
    wf = wf_ref[...].reshape(D, CHUNK)
    wp = wp_ref[...].reshape(CHUNK, D)
    wo = wo_ref[...].reshape(D, D)

    @pl.when(step == 0)
    def _():
        for t in range(HEADS // 2):
            one = o_ref[2 * t // OWN, 2 * t % OWN].astype(f32)
            two = o_ref[(2 * t + 1) // OWN, (2 * t + 1) % OWN].astype(f32)
            at = slice(2 * t * HEAD, (2 * t + 2) * HEAD)
            first = jnp.where(half, one, pltpu.roll(two, HEAD, 1)).astype(bf16)
            second = jnp.where(half, pltpu.roll(one, HEAD, 1), two).astype(bf16)
            for left, right, size, to in PACK:
                o_s[left : left + size, at] = first[to : to + size]
                o_s[right : right + size, at] = second[to : to + size]
        h = x_ref[...].astype(f32) + dot(o_s[...], wo) + bo_ref[...]
        h_s[...] = h
        n, _ = moments(h)
        b_low = (n * g_ref[...] + s_ref[...]).astype(bf16)
        b_s[...] = b_low
        bt_s[...] = b_low.T
        y_s[...] = jnp.zeros_like(y_s)
        dn_s[...] = jnp.zeros_like(dn_s)

    dy = dy_ref[...]
    u = dot(b_s[...], wf) + bf_ref[...]
    square = u * u
    t = jnp.tanh(GELU_A * (u + GELU_B * (square * u)))
    m_low = (0.5 * u * (1.0 + t)).astype(bf16)
    slope = 0.5 * (1.0 + t) + 0.5 * u * (1.0 - t * t) * (GELU_A * (1.0 + 3.0 * GELU_B * square))
    y_s[...] += dot(m_low, wp)
    du = (dot_nt(dy, wp) * slope).astype(bf16)
    dbf_ref[...] = jnp.sum(du.astype(f32), axis=0, keepdims=True)
    dn_s[...] += dot_nt(du, wf)
    dwf_ref[...] = dot(bt_s[...], du).astype(bf16).reshape(dwf_ref.shape)
    dwp_ref[...] = dot_tn(m_low, dy).astype(bf16)

    @pl.when(step == pl.num_programs(0) - 1)
    def _():
        h = h_s[...]
        y_ref[...] = (h + y_s[...] + bp_ref[...]).astype(bf16)
        n, r = moments(h)
        dn = dn_s[...]
        grad = dy_ref[...].astype(f32)
        small_ref[...] = jnp.zeros_like(small_ref)
        small_ref[0:1, :] = jnp.sum(grad, axis=0, keepdims=True)
        small_ref[1:2, :] = jnp.sum(dn * n, axis=0, keepdims=True)
        small_ref[2:3, :] = jnp.sum(dn, axis=0, keepdims=True)
        e = dn * g_ref[...]
        lean = jnp.mean(e, axis=-1, keepdims=True) + n * jnp.mean(e * n, axis=-1, keepdims=True)
        dh = grad + r * (e - lean)
        dh_ref[...] = dh
        dh_low = dh.astype(bf16)
        small_ref[3:4, :] = jnp.sum(dh_low.astype(f32), axis=0, keepdims=True)
        dwo_ref[...] = dot_tn(o_s[...], dh_low).astype(bf16)
        h_s[...] = dot_nt(dh_low, wo)
        for t in range(HEADS // 2):
            at = slice(2 * t * HEAD, (2 * t + 2) * HEAD)
            for left, right, size, to in PACK:
                top, low = h_s[left : left + size, at], h_s[right : right + size, at]
                side = lanes(size) < HEAD
                one = jnp.where(side, top, pltpu.roll(low, HEAD, 1))
                two = jnp.where(side, pltpu.roll(top, HEAD, 1), low)
                do_ref[2 * t // OWN, 2 * t % OWN, to : to + size] = one.astype(bf16)
                do_ref[(2 * t + 1) // OWN, (2 * t + 1) % OWN, to : to + size] = two.astype(bf16)


def middle(x, o, dy, wall, bo, gain, shift, bf, bp):
    fixed2 = lambda i: (0, 0)
    fixed4 = lambda i: (0, 0, 0, 0)
    square = pl.BlockSpec((TOK, D), fixed2)
    row = pl.BlockSpec((1, D), fixed2)
    heads = pl.BlockSpec((GROUP, OWN, PAIR, 2 * HEAD), fixed4)
    columns = pl.BlockSpec((BLOCKS, 1, D // BLOCKS, D), lambda i: (0, i, 0, 0))
    down = pl.BlockSpec((CHUNK, D), lambda i: (i, 0))
    line = pl.BlockSpec((1, CHUNK), lambda i: (0, i))
    shape = jax.ShapeDtypeStruct
    return pl.pallas_call(
        middle_kernel,
        name="middle",
        grid=(FF // CHUNK,),
        out_shape=(
            shape((TOK, D), bf16),
            shape((BLOCKS, FF // D, D // BLOCKS, D), bf16),
            shape((FF, D), bf16),
            shape((1, FF), f32),
            shape((D, D), bf16),
            shape((TOK, D), f32),
            shape((GROUP, OWN, PAIR, 2 * HEAD), bf16),
            shape((8, D), f32),
        ),
        in_specs=[
            square, heads, square,
            pl.BlockSpec((BLOCKS, 48, D), lambda i: (0, 4, 0)),
            pl.BlockSpec((BLOCKS, 48, D), lambda i: (0, 5 + i, 0)),
            pl.BlockSpec((BLOCKS // 4, 192, D), lambda i: (i, 0, 0)),
            row, row, row, line, row,
        ],
        out_specs=(
            square, columns, down, line, square, square, heads, pl.BlockSpec((8, D), fixed2),
        ),
        scratch_shapes=[
            pltpu.VMEM((TOK, D), bf16),
            pltpu.VMEM((TOK, D), f32),
            pltpu.VMEM((TOK, D), bf16),
            pltpu.VMEM((D, TOK), bf16),
            pltpu.VMEM((TOK, D), f32),
            pltpu.VMEM((TOK, D), f32),
        ],
        compiler_params=params(60),
    )(x, o, dy, wall, wall, wall, bo, gain, shift, bf, bp)


ORDER = (4, -3, 3, -2, 2, -1, 1, 0)
SMALL = 16


def backward_kernel(
    do_ref, q_ref, k_ref, v_ref, f_ref, a_ref, w_ref, x_ref, dh_ref, lines_ref, sums_ref, dbf_ref,
    dwp_ref, dwo_ref, dwf_ref,
    grad_ref, gq_ref, gp_ref, go_ref, gf_ref, small_ref,
    g_b, q_s, k_s, v_s, f_b, a_b, w_s, x_s, dh_s, lines_s, sums_s, dbf_s,
    near_b, mine_b, y_b, ring_b, fin_b, fin_r, fin_o,
    g_s, dq_s, kt_s, dkv_s, dm_s, w_h, dw_s, db_s,
    dw_b, z_b, j_b, j_r, rep_b, rep_r, gq_o,
    dn_a, dn_b, dn_c, dn_ra, dn_rb, dn_rc, sm_b, sm_r,
    load, f_sem, a_sem, mine_sem, g_send, g_recv, n_send, n_recv, y_send, y_recv, r_send, r_recv, fin_send,
    fin_recv, z_send, z_recv, j_send, j_recv, rep_send, rep_recv, d_send, d_recv, s_send, s_recv, out_sem,
):
    n = BLOCKS
    me = lax.axis_index("fsdp")
    rep = lax.axis_index("rep")
    pos = lax.rem(me, GROUP)
    base = me - pos
    level = me // GROUP
    near, far = me ^ 1, me ^ 2
    place, device = ring_of(me)
    T = CONT
    W3 = 3 * HEAD
    other = {"rep": 1 - rep}

    def remote(src, dst, send, recv, peer):
        return pltpu.make_async_remote_copy(
            src_ref=src,
            dst_ref=dst,
            send_sem=send,
            recv_sem=recv,
            device_id=peer if isinstance(peer, dict) else {"fsdp": peer},
            device_id_type=MESH,
        )

    greet([me ^ i for i in range(1, n)], 1 - rep)

    def do_copy(kind, i):
        at = pl.ds(*((0, 128), (128, 256))[kind])
        src, dst = do_ref.at[pos ^ i, :, at], g_b.at[pos, :, at]
        return remote(src, dst, g_send.at[kind, i], g_recv.at[kind, i], me ^ i)

    own_do = pltpu.make_async_copy(do_ref.at[pos], g_b.at[pos], load.at[0])
    own_do.start()
    for i in range(1, GROUP):
        do_copy(0, i).start()

    stages = (
        tuple((c * TOK + PROMPT, CONT) for c in range(GROUP)),
        ((3 * TOK, PROMPT),),
        ((0, PROMPT),),
        ((TOK, PROMPT), (2 * TOK, PROMPT)),
    )
    loads = (stages[0], ((3 * TOK, PROMPT), (2 * TOK, PROMPT)), ((0, PROMPT), (TOK, PROMPT)))

    def f_copies(part):
        at, found = 0, []
        for i, (row, size) in enumerate(loads[part]):
            src, dst = f_ref.at[:, pl.ds(row, size)], f_b.at[:, pl.ds(at, size)]
            found.append(pltpu.make_async_copy(src, dst, f_sem.at[part, i]))
            at += size
        return found

    def a_copies(stage):
        at, found = 0, []
        for i, (row, size) in enumerate(stages[stage]):
            src, dst = a_ref.at[pl.ds(row, size)], a_b.at[pl.ds(at, size)]
            found.append(pltpu.make_async_copy(src, dst, a_sem.at[stage, i]))
            at += size
        return found

    first = [
        pltpu.make_async_copy(src, dst, load.at[1 + i])
        for i, (src, dst) in enumerate(
            ((k_ref, k_s), (v_ref, v_s), (q_ref, q_s), (lines_ref, lines_s), (w_ref, w_s))
        )
    ]
    later = [
        pltpu.make_async_copy(src, dst, load.at[6 + i])
        for i, (src, dst) in enumerate(
            ((x_ref, x_s), (dh_ref, dh_s), (sums_ref, sums_s), (dbf_ref, dbf_s))
        )
    ]
    for copy in f_copies(0) + first:
        copy.start()

    cut = ((0, 192), (192, 48), (240, 192))

    def near_copies(i):
        d = device(place + ORDER[i]) ^ 1
        return [
            remote(ref.at[d], near_b.at[i, pl.ds(at, size)], n_send.at[i, k], n_recv.at[i, k], near)
            for k, (ref, (at, size)) in enumerate(zip((dwp_ref, dwo_ref, dwf_ref), cut))
        ]

    def mine_copies(i):
        d = device(place + ORDER[i])
        return [
            pltpu.make_async_copy(ref.at[d], mine_b.at[i % 4, pl.ds(at, size)], mine_sem.at[i, k])
            for k, (ref, (at, size)) in enumerate(zip((dwp_ref, dwo_ref, dwf_ref), cut))
        ]

    for i in range(2):
        for copy in near_copies(i) + mine_copies(i):
            copy.start()
    for i in range(1, GROUP):
        do_copy(1, i).start()
    for i in range(2, 8):
        for copy in near_copies(i):
            copy.start()
    for copy in a_copies(0) + mine_copies(2) + mine_copies(3) + later:
        copy.start()

    def ready(i):
        for copy in near_copies(i):
            copy.wait_recv()
        for copy in mine_copies(i):
            copy.wait()

    mine = pl.ds(pl.multiple_of(rep * (D // 2), D // 2), D // 2)
    rest = pl.ds(pl.multiple_of((1 - rep) * (D // 2), D // 2), D // 2)

    def rounds(some):
        def chunk(c, carry):
            some(pl.ds(pl.multiple_of(c * 144, 144), 144))
            return carry

        lax.fori_loop(0, UNIT // 144, chunk, 0)

    def y_copy(i):
        return remote(near_b.at[i, :, rest], y_b.at[i], y_send.at[i], y_recv.at[i], other)

    def chip_sum(i):
        ready(i)

        def some(at):
            total = near_b[i, at, :].astype(f32) + mine_b[i % 4, at, :].astype(f32)
            near_b[i, at, :] = total.astype(bf16)

        rounds(some)
        y_copy(i).start()
        if i + 4 < 8:
            for copy in mine_copies(i + 4):
                copy.start()

    def ring_copy(t, right):
        i = 2 * t if right else 2 * t + 1
        slot = t if right else 4 + t
        peer = device(place + 1 if right else place - 1)
        return remote(near_b.at[i, :, mine], ring_b.at[slot], r_send.at[slot], r_recv.at[slot], peer)

    def ring_step(t):
        for right in (True, False) if t < 3 else (True,):
            i = 2 * t if right else 2 * t + 1
            y_copy(i).wait_recv()
            if t > 0:
                ring_copy(t - 1, right).wait_recv()
            slot = (t if right else 4 + t) - 1

            def some(at):
                total = near_b[i, at, mine].astype(f32) + y_b[i, at, :].astype(f32)
                if t > 0:
                    total = total + ring_b[slot, at, :].astype(f32)
                near_b[i, at, mine] = total.astype(bf16)

            rounds(some)
            ring_copy(t, right).start()

    fin_copy = remote(fin_b, fin_r, fin_send, fin_recv, other)

    def ring_end():
        y_copy(7).wait_recv()
        ring_copy(3, True).wait_recv()
        ring_copy(2, False).wait_recv()

        def some(at):
            total = near_b[7, at, mine].astype(f32) + y_b[7, at, :].astype(f32)
            fin_b[at, :] = (total + ring_b[3, at, :].astype(f32) + ring_b[6, at, :].astype(f32)).astype(bf16)

        rounds(some)
        fin_copy.start()

    def z_copy(h, i):
        return remote(
            dw_b.at[h, level ^ i], z_b.at[h, i], z_send.at[h, i], z_recv.at[h, i], me ^ (GROUP * i)
        )

    def j_copy(h, i):
        return remote(j_b.at[h, pos ^ i], j_r.at[pos, h], j_send.at[h, i], j_recv.at[h, i], me ^ i)

    def gather_rows(h):
        for i in range(1, GROUP):
            z_copy(h, i).wait_recv()
        total = dw_b[h, level].astype(f32)
        for i in range(1, GROUP):
            total = total + z_b[h, i].astype(f32)
        j_b[h] = total.astype(bf16).reshape(GROUP, D // n, W3)
        j_r[pos, h] = j_b[h, pos]
        for i in range(1, GROUP):
            j_copy(h, i).start()

    causal = below(T, T, True)
    key_row = lax.broadcasted_iota(jnp.int32, (PROMPT, T), 0).astype(f32)

    def prepare(part, h):
        at = 0
        for row, size in loads[part]:
            p = row // TOK
            left, right, count, to = PACK[0 if size == CONT else 1]
            packed = g_b[p, h, to : to + count, :].astype(f32)
            lane = lanes(count)
            for start, block in ((left, pltpu.roll(packed, HEAD, 1)), (right, packed)):
                off = at + start - (row - p * TOK)
                prod = jnp.where(lane >= HEAD, block * f_b[h, off : off + count, :], 0.0)
                inner = jnp.sum(prod, axis=1, keepdims=True)
                hi = inner.astype(bf16).astype(f32)
                mid = (inner - hi).astype(bf16).astype(f32)
                low = inner - hi - mid
                tail = jnp.where(lane == 0, -hi, jnp.where(lane == 1, -mid, -low))
                value = jnp.where(lane >= HEAD, block, jnp.where(lane < 3, tail, 0.0))
                g_s[h, p * TOK + start : p * TOK + start + count, :] = value.astype(bf16)
            at += size

    def block(h, keys, size, rows, count, mask, target):
        kb = k_s[h, pl.ds(keys, size), :]
        vb = v_s[h, pl.ds(keys, size), :]
        q = q_s[h, pl.ds(rows, count), :]
        g = g_s[h, pl.ds(rows, count), :]
        probs = jnp.exp(dot_nt(kb, q))
        if mask is not None:
            probs = jnp.where(mask, probs, 0.0)
        ds = (probs * dot_nt(vb, g)).astype(bf16)
        lane = lanes(count)
        none = jnp.zeros_like(q)
        pair = dot(ds, jnp.where(lane < HEAD, q, none))
        pair = pair + dot(probs.astype(bf16), jnp.where(lane < HEAD, none, g))
        dq_s[h, :, pl.ds(rows, count)] += dot(kt_s[h, :, pl.ds(keys, size)], ds)
        if target is None:
            return pair
        dkv_s[h, pl.ds(target, size), :] += pair

    def diagonal(h, p):
        row, at = p * TOK, p * PROMPT
        block(h, row, T, row, T, causal, at)
        block(h, row, T, row + T, T, None, at)
        block(h, row + T, T, row + T, T, causal, at + T)

    def flush_q(h, row, size):
        at = pl.ds(row, size)
        dm_s[h, at, 2 * HEAD :] = (dq_s[h, :, at].T * 0.125).astype(bf16)

    def flush(h, p):
        dm_s[h, p * TOK : p * TOK + PROMPT, : 2 * HEAD] = dkv_s[
            h, p * PROMPT : (p + 1) * PROMPT, :
        ].astype(bf16)
        flush_q(h, p * TOK, PROMPT)

    def add_weight(stage, h):
        at = 0
        total = jnp.zeros((W3, D), f32)
        for row, size in stages[stage]:
            total = total + dot_tn(dm_s[h, row : row + size, :], a_b[at : at + size, :])
            at += size
        if stage == 0:
            dw_s[h] = total
        else:
            dw_s[h] += total

    def dn_rows(owner, seg):
        rows = pl.ds(pl.multiple_of(owner * TOK + seg * T, T), T)
        total = dot_nt(dm_s[0, rows, :], w_h[0])
        for h in range(1, OWN):
            total = total + dot_nt(dm_s[h, rows, :], w_h[h])
        return total

    def dn_copy(kind, seg):
        at = pl.ds(seg * T, T)
        src, dst, peer = ((dn_a, dn_ra, near), (dn_b, dn_rb, far), (dn_c, dn_rc, near))[kind]
        return remote(src.at[at], dst.at[at], d_send.at[kind, seg], d_recv.at[kind, seg], peer)

    def put(kind, seg):
        at = slice(seg * T, (seg + 1) * T)
        rows = dn_rows(pos ^ (3, 2, 1)[kind], seg)
        if kind == 1:
            dn_copy(0, seg).wait_recv()
            rows = rows + dn_ra[at, :].astype(f32)
        (dn_a, dn_b, dn_c)[kind][at, :] = rows.astype(bf16)
        dn_copy(kind, seg).start()

    def put_prompt(p, kinds):
        for kind in kinds:

            @pl.when((pos ^ (3, 2, 1)[kind]) == p)
            def _():
                for seg in range(2):
                    put(kind, seg)

    first[3].wait()
    first[4].wait()
    for h in range(OWN):
        w_h[h] = jnp.concatenate(
            [w_s[:, part * SLICE + h * HEAD : part * SLICE + (h + 1) * HEAD] for part in (1, 2, 0)],
            axis=1,
        )
    dq_s[...] = jnp.zeros_like(dq_s)
    dkv_s[...] = jnp.zeros_like(dkv_s)
    for copy in first[:3]:
        copy.wait()

    def turn(h, carry):
        for p in range(GROUP):
            kt_s[h, :, p * TOK : (p + 1) * TOK] = k_s[h, p * TOK : (p + 1) * TOK, :].T[:HEAD]
        return carry

    lax.fori_loop(0, OWN, turn, 0)
    own_do.wait()
    for i in range(1, GROUP):
        do_copy(0, i).wait_recv()
    for copy in f_copies(0):
        copy.wait()
    chip_sum(0)
    chip_sum(1)

    def stage_cont(h, carry):
        prepare(0, h)

        def cont(c, carry):
            rows = pl.multiple_of(c * TOK + PROMPT, CONT)
            code = lines_s[base + c, 1:2, 0:128].astype(f32)
            reach = code[:, 0:1] * 16.0 + code[:, 1:2]
            for p in range(GROUP):
                block(h, p * TOK, PROMPT, rows, T, key_row < reach - p * PROMPT, p * PROMPT)
            pair = block(h, rows, T, rows, T, causal, None)
            dm_s[h, pl.ds(rows, T), : 2 * HEAD] = pair.astype(bf16)
            flush_q(h, rows, T)
            return carry

        lax.fori_loop(0, GROUP, cont, 0)

        for k in range(OWN):

            @pl.when(h == k)
            def _():
                chip_sum(2 + 2 * k)
                chip_sum(3 + 2 * k)

        return carry

    lax.fori_loop(0, OWN, stage_cont, 0)
    ring_step(0)
    for copy in f_copies(1):
        copy.start()
    for copy in a_copies(0):
        copy.wait()
    for kind in (0, 2, 1):
        put(kind, 2)
    lax.fori_loop(0, OWN, lambda h, carry: (add_weight(0, h), carry)[1], 0)
    for copy in a_copies(1):
        copy.start()
    for i in range(1, GROUP):
        do_copy(1, i).wait_recv()
    for copy in f_copies(1):
        copy.wait()

    def stage_last(h, carry):
        prepare(1, h)
        for p in range(3):
            block(h, p * TOK, PROMPT, 3 * TOK, PROMPT, None, p * PROMPT)
        diagonal(h, 3)
        flush(h, 3)

        return carry

    lax.fori_loop(0, OWN, stage_last, 0)
    ring_step(1)
    for copy in f_copies(2):
        copy.start()
    for copy in a_copies(1):
        copy.wait()
    put_prompt(3, (0, 2))
    lax.fori_loop(0, OWN, lambda h, carry: (add_weight(1, h), carry)[1], 0)
    for copy in a_copies(2):
        copy.start()
    put_prompt(3, (1,))
    for copy in f_copies(2):
        copy.wait()

    def stage_first(h, carry):
        prepare(2, h)
        diagonal(h, 0)
        for p in range(1, 3):
            block(h, 0, PROMPT, p * TOK, PROMPT, None, 0)
        flush(h, 0)

        return carry

    lax.fori_loop(0, OWN, stage_first, 0)
    for copy in a_copies(2):
        copy.wait()
    put_prompt(0, (0, 2))
    lax.fori_loop(0, OWN, lambda h, carry: (add_weight(2, h), carry)[1], 0)
    for copy in a_copies(3):
        copy.start()
    put_prompt(0, (1,))
    for copy in a_copies(3):
        copy.wait()

    def stage_middle(h, carry):
        block(h, TOK, PROMPT, 2 * TOK, PROMPT, None, PROMPT)
        diagonal(h, 1)
        flush(h, 1)
        diagonal(h, 2)
        flush(h, 2)
        add_weight(3, h)
        dw = dw_s[h].T
        dw_b[h] = dw.astype(bf16).reshape(GROUP, D // GROUP, W3)
        for i in range(1, GROUP):
            z_copy(h, i).start()
        db = jnp.zeros((1, W3), f32)
        for i in range(GROUP):
            db = db + jnp.sum(dm_s[h, i * TOK : (i + 1) * TOK, :].astype(f32), axis=0, keepdims=True)
        hi = db.astype(bf16)
        mid = (db - hi.astype(f32)).astype(bf16)
        low = (db - hi.astype(f32) - mid.astype(f32)).astype(bf16)
        split = jnp.concatenate([hi, mid, low, jnp.zeros((13, W3), bf16)], axis=0)
        ones = jnp.ones((8, W3), f32)
        gain_rows = lax.dot_general(
            ones,
            w_h[h].astype(f32) * dw,
            (((1,), (1,)), ((), ())),
            precision=lax.Precision.HIGHEST,
            preferred_element_type=f32,
        )
        db_s[h, 0:1, :W3] = db
        db_s[h, 1:2, W3 : W3 + D] = jnp.sum(dot_nt(split, w_h[h]), axis=0, keepdims=True)
        db_s[h, 2:3, W3 : W3 + D] = gain_rows[0:1]
        return carry

    lax.fori_loop(0, OWN, stage_middle, 0)
    for kind, owners in ((2, (0, 3)), (0, (1, 2)), (1, (0, 3))):
        inner = lax.rem(pos + 1, GROUP) // 2

        @pl.when(inner == (0 if owners == (0, 3) else 1))
        def _():
            for seg in range(2):
                put(kind, seg)

    ring_step(2)
    for copy in later:
        copy.wait()

    rows48 = D // n
    gain = jnp.concatenate([lines_s[d, 0:1, 0:rows48] for d in range(n)], axis=1).astype(f32)
    shift = jnp.concatenate([lines_s[d, 0:1, rows48 : 2 * rows48] for d in range(n)], axis=1).astype(f32)
    d_shift = db_s[0, 1:2, W3 : W3 + D] + db_s[1, 1:2, W3 : W3 + D] + db_s[2, 1:2, W3 : W3 + D]
    d_gain = db_s[0, 2:3, W3 : W3 + D] + db_s[1, 2:3, W3 : W3 + D] + db_s[2, 2:3, W3 : W3 + D]
    blank = jnp.zeros((1, D - SLICE), f32)

    def biases(lo):
        row = jnp.concatenate([db_s[h, 0:1, lo : lo + HEAD] for h in range(OWN)] + [blank], axis=1)
        return pltpu.roll(jnp.broadcast_to(row, (8, D)), pos * SLICE, 1)[0:1]

    sm_b[0] = jnp.concatenate(
        [
            (d_gain - shift * d_shift) / gain,
            d_shift,
            biases(2 * HEAD),
            biases(HEAD),
            sums_s[3:4, :],
            sums_s[1:2, :],
            sums_s[2:3, :],
            sums_s[0:1, :],
        ]
        + [dbf_s[0:1, c * D : (c + 1) * D] for c in range(FF // D)]
        + [jnp.zeros((SMALL - 12, D), f32)],
        axis=0,
    )
    peers = [me ^ 1, me ^ 2, me ^ 4, me ^ 8, other]

    def small_copy(i):
        return remote(sm_b.at[i], sm_r.at[i], s_send.at[i], s_recv.at[i], peers[i])

    def small_step(i):
        small_copy(i).wait_recv()
        sm_b[i + 1] = sm_b[i] + sm_r[i]
        if i < 4:
            small_copy(i + 1).start()

    small_copy(0).start()
    gather_rows(0)
    small_step(0)
    gather_rows(1)
    small_step(1)
    ring_step(3)
    gather_rows(2)
    small_step(2)
    for h in range(OWN):
        for i in range(1, GROUP):
            j_copy(h, i).wait_recv()
    rep_b[...] = j_r[...]
    rep_copy = remote(rep_b, rep_r, rep_send, rep_recv, other)
    rep_copy.start()
    small_step(3)
    ring_end()

    outs = []
    for seg in (2, 0, 1):
        at = slice(seg * T, (seg + 1) * T)
        rows = dn_rows(pos, seg)
        dn_copy(2, seg).wait_recv()
        dn_copy(1, seg).wait_recv()
        n_rows, r = moments(x_s[at, :].astype(f32))
        e = (rows + dn_rb[at, :].astype(f32) + dn_rc[at, :].astype(f32)) * gain
        lean = jnp.mean(e, axis=-1, keepdims=True) + n_rows * jnp.mean(e * n_rows, axis=-1, keepdims=True)
        dh_s[at, :] = dh_s[at, :] + r * (e - lean)
        copy = pltpu.make_async_copy(dh_s.at[at], grad_ref.at[at], out_sem.at[10 + seg])
        copy.start()
        outs.append(copy)

    small_step(4)
    total = sm_b[5]
    turned = pltpu.roll(total, lax.rem(n - me, n) * rows48, 1)
    eighth = lax.rem(me, 8)
    biased = pltpu.roll(total, lax.rem(8 - eighth, 8) * (2 * rows48), 1)
    quarter = lax.rem(me, 4)
    wide = pltpu.roll(total, lax.rem(4 - quarter, 4) * (4 * rows48), 1)
    row = lax.broadcasted_iota(jnp.int32, (SMALL, D), 0)
    bias_row = jnp.sum(jnp.where(row == 2 + me // 8, biased, 0.0), axis=0, keepdims=True)
    wide_row = jnp.sum(jnp.where(row == 8 + me // 4, wide, 0.0), axis=0, keepdims=True)
    small_copy(0).wait_send()
    sm_b[0] = jnp.where(row == 2, bias_row, jnp.where(row == 3, wide_row, turned))
    copy = pltpu.make_async_copy(sm_b.at[0], small_ref, out_sem.at[2])
    copy.start()
    outs.append(copy)

    rep_copy.wait_recv()
    for part, (at, piece) in enumerate(((2 * HEAD, 0), (0, 1), (HEAD, 2))):
        row = jnp.concatenate(
            [
                rep_b[j, h, :, at : at + HEAD].astype(f32) + rep_r[j, h, :, at : at + HEAD].astype(f32)
                for j in range(GROUP)
                for h in range(OWN)
            ],
            axis=1,
        )
        gq_o[:, piece * D : (piece + 1) * D] = row
    copy = pltpu.make_async_copy(gq_o, gq_ref, out_sem.at[3])
    copy.start()
    outs.append(copy)

    fin_copy.wait_recv()

    def some(at):
        fin_o[at, mine] = fin_b[at, :].astype(f32)
        fin_o[at, rest] = fin_r[at, :].astype(f32)

    rounds(some)
    targets = [(gp_ref, 0, 192), (go_ref, 192, 48)]
    targets += [(gf_ref.at[:, pl.ds(c * D, D)], 240 + 48 * c, 48) for c in range(FF // D)]
    for i, (ref, at, size) in enumerate(targets):
        copy = pltpu.make_async_copy(fin_o.at[pl.ds(at, size)], ref, out_sem.at[4 + i])
        copy.start()
        outs.append(copy)

    for h in range(OWN):
        for i in range(1, GROUP):
            for copy in (z_copy(h, i), j_copy(h, i)):
                copy.wait_send()
    for kind in range(2):
        for i in range(1, GROUP):
            do_copy(kind, i).wait_send()
    for i in range(8):
        y_copy(i).wait_send()
        for copy in near_copies(i):
            copy.wait_send()
    for t in range(4):
        for right in (True, False) if t < 3 else (True,):
            ring_copy(t, right).wait_send()
    for kind in range(3):
        for seg in range(3):
            dn_copy(kind, seg).wait_send()
    for i in range(1, 5):
        small_copy(i).wait_send()
    rep_copy.wait_send()
    fin_copy.wait_send()
    for copy in outs:
        copy.wait()


def backward(do, q, k, v, f, a, w, x, dh, lines, sums, dbf, dwp, dwo, dwf):
    dma = pltpu.SemaphoreType.DMA
    n = BLOCKS
    shape = jax.ShapeDtypeStruct
    vmem = pltpu.VMEM
    rows = D // n
    head = (OWN, ROWS, 2 * HEAD)
    W3 = 3 * HEAD
    pairs = (OWN, GROUP)
    return pl.pallas_call(
        backward_kernel,
        name="backward",
        out_shape=(
            shape((TOK, D), f32),
            shape((rows, 3 * D), f32),
            shape((FF // n, D), f32),
            shape((rows, D), f32),
            shape((rows, FF), f32),
            shape((SMALL, D), f32),
        ),
        in_specs=[ANY] * 15,
        out_specs=(ANY,) * 6,
        scratch_shapes=[
            vmem((GROUP, OWN, PAIR, 2 * HEAD), bf16),
            vmem(head, bf16),
            vmem(head, bf16),
            vmem(head, bf16),
            vmem((OWN, GROUP * CONT, 2 * HEAD), f32),
            vmem((GROUP * CONT, D), bf16),
            vmem((D, WIDE), bf16),
            vmem((TOK, D), bf16),
            vmem((TOK, D), f32),
            vmem(lines.shape, bf16),
            vmem(sums.shape, f32),
            vmem(dbf.shape, f32),
            vmem((8, UNIT, D), bf16),
            vmem((4, UNIT, D), bf16),
            vmem((8, UNIT, D // 2), bf16),
            vmem((7, UNIT, D // 2), bf16),
            vmem((UNIT, D // 2), bf16),
            vmem((UNIT, D // 2), bf16),
            vmem((UNIT, D), f32),
            vmem(head, bf16),
            vmem((OWN, HEAD, ROWS), f32),
            vmem((OWN, HEAD, ROWS), bf16),
            vmem((OWN, GROUP * PROMPT, 2 * HEAD), f32),
            vmem((OWN, ROWS, W3), bf16),
            vmem((OWN, D, W3), bf16),
            vmem((OWN, W3, D), f32),
            vmem((OWN, 8, W3 + D), f32),
            vmem((OWN, GROUP, D // GROUP, W3), bf16),
            vmem((OWN, GROUP, D // GROUP, W3), bf16),
            vmem((OWN, GROUP, rows, W3), bf16),
            vmem((GROUP, OWN, rows, W3), bf16),
            vmem((GROUP, OWN, rows, W3), bf16),
            vmem((GROUP, OWN, rows, W3), bf16),
            vmem((rows, 3 * D), f32),
            vmem((TOK, D), bf16),
            vmem((TOK, D), bf16),
            vmem((TOK, D), bf16),
            vmem((TOK, D), bf16),
            vmem((TOK, D), bf16),
            vmem((TOK, D), bf16),
            vmem((6, SMALL, D), f32),
            vmem((5, SMALL, D), f32),
            dma((10,)),
            dma((3, GROUP)),
            dma((4, GROUP)),
            dma((8, 3)),
            dma((2, GROUP)),
            dma((2, GROUP)),
            dma((8, 3)),
            dma((8, 3)),
            dma((8,)),
            dma((8,)),
            dma((7,)),
            dma((7,)),
            dma,
            dma,
            dma(pairs),
            dma(pairs),
            dma(pairs),
            dma(pairs),
            dma,
            dma,
            dma((3, 3)),
            dma((3, 3)),
            dma((5,)),
            dma((5,)),
            dma((13,)),
        ],
        compiler_params=params(63, collective_id=4, has_side_effects=True),
    )(do, q, k, v, f, a, w, x, dh, lines, sums, dbf, dwp, dwo, dwf)


def unproject_kernel(dq_ref, dk_ref, dv_ref, a_ref, w_ref, dn_ref, dw_ref, db_ref):
    step = pl.program_id(0)
    mixed = jnp.concatenate(
        [ref[h] for ref in (dq_ref, dk_ref, dv_ref) for h in range(OWN)], axis=1
    )
    dn_ref[...] = dot_nt(mixed, w_ref[...]).astype(bf16)
    dw = dot_tn(a_ref[...], mixed)
    db = jnp.sum(mixed.astype(f32), axis=0, keepdims=True)

    @pl.when(step == 0)
    def _():
        dw_ref[...] = dw
        db_ref[...] = db

    @pl.when(step > 0)
    def _():
        dw_ref[...] += dw
        db_ref[...] += db


def unproject(dq, dk, dv, a, w):
    tile = 768
    head = pl.BlockSpec((OWN, tile, HEAD), lambda i: (0, i, 0))
    whole = lambda i: (0, 0)
    shape = jax.ShapeDtypeStruct
    return pl.pallas_call(
        unproject_kernel,
        name="unproject",
        grid=(ROWS // tile,),
        out_shape=(shape((ROWS, D), bf16), shape((D, WIDE), f32), shape((1, WIDE), f32)),
        in_specs=[
            head, head, head,
            pl.BlockSpec((tile, D), lambda i: (i, 0)),
            pl.BlockSpec((D, WIDE), whole),
        ],
        out_specs=(
            pl.BlockSpec((tile, D), lambda i: (i, 0)),
            pl.BlockSpec((D, WIDE), whole),
            pl.BlockSpec((1, WIDE), whole),
        ),
        compiler_params=params(48),
    )(dq, dk, dv, a, w)


def finish_kernel(x_ref, dh_ref, g_ref, one_ref, two_ref, three_ref, out_ref):
    n, r = moments(x_ref[...].astype(f32))
    dn = one_ref[...].astype(f32) + two_ref[...].astype(f32) + three_ref[...].astype(f32)
    e = dn * g_ref[...]
    lean = jnp.mean(e, axis=-1, keepdims=True) + n * jnp.mean(e * n, axis=-1, keepdims=True)
    out_ref[...] = dh_ref[...] + r * (e - lean)


def finish(x, dh, gain, one, two, three):
    tile = 256
    rows = pl.BlockSpec((tile, D), lambda i: (i, 0))
    return pl.pallas_call(
        finish_kernel,
        name="finish",
        grid=(TOK // tile,),
        out_shape=jax.ShapeDtypeStruct((TOK, D), f32),
        in_specs=[rows, rows, pl.BlockSpec((1, D), lambda i: (0, 0)), rows, rows, rows],
        out_specs=rows,
        compiler_params=params(48),
    )(x, dh, gain, one, two, three)


def flip(block, bit):
    count = lax.axis_size("fsdp")
    return lax.ppermute(block, "fsdp", [(i, i ^ bit) for i in range(count)])


def repack(packed, old, new):
    rows = []
    for left, right, size, at in old:
        rows.append((left, packed[:, :, at : at + size, :HEAD]))
        rows.append((right, packed[:, :, at : at + size, HEAD:]))
    rows = jnp.concatenate([part for _, part in sorted(rows, key=lambda entry: entry[0])], axis=2)
    parts = [
        jnp.concatenate([rows[:, :, left : left + size], rows[:, :, right : right + size]], axis=3)
        for left, right, size, _ in sorted(new, key=lambda entry: entry[3])
    ]
    return jnp.concatenate(parts, axis=2)


def over_replicas(block):
    count = lax.axis_size("rep")
    held = lax.optimization_barrier(block)
    if count == 2:
        other = lax.ppermute(held, "rep", [(0, 1), (1, 0)])
        return held.astype(f32) + other.astype(f32)
    return lax.psum(held.astype(f32), "rep")


def body(
    block_input, cotangent, tie_index, prefix_len, pre_gain, pre_shift, w_qkv, b_qv, w_out, b_out,
    mid_gain, mid_shift, w_fc, b_fc, w_proj, b_proj,
):
    n = lax.axis_size("fsdp")
    me = lax.axis_index("fsdp")
    pos = lax.rem(me, GROUP)
    rows = D // n
    index = tie_index[0]

    def chosen(bank):
        return lax.dynamic_index_in_dim(bank, index, 0, keepdims=False)

    vectors = (pre_gain, pre_shift, b_qv, b_out, mid_gain, mid_shift, b_fc, b_proj)
    sizes = [bank.shape[1] for bank in vectors]
    count = sum(sizes)
    high = -(-(rows + 2) // 16) * 16
    cuts = [sum(sizes[:i]) for i in range(len(sizes) + 1)]

    def vectors_of(lines):
        smalls = lines[:, 0, :count].astype(f32)
        group_rows = lax.dynamic_slice_in_dim(lines[:, 1, :2], me - pos, GROUP, 0)
        reaches = group_rows[:, 0].astype(f32) * 16 + group_rows[:, 1].astype(f32)
        return [
            smalls[:, cuts[i] : cuts[i + 1]].reshape(1, -1) for i in range(len(sizes))
        ], reaches.astype(jnp.int32)

    fused = n == BLOCKS and lax.axis_size("rep") == 2
    if fused:
        small, pieces, shard = pick(tie_index, prefix_len, vectors, w_qkv, w_out, w_fc, w_proj)
        wall, lines, wq, a_low, qx, k, v, o_full, o_recv = forward(block_input, small, pieces, shard)
        a_low = a_low.reshape(ROWS, D)
        (g1, s1, _, bo, g2, s2, bf, bp), reaches = vectors_of(lines)
    else:
        small = jnp.concatenate([chosen(bank) for bank in vectors])
        reach = prefix_len[0]
        reach_row = jnp.concatenate([reach // 16, reach % 16]).astype(bf16)
        wq = chosen(w_qkv).reshape(rows, 3, GROUP, SLICE).transpose(2, 0, 1, 3)
        wq = wq.reshape(GROUP, rows, WIDE)
        extra = jnp.stack([jnp.pad(line, (0, WIDE - line.shape[0])) for line in (small, reach_row)])
        wo, wf, wp = chosen(w_out), chosen(w_fc), chosen(w_proj)
        extra = jnp.pad(extra, ((0, high - rows - 2), (0, 0)))
        pieces = jnp.concatenate([wq, jnp.broadcast_to(extra, (GROUP,) + extra.shape)], axis=1)
        wo = lax.all_gather(wo, "fsdp", axis=0, tiled=True).reshape(BLOCKS, -1, D)
        wf = lax.all_gather(wf, "fsdp", axis=0, tiled=True)
        wf = wf.reshape(BLOCKS, D // BLOCKS, FF // D, D).transpose(0, 2, 1, 3)
        wp = lax.all_gather(wp, "fsdp", axis=0, tiled=True).reshape(BLOCKS, -1, D)
        wall = jnp.concatenate([wp, wo, wf.reshape(BLOCKS, -1, D)], axis=1)
        xg, wg = gather_group(n, block_input, pieces)
        wq = wg[:, :rows].reshape(D, WIDE)
        (g1, s1, bqv, bo, g2, s2, bf, bp), reaches = vectors_of(wg[:, rows : rows + 2])
        own_bias = lax.dynamic_index_in_dim(bqv.reshape(2, GROUP, SLICE), pos, 1, keepdims=False)
        bias = jnp.concatenate([own_bias[0], jnp.zeros((SLICE,), f32), own_bias[1]])[None]
        a_low, q, k, v = project(xg.reshape(ROWS, D), wq, g1, s1, bias)
        o_send, o_full, qx = attend(reaches, q, k, v)
        o_recv = repack(swap(o_send, 1, "swap_o"), ((0, 384, 384, 0),), PACK)

    y, dwf, dwp, dbf, dwo, dh, do_send, sums = middle(
        block_input, o_recv, cotangent, wall, bo, g2, s2, bf, bp
    )
    if fused:
        grad, dwq, dwp, dwo, dwf, sums = backward(
            do_send, qx, k, v, o_full, a_low, wq, block_input, dh, lines, sums, dbf,
            dwp.reshape(BLOCKS, -1, D), dwo.reshape(BLOCKS, -1, D), dwf.reshape(BLOCKS, -1, D),
        )
        rows48 = D // n
        dg1, ds1, dbo, dg2, ds2, dbp = (sums[i, :rows48] for i in (0, 1, 4, 5, 6, 7))
        dbqv, dbf = sums[2, : 2 * rows48], sums[3, : 4 * rows48]
        return (y, grad, dg1, ds1, dwq, dbqv, dwo, dbo, dg2, ds2, dwf, dbf, dwp, dbp)
    dwf = dwf.transpose(0, 2, 1, 3).reshape(D, FF)
    dwf = lax.psum_scatter(dwf, "fsdp", scatter_dimension=0, tiled=True)
    dwp = lax.psum_scatter(dwp, "fsdp", scatter_dimension=0, tiled=True)
    dwo = lax.psum_scatter(dwo, "fsdp", scatter_dimension=0, tiled=True)
    do_recv = repack(swap(do_send, 2, "swap_do"), PACK, ((0, 384, 384, 0),))
    dq, dk, dv = attend_back(reaches, qx, k, v, o_full, do_recv)
    dn, dwq, db = unproject(dq, dk, dv, a_low, wq)

    dn = dn.reshape(GROUP, TOK, D)
    block_of = lambda bit: lax.dynamic_index_in_dim(dn, pos ^ bit, 0, keepdims=False)
    beside = flip(block_of(1), 1)
    across = flip(block_of(3), 1)
    across = flip((across.astype(f32) + block_of(2).astype(f32)).astype(bf16), 2)

    wq_wide = wq.astype(f32)
    dshift = jnp.sum(wq_wide * db, axis=1)
    dgain = jnp.sum(wq_wide * (dwq - s1.reshape(D, 1) * db), axis=1) / g1.reshape(D)
    where = (jnp.arange(GROUP) == pos).astype(f32)[:, None]
    dbias = jnp.concatenate(
        [(where * db[:, :SLICE]).reshape(-1), (where * db[:, 2 * SLICE :]).reshape(-1)]
    )
    line = jnp.concatenate(
        [
            part.reshape(n, -1)
            for part in (dgain, dshift, dbias, sums[3], sums[1], sums[2], dbf, sums[0])
        ],
        axis=1,
    )
    line_hi = line.astype(bf16)
    line_low = (line - lax.reduce_precision(line, 8, 7)).astype(bf16)
    lines = jnp.pad(jnp.stack([line_hi, line_low], axis=1), ((0, 0), (0, 0), (0, WIDE - count)))
    lines = jnp.pad(lines, ((0, 0), (0, high - rows - 2), (0, 0)))
    back = jnp.concatenate([dwq.astype(bf16).reshape(n, rows, WIDE), lines], axis=1)
    back = swap(back, 3, "swap_grad")
    dwq = jnp.sum(back[:, :rows].astype(f32).reshape(n // GROUP, GROUP, rows, 3, SLICE), axis=0)
    dwq = dwq.transpose(1, 2, 0, 3).reshape(rows, 3 * D)
    line = jnp.sum(back[:, rows, :count].astype(f32) + back[:, rows + 1, :count].astype(f32), axis=0)

    grad = finish(block_input, dh, g1, block_of(0), beside, across)
    dwq = over_replicas(dwq.astype(bf16))
    dwo, dwf, dwp = over_replicas(dwo), over_replicas(dwf), over_replicas(dwp)
    line = over_replicas(line)
    dg1, ds1, dbqv, dbo, dg2, ds2, dbf, dbp = (
        line[cuts[i] : cuts[i + 1]] for i in range(len(sizes))
    )
    return (y, grad, dg1, ds1, dwq, dbqv, dwo, dbo, dg2, ds2, dwf, dbf, dwp, dbp)


def solution(mesh):
    tokens = P(("rep", "fsdp"), None)
    vector, matrix = P(None, "fsdp"), P(None, "fsdp", None)
    return jax.shard_map(
        body,
        mesh=mesh,
        in_specs=(
            tokens, tokens, P(), tokens, vector, vector, matrix, vector, matrix, vector,
            vector, vector, matrix, vector, matrix, vector,
        ),
        out_specs=(
            tokens, tokens, P("fsdp"), P("fsdp"), P("fsdp", None), P("fsdp"), P("fsdp", None),
            P("fsdp"), P("fsdp"), P("fsdp"), P("fsdp", None), P("fsdp"), P("fsdp", None), P("fsdp"),
        ),
        check_vma=False,
    )
```

```python
from functools import partial

import jax
import jax.numpy as jnp
from jax import lax
from jax.experimental import pallas as pl
from jax.experimental.pallas import tpu as pltpu
from jax.sharding import PartitionSpec as P

D = 768
HEADS = 12
HEAD = 64
FF = 3072
GROUP = 4
PROMPT = 512
CONT = 256
TOK = 768
ROWS = GROUP * TOK
OWN = HEADS // GROUP
SLICE = OWN * HEAD
WIDE = 3 * SLICE
PAIR = TOK // 2
CHUNK = 768
BLOCKS = 16
UNIT = 432
NEG = -1e30
EPS = 1e-5
PACK = ((512, 640, 128, 0), (0, 256, 256, 128))
GELU_A = 0.7978845608028654
GELU_B = 0.044715

f32 = jnp.float32
bf16 = jnp.bfloat16
MESH = pl.DeviceIdType.MESH
ANY = pl.BlockSpec(memory_space=pl.ANY)


def params(mib, **more):
    return pltpu.CompilerParams(vmem_limit_bytes=mib << 20, **more)


def dot(a, b):
    return jnp.dot(a, b, preferred_element_type=f32)


def dot_nt(a, b):
    return lax.dot_general(a, b, (((1,), (1,)), ((), ())), preferred_element_type=f32)


def dot_tn(a, b):
    return lax.dot_general(a, b, (((0,), (0,)), ((), ())), preferred_element_type=f32)


def moments(x):
    center = x - jnp.mean(x, axis=-1, keepdims=True)
    scale = lax.rsqrt(jnp.mean(center * center, axis=-1, keepdims=True) + EPS)
    return center * scale, scale


def greet(peers, replica=None):
    sem = pltpu.get_barrier_semaphore()
    for peer in peers:
        pl.semaphore_signal(sem, inc=1, device_id={"fsdp": peer}, device_id_type=MESH)
    if replica is not None:
        pl.semaphore_signal(sem, inc=1, device_id={"rep": replica}, device_id_type=MESH)
    pl.semaphore_wait(sem, len(peers) + (replica is not None))


def gather_kernel(n, parts, x_ref, w_ref, xg_ref, wg_ref, xs, xr, ws, wr, local):
    me = lax.axis_index("fsdp")
    pos = lax.rem(me, GROUP)
    near, far = me ^ 1, me ^ 2
    greet([me ^ i for i in range(1, n)])
    own = pltpu.make_async_copy(x_ref, xg_ref.at[pos], local.at[0])
    own.start()
    own_w = pltpu.make_async_copy(w_ref.at[pos], wg_ref.at[me], local.at[1])
    own_w.start()
    rows = TOK // parts

    def piece(src, slot, part, i, peer):
        at = pl.ds(part * rows, rows)
        return pltpu.make_async_remote_copy(
            src_ref=src.at[at],
            dst_ref=xg_ref.at[slot, at],
            send_sem=xs.at[i],
            recv_sem=xr.at[i],
            device_id={"fsdp": peer},
            device_id_type=MESH,
        )

    across = [piece(x_ref, pos, part, part, far) for part in range(parts)]
    for copy in across:
        copy.start()
    beside = pltpu.make_async_remote_copy(
        src_ref=x_ref,
        dst_ref=xg_ref.at[pos],
        send_sem=xs.at[2 * parts],
        recv_sem=xr.at[2 * parts],
        device_id={"fsdp": near},
        device_id_type=MESH,
    )
    beside.start()
    slices = []
    for i in range(1, n):
        peer = me ^ i
        copy = pltpu.make_async_remote_copy(
            src_ref=w_ref.at[lax.rem(peer, GROUP)],
            dst_ref=wg_ref.at[me],
            send_sem=ws.at[i],
            recv_sem=wr.at[i],
            device_id={"fsdp": peer},
            device_id_type=MESH,
        )
        copy.start()
        slices.append(copy)
    passed = []
    for part in range(parts):
        across[part].wait_recv()
        copy = piece(xg_ref.at[pos ^ 2], pos ^ 2, part, parts + part, near)
        copy.start()
        passed.append(copy)
    for copy in across:
        copy.wait_send()
    beside.wait()
    own.wait()
    own_w.wait()
    for copy in passed + slices:
        copy.wait()


def gather_group(n, x, pieces):
    parts = 4
    dma = pltpu.SemaphoreType.DMA
    return pl.pallas_call(
        partial(gather_kernel, n, parts),
        name="gather_group",
        out_shape=(
            jax.ShapeDtypeStruct((GROUP,) + x.shape, x.dtype),
            jax.ShapeDtypeStruct((n,) + pieces.shape[1:], pieces.dtype),
        ),
        in_specs=[ANY, ANY],
        out_specs=(ANY, ANY),
        scratch_shapes=[
            dma((2 * parts + 1,)),
            dma((2 * parts + 1,)),
            dma((n,)),
            dma((n,)),
            dma((2,)),
        ],
        compiler_params=params(32, collective_id=0, has_side_effects=True),
    )(x, pieces)


def swap_kernel(count, x_ref, o_ref, send, recv, local):
    me = lax.axis_index("fsdp")
    greet([me ^ i for i in range(1, count)])
    slot = lax.rem(me, count)
    own = pltpu.make_async_copy(x_ref.at[slot], o_ref.at[slot], local)
    own.start()
    copies = []
    for i in range(1, count):
        copy = pltpu.make_async_remote_copy(
            src_ref=x_ref.at[slot ^ i],
            dst_ref=o_ref.at[slot],
            send_sem=send.at[i],
            recv_sem=recv.at[i],
            device_id={"fsdp": me ^ i},
            device_id_type=MESH,
        )
        copy.start()
        copies.append(copy)
    own.wait()
    for copy in copies:
        copy.wait()


def swap(x, collective_id, name):
    count = x.shape[0]
    dma = pltpu.SemaphoreType.DMA
    return pl.pallas_call(
        partial(swap_kernel, count),
        name=name,
        out_shape=jax.ShapeDtypeStruct(x.shape, x.dtype),
        in_specs=[ANY],
        out_specs=ANY,
        scratch_shapes=[dma((count,)), dma((count,)), dma],
        compiler_params=params(32, collective_id=collective_id, has_side_effects=True),
    )(x)


def project_kernel(x_ref, w_ref, g_ref, s_ref, b_ref, a_ref, q_ref, k_ref, v_ref):
    n, _ = moments(x_ref[...].astype(f32))
    a_low = (n * g_ref[...] + s_ref[...]).astype(bf16)
    a_ref[...] = a_low
    mixed = (dot(a_low, w_ref[...]) + b_ref[...]).astype(bf16)
    ones = jnp.ones((x_ref.shape[0], HEAD), bf16)
    for h in range(OWN):
        q = mixed[:, h * HEAD : (h + 1) * HEAD] * 0.125
        k = mixed[:, SLICE + h * HEAD : SLICE + (h + 1) * HEAD]
        v = mixed[:, 2 * SLICE + h * HEAD : 2 * SLICE + (h + 1) * HEAD]
        q_ref[h] = jnp.concatenate([q.astype(bf16), jnp.zeros_like(ones)], axis=1)
        k_ref[h] = jnp.concatenate([k, ones], axis=1)
        v_ref[h] = jnp.concatenate([v, ones], axis=1)


def project(x, w, gain, shift, bias):
    tile = 384
    heads = jax.ShapeDtypeStruct((OWN, ROWS, 2 * HEAD), bf16)
    head_spec = pl.BlockSpec((OWN, tile, 2 * HEAD), lambda i: (0, i, 0))
    whole = lambda i: (0, 0)
    return pl.pallas_call(
        project_kernel,
        name="project",
        grid=(ROWS // tile,),
        out_shape=(jax.ShapeDtypeStruct((ROWS, D), bf16), heads, heads, heads),
        in_specs=[
            pl.BlockSpec((tile, D), lambda i: (i, 0)),
            pl.BlockSpec((D, WIDE), whole),
            pl.BlockSpec((1, D), whole),
            pl.BlockSpec((1, D), whole),
            pl.BlockSpec((1, WIDE), whole),
        ],
        out_specs=(pl.BlockSpec((tile, D), lambda i: (i, 0)), head_spec, head_spec, head_spec),
        compiler_params=params(48),
    )(x, w, gain, shift, bias)


def lanes(rows):
    return lax.broadcasted_iota(jnp.int32, (rows, 2 * HEAD), 1)


def split_columns(base, lane, column):
    hi = column.astype(bf16).astype(f32)
    mid = (column - hi).astype(bf16).astype(f32)
    low = column - hi - mid
    tail = jnp.where(lane == HEAD, -hi, jnp.where(lane == HEAD + 1, -mid, -low))
    return jnp.where(lane < HEAD, base, jnp.where(lane < HEAD + 3, tail, 0.0)).astype(bf16)


def below(rows, cols, low_key):
    row = lax.broadcasted_iota(jnp.int32, (rows, cols), 0)
    col = lax.broadcasted_iota(jnp.int32, (rows, cols), 1)
    return row <= col if low_key else col <= row


def attend_kernel(reach_ref, q_ref, k_ref, v_ref, o_ref, f_ref, x_ref):
    T = CONT
    lane = lanes(T)
    causal = below(T, T, False)

    def tile(at, blocks):
        q = q_ref[0, pl.ds(at, T), :]
        scores = []
        for start, size, mask in blocks:
            s = dot_nt(q, k_ref[0, pl.ds(start, size), :])
            scores.append(s if mask is None else jnp.where(mask, s, NEG))
        peak = scores[0].max(axis=1, keepdims=True)
        for s in scores[1:]:
            peak = jnp.maximum(peak, s.max(axis=1, keepdims=True))
        total = jnp.zeros((T, 2 * HEAD), f32)
        for s, (start, size, _) in zip(scores, blocks):
            total += dot(jnp.exp(s - peak).astype(bf16), v_ref[0, pl.ds(start, size), :])
        mass = total[:, HEAD : HEAD + 1]
        f_ref[0, pl.ds(at, T), :] = total / mass
        lse = peak + jnp.log(mass)
        x_ref[0, pl.ds(at, T), :] = split_columns(q.astype(f32), lane, lse)

    for p in range(GROUP):
        past = [(i * TOK, PROMPT, None) for i in range(p)]
        base = p * TOK
        tile(base, past + [(base, T, causal)])
        tile(base + T, past + [(base, T, None), (base + T, T, causal)])

    def cont(c, carry):
        at = pl.multiple_of(c * TOK + PROMPT, CONT)
        reach = reach_ref[c]
        col = lax.broadcasted_iota(jnp.int32, (T, PROMPT), 1)
        blocks = [(i * TOK, PROMPT, col < reach - i * PROMPT) for i in range(GROUP)]
        tile(at, blocks + [(at, T, causal)])
        return carry

    lax.fori_loop(0, GROUP, cont, 0)

    half = lanes(PAIR) < HEAD
    for p in range(GROUP):
        top = f_ref[0, p * TOK : p * TOK + PAIR, :]
        low = f_ref[0, p * TOK + PAIR : (p + 1) * TOK, :]
        o_ref[p, 0] = jnp.where(half, top, pltpu.roll(low, HEAD, 1)).astype(bf16)


def attend(reach, q, k, v):
    head = lambda h: (h, 0, 0)
    spec = pl.BlockSpec((1, ROWS, 2 * HEAD), head)
    return pl.pallas_call(
        attend_kernel,
        name="attend",
        grid=(OWN,),
        out_shape=(
            jax.ShapeDtypeStruct((GROUP, OWN, PAIR, 2 * HEAD), bf16),
            jax.ShapeDtypeStruct((OWN, ROWS, 2 * HEAD), f32),
            jax.ShapeDtypeStruct((OWN, ROWS, 2 * HEAD), bf16),
        ),
        in_specs=[pl.BlockSpec(memory_space=pltpu.SMEM), spec, spec, spec],
        out_specs=(
            pl.BlockSpec((GROUP, 1, PAIR, 2 * HEAD), lambda h: (0, h, 0, 0)),
            spec,
            spec,
        ),
        compiler_params=params(56),
    )(reach, q, k, v)


def attend_back_kernel(
    reach_ref, q_ref, k_ref, v_ref, f_ref, g_ref, dq_ref, dk_ref, dv_ref, g_s, dq_s, kt_s, dk_s, dv_s
):
    T = CONT
    half = lanes(PAIR) < HEAD
    lane = lanes(PAIR)
    for p in range(GROUP):
        packed = g_ref[p, 0].astype(f32)
        for i, block in enumerate((packed, pltpu.roll(packed, HEAD, 1))):
            at = p * TOK + i * PAIR
            prod = jnp.where(half, block * f_ref[0, at : at + PAIR, :], 0.0)
            inner = jnp.sum(prod, axis=1, keepdims=True)
            g_s[at : at + PAIR, :] = split_columns(block, lane, inner)
        kt_s[:, p * TOK : (p + 1) * TOK] = k_ref[0, p * TOK : (p + 1) * TOK, :].T[:HEAD]
    dq_s[...] = jnp.zeros_like(dq_s)

    def block(keys, size, rows, count, mask, first, key_at):
        kb = k_ref[0, pl.ds(keys, size), :]
        vb = v_ref[0, pl.ds(keys, size), :]
        q = q_ref[0, pl.ds(rows, count), :]
        g = g_s[pl.ds(rows, count), :]
        probs = jnp.exp(dot_nt(kb, q))
        if mask is not None:
            probs = jnp.where(mask, probs, 0.0)
        ds = (probs * dot_nt(vb, g)).astype(bf16)
        dv = dot(probs.astype(bf16), g)
        dk = dot(ds, q)
        at = pl.ds(key_at, size)
        dv_s[at, :] = dv if first else dv_s[at, :] + dv
        dk_s[at, :] = dk if first else dk_s[at, :] + dk
        dq_s[:, pl.ds(rows, count)] += dot(kt_s[:, pl.ds(keys, size)], ds)

    causal = below(T, T, True)
    for p in range(GROUP):
        base = p * TOK
        block(base, T, base, T, causal, True, 0)
        block(base + T, T, base + T, T, causal, True, T)
        block(base, T, base + T, T, None, False, 0)

        def later(i, carry):
            rows = pl.multiple_of(i * TOK, CONT)
            block(base, PROMPT, rows, PROMPT, None, False, 0)
            return carry

        lax.fori_loop(p + 1, GROUP, later, 0)

        def cont(c, carry):
            rows = pl.multiple_of(c * TOK + PROMPT, CONT)
            key = lax.broadcasted_iota(jnp.int32, (PROMPT, T), 0)
            block(base, PROMPT, rows, T, key < reach_ref[c] - p * PROMPT, False, 0)
            return carry

        lax.fori_loop(0, GROUP, cont, 0)
        dk_ref[0, base : base + PROMPT, :] = dk_s[:, :HEAD].astype(bf16)
        dv_ref[0, base : base + PROMPT, :] = dv_s[:, :HEAD].astype(bf16)

    def own(c, carry):
        at = pl.multiple_of(c * TOK + PROMPT, CONT)
        block(at, T, at, T, causal, True, 0)
        dk_ref[0, pl.ds(at, T), :] = dk_s[:T, :HEAD].astype(bf16)
        dv_ref[0, pl.ds(at, T), :] = dv_s[:T, :HEAD].astype(bf16)
        return carry

    lax.fori_loop(0, GROUP, own, 0)
    for i in range(ROWS // PROMPT):
        at = i * PROMPT
        dq_ref[0, at : at + PROMPT, :] = (dq_s[:, at : at + PROMPT].T * 0.125).astype(bf16)


def attend_back(reach, q, k, v, f, g):
    head = lambda h: (h, 0, 0)
    spec = pl.BlockSpec((1, ROWS, 2 * HEAD), head)
    out = jax.ShapeDtypeStruct((OWN, ROWS, HEAD), bf16)
    out_spec = pl.BlockSpec((1, ROWS, HEAD), head)
    return pl.pallas_call(
        attend_back_kernel,
        name="attend_back",
        grid=(OWN,),
        out_shape=(out, out, out),
        in_specs=[pl.BlockSpec(memory_space=pltpu.SMEM), spec, spec, spec, spec]
        + [pl.BlockSpec((GROUP, 1, PAIR, 2 * HEAD), lambda h: (0, h, 0, 0))],
        out_specs=(out_spec, out_spec, out_spec),
        scratch_shapes=[
            pltpu.VMEM((ROWS, 2 * HEAD), bf16),
            pltpu.VMEM((HEAD, ROWS), f32),
            pltpu.VMEM((HEAD, ROWS), bf16),
            pltpu.VMEM((PROMPT, 2 * HEAD), f32),
            pltpu.VMEM((PROMPT, 2 * HEAD), f32),
        ],
        compiler_params=params(56),
    )(reach, q, k, v, f, g)


def pick_kernel(index_ref, reach_ref, *refs):
    vectors, (wq_ref, wo_ref, wf_ref, wp_ref), (small_ref, piece_ref, shard_ref) = (
        refs[:8], refs[8:12], refs[12:],
    )
    index = index_ref[0]
    rows = []
    for ref in vectors:
        bank = ref[...].astype(f32)
        chosen = lax.broadcasted_iota(jnp.int32, bank.shape, 0) == index
        rows.append(jnp.sum(jnp.where(chosen, bank, 0.0), axis=0, keepdims=True))
    width = sum(row.shape[1] for row in rows)
    rest = small_ref.shape[1] - width
    small_ref[0:1, :] = jnp.concatenate(rows + [jnp.zeros((1, rest), f32)], axis=1).astype(bf16)
    reach = reach_ref[0, 0]
    lane = lax.broadcasted_iota(jnp.int32, (1, small_ref.shape[1]), 1)
    code = jnp.where(lane == 0, reach // 16, jnp.where(lane == 1, lax.rem(reach, 16), 0))
    small_ref[1:2, :] = code.astype(f32).astype(bf16)
    for j in range(GROUP):
        for part in range(3):
            at = part * D + j * SLICE
            piece_ref[j, :, part * SLICE : (part + 1) * SLICE] = wq_ref[0, :, at : at + SLICE]
    shard_ref[:192, :] = wp_ref[0]
    shard_ref[192:240, :] = wo_ref[0]
    for c in range(FF // D):
        shard_ref[240 + 48 * c : 288 + 48 * c, :] = wf_ref[0, :, c * D : (c + 1) * D]


def pick(index, reach, vectors, wq, wo, wf, wp):
    shape = jax.ShapeDtypeStruct
    chosen = lambda bank: pl.BlockSpec((1,) + bank.shape[1:], lambda i, at: (at[0], 0, 0))
    whole = lambda bank: pl.BlockSpec(bank.shape, lambda i, at: (0, 0))
    fixed3 = lambda i, at: (0, 0, 0)
    return pl.pallas_call(
        pick_kernel,
        name="pick",
        out_shape=(
            shape((2, 640), bf16), shape((GROUP, D // BLOCKS, WIDE), bf16), shape((UNIT, D), bf16),
        ),
        grid_spec=pltpu.PrefetchScalarGridSpec(
            num_scalar_prefetch=1,
            grid=(1,),
            in_specs=[pl.BlockSpec(memory_space=pltpu.SMEM)]
            + [whole(bank) for bank in vectors]
            + [chosen(bank) for bank in (wq, wo, wf, wp)],
            out_specs=(
                pl.BlockSpec((2, 640), lambda i, at: (0, 0)),
                pl.BlockSpec((GROUP, D // BLOCKS, WIDE), fixed3),
                pl.BlockSpec((UNIT, D), lambda i, at: (0, 0)),
            ),
        ),
        compiler_params=params(60),
    )(index, reach, *vectors, wq, wo, wf, wp)


def ring_of(me):
    chip, core = me // 2, lax.rem(me, 2)
    z, x = chip // 2, lax.rem(chip, 2)
    chips = BLOCKS // 2
    half = chips // 2
    place = z * (1 - x) + (chips - 1 - z) * x

    def device(at):
        at = lax.rem(at + 2 * chips, chips)
        side = at // half
        z_at = at * (1 - side) + (chips - 1 - at) * side
        return (z_at * 2 + side) * 2 + core

    return place, device


def forward_kernel(
    x_ref, sm_ref, pc_ref, sh_ref,
    wall_ref, smo_ref, wq_ref, a_ref, q_ref, k_ref, v_ref, f_ref, o_ref,
    xg, smg, wg, w_s, q_s, k_s, v_s, f_s, o_s,
    local, sm_send, sm_recv, w_send, w_recv, x_send, x_recv, r_send, r_recv, n_send, n_recv,
    y_send, y_recv, o_send, o_recv, out_sem,
):
    n = BLOCKS
    me = lax.axis_index("fsdp")
    rep = lax.axis_index("rep")
    pos = lax.rem(me, GROUP)
    base = me - pos
    near, far = me ^ 1, me ^ 2
    place, device = ring_of(me)
    parts = 4
    part_rows = TOK // parts
    T = CONT

    def remote(src, dst, send, recv, peer):
        return pltpu.make_async_remote_copy(
            src_ref=src,
            dst_ref=dst,
            send_sem=send,
            recv_sem=recv,
            device_id=peer if isinstance(peer, dict) else {"fsdp": peer},
            device_id_type=MESH,
        )

    greet([me ^ i for i in range(1, n)], 1 - rep)

    own_block = pltpu.make_async_copy(sh_ref, wall_ref.at[me], local.at[0])
    own_x = pltpu.make_async_copy(x_ref, xg.at[pos], local.at[1])
    own_w = pltpu.make_async_copy(pc_ref.at[pos], wg.at[me], local.at[2])
    own_s = pltpu.make_async_copy(sm_ref, smg.at[me], local.at[3])
    for copy in (own_s, own_w, own_x, own_block):
        copy.start()

    slices = []
    for i in range(1, GROUP):
        copy = remote(pc_ref.at[pos ^ i], wg.at[me], w_send.at[i], w_recv.at[i], me ^ i)
        copy.start()
        slices.append(copy)
    smalls = []
    for i in range(1, n):
        copy = remote(sm_ref, smg.at[me], sm_send.at[i], sm_recv.at[i], me ^ i)
        copy.start()
        smalls.append(copy)
    beside = remote(x_ref, xg.at[pos], x_send.at[2 * parts], x_recv.at[2 * parts], near)
    beside.start()

    def x_part(src, slot, part, i, peer):
        at = pl.ds(part * part_rows, part_rows)
        return remote(src.at[at], xg.at[slot, at], x_send.at[i], x_recv.at[i], peer)

    across = [x_part(x_ref, pos, part, part, far) for part in range(parts)]
    for copy in across:
        copy.start()

    mine = pl.ds(pl.multiple_of(rep * (D // 2), D // 2), D // 2)
    other = pl.ds(pl.multiple_of((1 - rep) * (D // 2), D // 2), D // 2)
    sides = lambda t: (True, False) if t < 3 else (True,)
    key = lambda t, right: t if right else 4 + t

    def came(t, right):
        return device(place - 1 - t if right else place + 1 + t)

    def hop(t, right):
        block = wall_ref.at[device(place - t if right else place + t), :, mine]
        src = sh_ref.at[:, mine] if t == 0 else block
        i = key(t, right)
        return remote(src, block, r_send.at[i], r_recv.at[i], device(place + 1 if right else place - 1))

    def to_near(t, right, columns, i):
        block = wall_ref.at[came(t, right), :, columns]
        return remote(block, block, n_send.at[i], n_recv.at[i], near)

    def to_replica(t, right):
        block = wall_ref.at[came(t, right), :, mine]
        i = key(t, right)
        return remote(block, block, y_send.at[i], y_recv.at[i], {"rep": 1 - rep})

    def from_replica(t, right):
        block = wall_ref.at[came(t, right), :, other]
        i = key(t, right)
        return remote(block, block, y_send.at[i], y_recv.at[i], {"rep": 1 - rep})

    hops, sent, shared = {}, [], []

    def begin(copy, keep):
        copy.start()
        keep.append(copy)

    def launch(t):
        for right in sides(t):
            hops[t, right] = hop(t, right)
            hops[t, right].start()

    def arrive(t):
        for right in sides(t):
            hops[t, right].wait_recv()
        if t < 3:
            launch(t + 1)
        for right in sides(t):
            begin(to_replica(t, right), sent)
            begin(to_near(t, right, mine, 1 + key(t, right)), shared)

    def settle(t):
        for right in sides(t):
            from_replica(t, right).wait_recv()
            begin(to_near(t, right, other, 8 + key(t, right)), shared)

    launch(0)
    begin(remote(sh_ref, wall_ref.at[me], n_send.at[0], n_recv.at[0], near), shared)

    own_s.wait()
    for copy in smalls:
        copy.wait_recv()
    rows48 = D // n
    gain = jnp.concatenate([smg[d, 0:1, 0:rows48] for d in range(n)], axis=1).astype(f32)
    shift = jnp.concatenate([smg[d, 0:1, rows48 : 2 * rows48] for d in range(n)], axis=1).astype(f32)
    at = 2 * rows48
    two = 2 * rows48
    zeros = jnp.zeros((1, SLICE), bf16)
    bias = jnp.concatenate(
        [smg[2 * pos + i, 0:1, at : at + two] for i in range(2)]
        + [zeros]
        + [smg[n // 2 + 2 * pos + i, 0:1, at : at + two] for i in range(2)],
        axis=1,
    ).astype(f32)

    def norm(slot):
        def some(i, carry):
            at = pl.ds(pl.multiple_of(i * PAIR, PAIR), PAIR)
            n_rows, _ = moments(xg[slot, at, :].astype(f32))
            xg[slot, at, :] = (n_rows * gain + shift).astype(bf16)
            return carry

        lax.fori_loop(0, 2, some, 0)

    def project_block(slot):
        def some(i, carry):
            at = pl.ds(pl.multiple_of(i * PAIR, PAIR), PAIR)
            out = pl.ds(pl.multiple_of(slot * TOK + i * PAIR, PAIR), PAIR)
            mixed = (dot(xg[slot, at, :], w_s[...]) + bias).astype(bf16)
            ones = jnp.ones((PAIR, HEAD), bf16)
            for h in range(OWN):
                q = mixed[:, h * HEAD : (h + 1) * HEAD] * 0.125
                k = mixed[:, SLICE + h * HEAD : SLICE + (h + 1) * HEAD]
                v = mixed[:, 2 * SLICE + h * HEAD : 2 * SLICE + (h + 1) * HEAD]
                q_s[h, out, :] = jnp.concatenate([q.astype(bf16), jnp.zeros_like(ones)], axis=1)
                k_s[h, out, :] = jnp.concatenate([k, ones], axis=1)
                v_s[h, out, :] = jnp.concatenate([ones, v], axis=1)
            return carry

        lax.fori_loop(0, 2, some, 0)

    own_w.wait()
    for copy in slices:
        copy.wait_recv()
    group = pl.ds(base, GROUP)
    wide = []
    for i in range(1, n // GROUP):
        begin(
            remote(wg.at[group], wg.at[group], w_send.at[GROUP + i], w_recv.at[GROUP + i], me ^ (GROUP * i)),
            wide,
        )
    own_x.wait()
    norm(pos)
    beside.wait()
    norm(pos ^ 1)
    for copy in wide:
        copy.wait_recv()
    arrive(0)
    w_s[...] = wg[:, :rows48, :].reshape(D, WIDE)
    project_block(pos)
    project_block(pos ^ 1)
    passed = []
    for part in range(parts):
        across[part].wait_recv()
        copy = x_part(xg.at[pos ^ 2], pos ^ 2, part, parts + part, near)
        copy.start()
        passed.append(copy)
    for copy in passed:
        copy.wait()
    norm(pos ^ 2)
    project_block(pos ^ 2)
    norm(pos ^ 3)
    project_block(pos ^ 3)
    arrive(1)

    outs = [
        pltpu.make_async_copy(smg, smo_ref, out_sem.at[0]),
        pltpu.make_async_copy(w_s, wq_ref, out_sem.at[1]),
        pltpu.make_async_copy(xg, a_ref, out_sem.at[2]),
        pltpu.make_async_copy(k_s, k_ref, out_sem.at[3]),
        pltpu.make_async_copy(v_s, v_ref, out_sem.at[4]),
    ]
    for copy in outs:
        copy.start()

    lane = lanes(T)
    causal = below(T, T, False)
    code = [smg[base + c, 1:2, 0:2].astype(f32) for c in range(GROUP)]
    reaches = [c[:, 0:1] * 16.0 + c[:, 1:2] for c in code]
    column = lax.broadcasted_iota(jnp.int32, (T, PROMPT), 1).astype(f32)

    for h in range(OWN):

        def tile(at, blocks):
            q = q_s[h, pl.ds(at, T), :]
            scores = []
            for start, size, mask in blocks:
                s = dot_nt(q, k_s[h, pl.ds(start, size), :])
                scores.append(s if mask is None else jnp.where(mask, s, NEG))
            peak = scores[0].max(axis=1, keepdims=True)
            for s in scores[1:]:
                peak = jnp.maximum(peak, s.max(axis=1, keepdims=True))
            total = jnp.zeros((T, 2 * HEAD), f32)
            for s, (start, size, _) in zip(scores, blocks):
                total += dot(jnp.exp(s - peak).astype(bf16), v_s[h, pl.ds(start, size), :])
            mass = total[:, 0:1]
            f_s[h, pl.ds(at, T), :] = total / mass
            lse = peak + jnp.log(mass)
            q_s[h, pl.ds(at, T), :] = split_columns(q.astype(f32), lane, lse)

        for p in range(GROUP):
            past = [(i * TOK, PROMPT, None) for i in range(p)]
            at = p * TOK
            tile(at, past + [(at, T, causal)])
            tile(at + T, past + [(at, T, None), (at + T, T, causal)])
        if h == 0:
            arrive(2)
        if h == 1:
            arrive(3)
            settle(0)
        if h == 2:
            settle(1)
        for c in range(GROUP):
            at = c * TOK + PROMPT
            blocks = [(i * TOK, PROMPT, column < reaches[c] - i * PROMPT) for i in range(GROUP)]
            tile(at, blocks + [(at, T, causal)])
        for p in range(GROUP):
            for left, right, size, to in PACK:
                top = f_s[h, p * TOK + left : p * TOK + left + size, :]
                low = f_s[h, p * TOK + right : p * TOK + right + size, :]
                pair = jnp.where(lanes(size) < HEAD, pltpu.roll(top, HEAD, 1), low)
                o_s[h, p, to : to + size, :] = pair.astype(bf16)
        for i in range(1, GROUP):
            copy = remote(
                o_s.at[h, pos ^ i], o_ref.at[pos, h], o_send.at[h, i], o_recv.at[h, i], me ^ i
            )
            copy.start()
            shared.append(copy)
        for src, dst, i in (
            (o_s.at[h, pos], o_ref.at[pos, h], 5 + h),
            (f_s.at[h], f_ref.at[h], 8 + h),
            (q_s.at[h], q_ref.at[h], 11 + h),
        ):
            copy = pltpu.make_async_copy(src, dst, out_sem.at[i])
            copy.start()
            outs.append(copy)

    settle(2)
    settle(3)
    for copy in across + smalls + slices + wide + list(hops.values()) + sent:
        copy.wait_send()
    own_block.wait()
    for copy in shared + outs:
        copy.wait()


def forward(x, small, pieces, shard):
    dma = pltpu.SemaphoreType.DMA
    n = BLOCKS
    shape = jax.ShapeDtypeStruct
    head = (OWN, ROWS, 2 * HEAD)
    return pl.pallas_call(
        forward_kernel,
        name="forward",
        out_shape=(
            shape((n, UNIT, D), bf16),
            shape((n,) + small.shape, bf16),
            shape((D, WIDE), bf16),
            shape((GROUP, TOK, D), bf16),
            shape(head, bf16),
            shape(head, bf16),
            shape(head, bf16),
            shape(head, f32),
            shape((GROUP, OWN, PAIR, 2 * HEAD), bf16),
        ),
        in_specs=[ANY] * 4,
        out_specs=(ANY,) * 9,
        scratch_shapes=[
            pltpu.VMEM((GROUP, TOK, D), bf16),
            pltpu.VMEM((n,) + small.shape, bf16),
            pltpu.VMEM((n,) + pieces.shape[1:], bf16),
            pltpu.VMEM((D, WIDE), bf16),
            pltpu.VMEM(head, bf16),
            pltpu.VMEM(head, bf16),
            pltpu.VMEM(head, bf16),
            pltpu.VMEM(head, f32),
            pltpu.VMEM((OWN, GROUP, PAIR, 2 * HEAD), bf16),
            dma((4,)),
            dma((n,)),
            dma((n,)),
            dma((2 * GROUP,)),
            dma((2 * GROUP,)),
            dma((9,)),
            dma((9,)),
            dma((7,)),
            dma((7,)),
            dma((15,)),
            dma((15,)),
            dma((7,)),
            dma((7,)),
            dma((OWN, GROUP)),
            dma((OWN, GROUP)),
            dma((14,)),
        ],
        compiler_params=params(60, collective_id=0, has_side_effects=True),
    )(x, small, pieces, shard)


def middle_kernel(
    x_ref, o_ref, dy_ref, wo_ref, wf_ref, wp_ref, line_ref,
    y_ref, dwf_ref, dwp_ref, dbf_ref, dwo_ref, dh_ref, do_ref, small_ref,
    o_s, h_s, b_s, bt_s, y_s, dn_s, row_s,
):
    step = pl.program_id(0)
    part = D // BLOCKS
    half = lanes(PAIR) < HEAD
    wf = wf_ref[...].reshape(D, CHUNK)
    wp = wp_ref[...].reshape(CHUNK, D)
    wo = wo_ref[...].reshape(D, D)

    @pl.when(step == 0)
    def _():
        for t in range(HEADS // 2):
            one = o_ref[2 * t // OWN, 2 * t % OWN].astype(f32)
            two = o_ref[(2 * t + 1) // OWN, (2 * t + 1) % OWN].astype(f32)
            at = slice(2 * t * HEAD, (2 * t + 2) * HEAD)
            first = jnp.where(half, one, pltpu.roll(two, HEAD, 1)).astype(bf16)
            second = jnp.where(half, pltpu.roll(one, HEAD, 1), two).astype(bf16)
            for left, right, size, to in PACK:
                o_s[left : left + size, at] = first[to : to + size]
                o_s[right : right + size, at] = second[to : to + size]
        for i, at in enumerate((4 * part, 5 * part, 6 * part, 11 * part)):
            pieces = [line_ref[d, 0:1, at : at + part] for d in range(BLOCKS)]
            row_s[i : i + 1, :] = jnp.concatenate(pieces, axis=1).astype(f32)
        h = x_ref[...].astype(f32) + dot(o_s[...], wo) + row_s[0:1, :]
        h_s[...] = h
        n, _ = moments(h)
        b_low = (n * row_s[1:2, :] + row_s[2:3, :]).astype(bf16)
        b_s[...] = b_low
        bt_s[...] = b_low.T
        y_s[...] = jnp.zeros_like(y_s)
        dn_s[...] = jnp.zeros_like(dn_s)

    dy = dy_ref[...]
    pieces = [line_ref[4 * step + i, 0:1, 7 * part : 11 * part] for i in range(4)]
    u = dot(b_s[...], wf) + jnp.concatenate(pieces, axis=1).astype(f32)
    square = u * u
    t = jnp.tanh(GELU_A * (u + GELU_B * (square * u)))
    m_low = (0.5 * u * (1.0 + t)).astype(bf16)
    slope = 0.5 * (1.0 + t) + 0.5 * u * (1.0 - t * t) * (GELU_A * (1.0 + 3.0 * GELU_B * square))
    y_s[...] += dot(m_low, wp)
    du = (dot_nt(dy, wp) * slope).astype(bf16)
    dbf_ref[...] = jnp.sum(du.astype(f32), axis=0, keepdims=True)
    dn_s[...] += dot_nt(du, wf)
    dwf_ref[...] = dot(bt_s[...], du).astype(bf16).reshape(dwf_ref.shape)
    dwp_ref[...] = dot_tn(m_low, dy).astype(bf16)

    @pl.when(step == pl.num_programs(0) - 1)
    def _():
        h = h_s[...]
        y_ref[...] = (h + y_s[...] + row_s[3:4, :]).astype(bf16)
        n, r = moments(h)
        dn = dn_s[...]
        grad = dy_ref[...].astype(f32)
        small_ref[...] = jnp.zeros_like(small_ref)
        small_ref[0:1, :] = jnp.sum(grad, axis=0, keepdims=True)
        small_ref[1:2, :] = jnp.sum(dn * n, axis=0, keepdims=True)
        small_ref[2:3, :] = jnp.sum(dn, axis=0, keepdims=True)
        e = dn * row_s[1:2, :]
        lean = jnp.mean(e, axis=-1, keepdims=True) + n * jnp.mean(e * n, axis=-1, keepdims=True)
        dh = grad + r * (e - lean)
        dh_ref[...] = dh
        dh_low = dh.astype(bf16)
        small_ref[3:4, :] = jnp.sum(dh_low.astype(f32), axis=0, keepdims=True)
        dwo_ref[...] = dot_tn(o_s[...], dh_low).astype(bf16)
        h_s[...] = dot_nt(dh_low, wo)
        for t in range(HEADS // 2):
            at = slice(2 * t * HEAD, (2 * t + 2) * HEAD)
            for left, right, size, to in PACK:
                top, low = h_s[left : left + size, at], h_s[right : right + size, at]
                side = lanes(size) < HEAD
                one = jnp.where(side, top, pltpu.roll(low, HEAD, 1))
                two = jnp.where(side, pltpu.roll(top, HEAD, 1), low)
                do_ref[2 * t // OWN, 2 * t % OWN, to : to + size] = one.astype(bf16)
                do_ref[(2 * t + 1) // OWN, (2 * t + 1) % OWN, to : to + size] = two.astype(bf16)


def middle(x, o, dy, wall, lines):
    fixed2 = lambda i: (0, 0)
    fixed4 = lambda i: (0, 0, 0, 0)
    square = pl.BlockSpec((TOK, D), fixed2)
    heads = pl.BlockSpec((GROUP, OWN, PAIR, 2 * HEAD), fixed4)
    columns = pl.BlockSpec((BLOCKS, 1, D // BLOCKS, D), lambda i: (0, i, 0, 0))
    down = pl.BlockSpec((CHUNK, D), lambda i: (i, 0))
    line = pl.BlockSpec((1, CHUNK), lambda i: (0, i))
    shape = jax.ShapeDtypeStruct
    return pl.pallas_call(
        middle_kernel,
        name="middle",
        grid=(FF // CHUNK,),
        out_shape=(
            shape((TOK, D), bf16),
            shape((BLOCKS, FF // D, D // BLOCKS, D), bf16),
            shape((FF, D), bf16),
            shape((1, FF), f32),
            shape((D, D), bf16),
            shape((TOK, D), f32),
            shape((GROUP, OWN, PAIR, 2 * HEAD), bf16),
            shape((8, D), f32),
        ),
        in_specs=[
            square, heads, square,
            pl.BlockSpec((BLOCKS, 48, D), lambda i: (0, 4, 0)),
            pl.BlockSpec((BLOCKS, 48, D), lambda i: (0, 5 + i, 0)),
            pl.BlockSpec((BLOCKS // 4, 192, D), lambda i: (i, 0, 0)),
            pl.BlockSpec(lines.shape, lambda i: (0, 0, 0)),
        ],
        out_specs=(
            square, columns, down, line, square, square, heads, pl.BlockSpec((8, D), fixed2),
        ),
        scratch_shapes=[
            pltpu.VMEM((TOK, D), bf16),
            pltpu.VMEM((TOK, D), f32),
            pltpu.VMEM((TOK, D), bf16),
            pltpu.VMEM((D, TOK), bf16),
            pltpu.VMEM((TOK, D), f32),
            pltpu.VMEM((TOK, D), f32),
            pltpu.VMEM((8, D), f32),
        ],
        compiler_params=params(60),
    )(x, o, dy, wall, wall, wall, lines)


ORDER = (4, -3, 3, -2, 2, -1, 1, 0)
SMALL = 16


def backward_kernel(
    do_ref, q_ref, k_ref, v_ref, f_ref, a_ref, w_ref, x_ref, dh_ref, lines_ref, sums_ref, dbf_ref,
    dwp_ref, dwo_ref, dwf_ref,
    grad_ref, gq_ref, gp_ref, go_ref, gf_ref, small_ref,
    g_b, q_s, k_s, v_s, f_b, a_b, w_s, x_s, dh_s, lines_s, sums_s, dbf_s,
    near_b, mine_b, y_b, ring_b, fin_b, fin_r, fin_o,
    g_s, dq_s, kt_s, dkv_s, dm_s, w_h, dw_s, db_s,
    dw_b, z_b, j_b, j_r, rep_r, gq_o,
    dn_a, dn_b, dn_c, dn_ra, dn_rb, dn_rc, sm_b, sm_r,
    load, f_sem, a_sem, mine_sem, g_send, g_recv, n_send, n_recv, y_send, y_recv, r_send, r_recv, fin_send,
    fin_recv, z_send, z_recv, j_send, j_recv, rep_send, rep_recv, d_send, d_recv, s_send, s_recv, out_sem,
):
    n = BLOCKS
    me = lax.axis_index("fsdp")
    rep = lax.axis_index("rep")
    pos = lax.rem(me, GROUP)
    base = me - pos
    level = me // GROUP
    near, far = me ^ 1, me ^ 2
    place, device = ring_of(me)
    T = CONT
    W3 = 3 * HEAD
    other = {"rep": 1 - rep}

    def remote(src, dst, send, recv, peer):
        return pltpu.make_async_remote_copy(
            src_ref=src,
            dst_ref=dst,
            send_sem=send,
            recv_sem=recv,
            device_id=peer if isinstance(peer, dict) else {"fsdp": peer},
            device_id_type=MESH,
        )

    greet([me ^ i for i in range(1, n)], 1 - rep)

    def do_copy(kind, i):
        at = pl.ds(*((0, 128), (128, 256))[kind])
        src, dst = do_ref.at[pos ^ i, :, at], g_b.at[pos, :, at]
        return remote(src, dst, g_send.at[kind, i], g_recv.at[kind, i], me ^ i)

    own_do = pltpu.make_async_copy(do_ref.at[pos], g_b.at[pos], load.at[0])
    own_do.start()
    for i in range(1, GROUP):
        do_copy(0, i).start()

    stages = (
        tuple((c * TOK + PROMPT, CONT) for c in range(GROUP)),
        ((3 * TOK, PROMPT),),
        ((0, PROMPT),),
        ((TOK, PROMPT), (2 * TOK, PROMPT)),
    )
    loads = (stages[0], ((3 * TOK, PROMPT), (2 * TOK, PROMPT)), ((0, PROMPT), (TOK, PROMPT)))

    def f_copies(part):
        at, found = 0, []
        for i, (row, size) in enumerate(loads[part]):
            src, dst = f_ref.at[:, pl.ds(row, size)], f_b.at[:, pl.ds(at, size)]
            found.append(pltpu.make_async_copy(src, dst, f_sem.at[part, i]))
            at += size
        return found

    def a_copies(stage):
        at, found = 0, []
        for i, (row, size) in enumerate(stages[stage]):
            src, dst = a_ref.at[pl.ds(row, size)], a_b.at[pl.ds(at, size)]
            found.append(pltpu.make_async_copy(src, dst, a_sem.at[stage, i]))
            at += size
        return found

    first = [
        pltpu.make_async_copy(src, dst, load.at[1 + i])
        for i, (src, dst) in enumerate(
            ((k_ref, k_s), (v_ref, v_s), (q_ref, q_s), (lines_ref, lines_s), (w_ref, w_s))
        )
    ]
    later = [
        pltpu.make_async_copy(src, dst, load.at[6 + i])
        for i, (src, dst) in enumerate(
            ((x_ref, x_s), (dh_ref, dh_s), (sums_ref, sums_s), (dbf_ref, dbf_s))
        )
    ]
    for copy in f_copies(0) + first:
        copy.start()

    cut = ((0, 192), (192, 48), (240, 192))

    def near_copies(i):
        d = device(place + ORDER[i]) ^ 1
        return [
            remote(ref.at[d], near_b.at[i, pl.ds(at, size)], n_send.at[i, k], n_recv.at[i, k], near)
            for k, (ref, (at, size)) in enumerate(zip((dwp_ref, dwo_ref, dwf_ref), cut))
        ]

    def mine_copies(i):
        d = device(place + ORDER[i])
        return [
            pltpu.make_async_copy(ref.at[d], mine_b.at[i % 4, pl.ds(at, size)], mine_sem.at[i, k])
            for k, (ref, (at, size)) in enumerate(zip((dwp_ref, dwo_ref, dwf_ref), cut))
        ]

    for i in range(2):
        for copy in near_copies(i) + mine_copies(i):
            copy.start()
    for i in range(1, GROUP):
        do_copy(1, i).start()
    for i in range(2, 8):
        for copy in near_copies(i):
            copy.start()
    for copy in a_copies(0) + mine_copies(2) + mine_copies(3) + later:
        copy.start()

    def ready(i):
        for copy in near_copies(i):
            copy.wait_recv()
        for copy in mine_copies(i):
            copy.wait()

    mine = pl.ds(pl.multiple_of(rep * (D // 2), D // 2), D // 2)
    rest = pl.ds(pl.multiple_of((1 - rep) * (D // 2), D // 2), D // 2)

    def rounds(some):
        def chunk(c, carry):
            some(pl.ds(pl.multiple_of(c * 144, 144), 144))
            return carry

        lax.fori_loop(0, UNIT // 144, chunk, 0)

    def y_copy(i):
        return remote(near_b.at[i, :, rest], y_b.at[i], y_send.at[i], y_recv.at[i], other)

    def chip_sum(i):
        ready(i)

        def some(at):
            total = near_b[i, at, :].astype(f32) + mine_b[i % 4, at, :].astype(f32)
            near_b[i, at, :] = total.astype(bf16)

        rounds(some)
        y_copy(i).start()
        if i + 4 < 8:
            for copy in mine_copies(i + 4):
                copy.start()

    def ring_copy(t, right):
        i = 2 * t if right else 2 * t + 1
        slot = t if right else 4 + t
        peer = device(place + 1 if right else place - 1)
        return remote(near_b.at[i, :, mine], ring_b.at[slot], r_send.at[slot], r_recv.at[slot], peer)

    def ring_step(t):
        for right in (True, False) if t < 3 else (True,):
            i = 2 * t if right else 2 * t + 1
            y_copy(i).wait_recv()
            if t > 0:
                ring_copy(t - 1, right).wait_recv()
            slot = (t if right else 4 + t) - 1

            def some(at):
                total = near_b[i, at, mine].astype(f32) + y_b[i, at, :].astype(f32)
                if t > 0:
                    total = total + ring_b[slot, at, :].astype(f32)
                near_b[i, at, mine] = total.astype(bf16)

            rounds(some)
            ring_copy(t, right).start()

    fin_copy = remote(fin_b, fin_r, fin_send, fin_recv, other)

    def ring_end():
        y_copy(7).wait_recv()
        ring_copy(3, True).wait_recv()
        ring_copy(2, False).wait_recv()

        def some(at):
            total = near_b[7, at, mine].astype(f32) + y_b[7, at, :].astype(f32)
            fin_b[at, :] = (total + ring_b[3, at, :].astype(f32) + ring_b[6, at, :].astype(f32)).astype(bf16)

        rounds(some)
        fin_copy.start()

    def z_copy(h, i):
        return remote(
            dw_b.at[h, level ^ i], z_b.at[h, i], z_send.at[h, i], z_recv.at[h, i], me ^ (GROUP * i)
        )

    def j_copy(h, i):
        return remote(j_b.at[h, pos ^ i], j_r.at[h, pos], j_send.at[h, i], j_recv.at[h, i], me ^ i)

    def gather_rows(h):
        for i in range(1, GROUP):
            z_copy(h, i).wait_recv()
        total = dw_b[h, level].astype(f32)
        for i in range(1, GROUP):
            total = total + z_b[h, i].astype(f32)
        j_b[h] = total.astype(bf16).reshape(GROUP, D // n, W3)
        j_r[h, pos] = j_b[h, pos]
        for i in range(1, GROUP):
            j_copy(h, i).start()

    def rep_copy(h):
        return remote(j_r.at[h], rep_r.at[h], rep_send.at[h], rep_recv.at[h], other)

    def trade_rows(h):
        for i in range(1, GROUP):
            j_copy(h, i).wait_recv()
        rep_copy(h).start()

    causal = below(T, T, True)
    key_row = lax.broadcasted_iota(jnp.int32, (PROMPT, T), 0).astype(f32)

    def prepare(part, h):
        at = 0
        for row, size in loads[part]:
            p = row // TOK
            left, right, count, to = PACK[0 if size == CONT else 1]
            packed = g_b[p, h, to : to + count, :].astype(f32)
            lane = lanes(count)
            for start, block in ((left, pltpu.roll(packed, HEAD, 1)), (right, packed)):
                off = at + start - (row - p * TOK)
                prod = jnp.where(lane >= HEAD, block * f_b[h, off : off + count, :], 0.0)
                inner = jnp.sum(prod, axis=1, keepdims=True)
                hi = inner.astype(bf16).astype(f32)
                mid = (inner - hi).astype(bf16).astype(f32)
                low = inner - hi - mid
                tail = jnp.where(lane == 0, -hi, jnp.where(lane == 1, -mid, -low))
                value = jnp.where(lane >= HEAD, block, jnp.where(lane < 3, tail, 0.0))
                g_s[h, p * TOK + start : p * TOK + start + count, :] = value.astype(bf16)
            at += size

    def block(h, keys, size, rows, count, mask, target):
        kb = k_s[h, pl.ds(keys, size), :]
        vb = v_s[h, pl.ds(keys, size), :]
        q = q_s[h, pl.ds(rows, count), :]
        g = g_s[h, pl.ds(rows, count), :]
        probs = jnp.exp(dot_nt(kb, q))
        if mask is not None:
            probs = jnp.where(mask, probs, 0.0)
        ds = (probs * dot_nt(vb, g)).astype(bf16)
        lane = lanes(count)
        none = jnp.zeros_like(q)
        pair = dot(ds, jnp.where(lane < HEAD, q, none))
        pair = pair + dot(probs.astype(bf16), jnp.where(lane < HEAD, none, g))
        dq_s[h, :, pl.ds(rows, count)] += dot(kt_s[h, :, pl.ds(keys, size)], ds)
        if target is None:
            return pair
        dkv_s[h, pl.ds(target, size), :] += pair

    def diagonal(h, p):
        row, at = p * TOK, p * PROMPT
        block(h, row, T, row, T, causal, at)
        block(h, row, T, row + T, T, None, at)
        block(h, row + T, T, row + T, T, causal, at + T)

    def flush_q(h, row, size):
        at = pl.ds(row, size)
        dm_s[h, at, 2 * HEAD :] = (dq_s[h, :, at].T * 0.125).astype(bf16)

    def flush(h, p):
        dm_s[h, p * TOK : p * TOK + PROMPT, : 2 * HEAD] = dkv_s[
            h, p * PROMPT : (p + 1) * PROMPT, :
        ].astype(bf16)
        flush_q(h, p * TOK, PROMPT)

    def add_weight(stage, h):
        at = 0
        total = jnp.zeros((W3, D), f32)
        for row, size in stages[stage]:
            total = total + dot_tn(dm_s[h, row : row + size, :], a_b[at : at + size, :])
            at += size
        if stage == 0:
            dw_s[h] = total
        else:
            dw_s[h] += total

    def dn_rows(owner, seg):
        rows = pl.ds(pl.multiple_of(owner * TOK + seg * T, T), T)
        total = dot_nt(dm_s[0, rows, :], w_h[0])
        for h in range(1, OWN):
            total = total + dot_nt(dm_s[h, rows, :], w_h[h])
        return total

    def dn_copy(kind, seg):
        at = pl.ds(seg * T, T)
        src, dst, peer = ((dn_a, dn_ra, near), (dn_b, dn_rb, far), (dn_c, dn_rc, near))[kind]
        return remote(src.at[at], dst.at[at], d_send.at[kind, seg], d_recv.at[kind, seg], peer)

    def put(kind, seg):
        at = slice(seg * T, (seg + 1) * T)
        rows = dn_rows(pos ^ (3, 2, 1)[kind], seg)
        if kind == 1:
            dn_copy(0, seg).wait_recv()
            rows = rows + dn_ra[at, :].astype(f32)
        (dn_a, dn_b, dn_c)[kind][at, :] = rows.astype(bf16)
        dn_copy(kind, seg).start()

    def put_prompt(p, kinds):
        for kind in kinds:

            @pl.when((pos ^ (3, 2, 1)[kind]) == p)
            def _():
                for seg in range(2):
                    put(kind, seg)

    first[3].wait()
    first[4].wait()
    for h in range(OWN):
        w_h[h] = jnp.concatenate(
            [w_s[:, part * SLICE + h * HEAD : part * SLICE + (h + 1) * HEAD] for part in (1, 2, 0)],
            axis=1,
        )
    dq_s[...] = jnp.zeros_like(dq_s)
    dkv_s[...] = jnp.zeros_like(dkv_s)
    for copy in first[:3]:
        copy.wait()

    def turn(h, carry):
        for p in range(GROUP):
            kt_s[h, :, p * TOK : (p + 1) * TOK] = k_s[h, p * TOK : (p + 1) * TOK, :].T[:HEAD]
        return carry

    lax.fori_loop(0, OWN, turn, 0)
    own_do.wait()
    for i in range(1, GROUP):
        do_copy(0, i).wait_recv()
    for copy in f_copies(0):
        copy.wait()
    chip_sum(0)
    chip_sum(1)

    def stage_cont(h, carry):
        prepare(0, h)

        def cont(c, carry):
            rows = pl.multiple_of(c * TOK + PROMPT, CONT)
            code = lines_s[base + c, 1:2, 0:128].astype(f32)
            reach = code[:, 0:1] * 16.0 + code[:, 1:2]
            for p in range(GROUP):
                block(h, p * TOK, PROMPT, rows, T, key_row < reach - p * PROMPT, p * PROMPT)
            pair = block(h, rows, T, rows, T, causal, None)
            dm_s[h, pl.ds(rows, T), : 2 * HEAD] = pair.astype(bf16)
            flush_q(h, rows, T)
            return carry

        lax.fori_loop(0, GROUP, cont, 0)

        for k in range(OWN):

            @pl.when(h == k)
            def _():
                chip_sum(2 + 2 * k)
                chip_sum(3 + 2 * k)

        return carry

    lax.fori_loop(0, OWN, stage_cont, 0)
    ring_step(0)
    for copy in f_copies(1):
        copy.start()
    for copy in a_copies(0):
        copy.wait()
    for kind in (0, 2, 1):
        put(kind, 2)
    lax.fori_loop(0, OWN, lambda h, carry: (add_weight(0, h), carry)[1], 0)
    for copy in a_copies(1):
        copy.start()
    for i in range(1, GROUP):
        do_copy(1, i).wait_recv()
    for copy in f_copies(1):
        copy.wait()

    def stage_last(h, carry):
        prepare(1, h)
        for p in range(3):
            block(h, p * TOK, PROMPT, 3 * TOK, PROMPT, None, p * PROMPT)
        diagonal(h, 3)
        flush(h, 3)

        @pl.when(h == 1)
        def _():
            ring_step(1)

        return carry

    lax.fori_loop(0, OWN, stage_last, 0)
    for copy in f_copies(2):
        copy.start()
    for copy in a_copies(1):
        copy.wait()
    put_prompt(3, (0, 2))
    lax.fori_loop(0, OWN, lambda h, carry: (add_weight(1, h), carry)[1], 0)
    for copy in a_copies(2):
        copy.start()
    put_prompt(3, (1,))
    for copy in f_copies(2):
        copy.wait()

    def stage_first(h, carry):
        prepare(2, h)
        diagonal(h, 0)
        for p in range(1, 3):
            block(h, 0, PROMPT, p * TOK, PROMPT, None, 0)
        flush(h, 0)

        @pl.when(h == 1)
        def _():
            ring_step(2)

        return carry

    lax.fori_loop(0, OWN, stage_first, 0)
    for copy in a_copies(2):
        copy.wait()
    put_prompt(0, (0, 2))
    lax.fori_loop(0, OWN, lambda h, carry: (add_weight(2, h), carry)[1], 0)
    for copy in a_copies(3):
        copy.start()
    put_prompt(0, (1,))
    for copy in a_copies(3):
        copy.wait()

    def stage_middle(h, carry):
        block(h, TOK, PROMPT, 2 * TOK, PROMPT, None, PROMPT)
        diagonal(h, 1)
        flush(h, 1)
        diagonal(h, 2)
        flush(h, 2)
        add_weight(3, h)
        dw = dw_s[h].T
        dw_b[h] = dw.astype(bf16).reshape(GROUP, D // GROUP, W3)
        for i in range(1, GROUP):
            z_copy(h, i).start()
        db = jnp.zeros((1, W3), f32)
        for i in range(GROUP):
            db = db + jnp.sum(dm_s[h, i * TOK : (i + 1) * TOK, :].astype(f32), axis=0, keepdims=True)
        hi = db.astype(bf16)
        mid = (db - hi.astype(f32)).astype(bf16)
        low = (db - hi.astype(f32) - mid.astype(f32)).astype(bf16)
        split = jnp.concatenate([hi, mid, low, jnp.zeros((13, W3), bf16)], axis=0)
        ones = jnp.ones((8, W3), f32)
        gain_rows = lax.dot_general(
            ones,
            w_h[h].astype(f32) * dw,
            (((1,), (1,)), ((), ())),
            precision=lax.Precision.HIGHEST,
            preferred_element_type=f32,
        )
        db_s[h, 0:1, :W3] = db
        db_s[h, 1:2, W3 : W3 + D] = jnp.sum(dot_nt(split, w_h[h]), axis=0, keepdims=True)
        db_s[h, 2:3, W3 : W3 + D] = gain_rows[0:1]

        @pl.when(h == 0)
        def _():
            ring_step(3)

        return carry

    lax.fori_loop(0, OWN, stage_middle, 0)
    inner = lax.rem(pos + 1, GROUP) // 2

    def put_last(kind, side):
        @pl.when(inner == side)
        def _():
            for seg in range(2):
                put(kind, seg)

    put_last(2, 0)
    put_last(0, 1)
    gather_rows(0)
    put_last(1, 0)
    ring_end()
    for copy in later:
        copy.wait()

    rows48 = D // n
    gain = jnp.concatenate([lines_s[d, 0:1, 0:rows48] for d in range(n)], axis=1).astype(f32)
    shift = jnp.concatenate([lines_s[d, 0:1, rows48 : 2 * rows48] for d in range(n)], axis=1).astype(f32)
    d_shift = db_s[0, 1:2, W3 : W3 + D] + db_s[1, 1:2, W3 : W3 + D] + db_s[2, 1:2, W3 : W3 + D]
    d_gain = db_s[0, 2:3, W3 : W3 + D] + db_s[1, 2:3, W3 : W3 + D] + db_s[2, 2:3, W3 : W3 + D]
    blank = jnp.zeros((1, D - SLICE), f32)

    def biases(lo):
        row = jnp.concatenate([db_s[h, 0:1, lo : lo + HEAD] for h in range(OWN)] + [blank], axis=1)
        return pltpu.roll(jnp.broadcast_to(row, (8, D)), pos * SLICE, 1)[0:1]

    sm_b[0] = jnp.concatenate(
        [
            (d_gain - shift * d_shift) / gain,
            d_shift,
            biases(2 * HEAD),
            biases(HEAD),
            sums_s[3:4, :],
            sums_s[1:2, :],
            sums_s[2:3, :],
            sums_s[0:1, :],
        ]
        + [dbf_s[0:1, c * D : (c + 1) * D] for c in range(FF // D)]
        + [jnp.zeros((SMALL - 12, D), f32)],
        axis=0,
    )
    peers = [me ^ 1, me ^ 2, me ^ 4, me ^ 8, other]

    def small_copy(i):
        return remote(sm_b.at[i], sm_r.at[i], s_send.at[i], s_recv.at[i], peers[i])

    def small_step(i):
        small_copy(i).wait_recv()
        sm_b[i + 1] = sm_b[i] + sm_r[i]
        if i < 4:
            small_copy(i + 1).start()

    small_copy(0).start()

    outs = []

    def finish_rows(seg):
        at = slice(seg * T, (seg + 1) * T)
        rows = dn_rows(pos, seg)
        dn_copy(2, seg).wait_recv()
        dn_copy(1, seg).wait_recv()
        n_rows, r = moments(x_s[at, :].astype(f32))
        e = (rows + dn_rb[at, :].astype(f32) + dn_rc[at, :].astype(f32)) * gain
        lean = jnp.mean(e, axis=-1, keepdims=True) + n_rows * jnp.mean(e * n_rows, axis=-1, keepdims=True)
        dh_s[at, :] = dh_s[at, :] + r * (e - lean)
        copy = pltpu.make_async_copy(dh_s.at[at], grad_ref.at[at], out_sem.at[10 + seg])
        copy.start()
        outs.append(copy)

    finish_rows(2)
    gather_rows(1)
    small_step(0)
    trade_rows(0)
    small_step(1)
    gather_rows(2)
    trade_rows(1)
    small_step(2)
    finish_rows(0)
    finish_rows(1)
    trade_rows(2)
    small_step(3)

    small_step(4)
    total = sm_b[5]
    turned = pltpu.roll(total, lax.rem(n - me, n) * rows48, 1)
    eighth = lax.rem(me, 8)
    biased = pltpu.roll(total, lax.rem(8 - eighth, 8) * (2 * rows48), 1)
    quarter = lax.rem(me, 4)
    wide = pltpu.roll(total, lax.rem(4 - quarter, 4) * (4 * rows48), 1)
    row = lax.broadcasted_iota(jnp.int32, (SMALL, D), 0)
    bias_row = jnp.sum(jnp.where(row == 2 + me // 8, biased, 0.0), axis=0, keepdims=True)
    wide_row = jnp.sum(jnp.where(row == 8 + me // 4, wide, 0.0), axis=0, keepdims=True)
    small_copy(0).wait_send()
    sm_b[0] = jnp.where(row == 2, bias_row, jnp.where(row == 3, wide_row, turned))
    copy = pltpu.make_async_copy(sm_b.at[0], small_ref, out_sem.at[2])
    copy.start()
    outs.append(copy)

    for h in range(OWN):
        rep_copy(h).wait_recv()
    for part, (at, piece) in enumerate(((2 * HEAD, 0), (0, 1), (HEAD, 2))):
        row = jnp.concatenate(
            [
                j_r[h, j, :, at : at + HEAD].astype(f32) + rep_r[h, j, :, at : at + HEAD].astype(f32)
                for j in range(GROUP)
                for h in range(OWN)
            ],
            axis=1,
        )
        gq_o[:, piece * D : (piece + 1) * D] = row
    copy = pltpu.make_async_copy(gq_o, gq_ref, out_sem.at[3])
    copy.start()
    outs.append(copy)

    fin_copy.wait_recv()

    def some(at):
        fin_o[at, mine] = fin_b[at, :].astype(f32)
        fin_o[at, rest] = fin_r[at, :].astype(f32)

    rounds(some)
    targets = [(gp_ref, 0, 192), (go_ref, 192, 48)]
    targets += [(gf_ref.at[:, pl.ds(c * D, D)], 240 + 48 * c, 48) for c in range(FF // D)]
    for i, (ref, at, size) in enumerate(targets):
        copy = pltpu.make_async_copy(fin_o.at[pl.ds(at, size)], ref, out_sem.at[4 + i])
        copy.start()
        outs.append(copy)

    for h in range(OWN):
        for i in range(1, GROUP):
            for copy in (z_copy(h, i), j_copy(h, i)):
                copy.wait_send()
    for kind in range(2):
        for i in range(1, GROUP):
            do_copy(kind, i).wait_send()
    for i in range(8):
        y_copy(i).wait_send()
        for copy in near_copies(i):
            copy.wait_send()
    for t in range(4):
        for right in (True, False) if t < 3 else (True,):
            ring_copy(t, right).wait_send()
    for kind in range(3):
        for seg in range(3):
            dn_copy(kind, seg).wait_send()
    for i in range(1, 5):
        small_copy(i).wait_send()
    for h in range(OWN):
        rep_copy(h).wait_send()
    fin_copy.wait_send()
    for copy in outs:
        copy.wait()


def backward(do, q, k, v, f, a, w, x, dh, lines, sums, dbf, dwp, dwo, dwf):
    dma = pltpu.SemaphoreType.DMA
    n = BLOCKS
    shape = jax.ShapeDtypeStruct
    vmem = pltpu.VMEM
    rows = D // n
    head = (OWN, ROWS, 2 * HEAD)
    W3 = 3 * HEAD
    pairs = (OWN, GROUP)
    return pl.pallas_call(
        backward_kernel,
        name="backward",
        out_shape=(
            shape((TOK, D), f32),
            shape((rows, 3 * D), f32),
            shape((FF // n, D), f32),
            shape((rows, D), f32),
            shape((rows, FF), f32),
            shape((SMALL, D), f32),
        ),
        in_specs=[ANY] * 15,
        out_specs=(ANY,) * 6,
        scratch_shapes=[
            vmem((GROUP, OWN, PAIR, 2 * HEAD), bf16),
            vmem(head, bf16),
            vmem(head, bf16),
            vmem(head, bf16),
            vmem((OWN, GROUP * CONT, 2 * HEAD), f32),
            vmem((GROUP * CONT, D), bf16),
            vmem((D, WIDE), bf16),
            vmem((TOK, D), bf16),
            vmem((TOK, D), f32),
            vmem(lines.shape, bf16),
            vmem(sums.shape, f32),
            vmem(dbf.shape, f32),
            vmem((8, UNIT, D), bf16),
            vmem((4, UNIT, D), bf16),
            vmem((8, UNIT, D // 2), bf16),
            vmem((7, UNIT, D // 2), bf16),
            vmem((UNIT, D // 2), bf16),
            vmem((UNIT, D // 2), bf16),
            vmem((UNIT, D), f32),
            vmem(head, bf16),
            vmem((OWN, HEAD, ROWS), f32),
            vmem((OWN, HEAD, ROWS), bf16),
            vmem((OWN, GROUP * PROMPT, 2 * HEAD), f32),
            vmem((OWN, ROWS, W3), bf16),
            vmem((OWN, D, W3), bf16),
            vmem((OWN, W3, D), f32),
            vmem((OWN, 8, W3 + D), f32),
            vmem((OWN, GROUP, D // GROUP, W3), bf16),
            vmem((OWN, GROUP, D // GROUP, W3), bf16),
            vmem((OWN, GROUP, rows, W3), bf16),
            vmem((OWN, GROUP, rows, W3), bf16),
            vmem((OWN, GROUP, rows, W3), bf16),
            vmem((rows, 3 * D), f32),
            vmem((TOK, D), bf16),
            vmem((TOK, D), bf16),
            vmem((TOK, D), bf16),
            vmem((TOK, D), bf16),
            vmem((TOK, D), bf16),
            vmem((TOK, D), bf16),
            vmem((6, SMALL, D), f32),
            vmem((5, SMALL, D), f32),
            dma((10,)),
            dma((3, GROUP)),
            dma((4, GROUP)),
            dma((8, 3)),
            dma((2, GROUP)),
            dma((2, GROUP)),
            dma((8, 3)),
            dma((8, 3)),
            dma((8,)),
            dma((8,)),
            dma((7,)),
            dma((7,)),
            dma,
            dma,
            dma(pairs),
            dma(pairs),
            dma(pairs),
            dma(pairs),
            dma((OWN,)),
            dma((OWN,)),
            dma((3, 3)),
            dma((3, 3)),
            dma((5,)),
            dma((5,)),
            dma((13,)),
        ],
        compiler_params=params(63, collective_id=4, has_side_effects=True),
    )(do, q, k, v, f, a, w, x, dh, lines, sums, dbf, dwp, dwo, dwf)


def land_kernel(sums_ref, *refs):
    sources, targets, rows, held, sem = refs[:5], refs[5:10], refs[10:18], refs[18:23], refs[23]
    parts = []
    for i, ref in enumerate(held):
        count = 4 if i == 0 else 1
        size = ref.shape[0] // count
        parts += [(i, pl.ds(k * size, size)) for k in range(count)]

    def inward(k):
        i, at = parts[k]
        return pltpu.make_async_copy(sources[i].at[at], held[i].at[at], sem.at[0, k])

    def outward(k):
        i, at = parts[k]
        return pltpu.make_async_copy(held[i].at[at], targets[i].at[at], sem.at[1, k])

    for k in range(len(parts)):
        inward(k).start()
    for i, ref in zip((0, 1, 2, 4, 5, 6, 3, 7), rows):
        ref[...] = sums_ref[i, : ref.shape[0]]
    for k in range(len(parts)):
        inward(k).wait()
        outward(k).start()
    for k in range(len(parts)):
        outward(k).wait()


def land(sums, matrices):
    part = D // BLOCKS
    shape = jax.ShapeDtypeStruct
    vector = pl.BlockSpec(memory_space=pltpu.VMEM)
    return pl.pallas_call(
        land_kernel,
        name="land",
        out_shape=tuple(shape(m.shape, f32) for m in matrices)
        + tuple(shape((k * part,), f32) for k in (1, 1, 2, 1, 1, 1, 4, 1)),
        in_specs=[vector] + [ANY] * 5,
        out_specs=(ANY,) * 5 + (vector,) * 8,
        scratch_shapes=[pltpu.VMEM(m.shape, f32) for m in matrices]
        + [pltpu.SemaphoreType.DMA((2, 8))],
        compiler_params=params(60),
    )(sums, *matrices)


def unproject_kernel(dq_ref, dk_ref, dv_ref, a_ref, w_ref, dn_ref, dw_ref, db_ref):
    step = pl.program_id(0)
    mixed = jnp.concatenate(
        [ref[h] for ref in (dq_ref, dk_ref, dv_ref) for h in range(OWN)], axis=1
    )
    dn_ref[...] = dot_nt(mixed, w_ref[...]).astype(bf16)
    dw = dot_tn(a_ref[...], mixed)
    db = jnp.sum(mixed.astype(f32), axis=0, keepdims=True)

    @pl.when(step == 0)
    def _():
        dw_ref[...] = dw
        db_ref[...] = db

    @pl.when(step > 0)
    def _():
        dw_ref[...] += dw
        db_ref[...] += db


def unproject(dq, dk, dv, a, w):
    tile = 768
    head = pl.BlockSpec((OWN, tile, HEAD), lambda i: (0, i, 0))
    whole = lambda i: (0, 0)
    shape = jax.ShapeDtypeStruct
    return pl.pallas_call(
        unproject_kernel,
        name="unproject",
        grid=(ROWS // tile,),
        out_shape=(shape((ROWS, D), bf16), shape((D, WIDE), f32), shape((1, WIDE), f32)),
        in_specs=[
            head, head, head,
            pl.BlockSpec((tile, D), lambda i: (i, 0)),
            pl.BlockSpec((D, WIDE), whole),
        ],
        out_specs=(
            pl.BlockSpec((tile, D), lambda i: (i, 0)),
            pl.BlockSpec((D, WIDE), whole),
            pl.BlockSpec((1, WIDE), whole),
        ),
        compiler_params=params(48),
    )(dq, dk, dv, a, w)


def finish_kernel(x_ref, dh_ref, g_ref, one_ref, two_ref, three_ref, out_ref):
    n, r = moments(x_ref[...].astype(f32))
    dn = one_ref[...].astype(f32) + two_ref[...].astype(f32) + three_ref[...].astype(f32)
    e = dn * g_ref[...]
    lean = jnp.mean(e, axis=-1, keepdims=True) + n * jnp.mean(e * n, axis=-1, keepdims=True)
    out_ref[...] = dh_ref[...] + r * (e - lean)


def finish(x, dh, gain, one, two, three):
    tile = 256
    rows = pl.BlockSpec((tile, D), lambda i: (i, 0))
    return pl.pallas_call(
        finish_kernel,
        name="finish",
        grid=(TOK // tile,),
        out_shape=jax.ShapeDtypeStruct((TOK, D), f32),
        in_specs=[rows, rows, pl.BlockSpec((1, D), lambda i: (0, 0)), rows, rows, rows],
        out_specs=rows,
        compiler_params=params(48),
    )(x, dh, gain, one, two, three)


def flip(block, bit):
    count = lax.axis_size("fsdp")
    return lax.ppermute(block, "fsdp", [(i, i ^ bit) for i in range(count)])


def repack(packed, old, new):
    rows = []
    for left, right, size, at in old:
        rows.append((left, packed[:, :, at : at + size, :HEAD]))
        rows.append((right, packed[:, :, at : at + size, HEAD:]))
    rows = jnp.concatenate([part for _, part in sorted(rows, key=lambda entry: entry[0])], axis=2)
    parts = [
        jnp.concatenate([rows[:, :, left : left + size], rows[:, :, right : right + size]], axis=3)
        for left, right, size, _ in sorted(new, key=lambda entry: entry[3])
    ]
    return jnp.concatenate(parts, axis=2)


def over_replicas(block):
    count = lax.axis_size("rep")
    held = lax.optimization_barrier(block)
    if count == 2:
        other = lax.ppermute(held, "rep", [(0, 1), (1, 0)])
        return held.astype(f32) + other.astype(f32)
    return lax.psum(held.astype(f32), "rep")


def body(
    block_input, cotangent, tie_index, prefix_len, pre_gain, pre_shift, w_qkv, b_qv, w_out, b_out,
    mid_gain, mid_shift, w_fc, b_fc, w_proj, b_proj,
):
    n = lax.axis_size("fsdp")
    me = lax.axis_index("fsdp")
    pos = lax.rem(me, GROUP)
    rows = D // n
    index = tie_index[0]

    def chosen(bank):
        return lax.dynamic_index_in_dim(bank, index, 0, keepdims=False)

    vectors = (pre_gain, pre_shift, b_qv, b_out, mid_gain, mid_shift, b_fc, b_proj)
    sizes = [bank.shape[1] for bank in vectors]
    count = sum(sizes)
    high = -(-(rows + 2) // 16) * 16
    cuts = [sum(sizes[:i]) for i in range(len(sizes) + 1)]

    def vectors_of(lines):
        smalls = lines[:, 0, :count].astype(f32)
        group_rows = lax.dynamic_slice_in_dim(lines[:, 1, :2], me - pos, GROUP, 0)
        reaches = group_rows[:, 0].astype(f32) * 16 + group_rows[:, 1].astype(f32)
        return [
            smalls[:, cuts[i] : cuts[i + 1]].reshape(1, -1) for i in range(len(sizes))
        ], reaches.astype(jnp.int32)

    fused = n == BLOCKS and lax.axis_size("rep") == 2
    if fused:
        small, pieces, shard = pick(tie_index, prefix_len, vectors, w_qkv, w_out, w_fc, w_proj)
        wall, lines, wq, a_low, qx, k, v, o_full, o_recv = forward(block_input, small, pieces, shard)
        a_low = a_low.reshape(ROWS, D)
    else:
        small = jnp.concatenate([chosen(bank) for bank in vectors])
        reach = prefix_len[0]
        reach_row = jnp.concatenate([reach // 16, reach % 16]).astype(bf16)
        wq = chosen(w_qkv).reshape(rows, 3, GROUP, SLICE).transpose(2, 0, 1, 3)
        wq = wq.reshape(GROUP, rows, WIDE)
        extra = jnp.stack([jnp.pad(line, (0, WIDE - line.shape[0])) for line in (small, reach_row)])
        wo, wf, wp = chosen(w_out), chosen(w_fc), chosen(w_proj)
        extra = jnp.pad(extra, ((0, high - rows - 2), (0, 0)))
        pieces = jnp.concatenate([wq, jnp.broadcast_to(extra, (GROUP,) + extra.shape)], axis=1)
        wo = lax.all_gather(wo, "fsdp", axis=0, tiled=True).reshape(BLOCKS, -1, D)
        wf = lax.all_gather(wf, "fsdp", axis=0, tiled=True)
        wf = wf.reshape(BLOCKS, D // BLOCKS, FF // D, D).transpose(0, 2, 1, 3)
        wp = lax.all_gather(wp, "fsdp", axis=0, tiled=True).reshape(BLOCKS, -1, D)
        wall = jnp.concatenate([wp, wo, wf.reshape(BLOCKS, -1, D)], axis=1)
        xg, wg = gather_group(n, block_input, pieces)
        wq = wg[:, :rows].reshape(D, WIDE)
        found, reaches = vectors_of(wg[:, rows : rows + 2])
        g1, s1, bqv = found[:3]
        lines = jnp.concatenate([row.reshape(BLOCKS, -1) for row in found], axis=1).astype(bf16)
        lines = jnp.pad(lines[:, None], ((0, 0), (0, 1), (0, 640 - lines.shape[1])))
        own_bias = lax.dynamic_index_in_dim(bqv.reshape(2, GROUP, SLICE), pos, 1, keepdims=False)
        bias = jnp.concatenate([own_bias[0], jnp.zeros((SLICE,), f32), own_bias[1]])[None]
        a_low, q, k, v = project(xg.reshape(ROWS, D), wq, g1, s1, bias)
        o_send, o_full, qx = attend(reaches, q, k, v)
        o_recv = repack(swap(o_send, 1, "swap_o"), ((0, 384, 384, 0),), PACK)

    y, dwf, dwp, dbf, dwo, dh, do_send, sums = middle(
        block_input, o_recv, cotangent, wall, lines
    )
    if fused:
        grad, dwq, dwp, dwo, dwf, sums = backward(
            do_send, qx, k, v, o_full, a_low, wq, block_input, dh, lines, sums, dbf,
            dwp.reshape(BLOCKS, -1, D), dwo.reshape(BLOCKS, -1, D), dwf.reshape(BLOCKS, -1, D),
        )
        landed = land(sums, (grad, dwq, dwo, dwf, dwp))
        grad, dwq, dwo, dwf, dwp, dg1, ds1, dbqv, dbo, dg2, ds2, dbf, dbp = landed
        return (y, grad, dg1, ds1, dwq, dbqv, dwo, dbo, dg2, ds2, dwf, dbf, dwp, dbp)
    dwf = dwf.transpose(0, 2, 1, 3).reshape(D, FF)
    dwf = lax.psum_scatter(dwf, "fsdp", scatter_dimension=0, tiled=True)
    dwp = lax.psum_scatter(dwp, "fsdp", scatter_dimension=0, tiled=True)
    dwo = lax.psum_scatter(dwo, "fsdp", scatter_dimension=0, tiled=True)
    do_recv = repack(swap(do_send, 2, "swap_do"), PACK, ((0, 384, 384, 0),))
    dq, dk, dv = attend_back(reaches, qx, k, v, o_full, do_recv)
    dn, dwq, db = unproject(dq, dk, dv, a_low, wq)

    dn = dn.reshape(GROUP, TOK, D)
    block_of = lambda bit: lax.dynamic_index_in_dim(dn, pos ^ bit, 0, keepdims=False)
    beside = flip(block_of(1), 1)
    across = flip(block_of(3), 1)
    across = flip((across.astype(f32) + block_of(2).astype(f32)).astype(bf16), 2)

    wq_wide = wq.astype(f32)
    dshift = jnp.sum(wq_wide * db, axis=1)
    dgain = jnp.sum(wq_wide * (dwq - s1.reshape(D, 1) * db), axis=1) / g1.reshape(D)
    where = (jnp.arange(GROUP) == pos).astype(f32)[:, None]
    dbias = jnp.concatenate(
        [(where * db[:, :SLICE]).reshape(-1), (where * db[:, 2 * SLICE :]).reshape(-1)]
    )
    line = jnp.concatenate(
        [
            part.reshape(n, -1)
            for part in (dgain, dshift, dbias, sums[3], sums[1], sums[2], dbf, sums[0])
        ],
        axis=1,
    )
    line_hi = line.astype(bf16)
    line_low = (line - lax.reduce_precision(line, 8, 7)).astype(bf16)
    lines = jnp.pad(jnp.stack([line_hi, line_low], axis=1), ((0, 0), (0, 0), (0, WIDE - count)))
    lines = jnp.pad(lines, ((0, 0), (0, high - rows - 2), (0, 0)))
    back = jnp.concatenate([dwq.astype(bf16).reshape(n, rows, WIDE), lines], axis=1)
    back = swap(back, 3, "swap_grad")
    dwq = jnp.sum(back[:, :rows].astype(f32).reshape(n // GROUP, GROUP, rows, 3, SLICE), axis=0)
    dwq = dwq.transpose(1, 2, 0, 3).reshape(rows, 3 * D)
    line = jnp.sum(back[:, rows, :count].astype(f32) + back[:, rows + 1, :count].astype(f32), axis=0)

    grad = finish(block_input, dh, g1, block_of(0), beside, across)
    dwq = over_replicas(dwq.astype(bf16))
    dwo, dwf, dwp = over_replicas(dwo), over_replicas(dwf), over_replicas(dwp)
    line = over_replicas(line)
    dg1, ds1, dbqv, dbo, dg2, ds2, dbf, dbp = (
        line[cuts[i] : cuts[i + 1]] for i in range(len(sizes))
    )
    return (y, grad, dg1, ds1, dwq, dbqv, dwo, dbo, dg2, ds2, dwf, dbf, dwp, dbp)


def solution(mesh):
    tokens = P(("rep", "fsdp"), None)
    vector, matrix = P(None, "fsdp"), P(None, "fsdp", None)
    return jax.shard_map(
        body,
        mesh=mesh,
        in_specs=(
            tokens, tokens, P(), tokens, vector, vector, matrix, vector, matrix, vector,
            vector, vector, matrix, vector, matrix, vector,
        ),
        out_specs=(
            tokens, tokens, P("fsdp"), P("fsdp"), P("fsdp", None), P("fsdp"), P("fsdp", None),
            P("fsdp"), P("fsdp"), P("fsdp"), P("fsdp", None), P("fsdp"), P("fsdp", None), P("fsdp"),
        ),
        check_vma=False,
    )
```

```python
from functools import partial

import jax
import jax.numpy as jnp
from jax import lax
from jax.experimental import pallas as pl
from jax.experimental.pallas import tpu as pltpu
from jax.sharding import PartitionSpec as P

D = 768
HEADS = 12
HEAD = 64
FF = 3072
GROUP = 4
PROMPT = 512
CONT = 256
TOK = 768
ROWS = GROUP * TOK
OWN = HEADS // GROUP
SLICE = OWN * HEAD
WIDE = 3 * SLICE
PAIR = TOK // 2
CHUNK = 768
BLOCKS = 16
UNIT = 432
NEG = -1e30
EPS = 1e-5
PACK = ((512, 640, 128, 0), (0, 256, 256, 128))
GELU_A = 0.7978845608028654
GELU_B = 0.044715

f32 = jnp.float32
bf16 = jnp.bfloat16
MESH = pl.DeviceIdType.MESH
ANY = pl.BlockSpec(memory_space=pl.ANY)


def params(mib, **more):
    return pltpu.CompilerParams(vmem_limit_bytes=mib << 20, **more)


def dot(a, b):
    return jnp.dot(a, b, preferred_element_type=f32)


def dot_nt(a, b):
    return lax.dot_general(a, b, (((1,), (1,)), ((), ())), preferred_element_type=f32)


def dot_tn(a, b):
    return lax.dot_general(a, b, (((0,), (0,)), ((), ())), preferred_element_type=f32)


def moments(x):
    center = x - jnp.mean(x, axis=-1, keepdims=True)
    scale = lax.rsqrt(jnp.mean(center * center, axis=-1, keepdims=True) + EPS)
    return center * scale, scale


def greet(peers, replica=None):
    sem = pltpu.get_barrier_semaphore()
    for peer in peers:
        pl.semaphore_signal(sem, inc=1, device_id={"fsdp": peer}, device_id_type=MESH)
    if replica is not None:
        pl.semaphore_signal(sem, inc=1, device_id={"rep": replica}, device_id_type=MESH)
    pl.semaphore_wait(sem, len(peers) + (replica is not None))


def gather_kernel(n, parts, x_ref, w_ref, xg_ref, wg_ref, xs, xr, ws, wr, local):
    me = lax.axis_index("fsdp")
    pos = lax.rem(me, GROUP)
    near, far = me ^ 1, me ^ 2
    greet([me ^ i for i in range(1, n)])
    own = pltpu.make_async_copy(x_ref, xg_ref.at[pos], local.at[0])
    own.start()
    own_w = pltpu.make_async_copy(w_ref.at[pos], wg_ref.at[me], local.at[1])
    own_w.start()
    rows = TOK // parts

    def piece(src, slot, part, i, peer):
        at = pl.ds(part * rows, rows)
        return pltpu.make_async_remote_copy(
            src_ref=src.at[at],
            dst_ref=xg_ref.at[slot, at],
            send_sem=xs.at[i],
            recv_sem=xr.at[i],
            device_id={"fsdp": peer},
            device_id_type=MESH,
        )

    across = [piece(x_ref, pos, part, part, far) for part in range(parts)]
    for copy in across:
        copy.start()
    beside = pltpu.make_async_remote_copy(
        src_ref=x_ref,
        dst_ref=xg_ref.at[pos],
        send_sem=xs.at[2 * parts],
        recv_sem=xr.at[2 * parts],
        device_id={"fsdp": near},
        device_id_type=MESH,
    )
    beside.start()
    slices = []
    for i in range(1, n):
        peer = me ^ i
        copy = pltpu.make_async_remote_copy(
            src_ref=w_ref.at[lax.rem(peer, GROUP)],
            dst_ref=wg_ref.at[me],
            send_sem=ws.at[i],
            recv_sem=wr.at[i],
            device_id={"fsdp": peer},
            device_id_type=MESH,
        )
        copy.start()
        slices.append(copy)
    passed = []
    for part in range(parts):
        across[part].wait_recv()
        copy = piece(xg_ref.at[pos ^ 2], pos ^ 2, part, parts + part, near)
        copy.start()
        passed.append(copy)
    for copy in across:
        copy.wait_send()
    beside.wait()
    own.wait()
    own_w.wait()
    for copy in passed + slices:
        copy.wait()


def gather_group(n, x, pieces):
    parts = 4
    dma = pltpu.SemaphoreType.DMA
    return pl.pallas_call(
        partial(gather_kernel, n, parts),
        name="gather_group",
        out_shape=(
            jax.ShapeDtypeStruct((GROUP,) + x.shape, x.dtype),
            jax.ShapeDtypeStruct((n,) + pieces.shape[1:], pieces.dtype),
        ),
        in_specs=[ANY, ANY],
        out_specs=(ANY, ANY),
        scratch_shapes=[
            dma((2 * parts + 1,)),
            dma((2 * parts + 1,)),
            dma((n,)),
            dma((n,)),
            dma((2,)),
        ],
        compiler_params=params(32, collective_id=0, has_side_effects=True),
    )(x, pieces)


def swap_kernel(count, x_ref, o_ref, send, recv, local):
    me = lax.axis_index("fsdp")
    greet([me ^ i for i in range(1, count)])
    slot = lax.rem(me, count)
    own = pltpu.make_async_copy(x_ref.at[slot], o_ref.at[slot], local)
    own.start()
    copies = []
    for i in range(1, count):
        copy = pltpu.make_async_remote_copy(
            src_ref=x_ref.at[slot ^ i],
            dst_ref=o_ref.at[slot],
            send_sem=send.at[i],
            recv_sem=recv.at[i],
            device_id={"fsdp": me ^ i},
            device_id_type=MESH,
        )
        copy.start()
        copies.append(copy)
    own.wait()
    for copy in copies:
        copy.wait()


def swap(x, collective_id, name):
    count = x.shape[0]
    dma = pltpu.SemaphoreType.DMA
    return pl.pallas_call(
        partial(swap_kernel, count),
        name=name,
        out_shape=jax.ShapeDtypeStruct(x.shape, x.dtype),
        in_specs=[ANY],
        out_specs=ANY,
        scratch_shapes=[dma((count,)), dma((count,)), dma],
        compiler_params=params(32, collective_id=collective_id, has_side_effects=True),
    )(x)


def project_kernel(x_ref, w_ref, g_ref, s_ref, b_ref, a_ref, q_ref, k_ref, v_ref):
    n, _ = moments(x_ref[...].astype(f32))
    a_low = (n * g_ref[...] + s_ref[...]).astype(bf16)
    a_ref[...] = a_low
    mixed = (dot(a_low, w_ref[...]) + b_ref[...]).astype(bf16)
    ones = jnp.ones((x_ref.shape[0], HEAD), bf16)
    for h in range(OWN):
        q = mixed[:, h * HEAD : (h + 1) * HEAD] * 0.125
        k = mixed[:, SLICE + h * HEAD : SLICE + (h + 1) * HEAD]
        v = mixed[:, 2 * SLICE + h * HEAD : 2 * SLICE + (h + 1) * HEAD]
        q_ref[h] = jnp.concatenate([q.astype(bf16), jnp.zeros_like(ones)], axis=1)
        k_ref[h] = jnp.concatenate([k, ones], axis=1)
        v_ref[h] = jnp.concatenate([v, ones], axis=1)


def project(x, w, gain, shift, bias):
    tile = 384
    heads = jax.ShapeDtypeStruct((OWN, ROWS, 2 * HEAD), bf16)
    head_spec = pl.BlockSpec((OWN, tile, 2 * HEAD), lambda i: (0, i, 0))
    whole = lambda i: (0, 0)
    return pl.pallas_call(
        project_kernel,
        name="project",
        grid=(ROWS // tile,),
        out_shape=(jax.ShapeDtypeStruct((ROWS, D), bf16), heads, heads, heads),
        in_specs=[
            pl.BlockSpec((tile, D), lambda i: (i, 0)),
            pl.BlockSpec((D, WIDE), whole),
            pl.BlockSpec((1, D), whole),
            pl.BlockSpec((1, D), whole),
            pl.BlockSpec((1, WIDE), whole),
        ],
        out_specs=(pl.BlockSpec((tile, D), lambda i: (i, 0)), head_spec, head_spec, head_spec),
        compiler_params=params(48),
    )(x, w, gain, shift, bias)


def lanes(rows):
    return lax.broadcasted_iota(jnp.int32, (rows, 2 * HEAD), 1)


def split_columns(base, lane, column):
    hi = column.astype(bf16).astype(f32)
    mid = (column - hi).astype(bf16).astype(f32)
    low = column - hi - mid
    tail = jnp.where(lane == HEAD, -hi, jnp.where(lane == HEAD + 1, -mid, -low))
    return jnp.where(lane < HEAD, base, jnp.where(lane < HEAD + 3, tail, 0.0)).astype(bf16)


def below(rows, cols, low_key):
    row = lax.broadcasted_iota(jnp.int32, (rows, cols), 0)
    col = lax.broadcasted_iota(jnp.int32, (rows, cols), 1)
    return row <= col if low_key else col <= row


def attend_kernel(reach_ref, q_ref, k_ref, v_ref, o_ref, f_ref, x_ref):
    T = CONT
    lane = lanes(T)
    causal = below(T, T, False)

    def tile(at, blocks):
        q = q_ref[0, pl.ds(at, T), :]
        scores = []
        for start, size, mask in blocks:
            s = dot_nt(q, k_ref[0, pl.ds(start, size), :])
            scores.append(s if mask is None else jnp.where(mask, s, NEG))
        peak = scores[0].max(axis=1, keepdims=True)
        for s in scores[1:]:
            peak = jnp.maximum(peak, s.max(axis=1, keepdims=True))
        total = jnp.zeros((T, 2 * HEAD), f32)
        for s, (start, size, _) in zip(scores, blocks):
            total += dot(jnp.exp(s - peak).astype(bf16), v_ref[0, pl.ds(start, size), :])
        mass = total[:, HEAD : HEAD + 1]
        f_ref[0, pl.ds(at, T), :] = total / mass
        lse = peak + jnp.log(mass)
        x_ref[0, pl.ds(at, T), :] = split_columns(q.astype(f32), lane, lse)

    for p in range(GROUP):
        past = [(i * TOK, PROMPT, None) for i in range(p)]
        base = p * TOK
        tile(base, past + [(base, T, causal)])
        tile(base + T, past + [(base, T, None), (base + T, T, causal)])

    def cont(c, carry):
        at = pl.multiple_of(c * TOK + PROMPT, CONT)
        reach = reach_ref[c]
        col = lax.broadcasted_iota(jnp.int32, (T, PROMPT), 1)
        blocks = [(i * TOK, PROMPT, col < reach - i * PROMPT) for i in range(GROUP)]
        tile(at, blocks + [(at, T, causal)])
        return carry

    lax.fori_loop(0, GROUP, cont, 0)

    half = lanes(PAIR) < HEAD
    for p in range(GROUP):
        top = f_ref[0, p * TOK : p * TOK + PAIR, :]
        low = f_ref[0, p * TOK + PAIR : (p + 1) * TOK, :]
        o_ref[p, 0] = jnp.where(half, top, pltpu.roll(low, HEAD, 1)).astype(bf16)


def attend(reach, q, k, v):
    head = lambda h: (h, 0, 0)
    spec = pl.BlockSpec((1, ROWS, 2 * HEAD), head)
    return pl.pallas_call(
        attend_kernel,
        name="attend",
        grid=(OWN,),
        out_shape=(
            jax.ShapeDtypeStruct((GROUP, OWN, PAIR, 2 * HEAD), bf16),
            jax.ShapeDtypeStruct((OWN, ROWS, 2 * HEAD), f32),
            jax.ShapeDtypeStruct((OWN, ROWS, 2 * HEAD), bf16),
        ),
        in_specs=[pl.BlockSpec(memory_space=pltpu.SMEM), spec, spec, spec],
        out_specs=(
            pl.BlockSpec((GROUP, 1, PAIR, 2 * HEAD), lambda h: (0, h, 0, 0)),
            spec,
            spec,
        ),
        compiler_params=params(56),
    )(reach, q, k, v)


def attend_back_kernel(
    reach_ref, q_ref, k_ref, v_ref, f_ref, g_ref, dq_ref, dk_ref, dv_ref, g_s, dq_s, kt_s, dk_s, dv_s
):
    T = CONT
    half = lanes(PAIR) < HEAD
    lane = lanes(PAIR)
    for p in range(GROUP):
        packed = g_ref[p, 0].astype(f32)
        for i, block in enumerate((packed, pltpu.roll(packed, HEAD, 1))):
            at = p * TOK + i * PAIR
            prod = jnp.where(half, block * f_ref[0, at : at + PAIR, :], 0.0)
            inner = jnp.sum(prod, axis=1, keepdims=True)
            g_s[at : at + PAIR, :] = split_columns(block, lane, inner)
        kt_s[:, p * TOK : (p + 1) * TOK] = k_ref[0, p * TOK : (p + 1) * TOK, :].T[:HEAD]
    dq_s[...] = jnp.zeros_like(dq_s)

    def block(keys, size, rows, count, mask, first, key_at):
        kb = k_ref[0, pl.ds(keys, size), :]
        vb = v_ref[0, pl.ds(keys, size), :]
        q = q_ref[0, pl.ds(rows, count), :]
        g = g_s[pl.ds(rows, count), :]
        probs = jnp.exp(dot_nt(kb, q))
        if mask is not None:
            probs = jnp.where(mask, probs, 0.0)
        ds = (probs * dot_nt(vb, g)).astype(bf16)
        dv = dot(probs.astype(bf16), g)
        dk = dot(ds, q)
        at = pl.ds(key_at, size)
        dv_s[at, :] = dv if first else dv_s[at, :] + dv
        dk_s[at, :] = dk if first else dk_s[at, :] + dk
        dq_s[:, pl.ds(rows, count)] += dot(kt_s[:, pl.ds(keys, size)], ds)

    causal = below(T, T, True)
    for p in range(GROUP):
        base = p * TOK
        block(base, T, base, T, causal, True, 0)
        block(base + T, T, base + T, T, causal, True, T)
        block(base, T, base + T, T, None, False, 0)

        def later(i, carry):
            rows = pl.multiple_of(i * TOK, CONT)
            block(base, PROMPT, rows, PROMPT, None, False, 0)
            return carry

        lax.fori_loop(p + 1, GROUP, later, 0)

        def cont(c, carry):
            rows = pl.multiple_of(c * TOK + PROMPT, CONT)
            key = lax.broadcasted_iota(jnp.int32, (PROMPT, T), 0)
            block(base, PROMPT, rows, T, key < reach_ref[c] - p * PROMPT, False, 0)
            return carry

        lax.fori_loop(0, GROUP, cont, 0)
        dk_ref[0, base : base + PROMPT, :] = dk_s[:, :HEAD].astype(bf16)
        dv_ref[0, base : base + PROMPT, :] = dv_s[:, :HEAD].astype(bf16)

    def own(c, carry):
        at = pl.multiple_of(c * TOK + PROMPT, CONT)
        block(at, T, at, T, causal, True, 0)
        dk_ref[0, pl.ds(at, T), :] = dk_s[:T, :HEAD].astype(bf16)
        dv_ref[0, pl.ds(at, T), :] = dv_s[:T, :HEAD].astype(bf16)
        return carry

    lax.fori_loop(0, GROUP, own, 0)
    for i in range(ROWS // PROMPT):
        at = i * PROMPT
        dq_ref[0, at : at + PROMPT, :] = (dq_s[:, at : at + PROMPT].T * 0.125).astype(bf16)


def attend_back(reach, q, k, v, f, g):
    head = lambda h: (h, 0, 0)
    spec = pl.BlockSpec((1, ROWS, 2 * HEAD), head)
    out = jax.ShapeDtypeStruct((OWN, ROWS, HEAD), bf16)
    out_spec = pl.BlockSpec((1, ROWS, HEAD), head)
    return pl.pallas_call(
        attend_back_kernel,
        name="attend_back",
        grid=(OWN,),
        out_shape=(out, out, out),
        in_specs=[pl.BlockSpec(memory_space=pltpu.SMEM), spec, spec, spec, spec]
        + [pl.BlockSpec((GROUP, 1, PAIR, 2 * HEAD), lambda h: (0, h, 0, 0))],
        out_specs=(out_spec, out_spec, out_spec),
        scratch_shapes=[
            pltpu.VMEM((ROWS, 2 * HEAD), bf16),
            pltpu.VMEM((HEAD, ROWS), f32),
            pltpu.VMEM((HEAD, ROWS), bf16),
            pltpu.VMEM((PROMPT, 2 * HEAD), f32),
            pltpu.VMEM((PROMPT, 2 * HEAD), f32),
        ],
        compiler_params=params(56),
    )(reach, q, k, v, f, g)


def pick_kernel(index_ref, reach_ref, *refs):
    vectors, (wq_ref, wo_ref, wf_ref, wp_ref), (small_ref, piece_ref, shard_ref) = (
        refs[:8], refs[8:12], refs[12:],
    )
    index = index_ref[0]
    rows = []
    for ref in vectors:
        bank = ref[...].astype(f32)
        chosen = lax.broadcasted_iota(jnp.int32, bank.shape, 0) == index
        rows.append(jnp.sum(jnp.where(chosen, bank, 0.0), axis=0, keepdims=True))
    width = sum(row.shape[1] for row in rows)
    rest = small_ref.shape[1] - width
    small_ref[0:1, :] = jnp.concatenate(rows + [jnp.zeros((1, rest), f32)], axis=1).astype(bf16)
    reach = reach_ref[0, 0]
    lane = lax.broadcasted_iota(jnp.int32, (1, small_ref.shape[1]), 1)
    code = jnp.where(lane == 0, reach // 16, jnp.where(lane == 1, lax.rem(reach, 16), 0))
    small_ref[1:2, :] = code.astype(f32).astype(bf16)
    for j in range(GROUP):
        for part in range(3):
            at = part * D + j * SLICE
            piece_ref[j, :, part * SLICE : (part + 1) * SLICE] = wq_ref[0, :, at : at + SLICE]
    shard_ref[:192, :] = wp_ref[0]
    shard_ref[192:240, :] = wo_ref[0]
    for c in range(FF // D):
        shard_ref[240 + 48 * c : 288 + 48 * c, :] = wf_ref[0, :, c * D : (c + 1) * D]


def pick(index, reach, vectors, wq, wo, wf, wp):
    shape = jax.ShapeDtypeStruct
    chosen = lambda bank: pl.BlockSpec((1,) + bank.shape[1:], lambda i, at: (at[0], 0, 0))
    whole = lambda bank: pl.BlockSpec(bank.shape, lambda i, at: (0, 0))
    fixed3 = lambda i, at: (0, 0, 0)
    return pl.pallas_call(
        pick_kernel,
        name="pick",
        out_shape=(
            shape((2, 640), bf16), shape((GROUP, D // BLOCKS, WIDE), bf16), shape((UNIT, D), bf16),
        ),
        grid_spec=pltpu.PrefetchScalarGridSpec(
            num_scalar_prefetch=1,
            grid=(1,),
            in_specs=[pl.BlockSpec(memory_space=pltpu.SMEM)]
            + [whole(bank) for bank in vectors]
            + [chosen(bank) for bank in (wq, wo, wf, wp)],
            out_specs=(
                pl.BlockSpec((2, 640), lambda i, at: (0, 0)),
                pl.BlockSpec((GROUP, D // BLOCKS, WIDE), fixed3),
                pl.BlockSpec((UNIT, D), lambda i, at: (0, 0)),
            ),
        ),
        compiler_params=params(60),
    )(index, reach, *vectors, wq, wo, wf, wp)


def ring_of(me):
    chip, core = me // 2, lax.rem(me, 2)
    z, x = chip // 2, lax.rem(chip, 2)
    chips = BLOCKS // 2
    half = chips // 2
    place = z * (1 - x) + (chips - 1 - z) * x

    def device(at):
        at = lax.rem(at + 2 * chips, chips)
        side = at // half
        z_at = at * (1 - side) + (chips - 1 - at) * side
        return (z_at * 2 + side) * 2 + core

    return place, device


def forward_kernel(
    x_ref, sm_ref, pc_ref, sh_ref,
    wall_ref, smo_ref, wq_ref, a_ref, q_ref, k_ref, v_ref, f_ref, o_ref,
    xg, smg, wg, w_s, q_s, k_s, v_s, f_s, o_s, sh_s,
    local, sm_send, sm_recv, w_send, w_recv, x_send, x_recv, r_send, r_recv, n_send, n_recv,
    y_send, y_recv, o_send, o_recv, out_sem,
):
    n = BLOCKS
    me = lax.axis_index("fsdp")
    rep = lax.axis_index("rep")
    pos = lax.rem(me, GROUP)
    base = me - pos
    near, far = me ^ 1, me ^ 2
    level, xside = me // GROUP, lax.rem(me, GROUP) // 2
    core = lax.rem(me, 2)
    levels = n // GROUP
    parts = TOK // CONT
    part_rows = CONT
    T = CONT

    def remote(src, dst, send, recv, peer):
        return pltpu.make_async_remote_copy(
            src_ref=src,
            dst_ref=dst,
            send_sem=send,
            recv_sem=recv,
            device_id=peer if isinstance(peer, dict) else {"fsdp": peer},
            device_id_type=MESH,
        )

    greet([me ^ i for i in range(1, n)], 1 - rep)

    own_block = pltpu.make_async_copy(sh_ref, sh_s, local.at[0])
    own_store = pltpu.make_async_copy(sh_s, wall_ref.at[me], local.at[4])
    own_x = pltpu.make_async_copy(x_ref, xg.at[pos], local.at[1])
    own_w = pltpu.make_async_copy(pc_ref.at[pos], wg.at[me], local.at[2])
    own_s = pltpu.make_async_copy(sm_ref, smg.at[me], local.at[3])
    for copy in (own_s, own_w, own_x, own_block):
        copy.start()

    slices = []
    for i in range(1, GROUP):
        copy = remote(pc_ref.at[pos ^ i], wg.at[me], w_send.at[i], w_recv.at[i], me ^ i)
        copy.start()
        slices.append(copy)
    smalls = []
    for i in range(1, n):
        copy = remote(sm_ref, smg.at[me], sm_send.at[i], sm_recv.at[i], me ^ i)
        copy.start()
        smalls.append(copy)
    beside = remote(x_ref, xg.at[pos], x_send.at[2 * parts], x_recv.at[2 * parts], near)
    beside.start()

    def x_part(src, slot, part, i, peer):
        at = pl.ds(part * part_rows, part_rows)
        return remote(src.at[at], xg.at[slot, at], x_send.at[i], x_recv.at[i], peer)

    across = [x_part(x_ref, pos, part, part, far) for part in range(parts)]
    own_block.wait()
    own_store.start()
    mine = pl.ds(pl.multiple_of(rep * (D // 2), D // 2), D // 2)
    other = pl.ds(pl.multiple_of((1 - rep) * (D // 2), D // 2), D // 2)
    hops, sent, shared = [], [], []

    def begin(copy, keep):
        copy.start()
        keep.append((None, copy))

    def block_of(stream, at):
        side = xside if stream == 0 else 1 - xside
        return (at * 2 + side) * 2 + core

    def slot(stream, t, up):
        return 6 * stream + 2 * t + (0 if up else 1)

    def sends(t, up):
        return (level >= t) & (level < levels - 1) if up else (level + t < levels) & (level > 0)

    def comes(t, up):
        return level > t if up else level + t < levels - 1

    def when(cond, keep, copies):
        @pl.when(cond)
        def _():
            for copy in copies:
                copy.start()

        keep.extend((cond, copy) for copy in copies)

    def hop(stream, t, up):
        at = block_of(stream, level - t if up else level + t)
        block = wall_ref.at[at, :, mine]
        src = sh_s.at[:, mine] if stream == 0 and t == 0 else block
        i = slot(stream, t, up)
        return remote(src, block, r_send.at[i], r_recv.at[i], me + GROUP if up else me - GROUP)

    def to_near(d, columns, i):
        block = wall_ref.at[d, :, columns]
        return remote(block, block, n_send.at[i], n_recv.at[i], near)

    def to_replica(d, columns, i):
        block = wall_ref.at[d, :, columns]
        return remote(block, block, y_send.at[i], y_recv.at[i], {"rep": 1 - rep})

    def launch(stream, t):
        for up in (True, False):
            when(sends(t, up), hops, [hop(stream, t, up)])

    def came(stream, t, up):
        return block_of(stream, level - 1 - t if up else level + 1 + t)

    def arrive(stream, t):
        for up in (True, False):
            copy = hop(stream, t, up)

            @pl.when(comes(t, up))
            def _():
                copy.wait_recv()

        if t < levels - 2:
            launch(stream, t + 1)
        for up in (True, False):
            d, i = came(stream, t, up), slot(stream, t, up)
            when(comes(t, up), sent, [to_replica(d, mine, i)])
            when(comes(t, up), shared, [to_near(d, mine, 1 + i)])

    def settle(stream, t):
        for up in (True, False):
            d, i = came(stream, t, up), slot(stream, t, up)
            copy = to_replica(d, other, i)

            @pl.when(comes(t, up))
            def _():
                copy.wait_recv()

            when(comes(t, up), shared, [to_near(d, other, 14 + i)])

    facing = block_of(1, level)
    cross = remote(sh_s.at[:, mine], wall_ref.at[me, :, mine], r_send.at[12], r_recv.at[12], far)
    crossed = remote(wall_ref.at[facing, :, mine], wall_ref.at[facing, :, mine], r_send.at[12], r_recv.at[12], far)

    def arrive_across():
        crossed.wait_recv()
        launch(1, 0)
        begin(to_replica(facing, mine, 12), sent)
        begin(to_near(facing, mine, 13), shared)

    def settle_across():
        to_replica(facing, other, 12).wait_recv()
        begin(to_near(facing, other, 26), shared)

    def drain(kept, both):
        for cond, copy in kept:
            if cond is None:
                copy.wait() if both else copy.wait_send()
            else:

                @pl.when(cond)
                def _():
                    copy.wait() if both else copy.wait_send()

    cross.start()
    for copy in across:
        copy.start()
    launch(0, 0)
    begin(remote(sh_s, wall_ref.at[me], n_send.at[0], n_recv.at[0], near), shared)

    own_s.wait()
    for copy in smalls:
        copy.wait_recv()
    rows48 = D // n
    gain = jnp.concatenate([smg[d, 0:1, 0:rows48] for d in range(n)], axis=1).astype(f32)
    shift = jnp.concatenate([smg[d, 0:1, rows48 : 2 * rows48] for d in range(n)], axis=1).astype(f32)
    at = 2 * rows48
    two = 2 * rows48
    zeros = jnp.zeros((1, SLICE), bf16)
    bias = jnp.concatenate(
        [smg[2 * pos + i, 0:1, at : at + two] for i in range(2)]
        + [zeros]
        + [smg[n // 2 + 2 * pos + i, 0:1, at : at + two] for i in range(2)],
        axis=1,
    ).astype(f32)

    def norm(slot, lo, hi):
        def some(i, carry):
            at = pl.ds(pl.multiple_of(i * T, T), T)
            n_rows, _ = moments(xg[slot, at, :].astype(f32))
            xg[slot, at, :] = (n_rows * gain + shift).astype(bf16)
            return carry

        lax.fori_loop(lo, hi, some, 0)

    def project_block(slot, lo, hi):
        def some(i, carry):
            at = pl.ds(pl.multiple_of(i * T, T), T)
            out = pl.ds(pl.multiple_of(slot * TOK + i * T, T), T)
            mixed = (dot(xg[slot, at, :], w_s[...]) + bias).astype(bf16)
            ones = jnp.ones((T, HEAD), bf16)
            for h in range(OWN):
                q = mixed[:, h * HEAD : (h + 1) * HEAD] * 0.125
                k = mixed[:, SLICE + h * HEAD : SLICE + (h + 1) * HEAD]
                v = mixed[:, 2 * SLICE + h * HEAD : 2 * SLICE + (h + 1) * HEAD]
                q_s[h, out, :] = jnp.concatenate([q.astype(bf16), jnp.zeros_like(ones)], axis=1)
                k_s[h, out, :] = jnp.concatenate([k, ones], axis=1)
                v_s[h, out, :] = jnp.concatenate([ones, v], axis=1)
            return carry

        lax.fori_loop(lo, hi, some, 0)

    own_w.wait()
    for copy in slices:
        copy.wait_recv()
    group = pl.ds(base, GROUP)
    wide = []
    for i in range(1, n // GROUP):
        begin(
            remote(wg.at[group], wg.at[group], w_send.at[GROUP + i], w_recv.at[GROUP + i], me ^ (GROUP * i)),
            wide,
        )
    own_x.wait()
    norm(pos, 0, 3)
    beside.wait()
    norm(pos ^ 1, 0, 3)
    arrive(0, 0)
    arrive_across()
    for _, copy in wide:
        copy.wait_recv()
    w_s[...] = wg[:, :rows48, :].reshape(D, WIDE)
    project_block(pos, 0, 3)
    project_block(pos ^ 1, 0, 3)
    passed = []

    def take(part):
        across[part].wait_recv()
        begin(x_part(xg.at[pos ^ 2], pos ^ 2, part, parts + part, near), passed)

    take(0)
    take(1)
    arrive(0, 1)
    for _, copy in passed:
        copy.wait()
    for i in (2, 3):
        norm(pos ^ i, 0, 2)
        project_block(pos ^ i, 0, 2)
    outs = []

    def last_rows():
        take(2)
        passed[2][1].wait()
        for i in (2, 3):
            norm(pos ^ i, 2, 3)
            project_block(pos ^ i, 2, 3)
        for i, (src, dst) in enumerate(
            ((smg, smo_ref), (w_s, wq_ref), (xg, a_ref), (k_s, k_ref), (v_s, v_ref))
        ):
            begin(pltpu.make_async_copy(src, dst, out_sem.at[i]), outs)

    lane = lanes(T)
    causal = below(T, T, False)
    code = [smg[base + c, 1:2, 0:2].astype(f32) for c in range(GROUP)]
    reaches = [c[:, 0:1] * 16.0 + c[:, 1:2] for c in code]
    column = lax.broadcasted_iota(jnp.int32, (T, PROMPT), 1).astype(f32)

    for h in range(OWN):

        def tile(at, blocks):
            q = q_s[h, pl.ds(at, T), :]
            scores = []
            for start, size, mask in blocks:
                s = dot_nt(q, k_s[h, pl.ds(start, size), :])
                scores.append(s if mask is None else jnp.where(mask, s, NEG))
            peak = scores[0].max(axis=1, keepdims=True)
            for s in scores[1:]:
                peak = jnp.maximum(peak, s.max(axis=1, keepdims=True))
            total = jnp.zeros((T, 2 * HEAD), f32)
            for s, (start, size, _) in zip(scores, blocks):
                total += dot(jnp.exp(s - peak).astype(bf16), v_s[h, pl.ds(start, size), :])
            mass = total[:, 0:1]
            f_s[h, pl.ds(at, T), :] = total / mass
            lse = peak + jnp.log(mass)
            q_s[h, pl.ds(at, T), :] = split_columns(q.astype(f32), lane, lse)

        for p in range(GROUP):
            past = [(i * TOK, PROMPT, None) for i in range(p)]
            at = p * TOK
            tile(at, past + [(at, T, causal)])
            tile(at + T, past + [(at, T, None), (at + T, T, causal)])
        if h == 0:
            arrive(0, 2)
            arrive(1, 0)
            last_rows()
        if h == 1:
            arrive(1, 2)
        if h == 2:
            settle_across()
            settle(1, 0)
        for c in range(GROUP):
            at = c * TOK + PROMPT
            blocks = [(i * TOK, PROMPT, column < reaches[c] - i * PROMPT) for i in range(GROUP)]
            tile(at, blocks + [(at, T, causal)])
        for p in range(GROUP):
            for left, right, size, to in PACK:
                top = f_s[h, p * TOK + left : p * TOK + left + size, :]
                low = f_s[h, p * TOK + right : p * TOK + right + size, :]
                pair = jnp.where(lanes(size) < HEAD, pltpu.roll(top, HEAD, 1), low)
                o_s[h, p, to : to + size, :] = pair.astype(bf16)
        if h == 0:
            arrive(1, 1)
        if h == 1:
            settle(0, 0)
            settle(0, 1)
            settle(0, 2)
        for i in range(1, GROUP):
            copy = remote(
                o_s.at[h, pos ^ i], o_ref.at[pos, h], o_send.at[h, i], o_recv.at[h, i], me ^ i
            )
            begin(copy, shared)
        for src, dst, i in (
            (o_s.at[h, pos], o_ref.at[pos, h], 5 + h),
            (f_s.at[h], f_ref.at[h], 8 + h),
            (q_s.at[h], q_ref.at[h], 11 + h),
        ):
            copy = pltpu.make_async_copy(src, dst, out_sem.at[i])
            begin(copy, outs)

    settle(1, 1)
    settle(1, 2)
    for copy in across + smalls + slices + [cross]:
        copy.wait_send()
    drain(wide + hops + sent, False)
    own_store.wait()
    drain(shared + outs, True)


def forward(x, small, pieces, shard):
    dma = pltpu.SemaphoreType.DMA
    n = BLOCKS
    shape = jax.ShapeDtypeStruct
    head = (OWN, ROWS, 2 * HEAD)
    return pl.pallas_call(
        forward_kernel,
        name="forward",
        out_shape=(
            shape((n, UNIT, D), bf16),
            shape((n,) + small.shape, bf16),
            shape((D, WIDE), bf16),
            shape((GROUP, TOK, D), bf16),
            shape(head, bf16),
            shape(head, bf16),
            shape(head, bf16),
            shape(head, f32),
            shape((GROUP, OWN, PAIR, 2 * HEAD), bf16),
        ),
        in_specs=[ANY] * 4,
        out_specs=(ANY,) * 9,
        scratch_shapes=[
            pltpu.VMEM((GROUP, TOK, D), bf16),
            pltpu.VMEM((n,) + small.shape, bf16),
            pltpu.VMEM((n,) + pieces.shape[1:], bf16),
            pltpu.VMEM((D, WIDE), bf16),
            pltpu.VMEM(head, bf16),
            pltpu.VMEM(head, bf16),
            pltpu.VMEM(head, bf16),
            pltpu.VMEM(head, f32),
            pltpu.VMEM((OWN, GROUP, PAIR, 2 * HEAD), bf16),
            pltpu.VMEM(shard.shape, bf16),
            dma((5,)),
            dma((n,)),
            dma((n,)),
            dma((2 * GROUP,)),
            dma((2 * GROUP,)),
            dma((9,)),
            dma((9,)),
            dma((13,)),
            dma((13,)),
            dma((27,)),
            dma((27,)),
            dma((13,)),
            dma((13,)),
            dma((OWN, GROUP)),
            dma((OWN, GROUP)),
            dma((14,)),
        ],
        compiler_params=params(60, collective_id=0, has_side_effects=True),
    )(x, small, pieces, shard)


def middle_kernel(
    x_ref, o_ref, dy_ref, wo_ref, wf_ref, wp_ref, line_ref,
    y_ref, dwf_ref, dwp_ref, dbf_ref, dwo_ref, dh_ref, do_ref, small_ref,
    o_s, h_s, b_s, bt_s, y_s, dn_s, row_s,
):
    step = pl.program_id(0)
    part = D // BLOCKS
    half = lanes(PAIR) < HEAD
    wf = wf_ref[...].reshape(D, CHUNK)
    wp = wp_ref[...].reshape(CHUNK, D)
    wo = wo_ref[...].reshape(D, D)

    @pl.when(step == 0)
    def _():
        for t in range(HEADS // 2):
            one = o_ref[2 * t // OWN, 2 * t % OWN].astype(f32)
            two = o_ref[(2 * t + 1) // OWN, (2 * t + 1) % OWN].astype(f32)
            at = slice(2 * t * HEAD, (2 * t + 2) * HEAD)
            first = jnp.where(half, one, pltpu.roll(two, HEAD, 1)).astype(bf16)
            second = jnp.where(half, pltpu.roll(one, HEAD, 1), two).astype(bf16)
            for left, right, size, to in PACK:
                o_s[left : left + size, at] = first[to : to + size]
                o_s[right : right + size, at] = second[to : to + size]
        for i, at in enumerate((4 * part, 5 * part, 6 * part, 11 * part)):
            pieces = [line_ref[d, 0:1, at : at + part] for d in range(BLOCKS)]
            row_s[i : i + 1, :] = jnp.concatenate(pieces, axis=1).astype(f32)
        h = x_ref[...].astype(f32) + dot(o_s[...], wo) + row_s[0:1, :]
        h_s[...] = h
        n, _ = moments(h)
        b_low = (n * row_s[1:2, :] + row_s[2:3, :]).astype(bf16)
        b_s[...] = b_low
        bt_s[...] = b_low.T
        y_s[...] = jnp.zeros_like(y_s)
        dn_s[...] = jnp.zeros_like(dn_s)

    dy = dy_ref[...]
    pieces = [line_ref[4 * step + i, 0:1, 7 * part : 11 * part] for i in range(4)]
    u = dot(b_s[...], wf) + jnp.concatenate(pieces, axis=1).astype(f32)
    square = u * u
    t = jnp.tanh(GELU_A * (u + GELU_B * (square * u)))
    m_low = (0.5 * u * (1.0 + t)).astype(bf16)
    slope = 0.5 * (1.0 + t) + 0.5 * u * (1.0 - t * t) * (GELU_A * (1.0 + 3.0 * GELU_B * square))
    y_s[...] += dot(m_low, wp)
    du = (dot_nt(dy, wp) * slope).astype(bf16)
    dbf_ref[...] = jnp.sum(du.astype(f32), axis=0, keepdims=True)
    dn_s[...] += dot_nt(du, wf)
    dwf_ref[...] = dot(bt_s[...], du).astype(bf16).reshape(dwf_ref.shape)
    dwp_ref[...] = dot_tn(m_low, dy).astype(bf16)

    @pl.when(step == pl.num_programs(0) - 1)
    def _():
        h = h_s[...]
        y_ref[...] = (h + y_s[...] + row_s[3:4, :]).astype(bf16)
        n, r = moments(h)
        dn = dn_s[...]
        grad = dy_ref[...].astype(f32)
        small_ref[...] = jnp.zeros_like(small_ref)
        small_ref[0:1, :] = jnp.sum(grad, axis=0, keepdims=True)
        small_ref[1:2, :] = jnp.sum(dn * n, axis=0, keepdims=True)
        small_ref[2:3, :] = jnp.sum(dn, axis=0, keepdims=True)
        e = dn * row_s[1:2, :]
        lean = jnp.mean(e, axis=-1, keepdims=True) + n * jnp.mean(e * n, axis=-1, keepdims=True)
        dh = grad + r * (e - lean)
        dh_ref[...] = dh
        dh_low = dh.astype(bf16)
        small_ref[3:4, :] = jnp.sum(dh_low.astype(f32), axis=0, keepdims=True)
        dwo_ref[...] = dot_tn(o_s[...], dh_low).astype(bf16)
        h_s[...] = dot_nt(dh_low, wo)
        for t in range(HEADS // 2):
            at = slice(2 * t * HEAD, (2 * t + 2) * HEAD)
            for left, right, size, to in PACK:
                top, low = h_s[left : left + size, at], h_s[right : right + size, at]
                side = lanes(size) < HEAD
                one = jnp.where(side, top, pltpu.roll(low, HEAD, 1))
                two = jnp.where(side, pltpu.roll(top, HEAD, 1), low)
                do_ref[2 * t // OWN, 2 * t % OWN, to : to + size] = one.astype(bf16)
                do_ref[(2 * t + 1) // OWN, (2 * t + 1) % OWN, to : to + size] = two.astype(bf16)


def middle(x, o, dy, wall, lines):
    fixed2 = lambda i: (0, 0)
    fixed4 = lambda i: (0, 0, 0, 0)
    square = pl.BlockSpec((TOK, D), fixed2)
    heads = pl.BlockSpec((GROUP, OWN, PAIR, 2 * HEAD), fixed4)
    columns = pl.BlockSpec((BLOCKS, 1, D // BLOCKS, D), lambda i: (0, i, 0, 0))
    down = pl.BlockSpec((CHUNK, D), lambda i: (i, 0))
    line = pl.BlockSpec((1, CHUNK), lambda i: (0, i))
    shape = jax.ShapeDtypeStruct
    return pl.pallas_call(
        middle_kernel,
        name="middle",
        grid=(FF // CHUNK,),
        out_shape=(
            shape((TOK, D), bf16),
            shape((BLOCKS, FF // D, D // BLOCKS, D), bf16),
            shape((FF, D), bf16),
            shape((1, FF), f32),
            shape((D, D), bf16),
            shape((TOK, D), f32),
            shape((GROUP, OWN, PAIR, 2 * HEAD), bf16),
            shape((8, D), f32),
        ),
        in_specs=[
            square, heads, square,
            pl.BlockSpec((BLOCKS, 48, D), lambda i: (0, 4, 0)),
            pl.BlockSpec((BLOCKS, 48, D), lambda i: (0, 5 + i, 0)),
            pl.BlockSpec((BLOCKS // 4, 192, D), lambda i: (i, 0, 0)),
            pl.BlockSpec(lines.shape, lambda i: (0, 0, 0)),
        ],
        out_specs=(
            square, columns, down, line, square, square, heads, pl.BlockSpec((8, D), fixed2),
        ),
        scratch_shapes=[
            pltpu.VMEM((TOK, D), bf16),
            pltpu.VMEM((TOK, D), f32),
            pltpu.VMEM((TOK, D), bf16),
            pltpu.VMEM((D, TOK), bf16),
            pltpu.VMEM((TOK, D), f32),
            pltpu.VMEM((TOK, D), f32),
            pltpu.VMEM((8, D), f32),
        ],
        compiler_params=params(60),
    )(x, o, dy, wall, wall, wall, lines)


ORDER = (4, -3, 3, -2, 2, -1, 1, 0)
SMALL = 16


def backward_kernel(
    do_ref, q_ref, k_ref, v_ref, f_ref, a_ref, w_ref, x_ref, dh_ref, lines_ref, sums_ref, dbf_ref,
    dwp_ref, dwo_ref, dwf_ref,
    grad_ref, gq_ref, gp_ref, go_ref, gf_ref, small_ref,
    g_b, q_s, k_s, v_s, f_b, a_b, w_s, x_s, dh_s, lines_s, sums_s, dbf_s,
    near_b, mine_b, y_b, ring_b, fin_b, fin_r, fin_o,
    g_s, dq_s, kt_s, dkv_s, dm_s, w_h, dw_s, db_s,
    dw_b, z_b, j_b, j_r, rep_r, gq_o,
    dn_a, dn_b, dn_c, dn_ra, dn_rb, dn_rc, sm_b, sm_r,
    load, f_sem, a_sem, mine_sem, g_send, g_recv, n_send, n_recv, y_send, y_recv, r_send, r_recv, fin_send,
    fin_recv, z_send, z_recv, j_send, j_recv, rep_send, rep_recv, d_send, d_recv, s_send, s_recv, out_sem,
):
    n = BLOCKS
    me = lax.axis_index("fsdp")
    rep = lax.axis_index("rep")
    pos = lax.rem(me, GROUP)
    base = me - pos
    level = me // GROUP
    near, far = me ^ 1, me ^ 2
    place, device = ring_of(me)
    T = CONT
    W3 = 3 * HEAD
    other = {"rep": 1 - rep}

    def remote(src, dst, send, recv, peer):
        return pltpu.make_async_remote_copy(
            src_ref=src,
            dst_ref=dst,
            send_sem=send,
            recv_sem=recv,
            device_id=peer if isinstance(peer, dict) else {"fsdp": peer},
            device_id_type=MESH,
        )

    greet([me ^ i for i in range(1, n)], 1 - rep)

    def do_copy(kind, i):
        at = pl.ds(*((0, 128), (128, 256))[kind])
        src, dst = do_ref.at[pos ^ i, :, at], g_b.at[pos, :, at]
        return remote(src, dst, g_send.at[kind, i], g_recv.at[kind, i], me ^ i)

    own_do = pltpu.make_async_copy(do_ref.at[pos], g_b.at[pos], load.at[0])
    own_do.start()
    for i in range(1, GROUP):
        do_copy(0, i).start()

    stages = (
        tuple((c * TOK + PROMPT, CONT) for c in range(GROUP)),
        ((3 * TOK, PROMPT),),
        ((0, PROMPT),),
        ((TOK, PROMPT), (2 * TOK, PROMPT)),
    )
    loads = (stages[0], ((3 * TOK, PROMPT), (2 * TOK, PROMPT)), ((0, PROMPT), (TOK, PROMPT)))

    def f_copies(part):
        at, found = 0, []
        for i, (row, size) in enumerate(loads[part]):
            src, dst = f_ref.at[:, pl.ds(row, size)], f_b.at[:, pl.ds(at, size)]
            found.append(pltpu.make_async_copy(src, dst, f_sem.at[part, i]))
            at += size
        return found

    def a_copies(stage):
        at, found = 0, []
        for i, (row, size) in enumerate(stages[stage]):
            src, dst = a_ref.at[pl.ds(row, size)], a_b.at[pl.ds(at, size)]
            found.append(pltpu.make_async_copy(src, dst, a_sem.at[stage, i]))
            at += size
        return found

    first = [
        pltpu.make_async_copy(src, dst, load.at[1 + i])
        for i, (src, dst) in enumerate(
            ((k_ref, k_s), (v_ref, v_s), (q_ref, q_s), (lines_ref, lines_s), (w_ref, w_s))
        )
    ]
    later = [
        pltpu.make_async_copy(src, dst, load.at[6 + i])
        for i, (src, dst) in enumerate(
            ((x_ref, x_s), (dh_ref, dh_s), (sums_ref, sums_s), (dbf_ref, dbf_s))
        )
    ]
    for copy in f_copies(0) + first:
        copy.start()

    cut = ((0, 192), (192, 48), (240, 192))

    def near_copies(i):
        d = device(place + ORDER[i]) ^ 1
        return [
            remote(ref.at[d], near_b.at[i, pl.ds(at, size)], n_send.at[i, k], n_recv.at[i, k], near)
            for k, (ref, (at, size)) in enumerate(zip((dwp_ref, dwo_ref, dwf_ref), cut))
        ]

    def mine_copies(i):
        d = device(place + ORDER[i])
        return [
            pltpu.make_async_copy(ref.at[d], mine_b.at[i % 4, pl.ds(at, size)], mine_sem.at[i, k])
            for k, (ref, (at, size)) in enumerate(zip((dwp_ref, dwo_ref, dwf_ref), cut))
        ]

    for i in range(2):
        for copy in near_copies(i) + mine_copies(i):
            copy.start()
    for i in range(1, GROUP):
        do_copy(1, i).start()
    for i in range(2, 8):
        for copy in near_copies(i):
            copy.start()
    for copy in a_copies(0) + mine_copies(2) + mine_copies(3) + later:
        copy.start()

    def ready(i):
        for copy in near_copies(i):
            copy.wait_recv()
        for copy in mine_copies(i):
            copy.wait()

    mine = pl.ds(pl.multiple_of(rep * (D // 2), D // 2), D // 2)
    rest = pl.ds(pl.multiple_of((1 - rep) * (D // 2), D // 2), D // 2)

    def rounds(some):
        def chunk(c, carry):
            some(pl.ds(pl.multiple_of(c * 144, 144), 144))
            return carry

        lax.fori_loop(0, UNIT // 144, chunk, 0)

    def y_copy(i):
        return remote(near_b.at[i, :, rest], y_b.at[i], y_send.at[i], y_recv.at[i], other)

    def chip_sum(i):
        ready(i)

        def some(at):
            total = near_b[i, at, :].astype(f32) + mine_b[i % 4, at, :].astype(f32)
            near_b[i, at, :] = total.astype(bf16)

        rounds(some)
        y_copy(i).start()
        if i + 4 < 8:
            for copy in mine_copies(i + 4):
                copy.start()

    def ring_copy(t, right):
        i = 2 * t if right else 2 * t + 1
        slot = t if right else 4 + t
        peer = device(place + 1 if right else place - 1)
        return remote(near_b.at[i, :, mine], ring_b.at[slot], r_send.at[slot], r_recv.at[slot], peer)

    def ring_step(t):
        for right in (True, False) if t < 3 else (True,):
            i = 2 * t if right else 2 * t + 1
            y_copy(i).wait_recv()
            if t > 0:
                ring_copy(t - 1, right).wait_recv()
            slot = (t if right else 4 + t) - 1

            def some(at):
                total = near_b[i, at, mine].astype(f32) + y_b[i, at, :].astype(f32)
                if t > 0:
                    total = total + ring_b[slot, at, :].astype(f32)
                near_b[i, at, mine] = total.astype(bf16)

            rounds(some)
            ring_copy(t, right).start()

    fin_copy = remote(fin_b, fin_r, fin_send, fin_recv, other)

    def ring_end():
        y_copy(7).wait_recv()
        ring_copy(3, True).wait_recv()
        ring_copy(2, False).wait_recv()

        def some(at):
            total = near_b[7, at, mine].astype(f32) + y_b[7, at, :].astype(f32)
            fin_b[at, :] = (total + ring_b[3, at, :].astype(f32) + ring_b[6, at, :].astype(f32)).astype(bf16)

        rounds(some)
        fin_copy.start()

    def z_copy(h, i):
        return remote(
            dw_b.at[h, level ^ i], z_b.at[h, i], z_send.at[h, i], z_recv.at[h, i], me ^ (GROUP * i)
        )

    def j_copy(h, i):
        return remote(j_b.at[h, pos ^ i], j_r.at[h, pos], j_send.at[h, i], j_recv.at[h, i], me ^ i)

    def gather_rows(h):
        for i in range(1, GROUP):
            z_copy(h, i).wait_recv()
        total = dw_b[h, level].astype(f32)
        for i in range(1, GROUP):
            total = total + z_b[h, i].astype(f32)
        j_b[h] = total.astype(bf16).reshape(GROUP, D // n, W3)
        j_r[h, pos] = j_b[h, pos]
        for i in range(1, GROUP):
            j_copy(h, i).start()

    def rep_copy(h):
        return remote(j_r.at[h], rep_r.at[h], rep_send.at[h], rep_recv.at[h], other)

    def trade_rows(h):
        for i in range(1, GROUP):
            j_copy(h, i).wait_recv()
        rep_copy(h).start()

    causal = below(T, T, True)
    key_row = lax.broadcasted_iota(jnp.int32, (PROMPT, T), 0).astype(f32)

    def prepare(part, h):
        at = 0
        for row, size in loads[part]:
            p = row // TOK
            left, right, count, to = PACK[0 if size == CONT else 1]
            packed = g_b[p, h, to : to + count, :].astype(f32)
            lane = lanes(count)
            for start, block in ((left, pltpu.roll(packed, HEAD, 1)), (right, packed)):
                off = at + start - (row - p * TOK)
                prod = jnp.where(lane >= HEAD, block * f_b[h, off : off + count, :], 0.0)
                inner = jnp.sum(prod, axis=1, keepdims=True)
                hi = inner.astype(bf16).astype(f32)
                mid = (inner - hi).astype(bf16).astype(f32)
                low = inner - hi - mid
                tail = jnp.where(lane == 0, -hi, jnp.where(lane == 1, -mid, -low))
                value = jnp.where(lane >= HEAD, block, jnp.where(lane < 3, tail, 0.0))
                g_s[h, p * TOK + start : p * TOK + start + count, :] = value.astype(bf16)
            at += size

    def block(h, keys, size, rows, count, mask, target):
        kb = k_s[h, pl.ds(keys, size), :]
        vb = v_s[h, pl.ds(keys, size), :]
        q = q_s[h, pl.ds(rows, count), :]
        g = g_s[h, pl.ds(rows, count), :]
        probs = jnp.exp(dot_nt(kb, q))
        if mask is not None:
            probs = jnp.where(mask, probs, 0.0)
        ds = (probs * dot_nt(vb, g)).astype(bf16)
        lane = lanes(count)
        none = jnp.zeros_like(q)
        pair = dot(ds, jnp.where(lane < HEAD, q, none))
        pair = pair + dot(probs.astype(bf16), jnp.where(lane < HEAD, none, g))
        dq_s[h, :, pl.ds(rows, count)] += dot(kt_s[h, :, pl.ds(keys, size)], ds)
        if target is None:
            return pair
        dkv_s[h, pl.ds(target, size), :] += pair

    def diagonal(h, p):
        row, at = p * TOK, p * PROMPT
        block(h, row, T, row, T, causal, at)
        block(h, row, T, row + T, T, None, at)
        block(h, row + T, T, row + T, T, causal, at + T)

    def flush_q(h, row, size):
        at = pl.ds(row, size)
        dm_s[h, at, 2 * HEAD :] = (dq_s[h, :, at].T * 0.125).astype(bf16)

    def flush(h, p):
        dm_s[h, p * TOK : p * TOK + PROMPT, : 2 * HEAD] = dkv_s[
            h, p * PROMPT : (p + 1) * PROMPT, :
        ].astype(bf16)
        flush_q(h, p * TOK, PROMPT)

    def add_weight(stage, h):
        at = 0
        total = jnp.zeros((W3, D), f32)
        for row, size in stages[stage]:
            total = total + dot_tn(dm_s[h, row : row + size, :], a_b[at : at + size, :])
            at += size
        if stage == 0:
            dw_s[h] = total
        else:
            dw_s[h] += total

    def dn_rows(owner, seg):
        rows = pl.ds(pl.multiple_of(owner * TOK + seg * T, T), T)
        total = dot_nt(dm_s[0, rows, :], w_h[0])
        for h in range(1, OWN):
            total = total + dot_nt(dm_s[h, rows, :], w_h[h])
        return total

    def dn_copy(kind, seg):
        at = pl.ds(seg * T, T)
        src, dst, peer = ((dn_a, dn_ra, near), (dn_b, dn_rb, far), (dn_c, dn_rc, near))[kind]
        return remote(src.at[at], dst.at[at], d_send.at[kind, seg], d_recv.at[kind, seg], peer)

    def put(kind, seg):
        at = slice(seg * T, (seg + 1) * T)
        rows = dn_rows(pos ^ (3, 2, 1)[kind], seg)
        if kind == 1:
            dn_copy(0, seg).wait_recv()
            rows = rows + dn_ra[at, :].astype(f32)
        (dn_a, dn_b, dn_c)[kind][at, :] = rows.astype(bf16)
        dn_copy(kind, seg).start()

    def put_prompt(p, kinds):
        for kind in kinds:

            @pl.when((pos ^ (3, 2, 1)[kind]) == p)
            def _():
                for seg in range(2):
                    put(kind, seg)

    first[3].wait()
    first[4].wait()
    for h in range(OWN):
        w_h[h] = jnp.concatenate(
            [w_s[:, part * SLICE + h * HEAD : part * SLICE + (h + 1) * HEAD] for part in (1, 2, 0)],
            axis=1,
        )
    dq_s[...] = jnp.zeros_like(dq_s)
    dkv_s[...] = jnp.zeros_like(dkv_s)
    for copy in first[:3]:
        copy.wait()

    def turn(h, carry):
        for p in range(GROUP):
            kt_s[h, :, p * TOK : (p + 1) * TOK] = k_s[h, p * TOK : (p + 1) * TOK, :].T[:HEAD]
        return carry

    lax.fori_loop(0, OWN, turn, 0)
    own_do.wait()
    for i in range(1, GROUP):
        do_copy(0, i).wait_recv()
    for copy in f_copies(0):
        copy.wait()
    chip_sum(0)
    chip_sum(1)

    def stage_cont(h, carry):
        prepare(0, h)

        def cont(c, carry):
            rows = pl.multiple_of(c * TOK + PROMPT, CONT)
            code = lines_s[base + c, 1:2, 0:128].astype(f32)
            reach = code[:, 0:1] * 16.0 + code[:, 1:2]
            for p in range(GROUP):
                block(h, p * TOK, PROMPT, rows, T, key_row < reach - p * PROMPT, p * PROMPT)
            pair = block(h, rows, T, rows, T, causal, None)
            dm_s[h, pl.ds(rows, T), : 2 * HEAD] = pair.astype(bf16)
            flush_q(h, rows, T)
            return carry

        lax.fori_loop(0, GROUP, cont, 0)

        for k in range(OWN):

            @pl.when(h == k)
            def _():
                chip_sum(2 + 2 * k)
                chip_sum(3 + 2 * k)

        return carry

    lax.fori_loop(0, OWN, stage_cont, 0)
    ring_step(0)
    for copy in f_copies(1):
        copy.start()
    for copy in a_copies(0):
        copy.wait()
    for kind in (0, 2, 1):
        put(kind, 2)
    lax.fori_loop(0, OWN, lambda h, carry: (add_weight(0, h), carry)[1], 0)
    for copy in a_copies(1):
        copy.start()
    for i in range(1, GROUP):
        do_copy(1, i).wait_recv()
    for copy in f_copies(1):
        copy.wait()

    def stage_last(h, carry):
        prepare(1, h)
        for p in range(3):
            block(h, p * TOK, PROMPT, 3 * TOK, PROMPT, None, p * PROMPT)
        diagonal(h, 3)
        flush(h, 3)

        @pl.when(h == 1)
        def _():
            ring_step(1)

        return carry

    lax.fori_loop(0, OWN, stage_last, 0)
    for copy in f_copies(2):
        copy.start()
    for copy in a_copies(1):
        copy.wait()
    put_prompt(3, (0, 2))
    lax.fori_loop(0, OWN, lambda h, carry: (add_weight(1, h), carry)[1], 0)
    for copy in a_copies(2):
        copy.start()
    put_prompt(3, (1,))
    for copy in f_copies(2):
        copy.wait()

    def stage_first(h, carry):
        prepare(2, h)
        diagonal(h, 0)
        for p in range(1, 3):
            block(h, 0, PROMPT, p * TOK, PROMPT, None, 0)
        flush(h, 0)

        @pl.when(h == 1)
        def _():
            ring_step(2)

        return carry

    lax.fori_loop(0, OWN, stage_first, 0)
    for copy in a_copies(2):
        copy.wait()
    put_prompt(0, (0, 2))
    lax.fori_loop(0, OWN, lambda h, carry: (add_weight(2, h), carry)[1], 0)
    for copy in a_copies(3):
        copy.start()
    put_prompt(0, (1,))
    for copy in a_copies(3):
        copy.wait()

    def stage_middle(h, carry):
        block(h, TOK, PROMPT, 2 * TOK, PROMPT, None, PROMPT)
        diagonal(h, 1)
        flush(h, 1)
        diagonal(h, 2)
        flush(h, 2)
        add_weight(3, h)
        dw = dw_s[h].T
        dw_b[h] = dw.astype(bf16).reshape(GROUP, D // GROUP, W3)
        for i in range(1, GROUP):
            z_copy(h, i).start()
        db = jnp.zeros((1, W3), f32)
        for i in range(GROUP):
            db = db + jnp.sum(dm_s[h, i * TOK : (i + 1) * TOK, :].astype(f32), axis=0, keepdims=True)
        hi = db.astype(bf16)
        mid = (db - hi.astype(f32)).astype(bf16)
        low = (db - hi.astype(f32) - mid.astype(f32)).astype(bf16)
        split = jnp.concatenate([hi, mid, low, jnp.zeros((13, W3), bf16)], axis=0)
        ones = jnp.ones((8, W3), f32)
        gain_rows = lax.dot_general(
            ones,
            w_h[h].astype(f32) * dw,
            (((1,), (1,)), ((), ())),
            precision=lax.Precision.HIGHEST,
            preferred_element_type=f32,
        )
        db_s[h, 0:1, :W3] = db
        db_s[h, 1:2, W3 : W3 + D] = jnp.sum(dot_nt(split, w_h[h]), axis=0, keepdims=True)
        db_s[h, 2:3, W3 : W3 + D] = gain_rows[0:1]

        @pl.when(h == 0)
        def _():
            ring_step(3)

        return carry

    lax.fori_loop(0, OWN, stage_middle, 0)
    inner = lax.rem(pos + 1, GROUP) // 2

    def put_last(kind, side):
        @pl.when(inner == side)
        def _():
            for seg in range(2):
                put(kind, seg)

    put_last(2, 0)
    put_last(0, 1)
    gather_rows(0)
    put_last(1, 0)
    ring_end()
    for copy in later:
        copy.wait()

    rows48 = D // n
    gain = jnp.concatenate([lines_s[d, 0:1, 0:rows48] for d in range(n)], axis=1).astype(f32)
    shift = jnp.concatenate([lines_s[d, 0:1, rows48 : 2 * rows48] for d in range(n)], axis=1).astype(f32)
    d_shift = db_s[0, 1:2, W3 : W3 + D] + db_s[1, 1:2, W3 : W3 + D] + db_s[2, 1:2, W3 : W3 + D]
    d_gain = db_s[0, 2:3, W3 : W3 + D] + db_s[1, 2:3, W3 : W3 + D] + db_s[2, 2:3, W3 : W3 + D]
    blank = jnp.zeros((1, D - SLICE), f32)

    def biases(lo):
        row = jnp.concatenate([db_s[h, 0:1, lo : lo + HEAD] for h in range(OWN)] + [blank], axis=1)
        return pltpu.roll(jnp.broadcast_to(row, (8, D)), pos * SLICE, 1)[0:1]

    sm_b[0] = jnp.concatenate(
        [
            (d_gain - shift * d_shift) / gain,
            d_shift,
            biases(2 * HEAD),
            biases(HEAD),
            sums_s[3:4, :],
            sums_s[1:2, :],
            sums_s[2:3, :],
            sums_s[0:1, :],
        ]
        + [dbf_s[0:1, c * D : (c + 1) * D] for c in range(FF // D)]
        + [jnp.zeros((SMALL - 12, D), f32)],
        axis=0,
    )
    peers = [me ^ 1, me ^ 2, me ^ 4, me ^ 8, other]

    def small_copy(i):
        return remote(sm_b.at[i], sm_r.at[i], s_send.at[i], s_recv.at[i], peers[i])

    def small_step(i):
        small_copy(i).wait_recv()
        sm_b[i + 1] = sm_b[i] + sm_r[i]
        if i < 4:
            small_copy(i + 1).start()

    small_copy(0).start()

    outs = []

    def finish_rows(seg):
        at = slice(seg * T, (seg + 1) * T)
        rows = dn_rows(pos, seg)
        dn_copy(2, seg).wait_recv()
        dn_copy(1, seg).wait_recv()
        n_rows, r = moments(x_s[at, :].astype(f32))
        e = (rows + dn_rb[at, :].astype(f32) + dn_rc[at, :].astype(f32)) * gain
        lean = jnp.mean(e, axis=-1, keepdims=True) + n_rows * jnp.mean(e * n_rows, axis=-1, keepdims=True)
        dh_s[at, :] = dh_s[at, :] + r * (e - lean)
        copy = pltpu.make_async_copy(dh_s.at[at], grad_ref.at[at], out_sem.at[10 + seg])
        copy.start()
        outs.append(copy)

    finish_rows(2)
    gather_rows(1)
    small_step(0)
    trade_rows(0)
    small_step(1)
    gather_rows(2)
    trade_rows(1)
    small_step(2)
    finish_rows(0)
    finish_rows(1)
    trade_rows(2)
    small_step(3)

    small_step(4)
    total = sm_b[5]
    turned = pltpu.roll(total, lax.rem(n - me, n) * rows48, 1)
    eighth = lax.rem(me, 8)
    biased = pltpu.roll(total, lax.rem(8 - eighth, 8) * (2 * rows48), 1)
    quarter = lax.rem(me, 4)
    wide = pltpu.roll(total, lax.rem(4 - quarter, 4) * (4 * rows48), 1)
    row = lax.broadcasted_iota(jnp.int32, (SMALL, D), 0)
    bias_row = jnp.sum(jnp.where(row == 2 + me // 8, biased, 0.0), axis=0, keepdims=True)
    wide_row = jnp.sum(jnp.where(row == 8 + me // 4, wide, 0.0), axis=0, keepdims=True)
    small_copy(0).wait_send()
    sm_b[0] = jnp.where(row == 2, bias_row, jnp.where(row == 3, wide_row, turned))
    copy = pltpu.make_async_copy(sm_b.at[0], small_ref, out_sem.at[2])
    copy.start()
    outs.append(copy)

    for h in range(OWN):
        rep_copy(h).wait_recv()
    for part, (at, piece) in enumerate(((2 * HEAD, 0), (0, 1), (HEAD, 2))):
        row = jnp.concatenate(
            [
                j_r[h, j, :, at : at + HEAD].astype(f32) + rep_r[h, j, :, at : at + HEAD].astype(f32)
                for j in range(GROUP)
                for h in range(OWN)
            ],
            axis=1,
        )
        gq_o[:, piece * D : (piece + 1) * D] = row
    copy = pltpu.make_async_copy(gq_o, gq_ref, out_sem.at[3])
    copy.start()
    outs.append(copy)

    fin_copy.wait_recv()

    def some(at):
        fin_o[at, mine] = fin_b[at, :].astype(f32)
        fin_o[at, rest] = fin_r[at, :].astype(f32)

    rounds(some)
    targets = [(gp_ref, 0, 192), (go_ref, 192, 48)]
    targets += [(gf_ref.at[:, pl.ds(c * D, D)], 240 + 48 * c, 48) for c in range(FF // D)]
    for i, (ref, at, size) in enumerate(targets):
        copy = pltpu.make_async_copy(fin_o.at[pl.ds(at, size)], ref, out_sem.at[4 + i])
        copy.start()
        outs.append(copy)

    for h in range(OWN):
        for i in range(1, GROUP):
            for copy in (z_copy(h, i), j_copy(h, i)):
                copy.wait_send()
    for kind in range(2):
        for i in range(1, GROUP):
            do_copy(kind, i).wait_send()
    for i in range(8):
        y_copy(i).wait_send()
        for copy in near_copies(i):
            copy.wait_send()
    for t in range(4):
        for right in (True, False) if t < 3 else (True,):
            ring_copy(t, right).wait_send()
    for kind in range(3):
        for seg in range(3):
            dn_copy(kind, seg).wait_send()
    for i in range(1, 5):
        small_copy(i).wait_send()
    for h in range(OWN):
        rep_copy(h).wait_send()
    fin_copy.wait_send()
    for copy in outs:
        copy.wait()


def backward(do, q, k, v, f, a, w, x, dh, lines, sums, dbf, dwp, dwo, dwf):
    dma = pltpu.SemaphoreType.DMA
    n = BLOCKS
    shape = jax.ShapeDtypeStruct
    vmem = pltpu.VMEM
    rows = D // n
    head = (OWN, ROWS, 2 * HEAD)
    W3 = 3 * HEAD
    pairs = (OWN, GROUP)
    return pl.pallas_call(
        backward_kernel,
        name="backward",
        out_shape=(
            shape((TOK, D), f32),
            shape((rows, 3 * D), f32),
            shape((FF // n, D), f32),
            shape((rows, D), f32),
            shape((rows, FF), f32),
            shape((SMALL, D), f32),
        ),
        in_specs=[ANY] * 15,
        out_specs=(ANY,) * 6,
        scratch_shapes=[
            vmem((GROUP, OWN, PAIR, 2 * HEAD), bf16),
            vmem(head, bf16),
            vmem(head, bf16),
            vmem(head, bf16),
            vmem((OWN, GROUP * CONT, 2 * HEAD), f32),
            vmem((GROUP * CONT, D), bf16),
            vmem((D, WIDE), bf16),
            vmem((TOK, D), bf16),
            vmem((TOK, D), f32),
            vmem(lines.shape, bf16),
            vmem(sums.shape, f32),
            vmem(dbf.shape, f32),
            vmem((8, UNIT, D), bf16),
            vmem((4, UNIT, D), bf16),
            vmem((8, UNIT, D // 2), bf16),
            vmem((7, UNIT, D // 2), bf16),
            vmem((UNIT, D // 2), bf16),
            vmem((UNIT, D // 2), bf16),
            vmem((UNIT, D), f32),
            vmem(head, bf16),
            vmem((OWN, HEAD, ROWS), f32),
            vmem((OWN, HEAD, ROWS), bf16),
            vmem((OWN, GROUP * PROMPT, 2 * HEAD), f32),
            vmem((OWN, ROWS, W3), bf16),
            vmem((OWN, D, W3), bf16),
            vmem((OWN, W3, D), f32),
            vmem((OWN, 8, W3 + D), f32),
            vmem((OWN, GROUP, D // GROUP, W3), bf16),
            vmem((OWN, GROUP, D // GROUP, W3), bf16),
            vmem((OWN, GROUP, rows, W3), bf16),
            vmem((OWN, GROUP, rows, W3), bf16),
            vmem((OWN, GROUP, rows, W3), bf16),
            vmem((rows, 3 * D), f32),
            vmem((TOK, D), bf16),
            vmem((TOK, D), bf16),
            vmem((TOK, D), bf16),
            vmem((TOK, D), bf16),
            vmem((TOK, D), bf16),
            vmem((TOK, D), bf16),
            vmem((6, SMALL, D), f32),
            vmem((5, SMALL, D), f32),
            dma((10,)),
            dma((3, GROUP)),
            dma((4, GROUP)),
            dma((8, 3)),
            dma((2, GROUP)),
            dma((2, GROUP)),
            dma((8, 3)),
            dma((8, 3)),
            dma((8,)),
            dma((8,)),
            dma((7,)),
            dma((7,)),
            dma,
            dma,
            dma(pairs),
            dma(pairs),
            dma(pairs),
            dma(pairs),
            dma((OWN,)),
            dma((OWN,)),
            dma((3, 3)),
            dma((3, 3)),
            dma((5,)),
            dma((5,)),
            dma((13,)),
        ],
        compiler_params=params(63, collective_id=4, has_side_effects=True),
    )(do, q, k, v, f, a, w, x, dh, lines, sums, dbf, dwp, dwo, dwf)


def land_kernel(sums_ref, *refs):
    sources, targets, rows, held, sem = refs[:5], refs[5:10], refs[10:18], refs[18:23], refs[23]
    parts = []
    for i, ref in enumerate(held):
        count = 4 if i == 0 else 1
        size = ref.shape[0] // count
        parts += [(i, pl.ds(k * size, size)) for k in range(count)]

    def inward(k):
        i, at = parts[k]
        return pltpu.make_async_copy(sources[i].at[at], held[i].at[at], sem.at[0, k])

    def outward(k):
        i, at = parts[k]
        return pltpu.make_async_copy(held[i].at[at], targets[i].at[at], sem.at[1, k])

    for k in range(len(parts)):
        inward(k).start()
    for i, ref in zip((0, 1, 2, 4, 5, 6, 3, 7), rows):
        ref[...] = sums_ref[i, : ref.shape[0]]
    for k in range(len(parts)):
        inward(k).wait()
        outward(k).start()
    for k in range(len(parts)):
        outward(k).wait()


def land(sums, matrices):
    part = D // BLOCKS
    shape = jax.ShapeDtypeStruct
    vector = pl.BlockSpec(memory_space=pltpu.VMEM)
    return pl.pallas_call(
        land_kernel,
        name="land",
        out_shape=tuple(shape(m.shape, f32) for m in matrices)
        + tuple(shape((k * part,), f32) for k in (1, 1, 2, 1, 1, 1, 4, 1)),
        in_specs=[vector] + [ANY] * 5,
        out_specs=(ANY,) * 5 + (vector,) * 8,
        scratch_shapes=[pltpu.VMEM(m.shape, f32) for m in matrices]
        + [pltpu.SemaphoreType.DMA((2, 8))],
        compiler_params=params(60),
    )(sums, *matrices)


def unproject_kernel(dq_ref, dk_ref, dv_ref, a_ref, w_ref, dn_ref, dw_ref, db_ref):
    step = pl.program_id(0)
    mixed = jnp.concatenate(
        [ref[h] for ref in (dq_ref, dk_ref, dv_ref) for h in range(OWN)], axis=1
    )
    dn_ref[...] = dot_nt(mixed, w_ref[...]).astype(bf16)
    dw = dot_tn(a_ref[...], mixed)
    db = jnp.sum(mixed.astype(f32), axis=0, keepdims=True)

    @pl.when(step == 0)
    def _():
        dw_ref[...] = dw
        db_ref[...] = db

    @pl.when(step > 0)
    def _():
        dw_ref[...] += dw
        db_ref[...] += db


def unproject(dq, dk, dv, a, w):
    tile = 768
    head = pl.BlockSpec((OWN, tile, HEAD), lambda i: (0, i, 0))
    whole = lambda i: (0, 0)
    shape = jax.ShapeDtypeStruct
    return pl.pallas_call(
        unproject_kernel,
        name="unproject",
        grid=(ROWS // tile,),
        out_shape=(shape((ROWS, D), bf16), shape((D, WIDE), f32), shape((1, WIDE), f32)),
        in_specs=[
            head, head, head,
            pl.BlockSpec((tile, D), lambda i: (i, 0)),
            pl.BlockSpec((D, WIDE), whole),
        ],
        out_specs=(
            pl.BlockSpec((tile, D), lambda i: (i, 0)),
            pl.BlockSpec((D, WIDE), whole),
            pl.BlockSpec((1, WIDE), whole),
        ),
        compiler_params=params(48),
    )(dq, dk, dv, a, w)


def finish_kernel(x_ref, dh_ref, g_ref, one_ref, two_ref, three_ref, out_ref):
    n, r = moments(x_ref[...].astype(f32))
    dn = one_ref[...].astype(f32) + two_ref[...].astype(f32) + three_ref[...].astype(f32)
    e = dn * g_ref[...]
    lean = jnp.mean(e, axis=-1, keepdims=True) + n * jnp.mean(e * n, axis=-1, keepdims=True)
    out_ref[...] = dh_ref[...] + r * (e - lean)


def finish(x, dh, gain, one, two, three):
    tile = 256
    rows = pl.BlockSpec((tile, D), lambda i: (i, 0))
    return pl.pallas_call(
        finish_kernel,
        name="finish",
        grid=(TOK // tile,),
        out_shape=jax.ShapeDtypeStruct((TOK, D), f32),
        in_specs=[rows, rows, pl.BlockSpec((1, D), lambda i: (0, 0)), rows, rows, rows],
        out_specs=rows,
        compiler_params=params(48),
    )(x, dh, gain, one, two, three)


def flip(block, bit):
    count = lax.axis_size("fsdp")
    return lax.ppermute(block, "fsdp", [(i, i ^ bit) for i in range(count)])


def repack(packed, old, new):
    rows = []
    for left, right, size, at in old:
        rows.append((left, packed[:, :, at : at + size, :HEAD]))
        rows.append((right, packed[:, :, at : at + size, HEAD:]))
    rows = jnp.concatenate([part for _, part in sorted(rows, key=lambda entry: entry[0])], axis=2)
    parts = [
        jnp.concatenate([rows[:, :, left : left + size], rows[:, :, right : right + size]], axis=3)
        for left, right, size, _ in sorted(new, key=lambda entry: entry[3])
    ]
    return jnp.concatenate(parts, axis=2)


def over_replicas(block):
    count = lax.axis_size("rep")
    held = lax.optimization_barrier(block)
    if count == 2:
        other = lax.ppermute(held, "rep", [(0, 1), (1, 0)])
        return held.astype(f32) + other.astype(f32)
    return lax.psum(held.astype(f32), "rep")


def body(
    block_input, cotangent, tie_index, prefix_len, pre_gain, pre_shift, w_qkv, b_qv, w_out, b_out,
    mid_gain, mid_shift, w_fc, b_fc, w_proj, b_proj,
):
    n = lax.axis_size("fsdp")
    me = lax.axis_index("fsdp")
    pos = lax.rem(me, GROUP)
    rows = D // n
    index = tie_index[0]

    def chosen(bank):
        return lax.dynamic_index_in_dim(bank, index, 0, keepdims=False)

    vectors = (pre_gain, pre_shift, b_qv, b_out, mid_gain, mid_shift, b_fc, b_proj)
    sizes = [bank.shape[1] for bank in vectors]
    count = sum(sizes)
    high = -(-(rows + 2) // 16) * 16
    cuts = [sum(sizes[:i]) for i in range(len(sizes) + 1)]

    def vectors_of(lines):
        smalls = lines[:, 0, :count].astype(f32)
        group_rows = lax.dynamic_slice_in_dim(lines[:, 1, :2], me - pos, GROUP, 0)
        reaches = group_rows[:, 0].astype(f32) * 16 + group_rows[:, 1].astype(f32)
        return [
            smalls[:, cuts[i] : cuts[i + 1]].reshape(1, -1) for i in range(len(sizes))
        ], reaches.astype(jnp.int32)

    fused = n == BLOCKS and lax.axis_size("rep") == 2
    if fused:
        small, pieces, shard = pick(tie_index, prefix_len, vectors, w_qkv, w_out, w_fc, w_proj)
        wall, lines, wq, a_low, qx, k, v, o_full, o_recv = forward(block_input, small, pieces, shard)
        a_low = a_low.reshape(ROWS, D)
    else:
        small = jnp.concatenate([chosen(bank) for bank in vectors])
        reach = prefix_len[0]
        reach_row = jnp.concatenate([reach // 16, reach % 16]).astype(bf16)
        wq = chosen(w_qkv).reshape(rows, 3, GROUP, SLICE).transpose(2, 0, 1, 3)
        wq = wq.reshape(GROUP, rows, WIDE)
        extra = jnp.stack([jnp.pad(line, (0, WIDE - line.shape[0])) for line in (small, reach_row)])
        wo, wf, wp = chosen(w_out), chosen(w_fc), chosen(w_proj)
        extra = jnp.pad(extra, ((0, high - rows - 2), (0, 0)))
        pieces = jnp.concatenate([wq, jnp.broadcast_to(extra, (GROUP,) + extra.shape)], axis=1)
        wo = lax.all_gather(wo, "fsdp", axis=0, tiled=True).reshape(BLOCKS, -1, D)
        wf = lax.all_gather(wf, "fsdp", axis=0, tiled=True)
        wf = wf.reshape(BLOCKS, D // BLOCKS, FF // D, D).transpose(0, 2, 1, 3)
        wp = lax.all_gather(wp, "fsdp", axis=0, tiled=True).reshape(BLOCKS, -1, D)
        wall = jnp.concatenate([wp, wo, wf.reshape(BLOCKS, -1, D)], axis=1)
        xg, wg = gather_group(n, block_input, pieces)
        wq = wg[:, :rows].reshape(D, WIDE)
        found, reaches = vectors_of(wg[:, rows : rows + 2])
        g1, s1, bqv = found[:3]
        lines = jnp.concatenate([row.reshape(BLOCKS, -1) for row in found], axis=1).astype(bf16)
        lines = jnp.pad(lines[:, None], ((0, 0), (0, 1), (0, 640 - lines.shape[1])))
        own_bias = lax.dynamic_index_in_dim(bqv.reshape(2, GROUP, SLICE), pos, 1, keepdims=False)
        bias = jnp.concatenate([own_bias[0], jnp.zeros((SLICE,), f32), own_bias[1]])[None]
        a_low, q, k, v = project(xg.reshape(ROWS, D), wq, g1, s1, bias)
        o_send, o_full, qx = attend(reaches, q, k, v)
        o_recv = repack(swap(o_send, 1, "swap_o"), ((0, 384, 384, 0),), PACK)

    y, dwf, dwp, dbf, dwo, dh, do_send, sums = middle(
        block_input, o_recv, cotangent, wall, lines
    )
    if fused:
        grad, dwq, dwp, dwo, dwf, sums = backward(
            do_send, qx, k, v, o_full, a_low, wq, block_input, dh, lines, sums, dbf,
            dwp.reshape(BLOCKS, -1, D), dwo.reshape(BLOCKS, -1, D), dwf.reshape(BLOCKS, -1, D),
        )
        landed = land(sums, (grad, dwq, dwo, dwf, dwp))
        grad, dwq, dwo, dwf, dwp, dg1, ds1, dbqv, dbo, dg2, ds2, dbf, dbp = landed
        return (y, grad, dg1, ds1, dwq, dbqv, dwo, dbo, dg2, ds2, dwf, dbf, dwp, dbp)
    dwf = dwf.transpose(0, 2, 1, 3).reshape(D, FF)
    dwf = lax.psum_scatter(dwf, "fsdp", scatter_dimension=0, tiled=True)
    dwp = lax.psum_scatter(dwp, "fsdp", scatter_dimension=0, tiled=True)
    dwo = lax.psum_scatter(dwo, "fsdp", scatter_dimension=0, tiled=True)
    do_recv = repack(swap(do_send, 2, "swap_do"), PACK, ((0, 384, 384, 0),))
    dq, dk, dv = attend_back(reaches, qx, k, v, o_full, do_recv)
    dn, dwq, db = unproject(dq, dk, dv, a_low, wq)

    dn = dn.reshape(GROUP, TOK, D)
    block_of = lambda bit: lax.dynamic_index_in_dim(dn, pos ^ bit, 0, keepdims=False)
    beside = flip(block_of(1), 1)
    across = flip(block_of(3), 1)
    across = flip((across.astype(f32) + block_of(2).astype(f32)).astype(bf16), 2)

    wq_wide = wq.astype(f32)
    dshift = jnp.sum(wq_wide * db, axis=1)
    dgain = jnp.sum(wq_wide * (dwq - s1.reshape(D, 1) * db), axis=1) / g1.reshape(D)
    where = (jnp.arange(GROUP) == pos).astype(f32)[:, None]
    dbias = jnp.concatenate(
        [(where * db[:, :SLICE]).reshape(-1), (where * db[:, 2 * SLICE :]).reshape(-1)]
    )
    line = jnp.concatenate(
        [
            part.reshape(n, -1)
            for part in (dgain, dshift, dbias, sums[3], sums[1], sums[2], dbf, sums[0])
        ],
        axis=1,
    )
    line_hi = line.astype(bf16)
    line_low = (line - lax.reduce_precision(line, 8, 7)).astype(bf16)
    lines = jnp.pad(jnp.stack([line_hi, line_low], axis=1), ((0, 0), (0, 0), (0, WIDE - count)))
    lines = jnp.pad(lines, ((0, 0), (0, high - rows - 2), (0, 0)))
    back = jnp.concatenate([dwq.astype(bf16).reshape(n, rows, WIDE), lines], axis=1)
    back = swap(back, 3, "swap_grad")
    dwq = jnp.sum(back[:, :rows].astype(f32).reshape(n // GROUP, GROUP, rows, 3, SLICE), axis=0)
    dwq = dwq.transpose(1, 2, 0, 3).reshape(rows, 3 * D)
    line = jnp.sum(back[:, rows, :count].astype(f32) + back[:, rows + 1, :count].astype(f32), axis=0)

    grad = finish(block_input, dh, g1, block_of(0), beside, across)
    dwq = over_replicas(dwq.astype(bf16))
    dwo, dwf, dwp = over_replicas(dwo), over_replicas(dwf), over_replicas(dwp)
    line = over_replicas(line)
    dg1, ds1, dbqv, dbo, dg2, ds2, dbf, dbp = (
        line[cuts[i] : cuts[i + 1]] for i in range(len(sizes))
    )
    return (y, grad, dg1, ds1, dwq, dbqv, dwo, dbo, dg2, ds2, dwf, dbf, dwp, dbp)


def solution(mesh):
    tokens = P(("rep", "fsdp"), None)
    vector, matrix = P(None, "fsdp"), P(None, "fsdp", None)
    return jax.shard_map(
        body,
        mesh=mesh,
        in_specs=(
            tokens, tokens, P(), tokens, vector, vector, matrix, vector, matrix, vector,
            vector, vector, matrix, vector, matrix, vector,
        ),
        out_specs=(
            tokens, tokens, P("fsdp"), P("fsdp"), P("fsdp", None), P("fsdp"), P("fsdp", None),
            P("fsdp"), P("fsdp"), P("fsdp"), P("fsdp", None), P("fsdp"), P("fsdp", None), P("fsdp"),
        ),
        check_vma=False,
    )
```

```python
from functools import partial

import jax
import jax.numpy as jnp
from jax import lax
from jax.experimental import pallas as pl
from jax.experimental.pallas import tpu as pltpu
from jax.sharding import PartitionSpec as P

D = 768
HEADS = 12
HEAD = 64
FF = 3072
GROUP = 4
PROMPT = 512
CONT = 256
TOK = 768
ROWS = GROUP * TOK
OWN = HEADS // GROUP
SLICE = OWN * HEAD
WIDE = 3 * SLICE
PAIR = TOK // 2
CHUNK = 768
BLOCKS = 16
UNIT = 432
NEG = -1e30
EPS = 1e-5
PACK = ((512, 640, 128, 0), (0, 256, 256, 128))
GELU_A = 0.7978845608028654
GELU_B = 0.044715

f32 = jnp.float32
bf16 = jnp.bfloat16
MESH = pl.DeviceIdType.MESH
ANY = pl.BlockSpec(memory_space=pl.ANY)


def params(mib, **more):
    return pltpu.CompilerParams(vmem_limit_bytes=mib << 20, **more)


def dot(a, b):
    return jnp.dot(a, b, preferred_element_type=f32)


def dot_nt(a, b):
    return lax.dot_general(a, b, (((1,), (1,)), ((), ())), preferred_element_type=f32)


def dot_tn(a, b):
    return lax.dot_general(a, b, (((0,), (0,)), ((), ())), preferred_element_type=f32)


def moments(x):
    center = x - jnp.mean(x, axis=-1, keepdims=True)
    scale = lax.rsqrt(jnp.mean(center * center, axis=-1, keepdims=True) + EPS)
    return center * scale, scale


def greet(peers, replica=None):
    sem = pltpu.get_barrier_semaphore()
    for peer in peers:
        pl.semaphore_signal(sem, inc=1, device_id={"fsdp": peer}, device_id_type=MESH)
    if replica is not None:
        pl.semaphore_signal(sem, inc=1, device_id={"rep": replica}, device_id_type=MESH)
    pl.semaphore_wait(sem, len(peers) + (replica is not None))


def gather_kernel(n, parts, x_ref, w_ref, xg_ref, wg_ref, xs, xr, ws, wr, local):
    me = lax.axis_index("fsdp")
    pos = lax.rem(me, GROUP)
    near, far = me ^ 1, me ^ 2
    greet([me ^ i for i in range(1, n)])
    own = pltpu.make_async_copy(x_ref, xg_ref.at[pos], local.at[0])
    own.start()
    own_w = pltpu.make_async_copy(w_ref.at[pos], wg_ref.at[me], local.at[1])
    own_w.start()
    rows = TOK // parts

    def piece(src, slot, part, i, peer):
        at = pl.ds(part * rows, rows)
        return pltpu.make_async_remote_copy(
            src_ref=src.at[at],
            dst_ref=xg_ref.at[slot, at],
            send_sem=xs.at[i],
            recv_sem=xr.at[i],
            device_id={"fsdp": peer},
            device_id_type=MESH,
        )

    across = [piece(x_ref, pos, part, part, far) for part in range(parts)]
    for copy in across:
        copy.start()
    beside = pltpu.make_async_remote_copy(
        src_ref=x_ref,
        dst_ref=xg_ref.at[pos],
        send_sem=xs.at[2 * parts],
        recv_sem=xr.at[2 * parts],
        device_id={"fsdp": near},
        device_id_type=MESH,
    )
    beside.start()
    slices = []
    for i in range(1, n):
        peer = me ^ i
        copy = pltpu.make_async_remote_copy(
            src_ref=w_ref.at[lax.rem(peer, GROUP)],
            dst_ref=wg_ref.at[me],
            send_sem=ws.at[i],
            recv_sem=wr.at[i],
            device_id={"fsdp": peer},
            device_id_type=MESH,
        )
        copy.start()
        slices.append(copy)
    passed = []
    for part in range(parts):
        across[part].wait_recv()
        copy = piece(xg_ref.at[pos ^ 2], pos ^ 2, part, parts + part, near)
        copy.start()
        passed.append(copy)
    for copy in across:
        copy.wait_send()
    beside.wait()
    own.wait()
    own_w.wait()
    for copy in passed + slices:
        copy.wait()


def gather_group(n, x, pieces):
    parts = 4
    dma = pltpu.SemaphoreType.DMA
    return pl.pallas_call(
        partial(gather_kernel, n, parts),
        name="gather_group",
        out_shape=(
            jax.ShapeDtypeStruct((GROUP,) + x.shape, x.dtype),
            jax.ShapeDtypeStruct((n,) + pieces.shape[1:], pieces.dtype),
        ),
        in_specs=[ANY, ANY],
        out_specs=(ANY, ANY),
        scratch_shapes=[
            dma((2 * parts + 1,)),
            dma((2 * parts + 1,)),
            dma((n,)),
            dma((n,)),
            dma((2,)),
        ],
        compiler_params=params(32, collective_id=0, has_side_effects=True),
    )(x, pieces)


def swap_kernel(count, x_ref, o_ref, send, recv, local):
    me = lax.axis_index("fsdp")
    greet([me ^ i for i in range(1, count)])
    slot = lax.rem(me, count)
    own = pltpu.make_async_copy(x_ref.at[slot], o_ref.at[slot], local)
    own.start()
    copies = []
    for i in range(1, count):
        copy = pltpu.make_async_remote_copy(
            src_ref=x_ref.at[slot ^ i],
            dst_ref=o_ref.at[slot],
            send_sem=send.at[i],
            recv_sem=recv.at[i],
            device_id={"fsdp": me ^ i},
            device_id_type=MESH,
        )
        copy.start()
        copies.append(copy)
    own.wait()
    for copy in copies:
        copy.wait()


def swap(x, collective_id, name):
    count = x.shape[0]
    dma = pltpu.SemaphoreType.DMA
    return pl.pallas_call(
        partial(swap_kernel, count),
        name=name,
        out_shape=jax.ShapeDtypeStruct(x.shape, x.dtype),
        in_specs=[ANY],
        out_specs=ANY,
        scratch_shapes=[dma((count,)), dma((count,)), dma],
        compiler_params=params(32, collective_id=collective_id, has_side_effects=True),
    )(x)


def project_kernel(x_ref, w_ref, g_ref, s_ref, b_ref, a_ref, q_ref, k_ref, v_ref):
    n, _ = moments(x_ref[...].astype(f32))
    a_low = (n * g_ref[...] + s_ref[...]).astype(bf16)
    a_ref[...] = a_low
    mixed = (dot(a_low, w_ref[...]) + b_ref[...]).astype(bf16)
    ones = jnp.ones((x_ref.shape[0], HEAD), bf16)
    for h in range(OWN):
        q = mixed[:, h * HEAD : (h + 1) * HEAD] * 0.125
        k = mixed[:, SLICE + h * HEAD : SLICE + (h + 1) * HEAD]
        v = mixed[:, 2 * SLICE + h * HEAD : 2 * SLICE + (h + 1) * HEAD]
        q_ref[h] = jnp.concatenate([q.astype(bf16), jnp.zeros_like(ones)], axis=1)
        k_ref[h] = jnp.concatenate([k, ones], axis=1)
        v_ref[h] = jnp.concatenate([v, ones], axis=1)


def project(x, w, gain, shift, bias):
    tile = 384
    heads = jax.ShapeDtypeStruct((OWN, ROWS, 2 * HEAD), bf16)
    head_spec = pl.BlockSpec((OWN, tile, 2 * HEAD), lambda i: (0, i, 0))
    whole = lambda i: (0, 0)
    return pl.pallas_call(
        project_kernel,
        name="project",
        grid=(ROWS // tile,),
        out_shape=(jax.ShapeDtypeStruct((ROWS, D), bf16), heads, heads, heads),
        in_specs=[
            pl.BlockSpec((tile, D), lambda i: (i, 0)),
            pl.BlockSpec((D, WIDE), whole),
            pl.BlockSpec((1, D), whole),
            pl.BlockSpec((1, D), whole),
            pl.BlockSpec((1, WIDE), whole),
        ],
        out_specs=(pl.BlockSpec((tile, D), lambda i: (i, 0)), head_spec, head_spec, head_spec),
        compiler_params=params(48),
    )(x, w, gain, shift, bias)


def lanes(rows):
    return lax.broadcasted_iota(jnp.int32, (rows, 2 * HEAD), 1)


def split_columns(base, lane, column):
    hi = column.astype(bf16).astype(f32)
    mid = (column - hi).astype(bf16).astype(f32)
    low = column - hi - mid
    tail = jnp.where(lane == HEAD, -hi, jnp.where(lane == HEAD + 1, -mid, -low))
    return jnp.where(lane < HEAD, base, jnp.where(lane < HEAD + 3, tail, 0.0)).astype(bf16)


def below(rows, cols, low_key):
    row = lax.broadcasted_iota(jnp.int32, (rows, cols), 0)
    col = lax.broadcasted_iota(jnp.int32, (rows, cols), 1)
    return row <= col if low_key else col <= row


def attend_kernel(reach_ref, q_ref, k_ref, v_ref, o_ref, f_ref, x_ref):
    T = CONT
    lane = lanes(T)
    causal = below(T, T, False)

    def tile(at, blocks):
        q = q_ref[0, pl.ds(at, T), :]
        scores = []
        for start, size, mask in blocks:
            s = dot_nt(q, k_ref[0, pl.ds(start, size), :])
            scores.append(s if mask is None else jnp.where(mask, s, NEG))
        peak = scores[0].max(axis=1, keepdims=True)
        for s in scores[1:]:
            peak = jnp.maximum(peak, s.max(axis=1, keepdims=True))
        total = jnp.zeros((T, 2 * HEAD), f32)
        for s, (start, size, _) in zip(scores, blocks):
            total += dot(jnp.exp(s - peak).astype(bf16), v_ref[0, pl.ds(start, size), :])
        mass = total[:, HEAD : HEAD + 1]
        f_ref[0, pl.ds(at, T), :] = total / mass
        lse = peak + jnp.log(mass)
        x_ref[0, pl.ds(at, T), :] = split_columns(q.astype(f32), lane, lse)

    for p in range(GROUP):
        past = [(i * TOK, PROMPT, None) for i in range(p)]
        base = p * TOK
        tile(base, past + [(base, T, causal)])
        tile(base + T, past + [(base, T, None), (base + T, T, causal)])

    def cont(c, carry):
        at = pl.multiple_of(c * TOK + PROMPT, CONT)
        reach = reach_ref[c]
        col = lax.broadcasted_iota(jnp.int32, (T, PROMPT), 1)
        blocks = [(i * TOK, PROMPT, col < reach - i * PROMPT) for i in range(GROUP)]
        tile(at, blocks + [(at, T, causal)])
        return carry

    lax.fori_loop(0, GROUP, cont, 0)

    half = lanes(PAIR) < HEAD
    for p in range(GROUP):
        top = f_ref[0, p * TOK : p * TOK + PAIR, :]
        low = f_ref[0, p * TOK + PAIR : (p + 1) * TOK, :]
        o_ref[p, 0] = jnp.where(half, top, pltpu.roll(low, HEAD, 1)).astype(bf16)


def attend(reach, q, k, v):
    head = lambda h: (h, 0, 0)
    spec = pl.BlockSpec((1, ROWS, 2 * HEAD), head)
    return pl.pallas_call(
        attend_kernel,
        name="attend",
        grid=(OWN,),
        out_shape=(
            jax.ShapeDtypeStruct((GROUP, OWN, PAIR, 2 * HEAD), bf16),
            jax.ShapeDtypeStruct((OWN, ROWS, 2 * HEAD), f32),
            jax.ShapeDtypeStruct((OWN, ROWS, 2 * HEAD), bf16),
        ),
        in_specs=[pl.BlockSpec(memory_space=pltpu.SMEM), spec, spec, spec],
        out_specs=(
            pl.BlockSpec((GROUP, 1, PAIR, 2 * HEAD), lambda h: (0, h, 0, 0)),
            spec,
            spec,
        ),
        compiler_params=params(56),
    )(reach, q, k, v)


def attend_back_kernel(
    reach_ref, q_ref, k_ref, v_ref, f_ref, g_ref, dq_ref, dk_ref, dv_ref, g_s, dq_s, kt_s, dk_s, dv_s
):
    T = CONT
    half = lanes(PAIR) < HEAD
    lane = lanes(PAIR)
    for p in range(GROUP):
        packed = g_ref[p, 0].astype(f32)
        for i, block in enumerate((packed, pltpu.roll(packed, HEAD, 1))):
            at = p * TOK + i * PAIR
            prod = jnp.where(half, block * f_ref[0, at : at + PAIR, :], 0.0)
            inner = jnp.sum(prod, axis=1, keepdims=True)
            g_s[at : at + PAIR, :] = split_columns(block, lane, inner)
        kt_s[:, p * TOK : (p + 1) * TOK] = k_ref[0, p * TOK : (p + 1) * TOK, :].T[:HEAD]
    dq_s[...] = jnp.zeros_like(dq_s)

    def block(keys, size, rows, count, mask, first, key_at):
        kb = k_ref[0, pl.ds(keys, size), :]
        vb = v_ref[0, pl.ds(keys, size), :]
        q = q_ref[0, pl.ds(rows, count), :]
        g = g_s[pl.ds(rows, count), :]
        probs = jnp.exp(dot_nt(kb, q))
        if mask is not None:
            probs = jnp.where(mask, probs, 0.0)
        ds = (probs * dot_nt(vb, g)).astype(bf16)
        dv = dot(probs.astype(bf16), g)
        dk = dot(ds, q)
        at = pl.ds(key_at, size)
        dv_s[at, :] = dv if first else dv_s[at, :] + dv
        dk_s[at, :] = dk if first else dk_s[at, :] + dk
        dq_s[:, pl.ds(rows, count)] += dot(kt_s[:, pl.ds(keys, size)], ds)

    causal = below(T, T, True)
    for p in range(GROUP):
        base = p * TOK
        block(base, T, base, T, causal, True, 0)
        block(base + T, T, base + T, T, causal, True, T)
        block(base, T, base + T, T, None, False, 0)

        def later(i, carry):
            rows = pl.multiple_of(i * TOK, CONT)
            block(base, PROMPT, rows, PROMPT, None, False, 0)
            return carry

        lax.fori_loop(p + 1, GROUP, later, 0)

        def cont(c, carry):
            rows = pl.multiple_of(c * TOK + PROMPT, CONT)
            key = lax.broadcasted_iota(jnp.int32, (PROMPT, T), 0)
            block(base, PROMPT, rows, T, key < reach_ref[c] - p * PROMPT, False, 0)
            return carry

        lax.fori_loop(0, GROUP, cont, 0)
        dk_ref[0, base : base + PROMPT, :] = dk_s[:, :HEAD].astype(bf16)
        dv_ref[0, base : base + PROMPT, :] = dv_s[:, :HEAD].astype(bf16)

    def own(c, carry):
        at = pl.multiple_of(c * TOK + PROMPT, CONT)
        block(at, T, at, T, causal, True, 0)
        dk_ref[0, pl.ds(at, T), :] = dk_s[:T, :HEAD].astype(bf16)
        dv_ref[0, pl.ds(at, T), :] = dv_s[:T, :HEAD].astype(bf16)
        return carry

    lax.fori_loop(0, GROUP, own, 0)
    for i in range(ROWS // PROMPT):
        at = i * PROMPT
        dq_ref[0, at : at + PROMPT, :] = (dq_s[:, at : at + PROMPT].T * 0.125).astype(bf16)


def attend_back(reach, q, k, v, f, g):
    head = lambda h: (h, 0, 0)
    spec = pl.BlockSpec((1, ROWS, 2 * HEAD), head)
    out = jax.ShapeDtypeStruct((OWN, ROWS, HEAD), bf16)
    out_spec = pl.BlockSpec((1, ROWS, HEAD), head)
    return pl.pallas_call(
        attend_back_kernel,
        name="attend_back",
        grid=(OWN,),
        out_shape=(out, out, out),
        in_specs=[pl.BlockSpec(memory_space=pltpu.SMEM), spec, spec, spec, spec]
        + [pl.BlockSpec((GROUP, 1, PAIR, 2 * HEAD), lambda h: (0, h, 0, 0))],
        out_specs=(out_spec, out_spec, out_spec),
        scratch_shapes=[
            pltpu.VMEM((ROWS, 2 * HEAD), bf16),
            pltpu.VMEM((HEAD, ROWS), f32),
            pltpu.VMEM((HEAD, ROWS), bf16),
            pltpu.VMEM((PROMPT, 2 * HEAD), f32),
            pltpu.VMEM((PROMPT, 2 * HEAD), f32),
        ],
        compiler_params=params(56),
    )(reach, q, k, v, f, g)


def pick_kernel(index_ref, reach_ref, *refs):
    vectors, (wq_ref, wo_ref, wf_ref, wp_ref), (small_ref, piece_ref, shard_ref) = (
        refs[:8], refs[8:12], refs[12:],
    )
    index = index_ref[0]
    rows = []
    for ref in vectors:
        bank = ref[...].astype(f32)
        chosen = lax.broadcasted_iota(jnp.int32, bank.shape, 0) == index
        rows.append(jnp.sum(jnp.where(chosen, bank, 0.0), axis=0, keepdims=True))
    width = sum(row.shape[1] for row in rows)
    rest = small_ref.shape[1] - width
    small_ref[0:1, :] = jnp.concatenate(rows + [jnp.zeros((1, rest), f32)], axis=1).astype(bf16)
    reach = reach_ref[0, 0]
    lane = lax.broadcasted_iota(jnp.int32, (1, small_ref.shape[1]), 1)
    code = jnp.where(lane == 0, reach // 16, jnp.where(lane == 1, lax.rem(reach, 16), 0))
    small_ref[1:2, :] = code.astype(f32).astype(bf16)
    for j in range(GROUP):
        for part in range(3):
            at = part * D + j * SLICE
            piece_ref[j, :, part * SLICE : (part + 1) * SLICE] = wq_ref[0, :, at : at + SLICE]
    shard_ref[:192, :] = wp_ref[0]
    shard_ref[192:240, :] = wo_ref[0]
    for c in range(FF // D):
        shard_ref[240 + 48 * c : 288 + 48 * c, :] = wf_ref[0, :, c * D : (c + 1) * D]


def pick(index, reach, vectors, wq, wo, wf, wp):
    shape = jax.ShapeDtypeStruct
    chosen = lambda bank: pl.BlockSpec((1,) + bank.shape[1:], lambda i, at: (at[0], 0, 0))
    whole = lambda bank: pl.BlockSpec(bank.shape, lambda i, at: (0, 0))
    fixed3 = lambda i, at: (0, 0, 0)
    return pl.pallas_call(
        pick_kernel,
        name="pick",
        out_shape=(
            shape((2, 640), bf16), shape((GROUP, D // BLOCKS, WIDE), bf16), shape((UNIT, D), bf16),
        ),
        grid_spec=pltpu.PrefetchScalarGridSpec(
            num_scalar_prefetch=1,
            grid=(1,),
            in_specs=[pl.BlockSpec(memory_space=pltpu.SMEM)]
            + [whole(bank) for bank in vectors]
            + [chosen(bank) for bank in (wq, wo, wf, wp)],
            out_specs=(
                pl.BlockSpec((2, 640), lambda i, at: (0, 0)),
                pl.BlockSpec((GROUP, D // BLOCKS, WIDE), fixed3),
                pl.BlockSpec((UNIT, D), lambda i, at: (0, 0)),
            ),
        ),
        compiler_params=params(60),
    )(index, reach, *vectors, wq, wo, wf, wp)


def ring_of(me):
    chip, core = me // 2, lax.rem(me, 2)
    z, x = chip // 2, lax.rem(chip, 2)
    chips = BLOCKS // 2
    half = chips // 2
    place = z * (1 - x) + (chips - 1 - z) * x

    def device(at):
        at = lax.rem(at + 2 * chips, chips)
        side = at // half
        z_at = at * (1 - side) + (chips - 1 - at) * side
        return (z_at * 2 + side) * 2 + core

    return place, device


def forward_kernel(
    x_ref, sm_ref, pc_ref, sh_ref,
    wall_ref, smo_ref, wq_ref, a_ref, q_ref, k_ref, v_ref, f_ref, o_ref,
    xg, smg, wg, w_s, q_s, k_s, v_s, f_s, o_s, sh_s,
    local, sm_send, sm_recv, w_send, w_recv, x_send, x_recv, r_send, r_recv, n_send, n_recv,
    y_send, y_recv, o_send, o_recv, out_sem,
):
    n = BLOCKS
    me = lax.axis_index("fsdp")
    rep = lax.axis_index("rep")
    pos = lax.rem(me, GROUP)
    base = me - pos
    near, far = me ^ 1, me ^ 2
    level, xside = me // GROUP, lax.rem(me, GROUP) // 2
    core = lax.rem(me, 2)
    levels = n // GROUP
    parts = TOK // CONT
    part_rows = CONT
    T = CONT

    def remote(src, dst, send, recv, peer):
        return pltpu.make_async_remote_copy(
            src_ref=src,
            dst_ref=dst,
            send_sem=send,
            recv_sem=recv,
            device_id=peer if isinstance(peer, dict) else {"fsdp": peer},
            device_id_type=MESH,
        )

    greet([me ^ i for i in range(1, n)], 1 - rep)

    own_block = pltpu.make_async_copy(sh_ref, sh_s, local.at[0])
    own_store = pltpu.make_async_copy(sh_s, wall_ref.at[me], local.at[4])
    own_x = pltpu.make_async_copy(x_ref, xg.at[pos], local.at[1])
    own_w = pltpu.make_async_copy(pc_ref.at[pos], wg.at[me], local.at[2])
    own_s = pltpu.make_async_copy(sm_ref, smg.at[me], local.at[3])
    for copy in (own_s, own_w, own_x, own_block):
        copy.start()

    slices = []
    for i in range(1, GROUP):
        copy = remote(pc_ref.at[pos ^ i], wg.at[me], w_send.at[i], w_recv.at[i], me ^ i)
        copy.start()
        slices.append(copy)
    smalls = []
    for i in range(1, n):
        copy = remote(sm_ref, smg.at[me], sm_send.at[i], sm_recv.at[i], me ^ i)
        copy.start()
        smalls.append(copy)
    beside = remote(x_ref, xg.at[pos], x_send.at[2 * parts], x_recv.at[2 * parts], near)
    beside.start()

    def x_part(src, slot, part, i, peer):
        at = pl.ds(part * part_rows, part_rows)
        return remote(src.at[at], xg.at[slot, at], x_send.at[i], x_recv.at[i], peer)

    across = [x_part(x_ref, pos, part, part, far) for part in range(parts)]
    own_block.wait()
    own_store.start()
    mine = pl.ds(pl.multiple_of(rep * (D // 2), D // 2), D // 2)
    other = pl.ds(pl.multiple_of((1 - rep) * (D // 2), D // 2), D // 2)
    hops, sent, shared = [], [], []

    def begin(copy, keep):
        copy.start()
        keep.append((None, copy))

    def block_of(stream, at):
        side = xside if stream == 0 else 1 - xside
        return (at * 2 + side) * 2 + core

    def slot(stream, t, up):
        return 6 * stream + 2 * t + (0 if up else 1)

    def sends(t, up):
        return (level >= t) & (level < levels - 1) if up else (level + t < levels) & (level > 0)

    def comes(t, up):
        return level > t if up else level + t < levels - 1

    def when(cond, keep, copies):
        @pl.when(cond)
        def _():
            for copy in copies:
                copy.start()

        keep.extend((cond, copy) for copy in copies)

    def hop(stream, t, up):
        at = block_of(stream, level - t if up else level + t)
        block = wall_ref.at[at, :, mine]
        src = sh_s.at[:, mine] if stream == 0 and t == 0 else block
        i = slot(stream, t, up)
        return remote(src, block, r_send.at[i], r_recv.at[i], me + GROUP if up else me - GROUP)

    def to_near(d, columns, i):
        block = wall_ref.at[d, :, columns]
        return remote(block, block, n_send.at[i], n_recv.at[i], near)

    def to_replica(d, columns, i):
        block = wall_ref.at[d, :, columns]
        return remote(block, block, y_send.at[i], y_recv.at[i], {"rep": 1 - rep})

    def launch(stream, t):
        for up in (True, False):
            when(sends(t, up), hops, [hop(stream, t, up)])

    def came(stream, t, up):
        return block_of(stream, level - 1 - t if up else level + 1 + t)

    def arrive(stream, t):
        for up in (True, False):
            copy = hop(stream, t, up)

            @pl.when(comes(t, up))
            def _():
                copy.wait_recv()

        if t < levels - 2:
            launch(stream, t + 1)
        for up in (True, False):
            d, i = came(stream, t, up), slot(stream, t, up)
            when(comes(t, up), sent, [to_replica(d, mine, i)])
            when(comes(t, up), shared, [to_near(d, mine, 1 + i)])

    def settle(stream, t):
        for up in (True, False):
            d, i = came(stream, t, up), slot(stream, t, up)
            copy = to_replica(d, other, i)

            @pl.when(comes(t, up))
            def _():
                copy.wait_recv()

            when(comes(t, up), shared, [to_near(d, other, 14 + i)])

    facing = block_of(1, level)
    cross = remote(sh_s.at[:, mine], wall_ref.at[me, :, mine], r_send.at[12], r_recv.at[12], far)
    crossed = remote(wall_ref.at[facing, :, mine], wall_ref.at[facing, :, mine], r_send.at[12], r_recv.at[12], far)

    def arrive_across():
        crossed.wait_recv()
        launch(1, 0)
        begin(to_replica(facing, mine, 12), sent)
        begin(to_near(facing, mine, 13), shared)

    def settle_across():
        to_replica(facing, other, 12).wait_recv()
        begin(to_near(facing, other, 26), shared)

    def drain(kept, both):
        for cond, copy in kept:
            if cond is None:
                copy.wait() if both else copy.wait_send()
            else:

                @pl.when(cond)
                def _():
                    copy.wait() if both else copy.wait_send()

    cross.start()
    for copy in across:
        copy.start()
    launch(0, 0)
    begin(remote(sh_s, wall_ref.at[me], n_send.at[0], n_recv.at[0], near), shared)

    own_s.wait()
    for copy in smalls:
        copy.wait_recv()
    rows48 = D // n
    gain = jnp.concatenate([smg[d, 0:1, 0:rows48] for d in range(n)], axis=1).astype(f32)
    shift = jnp.concatenate([smg[d, 0:1, rows48 : 2 * rows48] for d in range(n)], axis=1).astype(f32)
    at = 2 * rows48
    two = 2 * rows48
    zeros = jnp.zeros((1, SLICE), bf16)
    bias = jnp.concatenate(
        [smg[2 * pos + i, 0:1, at : at + two] for i in range(2)]
        + [zeros]
        + [smg[n // 2 + 2 * pos + i, 0:1, at : at + two] for i in range(2)],
        axis=1,
    ).astype(f32)

    def norm(slot, lo, hi):
        def some(i, carry):
            at = pl.ds(pl.multiple_of(i * T, T), T)
            n_rows, _ = moments(xg[slot, at, :].astype(f32))
            xg[slot, at, :] = (n_rows * gain + shift).astype(bf16)
            return carry

        lax.fori_loop(lo, hi, some, 0)

    def project_block(slot, lo, hi):
        def some(i, carry):
            at = pl.ds(pl.multiple_of(i * T, T), T)
            out = pl.ds(pl.multiple_of(slot * TOK + i * T, T), T)
            mixed = (dot(xg[slot, at, :], w_s[...]) + bias).astype(bf16)
            ones = jnp.ones((T, HEAD), bf16)
            for h in range(OWN):
                q = mixed[:, h * HEAD : (h + 1) * HEAD] * 0.125
                k = mixed[:, SLICE + h * HEAD : SLICE + (h + 1) * HEAD]
                v = mixed[:, 2 * SLICE + h * HEAD : 2 * SLICE + (h + 1) * HEAD]
                q_s[h, out, :] = jnp.concatenate([q.astype(bf16), jnp.zeros_like(ones)], axis=1)
                k_s[h, out, :] = jnp.concatenate([k, ones], axis=1)
                v_s[h, out, :] = jnp.concatenate([ones, v], axis=1)
            return carry

        lax.fori_loop(lo, hi, some, 0)

    own_w.wait()
    for copy in slices:
        copy.wait_recv()
    group = pl.ds(base, GROUP)
    wide = []
    for i in range(1, n // GROUP):
        begin(
            remote(wg.at[group], wg.at[group], w_send.at[GROUP + i], w_recv.at[GROUP + i], me ^ (GROUP * i)),
            wide,
        )
    own_x.wait()
    norm(pos, 0, 3)
    beside.wait()
    norm(pos ^ 1, 0, 3)
    arrive(0, 0)
    arrive_across()
    for _, copy in wide:
        copy.wait_recv()
    w_s[...] = wg[:, :rows48, :].reshape(D, WIDE)
    project_block(pos, 0, 3)
    project_block(pos ^ 1, 0, 3)
    passed = []

    def take(part):
        across[part].wait_recv()
        begin(x_part(xg.at[pos ^ 2], pos ^ 2, part, parts + part, near), passed)

    take(0)
    take(1)
    arrive(0, 1)
    for _, copy in passed:
        copy.wait()
    for i in (2, 3):
        norm(pos ^ i, 0, 2)
        project_block(pos ^ i, 0, 2)
    outs = []

    def last_rows():
        take(2)
        passed[2][1].wait()
        for i in (2, 3):
            norm(pos ^ i, 2, 3)
            project_block(pos ^ i, 2, 3)
        for i, (src, dst) in enumerate(
            ((smg, smo_ref), (w_s, wq_ref), (xg, a_ref), (k_s, k_ref), (v_s, v_ref))
        ):
            begin(pltpu.make_async_copy(src, dst, out_sem.at[i]), outs)

    lane = lanes(T)
    causal = below(T, T, False)
    code = [smg[base + c, 1:2, 0:2].astype(f32) for c in range(GROUP)]
    reaches = [c[:, 0:1] * 16.0 + c[:, 1:2] for c in code]
    column = lax.broadcasted_iota(jnp.int32, (T, PROMPT), 1).astype(f32)

    for h in range(OWN):

        def tile(at, blocks):
            q = q_s[h, pl.ds(at, T), :]
            scores = []
            for start, size, mask in blocks:
                s = dot_nt(q, k_s[h, pl.ds(start, size), :])
                scores.append(s if mask is None else jnp.where(mask, s, NEG))
            peak = scores[0].max(axis=1, keepdims=True)
            for s in scores[1:]:
                peak = jnp.maximum(peak, s.max(axis=1, keepdims=True))
            total = jnp.zeros((T, 2 * HEAD), f32)
            for s, (start, size, _) in zip(scores, blocks):
                total += dot(jnp.exp(s - peak).astype(bf16), v_s[h, pl.ds(start, size), :])
            mass = total[:, 0:1]
            f_s[h, pl.ds(at, T), :] = total / mass
            lse = peak + jnp.log(mass)
            q_s[h, pl.ds(at, T), :] = split_columns(q.astype(f32), lane, lse)

        for p in range(GROUP):
            past = [(i * TOK, PROMPT, None) for i in range(p)]
            at = p * TOK
            tile(at, past + [(at, T, causal)])
            tile(at + T, past + [(at, T, None), (at + T, T, causal)])
        if h == 0:
            arrive(0, 2)
            arrive(1, 0)
            last_rows()
        if h == 1:
            arrive(1, 2)
        if h == 2:
            settle_across()
            settle(1, 0)
        for c in range(GROUP):
            at = c * TOK + PROMPT
            blocks = [(i * TOK, PROMPT, column < reaches[c] - i * PROMPT) for i in range(GROUP)]
            tile(at, blocks + [(at, T, causal)])
        for p in range(GROUP):
            for left, right, size, to in PACK:
                top = f_s[h, p * TOK + left : p * TOK + left + size, :]
                low = f_s[h, p * TOK + right : p * TOK + right + size, :]
                pair = jnp.where(lanes(size) < HEAD, pltpu.roll(top, HEAD, 1), low)
                o_s[h, p, to : to + size, :] = pair.astype(bf16)
        if h == 0:
            arrive(1, 1)
        if h == 1:
            settle(0, 0)
            settle(0, 1)
            settle(0, 2)
        for i in range(1, GROUP):
            copy = remote(
                o_s.at[h, pos ^ i], o_ref.at[pos, h], o_send.at[h, i], o_recv.at[h, i], me ^ i
            )
            begin(copy, shared)
        for src, dst, i in (
            (o_s.at[h, pos], o_ref.at[pos, h], 5 + h),
            (f_s.at[h], f_ref.at[h], 8 + h),
            (q_s.at[h], q_ref.at[h], 11 + h),
        ):
            copy = pltpu.make_async_copy(src, dst, out_sem.at[i])
            begin(copy, outs)

    settle(1, 1)
    settle(1, 2)
    for copy in across + smalls + slices + [cross]:
        copy.wait_send()
    drain(wide + hops + sent, False)
    own_store.wait()
    drain(shared + outs, True)


def forward(x, small, pieces, shard):
    dma = pltpu.SemaphoreType.DMA
    n = BLOCKS
    shape = jax.ShapeDtypeStruct
    head = (OWN, ROWS, 2 * HEAD)
    return pl.pallas_call(
        forward_kernel,
        name="forward",
        out_shape=(
            shape((n, UNIT, D), bf16),
            shape((n,) + small.shape, bf16),
            shape((D, WIDE), bf16),
            shape((GROUP, TOK, D), bf16),
            shape(head, bf16),
            shape(head, bf16),
            shape(head, bf16),
            shape(head, f32),
            shape((GROUP, OWN, PAIR, 2 * HEAD), bf16),
        ),
        in_specs=[ANY] * 4,
        out_specs=(ANY,) * 9,
        scratch_shapes=[
            pltpu.VMEM((GROUP, TOK, D), bf16),
            pltpu.VMEM((n,) + small.shape, bf16),
            pltpu.VMEM((n,) + pieces.shape[1:], bf16),
            pltpu.VMEM((D, WIDE), bf16),
            pltpu.VMEM(head, bf16),
            pltpu.VMEM(head, bf16),
            pltpu.VMEM(head, bf16),
            pltpu.VMEM(head, f32),
            pltpu.VMEM((OWN, GROUP, PAIR, 2 * HEAD), bf16),
            pltpu.VMEM(shard.shape, bf16),
            dma((5,)),
            dma((n,)),
            dma((n,)),
            dma((2 * GROUP,)),
            dma((2 * GROUP,)),
            dma((9,)),
            dma((9,)),
            dma((13,)),
            dma((13,)),
            dma((27,)),
            dma((27,)),
            dma((13,)),
            dma((13,)),
            dma((OWN, GROUP)),
            dma((OWN, GROUP)),
            dma((14,)),
        ],
        compiler_params=params(60, collective_id=0, has_side_effects=True),
    )(x, small, pieces, shard)


def middle_kernel(
    x_ref, o_ref, dy_ref, wo_ref, wf_ref, wp_ref, line_ref,
    y_ref, dwf_ref, dwp_ref, dbf_ref, dwo_ref, dh_ref, do_ref, small_ref,
    o_s, h_s, b_s, bt_s, y_s, dn_s, row_s,
):
    step = pl.program_id(0)
    part = D // BLOCKS
    half = lanes(PAIR) < HEAD
    wf = wf_ref[...].reshape(D, CHUNK)
    wp = wp_ref[...].reshape(CHUNK, D)
    wo = wo_ref[...].reshape(D, D)

    @pl.when(step == 0)
    def _():
        for t in range(HEADS // 2):
            one = o_ref[2 * t // OWN, 2 * t % OWN].astype(f32)
            two = o_ref[(2 * t + 1) // OWN, (2 * t + 1) % OWN].astype(f32)
            at = slice(2 * t * HEAD, (2 * t + 2) * HEAD)
            first = jnp.where(half, one, pltpu.roll(two, HEAD, 1)).astype(bf16)
            second = jnp.where(half, pltpu.roll(one, HEAD, 1), two).astype(bf16)
            for left, right, size, to in PACK:
                o_s[left : left + size, at] = first[to : to + size]
                o_s[right : right + size, at] = second[to : to + size]
        for i, at in enumerate((4 * part, 5 * part, 6 * part, 11 * part)):
            pieces = [line_ref[d, 0:1, at : at + part] for d in range(BLOCKS)]
            row_s[i : i + 1, :] = jnp.concatenate(pieces, axis=1).astype(f32)
        h = x_ref[...].astype(f32) + dot(o_s[...], wo) + row_s[0:1, :]
        h_s[...] = h
        n, _ = moments(h)
        b_low = (n * row_s[1:2, :] + row_s[2:3, :]).astype(bf16)
        b_s[...] = b_low
        bt_s[...] = b_low.T
        y_s[...] = jnp.zeros_like(y_s)
        dn_s[...] = jnp.zeros_like(dn_s)

    dy = dy_ref[...]
    pieces = [line_ref[4 * step + i, 0:1, 7 * part : 11 * part] for i in range(4)]
    u = dot(b_s[...], wf) + jnp.concatenate(pieces, axis=1).astype(f32)
    square = u * u
    t = jnp.tanh(GELU_A * (u + GELU_B * (square * u)))
    m_low = (0.5 * u * (1.0 + t)).astype(bf16)
    slope = 0.5 * (1.0 + t) + 0.5 * u * (1.0 - t * t) * (GELU_A * (1.0 + 3.0 * GELU_B * square))
    y_s[...] += dot(m_low, wp)
    du = (dot_nt(dy, wp) * slope).astype(bf16)
    dbf_ref[...] = jnp.sum(du.astype(f32), axis=0, keepdims=True)
    dn_s[...] += dot_nt(du, wf)
    dwf_ref[...] = dot(bt_s[...], du).astype(bf16).reshape(dwf_ref.shape)
    dwp_ref[...] = dot_tn(m_low, dy).astype(bf16)

    @pl.when(step == pl.num_programs(0) - 1)
    def _():
        h = h_s[...]
        y_ref[...] = (h + y_s[...] + row_s[3:4, :]).astype(bf16)
        n, r = moments(h)
        dn = dn_s[...]
        grad = dy_ref[...].astype(f32)
        small_ref[...] = jnp.zeros_like(small_ref)
        small_ref[0:1, :] = jnp.sum(grad, axis=0, keepdims=True)
        small_ref[1:2, :] = jnp.sum(dn * n, axis=0, keepdims=True)
        small_ref[2:3, :] = jnp.sum(dn, axis=0, keepdims=True)
        e = dn * row_s[1:2, :]
        lean = jnp.mean(e, axis=-1, keepdims=True) + n * jnp.mean(e * n, axis=-1, keepdims=True)
        dh = grad + r * (e - lean)
        dh_ref[...] = dh
        dh_low = dh.astype(bf16)
        small_ref[3:4, :] = jnp.sum(dh_low.astype(f32), axis=0, keepdims=True)
        dwo_ref[...] = dot_tn(o_s[...], dh_low).astype(bf16)
        h_s[...] = dot_nt(dh_low, wo)
        for t in range(HEADS // 2):
            at = slice(2 * t * HEAD, (2 * t + 2) * HEAD)
            for left, right, size, to in PACK:
                top, low = h_s[left : left + size, at], h_s[right : right + size, at]
                side = lanes(size) < HEAD
                one = jnp.where(side, top, pltpu.roll(low, HEAD, 1))
                two = jnp.where(side, pltpu.roll(top, HEAD, 1), low)
                do_ref[2 * t // OWN, 2 * t % OWN, to : to + size] = one.astype(bf16)
                do_ref[(2 * t + 1) // OWN, (2 * t + 1) % OWN, to : to + size] = two.astype(bf16)


def middle(x, o, dy, wall, lines):
    fixed2 = lambda i: (0, 0)
    fixed4 = lambda i: (0, 0, 0, 0)
    square = pl.BlockSpec((TOK, D), fixed2)
    heads = pl.BlockSpec((GROUP, OWN, PAIR, 2 * HEAD), fixed4)
    columns = pl.BlockSpec((BLOCKS, 1, D // BLOCKS, D), lambda i: (0, i, 0, 0))
    down = pl.BlockSpec((CHUNK, D), lambda i: (i, 0))
    line = pl.BlockSpec((1, CHUNK), lambda i: (0, i))
    shape = jax.ShapeDtypeStruct
    return pl.pallas_call(
        middle_kernel,
        name="middle",
        grid=(FF // CHUNK,),
        out_shape=(
            shape((TOK, D), bf16),
            shape((BLOCKS, FF // D, D // BLOCKS, D), bf16),
            shape((FF, D), bf16),
            shape((1, FF), f32),
            shape((D, D), bf16),
            shape((TOK, D), f32),
            shape((GROUP, OWN, PAIR, 2 * HEAD), bf16),
            shape((8, D), f32),
        ),
        in_specs=[
            square, heads, square,
            pl.BlockSpec((BLOCKS, 48, D), lambda i: (0, 4, 0)),
            pl.BlockSpec((BLOCKS, 48, D), lambda i: (0, 5 + i, 0)),
            pl.BlockSpec((BLOCKS // 4, 192, D), lambda i: (i, 0, 0)),
            pl.BlockSpec(lines.shape, lambda i: (0, 0, 0)),
        ],
        out_specs=(
            square, columns, down, line, square, square, heads, pl.BlockSpec((8, D), fixed2),
        ),
        scratch_shapes=[
            pltpu.VMEM((TOK, D), bf16),
            pltpu.VMEM((TOK, D), f32),
            pltpu.VMEM((TOK, D), bf16),
            pltpu.VMEM((D, TOK), bf16),
            pltpu.VMEM((TOK, D), f32),
            pltpu.VMEM((TOK, D), f32),
            pltpu.VMEM((8, D), f32),
        ],
        compiler_params=params(60),
    )(x, o, dy, wall, wall, wall, lines)


ORDER = (4, -3, 3, -2, 2, -1, 1, 0)
SMALL = 16


def backward_kernel(
    do_ref, q_ref, k_ref, v_ref, f_ref, a_ref, w_ref, x_ref, dh_ref, lines_ref, sums_ref, dbf_ref,
    dwp_ref, dwo_ref, dwf_ref,
    grad_ref, gq_ref, gp_ref, go_ref, gf_ref, small_ref,
    g_b, q_s, k_s, v_s, f_b, a_b, w_s, x_s, dh_s, lines_s, sums_s, dbf_s,
    near_b, mine_b, y_b, ring_b, fin_b, fin_r, fin_o,
    g_s, dq_s, kt_s, dkv_s, dm_s, w_h, dw_s, db_s,
    dw_b, z_b, j_b, j_r, rep_r, gq_o,
    dn_a, dn_b, dn_c, dn_ra, dn_rb, dn_rc, sm_b, sm_r,
    load, f_sem, a_sem, mine_sem, g_send, g_recv, n_send, n_recv, y_send, y_recv, r_send, r_recv, fin_send,
    fin_recv, z_send, z_recv, j_send, j_recv, rep_send, rep_recv, d_send, d_recv, s_send, s_recv, out_sem,
):
    n = BLOCKS
    me = lax.axis_index("fsdp")
    rep = lax.axis_index("rep")
    pos = lax.rem(me, GROUP)
    base = me - pos
    level = me // GROUP
    near, far = me ^ 1, me ^ 2
    place, device = ring_of(me)
    T = CONT
    W3 = 3 * HEAD
    other = {"rep": 1 - rep}

    def remote(src, dst, send, recv, peer):
        return pltpu.make_async_remote_copy(
            src_ref=src,
            dst_ref=dst,
            send_sem=send,
            recv_sem=recv,
            device_id=peer if isinstance(peer, dict) else {"fsdp": peer},
            device_id_type=MESH,
        )

    greet([me ^ i for i in range(1, n)], 1 - rep)

    def do_copy(kind, i):
        at = pl.ds(*((0, 128), (128, 256))[kind])
        src, dst = do_ref.at[pos ^ i, :, at], g_b.at[pos, :, at]
        return remote(src, dst, g_send.at[kind, i], g_recv.at[kind, i], me ^ i)

    own_do = pltpu.make_async_copy(do_ref.at[pos], g_b.at[pos], load.at[0])
    own_do.start()
    for i in range(1, GROUP):
        do_copy(0, i).start()

    stages = (
        tuple((c * TOK + PROMPT, CONT) for c in range(GROUP)),
        ((3 * TOK, PROMPT),),
        ((0, PROMPT),),
        ((TOK, PROMPT), (2 * TOK, PROMPT)),
    )
    loads = (stages[0], ((3 * TOK, PROMPT), (2 * TOK, PROMPT)), ((0, PROMPT), (TOK, PROMPT)))

    def f_copies(part):
        at, found = 0, []
        for i, (row, size) in enumerate(loads[part]):
            src, dst = f_ref.at[:, pl.ds(row, size)], f_b.at[:, pl.ds(at, size)]
            found.append(pltpu.make_async_copy(src, dst, f_sem.at[part, i]))
            at += size
        return found

    def a_copies(stage):
        at, found = 0, []
        for i, (row, size) in enumerate(stages[stage]):
            src, dst = a_ref.at[pl.ds(row, size)], a_b.at[pl.ds(at, size)]
            found.append(pltpu.make_async_copy(src, dst, a_sem.at[stage, i]))
            at += size
        return found

    first = [
        pltpu.make_async_copy(src, dst, load.at[1 + i])
        for i, (src, dst) in enumerate(
            ((k_ref, k_s), (v_ref, v_s), (q_ref, q_s), (lines_ref, lines_s), (w_ref, w_s))
        )
    ]
    later = [
        pltpu.make_async_copy(src, dst, load.at[6 + i])
        for i, (src, dst) in enumerate(
            ((x_ref, x_s), (dh_ref, dh_s), (sums_ref, sums_s), (dbf_ref, dbf_s))
        )
    ]
    for copy in f_copies(0) + first:
        copy.start()

    cut = ((0, 192), (192, 48), (240, 192))

    def near_copies(i):
        d = device(place + ORDER[i]) ^ 1
        return [
            remote(ref.at[d], near_b.at[i, pl.ds(at, size)], n_send.at[i, k], n_recv.at[i, k], near)
            for k, (ref, (at, size)) in enumerate(zip((dwp_ref, dwo_ref, dwf_ref), cut))
        ]

    def mine_copies(i):
        d = device(place + ORDER[i])
        return [
            pltpu.make_async_copy(ref.at[d], mine_b.at[i % 4, pl.ds(at, size)], mine_sem.at[i, k])
            for k, (ref, (at, size)) in enumerate(zip((dwp_ref, dwo_ref, dwf_ref), cut))
        ]

    for i in range(2):
        for copy in near_copies(i) + mine_copies(i):
            copy.start()
    for i in range(1, GROUP):
        do_copy(1, i).start()
    for i in range(2, 8):
        for copy in near_copies(i):
            copy.start()
    for copy in a_copies(0) + mine_copies(2) + mine_copies(3) + later:
        copy.start()

    def ready(i):
        for copy in near_copies(i):
            copy.wait_recv()
        for copy in mine_copies(i):
            copy.wait()

    mine = pl.ds(pl.multiple_of(rep * (D // 2), D // 2), D // 2)
    rest = pl.ds(pl.multiple_of((1 - rep) * (D // 2), D // 2), D // 2)

    def rounds(some):
        def chunk(c, carry):
            some(pl.ds(pl.multiple_of(c * 144, 144), 144))
            return carry

        lax.fori_loop(0, UNIT // 144, chunk, 0)

    def y_copy(i):
        return remote(near_b.at[i, :, rest], y_b.at[i], y_send.at[i], y_recv.at[i], other)

    def chip_sum(i):
        ready(i)

        def some(at):
            total = near_b[i, at, :].astype(f32) + mine_b[i % 4, at, :].astype(f32)
            near_b[i, at, :] = total.astype(bf16)

        rounds(some)
        y_copy(i).start()
        if i + 4 < 8:
            for copy in mine_copies(i + 4):
                copy.start()

    def ring_copy(t, right):
        i = 2 * t if right else 2 * t + 1
        slot = t if right else 4 + t
        peer = device(place + 1 if right else place - 1)
        return remote(near_b.at[i, :, mine], ring_b.at[slot], r_send.at[slot], r_recv.at[slot], peer)

    def ring_step(t):
        for right in (True, False) if t < 3 else (True,):
            i = 2 * t if right else 2 * t + 1
            y_copy(i).wait_recv()
            if t > 0:
                ring_copy(t - 1, right).wait_recv()
            slot = (t if right else 4 + t) - 1

            def some(at):
                total = near_b[i, at, mine].astype(f32) + y_b[i, at, :].astype(f32)
                if t > 0:
                    total = total + ring_b[slot, at, :].astype(f32)
                near_b[i, at, mine] = total.astype(bf16)

            rounds(some)
            ring_copy(t, right).start()

    fin_copy = remote(fin_b, fin_r, fin_send, fin_recv, other)

    def ring_end():
        y_copy(7).wait_recv()
        ring_copy(3, True).wait_recv()
        ring_copy(2, False).wait_recv()

        def some(at):
            total = near_b[7, at, mine].astype(f32) + y_b[7, at, :].astype(f32)
            fin_b[at, :] = (total + ring_b[3, at, :].astype(f32) + ring_b[6, at, :].astype(f32)).astype(bf16)

        rounds(some)
        fin_copy.start()

    def z_copy(h, i):
        return remote(
            dw_b.at[h, level ^ i], z_b.at[h, i], z_send.at[h, i], z_recv.at[h, i], me ^ (GROUP * i)
        )

    def j_copy(h, i):
        return remote(j_b.at[h, pos ^ i], j_r.at[h, pos], j_send.at[h, i], j_recv.at[h, i], me ^ i)

    def gather_rows(h):
        for i in range(1, GROUP):
            z_copy(h, i).wait_recv()
        total = dw_b[h, level].astype(f32)
        for i in range(1, GROUP):
            total = total + z_b[h, i].astype(f32)
        j_b[h] = total.astype(bf16).reshape(GROUP, D // n, W3)
        j_r[h, pos] = j_b[h, pos]
        for i in range(1, GROUP):
            j_copy(h, i).start()

    def rep_copy(h):
        return remote(j_r.at[h], rep_r.at[h], rep_send.at[h], rep_recv.at[h], other)

    def trade_rows(h):
        for i in range(1, GROUP):
            j_copy(h, i).wait_recv()
        rep_copy(h).start()

    causal = below(T, T, True)
    key_row = lax.broadcasted_iota(jnp.int32, (PROMPT, T), 0).astype(f32)

    def prepare(part, h):
        at = 0
        for row, size in loads[part]:
            p = row // TOK
            left, right, count, to = PACK[0 if size == CONT else 1]
            packed = g_b[p, h, to : to + count, :].astype(f32)
            lane = lanes(count)
            for start, block in ((left, pltpu.roll(packed, HEAD, 1)), (right, packed)):
                off = at + start - (row - p * TOK)
                prod = jnp.where(lane >= HEAD, block * f_b[h, off : off + count, :], 0.0)
                inner = jnp.sum(prod, axis=1, keepdims=True)
                hi = inner.astype(bf16).astype(f32)
                mid = (inner - hi).astype(bf16).astype(f32)
                low = inner - hi - mid
                tail = jnp.where(lane == 0, -hi, jnp.where(lane == 1, -mid, -low))
                value = jnp.where(lane >= HEAD, block, jnp.where(lane < 3, tail, 0.0))
                g_s[h, p * TOK + start : p * TOK + start + count, :] = value.astype(bf16)
            at += size

    def block(h, keys, size, rows, count, mask, target):
        kb = k_s[h, pl.ds(keys, size), :]
        vb = v_s[h, pl.ds(keys, size), :]
        q = q_s[h, pl.ds(rows, count), :]
        g = g_s[h, pl.ds(rows, count), :]
        probs = jnp.exp(dot_nt(kb, q))
        if mask is not None:
            probs = jnp.where(mask, probs, 0.0)
        ds = (probs * dot_nt(vb, g)).astype(bf16)
        lane = lanes(count)
        none = jnp.zeros_like(q)
        pair = dot(ds, jnp.where(lane < HEAD, q, none))
        pair = pair + dot(probs.astype(bf16), jnp.where(lane < HEAD, none, g))
        dq_s[h, :, pl.ds(rows, count)] += dot(kt_s[h, :, pl.ds(keys, size)], ds)
        if target is None:
            return pair
        dkv_s[h, pl.ds(target, size), :] += pair

    def diagonal(h, p):
        row, at = p * TOK, p * PROMPT
        block(h, row, T, row, T, causal, at)
        block(h, row, T, row + T, T, None, at)
        block(h, row + T, T, row + T, T, causal, at + T)

    def flush_q(h, row, size):
        at = pl.ds(row, size)
        dm_s[h, at, 2 * HEAD :] = (dq_s[h, :, at].T * 0.125).astype(bf16)

    def flush(h, p):
        dm_s[h, p * TOK : p * TOK + PROMPT, : 2 * HEAD] = dkv_s[
            h, p * PROMPT : (p + 1) * PROMPT, :
        ].astype(bf16)
        flush_q(h, p * TOK, PROMPT)

    def add_weight(stage, h):
        at = 0
        total = jnp.zeros((W3, D), f32)
        for row, size in stages[stage]:
            total = total + dot_tn(dm_s[h, row : row + size, :], a_b[at : at + size, :])
            at += size
        if stage == 0:
            dw_s[h] = total
        else:
            dw_s[h] += total

    def dn_rows(owner, seg):
        rows = pl.ds(pl.multiple_of(owner * TOK + seg * T, T), T)
        total = dot_nt(dm_s[0, rows, :], w_h[0])
        for h in range(1, OWN):
            total = total + dot_nt(dm_s[h, rows, :], w_h[h])
        return total

    def dn_copy(kind, seg):
        at = pl.ds(seg * T, T)
        src, dst, peer = ((dn_a, dn_ra, near), (dn_b, dn_rb, far), (dn_c, dn_rc, near))[kind]
        return remote(src.at[at], dst.at[at], d_send.at[kind, seg], d_recv.at[kind, seg], peer)

    def put(kind, seg):
        at = slice(seg * T, (seg + 1) * T)
        rows = dn_rows(pos ^ (3, 2, 1)[kind], seg)
        if kind == 1:
            dn_copy(0, seg).wait_recv()
            rows = rows + dn_ra[at, :].astype(f32)
        (dn_a, dn_b, dn_c)[kind][at, :] = rows.astype(bf16)
        dn_copy(kind, seg).start()

    def put_prompt(p, kinds):
        for kind in kinds:

            @pl.when((pos ^ (3, 2, 1)[kind]) == p)
            def _():
                for seg in range(2):
                    put(kind, seg)

    first[3].wait()
    first[4].wait()
    for h in range(OWN):
        w_h[h] = jnp.concatenate(
            [w_s[:, part * SLICE + h * HEAD : part * SLICE + (h + 1) * HEAD] for part in (1, 2, 0)],
            axis=1,
        )
    dq_s[...] = jnp.zeros_like(dq_s)
    dkv_s[...] = jnp.zeros_like(dkv_s)
    for copy in first[:3]:
        copy.wait()

    def turn(h, carry):
        for p in range(GROUP):
            kt_s[h, :, p * TOK : (p + 1) * TOK] = k_s[h, p * TOK : (p + 1) * TOK, :].T[:HEAD]
        return carry

    lax.fori_loop(0, OWN, turn, 0)
    own_do.wait()
    for i in range(1, GROUP):
        do_copy(0, i).wait_recv()
    for copy in f_copies(0):
        copy.wait()
    chip_sum(0)
    chip_sum(1)

    def stage_cont(h, carry):
        prepare(0, h)

        def cont(c, carry):
            rows = pl.multiple_of(c * TOK + PROMPT, CONT)
            code = lines_s[base + c, 1:2, 0:128].astype(f32)
            reach = code[:, 0:1] * 16.0 + code[:, 1:2]
            for p in range(GROUP):
                block(h, p * TOK, PROMPT, rows, T, key_row < reach - p * PROMPT, p * PROMPT)
            pair = block(h, rows, T, rows, T, causal, None)
            dm_s[h, pl.ds(rows, T), : 2 * HEAD] = pair.astype(bf16)
            flush_q(h, rows, T)
            return carry

        lax.fori_loop(0, GROUP, cont, 0)

        for k in range(OWN):

            @pl.when(h == k)
            def _():
                chip_sum(2 + 2 * k)
                chip_sum(3 + 2 * k)

        return carry

    lax.fori_loop(0, OWN, stage_cont, 0)
    ring_step(0)
    for copy in f_copies(1):
        copy.start()
    for copy in a_copies(0):
        copy.wait()
    for kind in (0, 2, 1):
        put(kind, 2)
    lax.fori_loop(0, OWN, lambda h, carry: (add_weight(0, h), carry)[1], 0)
    for copy in a_copies(1):
        copy.start()
    for i in range(1, GROUP):
        do_copy(1, i).wait_recv()
    for copy in f_copies(1):
        copy.wait()

    def stage_last(h, carry):
        prepare(1, h)
        for p in range(3):
            block(h, p * TOK, PROMPT, 3 * TOK, PROMPT, None, p * PROMPT)
        diagonal(h, 3)
        flush(h, 3)

        @pl.when(h == 1)
        def _():
            ring_step(1)

        return carry

    lax.fori_loop(0, OWN, stage_last, 0)
    for copy in f_copies(2):
        copy.start()
    for copy in a_copies(1):
        copy.wait()
    put_prompt(3, (0, 2))
    lax.fori_loop(0, OWN, lambda h, carry: (add_weight(1, h), carry)[1], 0)
    for copy in a_copies(2):
        copy.start()
    put_prompt(3, (1,))
    for copy in f_copies(2):
        copy.wait()

    def stage_first(h, carry):
        prepare(2, h)
        diagonal(h, 0)
        for p in range(1, 3):
            block(h, 0, PROMPT, p * TOK, PROMPT, None, 0)
        flush(h, 0)

        @pl.when(h == 1)
        def _():
            ring_step(2)

        return carry

    lax.fori_loop(0, OWN, stage_first, 0)
    for copy in a_copies(2):
        copy.wait()
    put_prompt(0, (0, 2))
    lax.fori_loop(0, OWN, lambda h, carry: (add_weight(2, h), carry)[1], 0)
    for copy in a_copies(3):
        copy.start()
    put_prompt(0, (1,))
    for copy in a_copies(3):
        copy.wait()

    def stage_middle(h, carry):
        block(h, TOK, PROMPT, 2 * TOK, PROMPT, None, PROMPT)
        diagonal(h, 1)
        flush(h, 1)
        diagonal(h, 2)
        flush(h, 2)
        add_weight(3, h)
        dw = dw_s[h].T
        dw_b[h] = dw.astype(bf16).reshape(GROUP, D // GROUP, W3)
        for i in range(1, GROUP):
            z_copy(h, i).start()
        db = jnp.zeros((1, W3), f32)
        for i in range(GROUP):
            db = db + jnp.sum(dm_s[h, i * TOK : (i + 1) * TOK, :].astype(f32), axis=0, keepdims=True)
        hi = db.astype(bf16)
        mid = (db - hi.astype(f32)).astype(bf16)
        low = (db - hi.astype(f32) - mid.astype(f32)).astype(bf16)
        split = jnp.concatenate([hi, mid, low, jnp.zeros((13, W3), bf16)], axis=0)
        ones = jnp.ones((8, W3), f32)
        gain_rows = lax.dot_general(
            ones,
            w_h[h].astype(f32) * dw,
            (((1,), (1,)), ((), ())),
            precision=lax.Precision.HIGHEST,
            preferred_element_type=f32,
        )
        db_s[h, 0:1, :W3] = db
        db_s[h, 1:2, W3 : W3 + D] = jnp.sum(dot_nt(split, w_h[h]), axis=0, keepdims=True)
        db_s[h, 2:3, W3 : W3 + D] = gain_rows[0:1]

        @pl.when(h == 1)
        def _():
            ring_step(3)

        return carry

    lax.fori_loop(0, OWN, stage_middle, 0)
    inner = lax.rem(pos + 1, GROUP) // 2

    def put_last(kind, side):
        @pl.when(inner == side)
        def _():
            for seg in range(2):
                put(kind, seg)

    put_last(2, 0)
    put_last(0, 1)
    gather_rows(0)
    put_last(1, 0)
    ring_end()
    for copy in later:
        copy.wait()

    rows48 = D // n
    gain = jnp.concatenate([lines_s[d, 0:1, 0:rows48] for d in range(n)], axis=1).astype(f32)
    shift = jnp.concatenate([lines_s[d, 0:1, rows48 : 2 * rows48] for d in range(n)], axis=1).astype(f32)
    d_shift = db_s[0, 1:2, W3 : W3 + D] + db_s[1, 1:2, W3 : W3 + D] + db_s[2, 1:2, W3 : W3 + D]
    d_gain = db_s[0, 2:3, W3 : W3 + D] + db_s[1, 2:3, W3 : W3 + D] + db_s[2, 2:3, W3 : W3 + D]
    blank = jnp.zeros((1, D - SLICE), f32)

    def biases(lo):
        row = jnp.concatenate([db_s[h, 0:1, lo : lo + HEAD] for h in range(OWN)] + [blank], axis=1)
        return pltpu.roll(jnp.broadcast_to(row, (8, D)), pos * SLICE, 1)[0:1]

    sm_b[0] = jnp.concatenate(
        [
            (d_gain - shift * d_shift) / gain,
            d_shift,
            biases(2 * HEAD),
            biases(HEAD),
            sums_s[3:4, :],
            sums_s[1:2, :],
            sums_s[2:3, :],
            sums_s[0:1, :],
        ]
        + [dbf_s[0:1, c * D : (c + 1) * D] for c in range(FF // D)]
        + [jnp.zeros((SMALL - 12, D), f32)],
        axis=0,
    )
    peers = [me ^ 1, me ^ 2, me ^ 4, me ^ 8, other]

    def small_copy(i):
        return remote(sm_b.at[i], sm_r.at[i], s_send.at[i], s_recv.at[i], peers[i])

    def small_step(i):
        small_copy(i).wait_recv()
        sm_b[i + 1] = sm_b[i] + sm_r[i]
        if i < 4:
            small_copy(i + 1).start()

    small_copy(0).start()

    outs = []

    def finish_rows(seg):
        at = slice(seg * T, (seg + 1) * T)
        rows = dn_rows(pos, seg)
        dn_copy(2, seg).wait_recv()
        dn_copy(1, seg).wait_recv()
        n_rows, r = moments(x_s[at, :].astype(f32))
        e = (rows + dn_rb[at, :].astype(f32) + dn_rc[at, :].astype(f32)) * gain
        lean = jnp.mean(e, axis=-1, keepdims=True) + n_rows * jnp.mean(e * n_rows, axis=-1, keepdims=True)
        dh_s[at, :] = dh_s[at, :] + r * (e - lean)
        copy = pltpu.make_async_copy(dh_s.at[at], grad_ref.at[at], out_sem.at[10 + seg])
        copy.start()
        outs.append(copy)

    finish_rows(2)
    gather_rows(1)
    small_step(0)
    trade_rows(0)
    small_step(1)
    gather_rows(2)
    trade_rows(1)
    small_step(2)
    finish_rows(0)
    finish_rows(1)
    trade_rows(2)
    small_step(3)

    small_step(4)
    total = sm_b[5]
    turned = pltpu.roll(total, lax.rem(n - me, n) * rows48, 1)
    eighth = lax.rem(me, 8)
    biased = pltpu.roll(total, lax.rem(8 - eighth, 8) * (2 * rows48), 1)
    quarter = lax.rem(me, 4)
    wide = pltpu.roll(total, lax.rem(4 - quarter, 4) * (4 * rows48), 1)
    row = lax.broadcasted_iota(jnp.int32, (SMALL, D), 0)
    bias_row = jnp.sum(jnp.where(row == 2 + me // 8, biased, 0.0), axis=0, keepdims=True)
    wide_row = jnp.sum(jnp.where(row == 8 + me // 4, wide, 0.0), axis=0, keepdims=True)
    small_copy(0).wait_send()
    sm_b[0] = jnp.where(row == 2, bias_row, jnp.where(row == 3, wide_row, turned))
    copy = pltpu.make_async_copy(sm_b.at[0], small_ref, out_sem.at[2])
    copy.start()
    outs.append(copy)

    for h in range(OWN):
        rep_copy(h).wait_recv()
    for part, (at, piece) in enumerate(((2 * HEAD, 0), (0, 1), (HEAD, 2))):
        row = jnp.concatenate(
            [
                j_r[h, j, :, at : at + HEAD].astype(f32) + rep_r[h, j, :, at : at + HEAD].astype(f32)
                for j in range(GROUP)
                for h in range(OWN)
            ],
            axis=1,
        )
        gq_o[:, piece * D : (piece + 1) * D] = row
    copy = pltpu.make_async_copy(gq_o, gq_ref, out_sem.at[3])
    copy.start()
    outs.append(copy)

    fin_copy.wait_recv()

    def some(at):
        fin_o[at, mine] = fin_b[at, :].astype(f32)
        fin_o[at, rest] = fin_r[at, :].astype(f32)

    rounds(some)
    targets = [(gp_ref, 0, 192), (go_ref, 192, 48)]
    targets += [(gf_ref.at[:, pl.ds(c * D, D)], 240 + 48 * c, 48) for c in range(FF // D)]
    for i, (ref, at, size) in enumerate(targets):
        copy = pltpu.make_async_copy(fin_o.at[pl.ds(at, size)], ref, out_sem.at[4 + i])
        copy.start()
        outs.append(copy)

    for h in range(OWN):
        for i in range(1, GROUP):
            for copy in (z_copy(h, i), j_copy(h, i)):
                copy.wait_send()
    for kind in range(2):
        for i in range(1, GROUP):
            do_copy(kind, i).wait_send()
    for i in range(8):
        y_copy(i).wait_send()
        for copy in near_copies(i):
            copy.wait_send()
    for t in range(4):
        for right in (True, False) if t < 3 else (True,):
            ring_copy(t, right).wait_send()
    for kind in range(3):
        for seg in range(3):
            dn_copy(kind, seg).wait_send()
    for i in range(1, 5):
        small_copy(i).wait_send()
    for h in range(OWN):
        rep_copy(h).wait_send()
    fin_copy.wait_send()
    for copy in outs:
        copy.wait()


def backward(do, q, k, v, f, a, w, x, dh, lines, sums, dbf, dwp, dwo, dwf):
    dma = pltpu.SemaphoreType.DMA
    n = BLOCKS
    shape = jax.ShapeDtypeStruct
    vmem = pltpu.VMEM
    rows = D // n
    head = (OWN, ROWS, 2 * HEAD)
    W3 = 3 * HEAD
    pairs = (OWN, GROUP)
    return pl.pallas_call(
        backward_kernel,
        name="backward",
        out_shape=(
            shape((TOK, D), f32),
            shape((rows, 3 * D), f32),
            shape((FF // n, D), f32),
            shape((rows, D), f32),
            shape((rows, FF), f32),
            shape((SMALL, D), f32),
        ),
        in_specs=[ANY] * 15,
        out_specs=(ANY,) * 6,
        scratch_shapes=[
            vmem((GROUP, OWN, PAIR, 2 * HEAD), bf16),
            vmem(head, bf16),
            vmem(head, bf16),
            vmem(head, bf16),
            vmem((OWN, GROUP * CONT, 2 * HEAD), f32),
            vmem((GROUP * CONT, D), bf16),
            vmem((D, WIDE), bf16),
            vmem((TOK, D), bf16),
            vmem((TOK, D), f32),
            vmem(lines.shape, bf16),
            vmem(sums.shape, f32),
            vmem(dbf.shape, f32),
            vmem((8, UNIT, D), bf16),
            vmem((4, UNIT, D), bf16),
            vmem((8, UNIT, D // 2), bf16),
            vmem((7, UNIT, D // 2), bf16),
            vmem((UNIT, D // 2), bf16),
            vmem((UNIT, D // 2), bf16),
            vmem((UNIT, D), f32),
            vmem(head, bf16),
            vmem((OWN, HEAD, ROWS), f32),
            vmem((OWN, HEAD, ROWS), bf16),
            vmem((OWN, GROUP * PROMPT, 2 * HEAD), f32),
            vmem((OWN, ROWS, W3), bf16),
            vmem((OWN, D, W3), bf16),
            vmem((OWN, W3, D), f32),
            vmem((OWN, 8, W3 + D), f32),
            vmem((OWN, GROUP, D // GROUP, W3), bf16),
            vmem((OWN, GROUP, D // GROUP, W3), bf16),
            vmem((OWN, GROUP, rows, W3), bf16),
            vmem((OWN, GROUP, rows, W3), bf16),
            vmem((OWN, GROUP, rows, W3), bf16),
            vmem((rows, 3 * D), f32),
            vmem((TOK, D), bf16),
            vmem((TOK, D), bf16),
            vmem((TOK, D), bf16),
            vmem((TOK, D), bf16),
            vmem((TOK, D), bf16),
            vmem((TOK, D), bf16),
            vmem((6, SMALL, D), f32),
            vmem((5, SMALL, D), f32),
            dma((10,)),
            dma((3, GROUP)),
            dma((4, GROUP)),
            dma((8, 3)),
            dma((2, GROUP)),
            dma((2, GROUP)),
            dma((8, 3)),
            dma((8, 3)),
            dma((8,)),
            dma((8,)),
            dma((7,)),
            dma((7,)),
            dma,
            dma,
            dma(pairs),
            dma(pairs),
            dma(pairs),
            dma(pairs),
            dma((OWN,)),
            dma((OWN,)),
            dma((3, 3)),
            dma((3, 3)),
            dma((5,)),
            dma((5,)),
            dma((13,)),
        ],
        compiler_params=params(63, collective_id=4, has_side_effects=True),
    )(do, q, k, v, f, a, w, x, dh, lines, sums, dbf, dwp, dwo, dwf)


def land_kernel(sums_ref, *refs):
    sources, targets, rows, held, sem = refs[:5], refs[5:10], refs[10:18], refs[18:23], refs[23]
    parts = []
    for i, ref in enumerate(held):
        count = 4 if i == 0 else 1
        size = ref.shape[0] // count
        parts += [(i, pl.ds(k * size, size)) for k in range(count)]

    def inward(k):
        i, at = parts[k]
        return pltpu.make_async_copy(sources[i].at[at], held[i].at[at], sem.at[0, k])

    def outward(k):
        i, at = parts[k]
        return pltpu.make_async_copy(held[i].at[at], targets[i].at[at], sem.at[1, k])

    for k in range(len(parts)):
        inward(k).start()
    for i, ref in zip((0, 1, 2, 4, 5, 6, 3, 7), rows):
        ref[...] = sums_ref[i, : ref.shape[0]]
    for k in range(len(parts)):
        inward(k).wait()
        outward(k).start()
    for k in range(len(parts)):
        outward(k).wait()


def land(sums, matrices):
    part = D // BLOCKS
    shape = jax.ShapeDtypeStruct
    vector = pl.BlockSpec(memory_space=pltpu.VMEM)
    return pl.pallas_call(
        land_kernel,
        name="land",
        out_shape=tuple(shape(m.shape, f32) for m in matrices)
        + tuple(shape((k * part,), f32) for k in (1, 1, 2, 1, 1, 1, 4, 1)),
        in_specs=[vector] + [ANY] * 5,
        out_specs=(ANY,) * 5 + (vector,) * 8,
        scratch_shapes=[pltpu.VMEM(m.shape, f32) for m in matrices]
        + [pltpu.SemaphoreType.DMA((2, 8))],
        compiler_params=params(60),
    )(sums, *matrices)


def unproject_kernel(dq_ref, dk_ref, dv_ref, a_ref, w_ref, dn_ref, dw_ref, db_ref):
    step = pl.program_id(0)
    mixed = jnp.concatenate(
        [ref[h] for ref in (dq_ref, dk_ref, dv_ref) for h in range(OWN)], axis=1
    )
    dn_ref[...] = dot_nt(mixed, w_ref[...]).astype(bf16)
    dw = dot_tn(a_ref[...], mixed)
    db = jnp.sum(mixed.astype(f32), axis=0, keepdims=True)

    @pl.when(step == 0)
    def _():
        dw_ref[...] = dw
        db_ref[...] = db

    @pl.when(step > 0)
    def _():
        dw_ref[...] += dw
        db_ref[...] += db


def unproject(dq, dk, dv, a, w):
    tile = 768
    head = pl.BlockSpec((OWN, tile, HEAD), lambda i: (0, i, 0))
    whole = lambda i: (0, 0)
    shape = jax.ShapeDtypeStruct
    return pl.pallas_call(
        unproject_kernel,
        name="unproject",
        grid=(ROWS // tile,),
        out_shape=(shape((ROWS, D), bf16), shape((D, WIDE), f32), shape((1, WIDE), f32)),
        in_specs=[
            head, head, head,
            pl.BlockSpec((tile, D), lambda i: (i, 0)),
            pl.BlockSpec((D, WIDE), whole),
        ],
        out_specs=(
            pl.BlockSpec((tile, D), lambda i: (i, 0)),
            pl.BlockSpec((D, WIDE), whole),
            pl.BlockSpec((1, WIDE), whole),
        ),
        compiler_params=params(48),
    )(dq, dk, dv, a, w)


def finish_kernel(x_ref, dh_ref, g_ref, one_ref, two_ref, three_ref, out_ref):
    n, r = moments(x_ref[...].astype(f32))
    dn = one_ref[...].astype(f32) + two_ref[...].astype(f32) + three_ref[...].astype(f32)
    e = dn * g_ref[...]
    lean = jnp.mean(e, axis=-1, keepdims=True) + n * jnp.mean(e * n, axis=-1, keepdims=True)
    out_ref[...] = dh_ref[...] + r * (e - lean)


def finish(x, dh, gain, one, two, three):
    tile = 256
    rows = pl.BlockSpec((tile, D), lambda i: (i, 0))
    return pl.pallas_call(
        finish_kernel,
        name="finish",
        grid=(TOK // tile,),
        out_shape=jax.ShapeDtypeStruct((TOK, D), f32),
        in_specs=[rows, rows, pl.BlockSpec((1, D), lambda i: (0, 0)), rows, rows, rows],
        out_specs=rows,
        compiler_params=params(48),
    )(x, dh, gain, one, two, three)


def flip(block, bit):
    count = lax.axis_size("fsdp")
    return lax.ppermute(block, "fsdp", [(i, i ^ bit) for i in range(count)])


def repack(packed, old, new):
    rows = []
    for left, right, size, at in old:
        rows.append((left, packed[:, :, at : at + size, :HEAD]))
        rows.append((right, packed[:, :, at : at + size, HEAD:]))
    rows = jnp.concatenate([part for _, part in sorted(rows, key=lambda entry: entry[0])], axis=2)
    parts = [
        jnp.concatenate([rows[:, :, left : left + size], rows[:, :, right : right + size]], axis=3)
        for left, right, size, _ in sorted(new, key=lambda entry: entry[3])
    ]
    return jnp.concatenate(parts, axis=2)


def over_replicas(block):
    count = lax.axis_size("rep")
    held = lax.optimization_barrier(block)
    if count == 2:
        other = lax.ppermute(held, "rep", [(0, 1), (1, 0)])
        return held.astype(f32) + other.astype(f32)
    return lax.psum(held.astype(f32), "rep")


def body(
    block_input, cotangent, tie_index, prefix_len, pre_gain, pre_shift, w_qkv, b_qv, w_out, b_out,
    mid_gain, mid_shift, w_fc, b_fc, w_proj, b_proj,
):
    n = lax.axis_size("fsdp")
    me = lax.axis_index("fsdp")
    pos = lax.rem(me, GROUP)
    rows = D // n
    index = tie_index[0]

    def chosen(bank):
        return lax.dynamic_index_in_dim(bank, index, 0, keepdims=False)

    vectors = (pre_gain, pre_shift, b_qv, b_out, mid_gain, mid_shift, b_fc, b_proj)
    sizes = [bank.shape[1] for bank in vectors]
    count = sum(sizes)
    high = -(-(rows + 2) // 16) * 16
    cuts = [sum(sizes[:i]) for i in range(len(sizes) + 1)]

    def vectors_of(lines):
        smalls = lines[:, 0, :count].astype(f32)
        group_rows = lax.dynamic_slice_in_dim(lines[:, 1, :2], me - pos, GROUP, 0)
        reaches = group_rows[:, 0].astype(f32) * 16 + group_rows[:, 1].astype(f32)
        return [
            smalls[:, cuts[i] : cuts[i + 1]].reshape(1, -1) for i in range(len(sizes))
        ], reaches.astype(jnp.int32)

    fused = n == BLOCKS and lax.axis_size("rep") == 2
    if fused:
        small, pieces, shard = pick(tie_index, prefix_len, vectors, w_qkv, w_out, w_fc, w_proj)
        wall, lines, wq, a_low, qx, k, v, o_full, o_recv = forward(block_input, small, pieces, shard)
        a_low = a_low.reshape(ROWS, D)
    else:
        small = jnp.concatenate([chosen(bank) for bank in vectors])
        reach = prefix_len[0]
        reach_row = jnp.concatenate([reach // 16, reach % 16]).astype(bf16)
        wq = chosen(w_qkv).reshape(rows, 3, GROUP, SLICE).transpose(2, 0, 1, 3)
        wq = wq.reshape(GROUP, rows, WIDE)
        extra = jnp.stack([jnp.pad(line, (0, WIDE - line.shape[0])) for line in (small, reach_row)])
        wo, wf, wp = chosen(w_out), chosen(w_fc), chosen(w_proj)
        extra = jnp.pad(extra, ((0, high - rows - 2), (0, 0)))
        pieces = jnp.concatenate([wq, jnp.broadcast_to(extra, (GROUP,) + extra.shape)], axis=1)
        wo = lax.all_gather(wo, "fsdp", axis=0, tiled=True).reshape(BLOCKS, -1, D)
        wf = lax.all_gather(wf, "fsdp", axis=0, tiled=True)
        wf = wf.reshape(BLOCKS, D // BLOCKS, FF // D, D).transpose(0, 2, 1, 3)
        wp = lax.all_gather(wp, "fsdp", axis=0, tiled=True).reshape(BLOCKS, -1, D)
        wall = jnp.concatenate([wp, wo, wf.reshape(BLOCKS, -1, D)], axis=1)
        xg, wg = gather_group(n, block_input, pieces)
        wq = wg[:, :rows].reshape(D, WIDE)
        found, reaches = vectors_of(wg[:, rows : rows + 2])
        g1, s1, bqv = found[:3]
        lines = jnp.concatenate([row.reshape(BLOCKS, -1) for row in found], axis=1).astype(bf16)
        lines = jnp.pad(lines[:, None], ((0, 0), (0, 1), (0, 640 - lines.shape[1])))
        own_bias = lax.dynamic_index_in_dim(bqv.reshape(2, GROUP, SLICE), pos, 1, keepdims=False)
        bias = jnp.concatenate([own_bias[0], jnp.zeros((SLICE,), f32), own_bias[1]])[None]
        a_low, q, k, v = project(xg.reshape(ROWS, D), wq, g1, s1, bias)
        o_send, o_full, qx = attend(reaches, q, k, v)
        o_recv = repack(swap(o_send, 1, "swap_o"), ((0, 384, 384, 0),), PACK)

    y, dwf, dwp, dbf, dwo, dh, do_send, sums = middle(
        block_input, o_recv, cotangent, wall, lines
    )
    if fused:
        grad, dwq, dwp, dwo, dwf, sums = backward(
            do_send, qx, k, v, o_full, a_low, wq, block_input, dh, lines, sums, dbf,
            dwp.reshape(BLOCKS, -1, D), dwo.reshape(BLOCKS, -1, D), dwf.reshape(BLOCKS, -1, D),
        )
        landed = land(sums, (grad, dwq, dwo, dwf, dwp))
        grad, dwq, dwo, dwf, dwp, dg1, ds1, dbqv, dbo, dg2, ds2, dbf, dbp = landed
        return (y, grad, dg1, ds1, dwq, dbqv, dwo, dbo, dg2, ds2, dwf, dbf, dwp, dbp)
    dwf = dwf.transpose(0, 2, 1, 3).reshape(D, FF)
    dwf = lax.psum_scatter(dwf, "fsdp", scatter_dimension=0, tiled=True)
    dwp = lax.psum_scatter(dwp, "fsdp", scatter_dimension=0, tiled=True)
    dwo = lax.psum_scatter(dwo, "fsdp", scatter_dimension=0, tiled=True)
    do_recv = repack(swap(do_send, 2, "swap_do"), PACK, ((0, 384, 384, 0),))
    dq, dk, dv = attend_back(reaches, qx, k, v, o_full, do_recv)
    dn, dwq, db = unproject(dq, dk, dv, a_low, wq)

    dn = dn.reshape(GROUP, TOK, D)
    block_of = lambda bit: lax.dynamic_index_in_dim(dn, pos ^ bit, 0, keepdims=False)
    beside = flip(block_of(1), 1)
    across = flip(block_of(3), 1)
    across = flip((across.astype(f32) + block_of(2).astype(f32)).astype(bf16), 2)

    wq_wide = wq.astype(f32)
    dshift = jnp.sum(wq_wide * db, axis=1)
    dgain = jnp.sum(wq_wide * (dwq - s1.reshape(D, 1) * db), axis=1) / g1.reshape(D)
    where = (jnp.arange(GROUP) == pos).astype(f32)[:, None]
    dbias = jnp.concatenate(
        [(where * db[:, :SLICE]).reshape(-1), (where * db[:, 2 * SLICE :]).reshape(-1)]
    )
    line = jnp.concatenate(
        [
            part.reshape(n, -1)
            for part in (dgain, dshift, dbias, sums[3], sums[1], sums[2], dbf, sums[0])
        ],
        axis=1,
    )
    line_hi = line.astype(bf16)
    line_low = (line - lax.reduce_precision(line, 8, 7)).astype(bf16)
    lines = jnp.pad(jnp.stack([line_hi, line_low], axis=1), ((0, 0), (0, 0), (0, WIDE - count)))
    lines = jnp.pad(lines, ((0, 0), (0, high - rows - 2), (0, 0)))
    back = jnp.concatenate([dwq.astype(bf16).reshape(n, rows, WIDE), lines], axis=1)
    back = swap(back, 3, "swap_grad")
    dwq = jnp.sum(back[:, :rows].astype(f32).reshape(n // GROUP, GROUP, rows, 3, SLICE), axis=0)
    dwq = dwq.transpose(1, 2, 0, 3).reshape(rows, 3 * D)
    line = jnp.sum(back[:, rows, :count].astype(f32) + back[:, rows + 1, :count].astype(f32), axis=0)

    grad = finish(block_input, dh, g1, block_of(0), beside, across)
    dwq = over_replicas(dwq.astype(bf16))
    dwo, dwf, dwp = over_replicas(dwo), over_replicas(dwf), over_replicas(dwp)
    line = over_replicas(line)
    dg1, ds1, dbqv, dbo, dg2, ds2, dbf, dbp = (
        line[cuts[i] : cuts[i + 1]] for i in range(len(sizes))
    )
    return (y, grad, dg1, ds1, dwq, dbqv, dwo, dbo, dg2, ds2, dwf, dbf, dwp, dbp)


def solution(mesh):
    tokens = P(("rep", "fsdp"), None)
    vector, matrix = P(None, "fsdp"), P(None, "fsdp", None)
    return jax.shard_map(
        body,
        mesh=mesh,
        in_specs=(
            tokens, tokens, P(), tokens, vector, vector, matrix, vector, matrix, vector,
            vector, vector, matrix, vector, matrix, vector,
        ),
        out_specs=(
            tokens, tokens, P("fsdp"), P("fsdp"), P("fsdp", None), P("fsdp"), P("fsdp", None),
            P("fsdp"), P("fsdp"), P("fsdp"), P("fsdp", None), P("fsdp"), P("fsdp", None), P("fsdp"),
        ),
        check_vma=False,
    )
```
